32 devices in a mesh: dp: 8 (over y, x, core), tensor: 4 (over z).
Axes of the slice: x: 2, y: 2, z: 4, core: 2. Of those that a mesh axis runs over, the one named last changes fastest.
Arguments:
- tokens: bfloat16 [16, 1024, 1152], P('dp', 'tensor'), may hold values from -6 to 6
- time_embed: bfloat16 [16, 4, 1152], P('dp'), may hold values from -6 to 6
- segments: int32 [16, 1024], P('dp'), may hold values from 0 to 3, as said below
- micro_order: int32 [16], P('dp'), may hold values from 0 to 1, as said below
- head_mask: int32 [16, 16], P('dp', 'tensor'), may hold values 0 or 1
- group_mask: int32 [16, 16], P('dp', 'tensor'), may hold values 0 or 1
- keep_route: int32 [16, 1024], P('dp', 'tensor'), may hold values 0 or 1
- w_qkv: bfloat16 [1152, 3456], P('dp', 'tensor'), may hold values from -0.1875 to 0.1875
- w_proj: bfloat16 [1152, 1152], P('dp', 'tensor'), may hold values from -1 to 1
- w_fc1: bfloat16 [1152, 4608], P('dp', 'tensor'), may hold values from -0.1875 to 0.1875
- w_fc2: bfloat16 [1152, 4608], P('dp', 'tensor'), may hold values from -0.09375 to 0.09375
- w_ada: bfloat16 [1152, 6912], P('dp', 'tensor'), may hold values from -0.1875 to 0.1875
- b_ada: float32 [6912], P('tensor'), may hold values from -3 to 3
- cotangent: bfloat16 [16, 1024, 1152], P('dp', 'tensor'), may hold values from -6 to 6
Outputs:
- out_tokens: bfloat16 [16, 1024, 1152], P('dp', 'tensor')
- d_tokens: bfloat16 [16, 1024, 1152], P('dp', 'tensor')
- g_qkv: float32 [1152, 3456], P('dp', 'tensor')
- g_proj: float32 [1152, 1152], P('dp', 'tensor')
- g_fc1: float32 [1152, 4608], P('dp', 'tensor')
- g_fc2: float32 [1152, 4608], P('dp', 'tensor')
- g_ada: float32 [1152, 6912], P('dp', 'tensor')
- g_bias: float32 [6912], P('tensor')
The draws below stay inside these ranges and needn't reach their ends.
Inputs may be any that keep to these rules, and one draw needn't show every extreme that they name: `segments`: within each slot the item numbers are all 0 (one item of 1024 tokens) or token i has number i // 256; both kinds occur. `micro_order`: the 2 entries of each index of dp are a permutation of 0 to 1.
All inputs are finite; a program needn't handle non-finite values. No bound on the sum of `head_mask` or of `group_mask` or of `keep_route` on one device may be relied on, other than what follows from the above.
Results may differ from the reference program's by a relative error of at most 0.022.
The reference program's roundings to bfloat16 on the way count: a program that leaves them out, or rounds other values in their place, can miss the bound.
Values may be sent and summed in bfloat16 or wider, within the bound.
A program may use at most 192 MiB of HBM per device.

```python
import jax
import jax.numpy as jnp
from jax import lax

D = 1152
HEADS = 16
HD = 72
FF = 4608
GROUPS = 16
ROWS = 1024
SEG_LEN = 256
MICRO = 2
SEGS = 4
SLOTS = 16


def draw_segments(key, part):
    kinds = jax.random.randint(key, (SLOTS,), 0, 2)
    kinds = kinds.at[0].set(0).at[1].set(1)
    positions = jnp.arange(ROWS, dtype=jnp.int32) // SEG_LEN
    return jnp.where(kinds[:, None] == 1, positions[None, :], 0).astype(jnp.int32)


def draw_micro_order(key, part):
    keys = jax.random.split(key, SLOTS // MICRO)
    perms = jax.vmap(lambda each_key: jax.random.permutation(each_key, MICRO))(keys)
    return perms.reshape(SLOTS).astype(jnp.int32)


def plant(drawn, stream_key, low, largest):
    longest = drawn.shape.index(max(drawn.shape))
    spots = []
    for shift in (0, 1):
        where = [jax.random.randint(jax.random.fold_in(stream_key, axis), (), 0, length) for axis, length in enumerate(drawn.shape)]
        where[longest] = (where[longest] + shift) % drawn.shape[longest]
        spots.append(tuple(where))
    return drawn.at[spots[0]].set(low).at[spots[1]].set(largest)


def block_scale(rng, shape, shards, low, high):
    level, own = 1.0, jax.random.fold_in(rng, 6)
    for axis_at, shards_of in shards:
        steps = jnp.exp(jax.random.uniform(jax.random.fold_in(own, axis_at), (shards_of,), jnp.float32, low / len(shards), high / len(shards)))
        level = level * jnp.repeat(steps, shape[axis_at] // shards_of).reshape([-1 if axis == axis_at else 1 for axis in range(len(shape))])
    return level


def noise(key, dims, scale, bound, shards=(), held_as=jnp.bfloat16):
    level = block_scale(key, dims, shards, -0.22, 0.18) if shards else 1.0
    values = jax.random.normal(key, dims, jnp.float32) * scale * level
    return jnp.minimum(jnp.maximum(values, -bound), bound).astype(held_as)


def setup_inputs(seed: int = 0) -> dict:
    streams_of = jax.random.split(jax.random.key(seed), 15)
    return {
        "tokens": noise(streams_of[0], (SLOTS, ROWS, D), 1.0, 6.0, ((0, 8), (1, 4))),
        "time_embed": noise(streams_of[1], (SLOTS, SEGS, D), 1.0, 6.0, ((0, 8),)),
        "segments": draw_segments(jax.random.fold_in(streams_of[14], 71), 0),
        "micro_order": draw_micro_order(jax.random.fold_in(streams_of[14], 71), 0),
        "head_mask": plant((jax.random.randint(streams_of[4], (SLOTS, HEADS), 0, 4) < 3).astype(jnp.int32), jax.random.fold_in(streams_of[4], 1), 0, 1),
        "group_mask": plant((jax.random.randint(streams_of[5], (SLOTS, GROUPS), 0, 4) < 3).astype(jnp.int32), jax.random.fold_in(streams_of[5], 1), 0, 1),
        "keep_route": plant((jax.random.randint(streams_of[6], (SLOTS, ROWS), 0, 4) < 3).astype(jnp.int32), jax.random.fold_in(streams_of[6], 1), 0, 1),
        "w_qkv": noise(streams_of[7], (D, 3 * HEADS * HD), D ** -0.5, 0.1875, ((0, 8), (1, 4))),
        "w_proj": noise(streams_of[8], (D, HEADS * HD), (HEADS * HD // 32) ** -0.5, 1.0, ((0, 8), (1, 4))),
        "w_fc1": noise(streams_of[9], (D, FF), D ** -0.5, 0.1875, ((0, 8), (1, 4))),
        "w_fc2": noise(streams_of[10], (D, FF), FF ** -0.5, 0.09375, ((0, 8), (1, 4))),
        "w_ada": noise(streams_of[11], (D, 6 * D), D ** -0.5, 0.1875, ((0, 8), (1, 4))),
        "b_ada": noise(streams_of[12], (6 * D,), 0.5, 3.0, ((0, 4),), jnp.float32),
        "cotangent": noise(streams_of[13], (SLOTS, ROWS, D), 1.0, 6.0, ((0, 8), (1, 4))),
    }


@jax.custom_vjp
def low(v):
    return lax.optimization_barrier(v.astype(jnp.bfloat16)).astype(jnp.float32)

@jax.custom_vjp
def low_back(v):
    return v

def low_keep(v):
    return (low(v), None)

def low_pass(kept, grad):
    return (grad,)

def back_keep(v):
    return (v, None)

def back_low(kept, grad):
    return (low(grad),)
low.defvjp(low_keep, low_pass)
low_back.defvjp(back_keep, back_low)
HIGH = lax.Precision.HIGHEST
EPSILON = 1e-06

def layer_norm(values):
    middle = lax.optimization_barrier(jnp.mean(values, axis=-1, keepdims=True))
    centred = values - middle
    spread = lax.optimization_barrier(jnp.mean(centred * centred, axis=-1, keepdims=True))
    return centred * lax.rsqrt(spread + EPSILON)

def slot_forward(slot_tokens, seg_ids, embed, hmask, gmask, keepf, w_qkv, w_proj, w_fc1, w_fc2, w_ada, b_ada):
    scond = low(jax.nn.silu(embed))
    mods = jnp.dot(scond, w_ada, precision=HIGH) + b_ada
    onehot = (seg_ids[:, None] == jnp.arange(SEGS, dtype=jnp.int32)[None, :]).astype(jnp.float32)
    modtok = jnp.dot(onehot, mods, precision=HIGH)
    shift1, scale1, gate1, shift2, scale2, gate2 = jnp.split(modtok, 6, axis=1)
    h_first = low(layer_norm(slot_tokens) * (1.0 + scale1) + shift1)
    packed = low_back(low(jnp.dot(h_first, w_qkv, precision=HIGH))).reshape(ROWS, HEADS, 3, HD)
    query = packed[:, :, 0]
    keys = packed[:, :, 1]
    values = packed[:, :, 2]
    block = min(512, ROWS)

    def attend(items):
        query_block, seg_block = items
        scores = low_back(jnp.einsum('qhe,khe->hqk', query_block, keys, precision=HIGH) * HD ** (-0.5))
        same = seg_block[:, None] == seg_ids[None, :]
        scores = jnp.where(same[None], scores, -1e+30)
        probs = low(jax.nn.softmax(scores, axis=-1))
        return jnp.einsum('hqk,khe->qhe', probs, values, precision=HIGH)
    outs = lax.map(jax.checkpoint(attend), (query.reshape(ROWS // block, block, HEADS, HD), seg_ids.reshape(ROWS // block, block)))
    attn = outs.reshape(ROWS, HEADS, HD) * hmask[None, :, None]
    attn = low_back(low(attn.reshape(ROWS, HEADS * HD)))
    branch = low_back(jnp.dot(attn, w_proj.T, precision=HIGH))
    first = slot_tokens + gate1 * branch
    h_second = low(layer_norm(first) * (1.0 + scale2) + shift2)
    upward = low_back(jnp.dot(h_second, w_fc1, precision=HIGH))
    act = low(jax.nn.gelu(upward, approximate=True) * gmask[None, :])
    mlp = low_back(jnp.dot(act, w_fc2.T, precision=HIGH))
    return first + gate2 * keepf[:, None] * mlp

def reference(tokens, time_embed, segments, micro_order, head_mask, group_mask, keep_route, w_qkv, w_proj, w_fc1, w_fc2, w_ada, b_ada, cotangent):
    slots = tokens.shape[0]
    mask_rows = (jnp.arange(slots, dtype=jnp.int32) // MICRO * MICRO + micro_order).astype(jnp.int32)
    hmask = head_mask[mask_rows].astype(jnp.float32)
    gmask = jnp.repeat(group_mask[mask_rows].astype(jnp.float32), FF // GROUPS, axis=1)
    keepf = keep_route.astype(jnp.float32)
    embed = time_embed.astype(jnp.float32)
    token_vals = tokens.astype(jnp.float32)
    weights = (w_qkv.astype(jnp.float32), w_proj.astype(jnp.float32), w_fc1.astype(jnp.float32), w_fc2.astype(jnp.float32), w_ada.astype(jnp.float32), b_ada.astype(jnp.float32))

    def forward(all_tokens, wq_in, wp_in, w1_in, w2_in, wa_in, ba_in):

        def run(carry, items):
            return (carry, slot_forward(*items, wq_in, wp_in, w1_in, w2_in, wa_in, ba_in))
        _, result = lax.scan(jax.checkpoint(run), jnp.zeros((), jnp.float32), (all_tokens, segments, embed, hmask, gmask, keepf))
        return result
    result, pull = jax.vjp(forward, token_vals, *weights)
    grads = pull(cotangent.astype(jnp.float32))
    return (result.astype(jnp.bfloat16), grads[0].astype(jnp.bfloat16), grads[1], grads[2], grads[3], grads[4], grads[5], grads[6])
```

```python
import jax
import jax.numpy as jnp
from jax import lax
from jax.sharding import PartitionSpec as P

HD = 72
FF = 4608
GROUPS = 16


EPSILON = 1e-06
HIGH = lax.Precision.HIGHEST


def layer_norm(values):
    middle = jnp.mean(values, axis=-1, keepdims=True)
    centred = values - middle
    spread = jnp.mean(centred * centred, axis=-1, keepdims=True)
    factor = lax.rsqrt(spread + EPSILON)
    return (centred * factor, factor)


def norm_back(grad, normed, factor):
    inner = (
        grad
        - jnp.mean(grad, axis=-1, keepdims=True)
        - normed * jnp.mean(grad * normed, axis=-1, keepdims=True)
    )
    return factor * inner


def contract_rows(left, right):
    return lax.dot_general(
        left, right, (((0,), (0,)), ((), ())), preferred_element_type=jnp.float32
    )


def contract_cols(left, right):
    return lax.dot_general(
        left, right, (((1,), (1,)), ((), ())), preferred_element_type=jnp.float32
    )


def score_block(query_block, keys, seg_block, seg_ids):
    scores = jnp.einsum(
        "qhe,khe->hqk", query_block, keys, preferred_element_type=jnp.float32
    ) * HD ** (-0.5)
    same = seg_block[:, None] == seg_ids[None, :]
    return jnp.where(same[None], scores, -1e30)


def attention_forward(query, keys, values, seg_ids):
    length = query.shape[0]
    block = min(512, length)
    outs = []
    totals = []
    for offset in range(0, length, block):
        scores = score_block(
            query[offset : offset + block], keys, seg_ids[offset : offset + block], seg_ids
        )
        peak = jnp.max(scores, axis=-1, keepdims=True)
        denom = jnp.sum(jnp.exp(scores - peak), axis=-1, keepdims=True)
        log_total = peak + jnp.log(denom)
        probs = jnp.exp(scores - log_total).astype(jnp.bfloat16)
        outs.append(jnp.einsum("hqk,khe->qhe", probs, values, preferred_element_type=jnp.float32))
        totals.append(log_total)
    return (jnp.concatenate(outs, axis=0), totals)


def attention_backward(query, keys, values, seg_ids, totals, d_attn):
    length = query.shape[0]
    block = min(512, length)
    scale = HD ** (-0.5)
    d_keys = jnp.zeros(keys.shape, jnp.float32)
    d_values = jnp.zeros(values.shape, jnp.float32)
    d_queries = []
    for number, offset in enumerate(range(0, length, block)):
        query_block = query[offset : offset + block]
        scores = score_block(query_block, keys, seg_ids[offset : offset + block], seg_ids)
        probs = jnp.exp(scores - totals[number])
        grad_block = d_attn[offset : offset + block]
        d_values = d_values + jnp.einsum(
            "hqk,qhe->khe",
            probs.astype(jnp.bfloat16),
            grad_block,
            preferred_element_type=jnp.float32,
        )
        d_probs = jnp.einsum("qhe,khe->hqk", grad_block, values, preferred_element_type=jnp.float32)
        d_scores = (probs * (d_probs - jnp.sum(probs * d_probs, axis=-1, keepdims=True))).astype(
            jnp.bfloat16
        )
        d_queries.append(
            jnp.einsum("hqk,khe->qhe", d_scores, keys, preferred_element_type=jnp.float32) * scale
        )
        d_keys = (
            d_keys
            + jnp.einsum("hqk,qhe->khe", d_scores, query_block, preferred_element_type=jnp.float32)
            * scale
        )
    stacked = jnp.stack([jnp.concatenate(d_queries, axis=0), d_keys, d_values], axis=2)
    return stacked.astype(jnp.bfloat16).reshape(length, -1)


def body(
    tokens,
    time_embed,
    segments,
    micro_order,
    head_mask,
    group_mask,
    keep_route,
    w_qkv,
    w_proj,
    w_fc1,
    w_fc2,
    w_ada,
    b_ada,
    cotangent,
):
    micro = tokens.shape[0]
    local_rows = tokens.shape[1]
    length = segments.shape[1]
    heads_here = head_mask.shape[1]
    segs = time_embed.shape[1]
    tensor_index = lax.axis_index("tensor")
    chooser = (micro_order[:, None] == jnp.arange(micro, dtype=jnp.int32)[None, :]).astype(
        jnp.float32
    )
    head_sel = jnp.dot(chooser, head_mask.astype(jnp.float32), precision=HIGH)
    group_sel = jnp.repeat(
        jnp.dot(chooser, group_mask.astype(jnp.float32), precision=HIGH), FF // GROUPS, axis=1
    )
    keep_float = keep_route.astype(jnp.float32)

    def reduce_grads(grad_qkv, grad_proj, grad_fc1, grad_fc2, grad_ada):
        return (
            lax.psum_scatter(
                grad_qkv.astype(jnp.bfloat16), "dp", scatter_dimension=0, tiled=True
            ).astype(jnp.float32),
            lax.psum_scatter(
                grad_proj.astype(jnp.bfloat16), "dp", scatter_dimension=0, tiled=True
            ).astype(jnp.float32),
            lax.psum_scatter(
                grad_fc1.astype(jnp.bfloat16), "dp", scatter_dimension=0, tiled=True
            ).astype(jnp.float32),
            lax.psum_scatter(
                grad_fc2.astype(jnp.bfloat16), "dp", scatter_dimension=0, tiled=True
            ).astype(jnp.float32),
            lax.psum_scatter(
                grad_ada.astype(jnp.bfloat16), "dp", scatter_dimension=0, tiled=True
            ).astype(jnp.float32),
        )

    shard_shapes = [w.shape for w in (w_qkv, w_proj, w_fc1, w_fc2, w_ada)]
    start_acc = tuple((jnp.zeros(shape, jnp.float32) for shape in shard_shapes))

    def slot_step(carry, items):
        acc, bias_acc = carry
        slot_tokens, slot_grad, seg_ids, embed, hmask, gcols, keepf = items
        full = (
            lax.all_gather(w_qkv, "dp", axis=0, tiled=True),
            lax.all_gather(w_proj, "dp", axis=0, tiled=True),
            lax.all_gather(w_fc1, "dp", axis=0, tiled=True),
            lax.all_gather(w_fc2, "dp", axis=0, tiled=True),
            lax.all_gather(w_ada, "dp", axis=0, tiled=True),
        )
        full_qkv, full_proj, full_fc1, full_fc2, full_ada = full
        seg_local = lax.dynamic_slice_in_dim(seg_ids, tensor_index * local_rows, local_rows)
        scond = jax.nn.silu(embed.astype(jnp.float32)).astype(jnp.bfloat16)
        part_mods = jnp.dot(scond, full_ada, preferred_element_type=jnp.float32) + b_ada[None, :]
        mods = lax.all_gather(part_mods, "tensor", axis=1, tiled=True)
        onehot = (seg_local[:, None] == jnp.arange(segs, dtype=jnp.int32)[None, :]).astype(
            jnp.float32
        )
        modtok = jnp.dot(onehot, mods, precision=HIGH)
        shift1, scale1, gate1, shift2, scale2, gate2 = jnp.split(modtok, 6, axis=1)
        token_vals = slot_tokens.astype(jnp.float32)
        normed1, factor1 = layer_norm(token_vals)
        h_first = lax.all_gather(
            (normed1 * (1.0 + scale1) + shift1).astype(jnp.bfloat16), "tensor", axis=0, tiled=True
        )
        packed = jnp.dot(h_first, full_qkv, preferred_element_type=jnp.float32).astype(jnp.bfloat16)
        packed = packed.reshape(length, heads_here, 3, HD)
        query = packed[:, :, 0]
        keys = packed[:, :, 1]
        values = packed[:, :, 2]
        outs, totals = attention_forward(query, keys, values, seg_ids)
        attn = (outs * hmask[None, :, None]).astype(jnp.bfloat16).reshape(length, heads_here * HD)
        branch = lax.psum_scatter(
            contract_cols(attn, full_proj).astype(jnp.bfloat16),
            "tensor",
            scatter_dimension=0,
            tiled=True,
        ).astype(jnp.float32)
        first = token_vals + gate1 * branch
        normed2, factor2 = layer_norm(first)
        h_second = lax.all_gather(
            (normed2 * (1.0 + scale2) + shift2).astype(jnp.bfloat16), "tensor", axis=0, tiled=True
        )
        upward = jnp.dot(h_second, full_fc1, preferred_element_type=jnp.float32)
        gelu_val, gelu_pull = jax.vjp(lambda inner: jax.nn.gelu(inner, approximate=True), upward)
        act = (gelu_val * gcols[None, :]).astype(jnp.bfloat16)
        mlp = lax.psum_scatter(
            contract_cols(act, full_fc2).astype(jnp.bfloat16),
            "tensor",
            scatter_dimension=0,
            tiled=True,
        ).astype(jnp.float32)
        keep_col = keepf[:, None]
        result = (first + gate2 * keep_col * mlp).astype(jnp.bfloat16)
        grad_out = slot_grad.astype(jnp.float32)
        d_mlp = lax.all_gather(
            (gate2 * keep_col * grad_out).astype(jnp.bfloat16), "tensor", axis=0, tiled=True
        )
        grad_fc2 = contract_rows(d_mlp, act)
        d_act = jnp.dot(d_mlp, full_fc2, preferred_element_type=jnp.float32)
        d_up = gelu_pull(d_act * gcols[None, :])[0].astype(jnp.bfloat16)
        grad_fc1 = contract_rows(h_second, d_up)
        d_second = lax.psum_scatter(
            contract_cols(d_up, full_fc1).astype(jnp.bfloat16),
            "tensor",
            scatter_dimension=0,
            tiled=True,
        ).astype(jnp.float32)
        d_first = grad_out + norm_back(d_second * (1.0 + scale2), normed2, factor2)
        d_branch = lax.all_gather(
            (gate1 * d_first).astype(jnp.bfloat16), "tensor", axis=0, tiled=True
        )
        grad_proj = contract_rows(d_branch, attn)
        d_attn = jnp.dot(d_branch, full_proj, preferred_element_type=jnp.float32).astype(
            jnp.bfloat16
        )
        d_attn = d_attn.reshape(length, heads_here, HD) * hmask[None, :, None].astype(jnp.bfloat16)
        d_packed = attention_backward(query, keys, values, seg_ids, totals, d_attn)
        grad_qkv = contract_rows(h_first, d_packed)
        d_h_first = lax.psum_scatter(
            contract_cols(d_packed, full_qkv).astype(jnp.bfloat16),
            "tensor",
            scatter_dimension=0,
            tiled=True,
        ).astype(jnp.float32)
        d_input = d_first + norm_back(d_h_first * (1.0 + scale1), normed1, factor1)
        d_modtok = jnp.concatenate(
            [
                d_h_first,
                d_h_first * normed1,
                d_first * branch,
                d_second,
                d_second * normed2,
                grad_out * keep_col * mlp,
            ],
            axis=1,
        )
        part_dmods = lax.dot_general(onehot, d_modtok, (((0,), (0,)), ((), ())), precision=HIGH)
        d_mods = lax.psum_scatter(
            part_dmods.astype(jnp.bfloat16), "tensor", scatter_dimension=1, tiled=True
        ).astype(jnp.float32)
        grad_ada = jnp.dot(scond.astype(jnp.float32).T, d_mods, precision=HIGH)
        bias_acc = bias_acc + jnp.sum(d_mods, axis=0)
        parts = reduce_grads(grad_qkv, grad_proj, grad_fc1, grad_fc2, grad_ada)
        acc = tuple((held + piece for held, piece in zip(acc, parts)))
        return ((acc, bias_acc), (result, d_input.astype(jnp.bfloat16)))

    start_bias = jnp.zeros(b_ada.shape, jnp.float32)
    (acc, bias_acc), (results, d_tokens) = lax.scan(
        slot_step,
        (start_acc, start_bias),
        (tokens, cotangent, segments, time_embed, head_sel, group_sel, keep_float),
    )
    g_bias = lax.psum(bias_acc, "dp")
    return (results, d_tokens, acc[0], acc[1], acc[2], acc[3], acc[4], g_bias)


AX = ("dp", "tensor")


def route(value, where):
    return lax.ppermute(value, AX, [(d * 4 + t, where(d, t)) for d in range(8) for t in range(4)])


def sibling(value):
    return route(value, lambda d, t: (d ^ 1) * 4 + t)


def over_x(value):
    return route(value, lambda d, t: (d ^ 2) * 4 + t)


def over_y(value):
    return route(value, lambda d, t: (d ^ 4) * 4 + t)


def deal_to(step):
    def where(d, t):
        slot = (t % 2 + step) % 2
        return ((d // 2) * 2 + t // 2) * 4 + 2 * (d % 2) + slot

    return where


def deal_back(step):
    forward = deal_to(step)
    back = {forward(d, t): d * 4 + t for d in range(8) for t in range(4)}
    return lambda d, t: back[d * 4 + t]


def pick(value, index):
    return lax.dynamic_index_in_dim(value, index, 0, keepdims=False)


def order(flag, first, second, axis=0):
    swapped = flag == 1
    return jnp.concatenate(
        [jnp.where(swapped, second, first), jnp.where(swapped, first, second)], axis=axis
    )


def deal(value, odd):
    parts = [route(pick(value, (odd + step) % 2), deal_to(step)) for step in range(2)]
    return order(odd, parts[0][None], parts[1][None])


def undeal(value, odd):
    parts = [route(pick(value, (odd + step) % 2), deal_back(step)) for step in range(2)]
    return order(odd, parts[0][None], parts[1][None])


def gather_weights(units, core, chip):
    lines = lax.all_gather(units, "tensor", axis=0, tiled=False)
    halves = lines.reshape(2, 2, *units.shape)
    mine = pick(halves, core)
    other = sibling(pick(halves, 1 - core))
    block = order(core, mine[:, :, None], other[:, :, None], axis=2)
    block = block.transpose(1, 0, 2, 3, 4)
    from_x = over_x(block)
    from_y = over_y(block)
    far = jnp.concatenate([over_y(from_x[:, :1]), over_x(from_y[:, 1:])], axis=1)
    odd_x, odd_y = chip % 2, chip // 2
    row_here = order(odd_x, block[:, :, None], from_x[:, :, None], axis=2)
    row_there = order(odd_x, from_y[:, :, None], far[:, :, None], axis=2)
    whole = order(odd_y, row_here[:, :, None], row_there[:, :, None], axis=2)
    return whole.reshape(units.shape[0], 2, 8 * units.shape[1], units.shape[2])


def scatter_grad(grad, core, chip):
    rows = grad.shape[1] // 8
    blocks = grad.reshape(2, 4, 2, rows, grad.shape[2]).transpose(1, 0, 2, 3, 4)
    own = pick(blocks, chip)
    to_x = pick(blocks, chip ^ 1)
    to_y = pick(blocks, chip ^ 2)
    far = pick(blocks, chip ^ 3)
    add = lambda one, two: (one.astype(jnp.float32) + two.astype(jnp.float32)).astype(jnp.bfloat16)
    via_x = over_x(far[0])
    via_y = over_y(far[1])
    got_y = over_y(jnp.stack([add(to_y[0], via_x), to_y[1]]))
    got_x = over_x(jnp.stack([to_x[0], add(to_x[1], via_y)]))
    total = (
        own.astype(jnp.float32) + got_x.astype(jnp.float32) + got_y.astype(jnp.float32)
    ).astype(jnp.bfloat16)
    total = total.transpose(1, 0, 2, 3)
    mine = pick(total, core)
    other = sibling(pick(total, 1 - core))
    lines = order(core, mine, other)
    return lax.psum_scatter(lines, "tensor", scatter_dimension=0, tiled=False).astype(jnp.float32)


def fast_body(
    tokens,
    time_embed,
    segments,
    micro_order,
    head_mask,
    group_mask,
    keep_route,
    w_qkv,
    w_proj,
    w_fc1,
    w_fc2,
    w_ada,
    b_ada,
    cotangent,
):
    dp = lax.axis_index("dp")
    line = lax.axis_index("tensor")
    core = dp % 2
    chip = dp // 2
    odd = line % 2
    owner = line // 2
    segs = time_embed.shape[1]
    part = tokens.shape[1]
    width = tokens.shape[2]
    length = segments.shape[1]
    qcols = w_qkv.shape[1]
    heads_here = head_mask.shape[1]

    hsel = head_mask[micro_order]
    gsel = group_mask[micro_order]
    packed_meta = jnp.concatenate([hsel, gsel, keep_route], axis=1)
    meta = lax.all_gather(packed_meta, "tensor", axis=0, tiled=False)
    meta_other, seg_other = sibling(meta), sibling(segments)
    meta = pick(jnp.where(core == owner, meta, meta_other).transpose(1, 0, 2), odd)
    seg_ids = pick(jnp.where(core == owner, segments, seg_other), odd)
    hmask = lax.dynamic_slice_in_dim(meta[:, :heads_here], 2 * core, 2).astype(jnp.float32)
    gmask = lax.dynamic_slice_in_dim(meta[:, heads_here : 2 * heads_here], 2 * core, 2)
    gcols = jnp.repeat(gmask.astype(jnp.float32), FF // GROUPS, axis=1)
    keepf = lax.dynamic_slice_in_dim(meta[:, 2 * heads_here :], 2 * core, 2).astype(jnp.float32)
    keep_col = keepf[:, :, None]

    te_all = lax.all_gather(time_embed, "dp", axis=0, tiled=True).reshape(-1, width)
    scond = jax.nn.silu(te_all.astype(jnp.float32)).astype(jnp.bfloat16)
    scond_rows = lax.dynamic_slice_in_dim(scond, dp * w_ada.shape[0], w_ada.shape[0], axis=1)
    part_mods = jnp.dot(scond_rows, w_ada, preferred_element_type=jnp.float32)
    my_mods = lax.psum_scatter(part_mods, "dp", scatter_dimension=0, tiled=True) + b_ada[None, :]
    line_mods = lax.all_gather(my_mods, "tensor", axis=1, tiled=True)
    other_mods = sibling(line_mods)
    mods = pick(jnp.where(core == owner, line_mods, other_mods).reshape(2, segs, -1), odd)
    block_item = lax.dynamic_slice_in_dim(seg_ids[:: length // 4], 2 * core, 2)
    modtok = mods[block_item][:, None, :]
    shift1, scale1, gate1, shift2, scale2, gate2 = jnp.split(modtok, 6, axis=2)

    units = jnp.stack([jnp.concatenate([w_qkv, w_proj], axis=1), w_fc1, w_fc2])
    weights = gather_weights(units, core, chip)
    full_qkv = weights[0, :, :, :qcols]
    full_proj = weights[0, :, :, qcols:]
    full_fc1 = weights[1]
    full_fc2 = weights[2]

    token_vals = deal(tokens, odd).astype(jnp.float32)
    grad_out = deal(cotangent, odd).astype(jnp.float32)

    def share(value):
        rows = value.astype(jnp.bfloat16).reshape(2 * part, width)
        return order(core, rows, sibling(rows))

    def collect(partial):
        theirs = lax.dynamic_slice_in_dim(partial, (1 - core) * 2 * part, 2 * part)
        mine = lax.dynamic_slice_in_dim(partial, core * 2 * part, 2 * part)
        got = sibling(theirs.astype(jnp.bfloat16)).astype(jnp.float32)
        return (mine + got).reshape(2, part, width)

    d_mlp = share(gate2 * keep_col * grad_out)
    normed1, factor1 = layer_norm(token_vals)
    h_first = share(normed1 * (1.0 + scale1) + shift1)
    packed = jnp.einsum("rd,zdc->rzc", h_first, full_qkv, preferred_element_type=jnp.float32)
    packed = packed.astype(jnp.bfloat16).reshape(length, 2 * heads_here, 3, HD)
    query, keys, values = packed[:, :, 0], packed[:, :, 1], packed[:, :, 2]
    outs, totals = attention_forward(query, keys, values, seg_ids)
    hm = hmask.reshape(-1)[None, :, None]
    attn = (outs * hm).astype(jnp.bfloat16).reshape(length, 2, heads_here * HD)
    branch = collect(
        jnp.einsum("rzk,zok->ro", attn, full_proj, preferred_element_type=jnp.float32)
    )
    first = token_vals + gate1 * branch
    normed2, factor2 = layer_norm(first)
    h_second = share(normed2 * (1.0 + scale2) + shift2)
    upward = jnp.einsum("rd,zdu->zru", h_second, full_fc1, preferred_element_type=jnp.float32)
    gelu_val, gelu_pull = jax.vjp(lambda inner: jax.nn.gelu(inner, approximate=True), upward)
    act = (gelu_val * gcols[:, None, :]).astype(jnp.bfloat16)
    mlp = collect(jnp.einsum("zru,zou->ro", act, full_fc2, preferred_element_type=jnp.float32))
    result = (first + gate2 * keep_col * mlp).astype(jnp.bfloat16)

    grad_fc2 = jnp.einsum("ro,zru->zou", d_mlp, act, preferred_element_type=jnp.float32)
    g_fc2 = scatter_grad(grad_fc2.astype(jnp.bfloat16), core, chip)
    d_act = jnp.einsum("ro,zou->zru", d_mlp, full_fc2, preferred_element_type=jnp.float32)
    d_up = gelu_pull(d_act * gcols[:, None, :])[0].astype(jnp.bfloat16)
    grad_fc1 = jnp.einsum("rd,zru->zdu", h_second, d_up, preferred_element_type=jnp.float32)
    g_fc1 = scatter_grad(grad_fc1.astype(jnp.bfloat16), core, chip)
    d_second = collect(
        jnp.einsum("zru,zdu->rd", d_up, full_fc1, preferred_element_type=jnp.float32)
    )
    d_first = grad_out + norm_back(d_second * (1.0 + scale2), normed2, factor2)
    d_branch = share(gate1 * d_first)
    grad_proj = jnp.einsum("ro,rzk->zok", d_branch, attn, preferred_element_type=jnp.float32)
    d_attn = jnp.einsum("ro,zok->rzk", d_branch, full_proj, preferred_element_type=jnp.float32)
    d_attn = d_attn.astype(jnp.bfloat16).reshape(length, 2 * heads_here, HD)
    d_attn = d_attn * hm.astype(jnp.bfloat16)
    d_packed = attention_backward(query, keys, values, seg_ids, totals, d_attn)
    d_packed = d_packed.reshape(length, 2, qcols)
    grad_qkv = jnp.einsum("rd,rzc->zdc", h_first, d_packed, preferred_element_type=jnp.float32)
    grad_head = jnp.concatenate([grad_qkv, grad_proj], axis=2).astype(jnp.bfloat16)
    g_head = scatter_grad(grad_head, core, chip)
    d_h_first = collect(
        jnp.einsum("rzc,zdc->rd", d_packed, full_qkv, preferred_element_type=jnp.float32)
    )
    d_input = d_first + norm_back(d_h_first * (1.0 + scale1), normed1, factor1)

    sums = jnp.concatenate(
        [
            jnp.sum(v, axis=1)
            for v in (
                d_h_first,
                d_h_first * normed1,
                d_first * branch,
                d_second,
                d_second * normed2,
                grad_out * keep_col * mlp,
            )
        ],
        axis=1,
    )
    onehot = (block_item[None, :] == jnp.arange(segs, dtype=jnp.int32)[:, None]).astype(jnp.float32)
    d_mods = jnp.sum(onehot[:, :, None] * sums[None], axis=1)
    cols = b_ada.shape[0]
    d_lines = lax.all_to_all(
        d_mods.reshape(segs, -1, cols).transpose(1, 0, 2), "tensor", 0, 0, tiled=False
    )
    d_all = lax.all_gather(d_lines, "dp", axis=0, tiled=False)
    d_all = d_all.reshape(-1, 2, *d_lines.shape).sum(axis=1).reshape(-1, cols)
    g_ada = jnp.dot(scond_rows.astype(jnp.float32).T, d_all, precision=HIGH)
    g_bias = jnp.sum(d_all, axis=0)

    return (
        undeal(result, odd),
        undeal(d_input.astype(jnp.bfloat16), odd),
        g_head[:, :qcols],
        g_head[:, qcols:],
        g_fc1,
        g_fc2,
        g_ada,
        g_bias,
    )


def solution(mesh):
    placed = (
        P("dp", "tensor", None),
        P("dp", None, None),
        P("dp", None),
        P("dp"),
        P("dp", "tensor"),
        P("dp", "tensor"),
        P("dp", "tensor"),
        P("dp", "tensor"),
        P("dp", "tensor"),
        P("dp", "tensor"),
        P("dp", "tensor"),
        P("dp", "tensor"),
        P("tensor"),
        P("dp", "tensor", None),
    )
    return jax.shard_map(
        fast_body if mesh.shape["dp"] == 8 and mesh.shape["tensor"] == 4 else body,
        mesh=mesh,
        in_specs=placed,
        out_specs=(
            P("dp", "tensor", None),
            P("dp", "tensor", None),
            P("dp", "tensor"),
            P("dp", "tensor"),
            P("dp", "tensor"),
            P("dp", "tensor"),
            P("dp", "tensor"),
            P("tensor"),
        ),
        check_vma=False,
    )
```

```python
import jax
import jax.numpy as jnp
from jax import lax
from jax.experimental import pallas as pl
from jax.experimental.pallas import tpu as pltpu
from jax.sharding import PartitionSpec as P

HD = 72
FF = 4608
GROUPS = 16


EPSILON = 1e-06
HIGH = lax.Precision.HIGHEST


def layer_norm(values):
    middle = jnp.mean(values, axis=-1, keepdims=True)
    centred = values - middle
    spread = jnp.mean(centred * centred, axis=-1, keepdims=True)
    factor = lax.rsqrt(spread + EPSILON)
    return (centred * factor, factor)


def norm_back(grad, normed, factor):
    inner = (
        grad
        - jnp.mean(grad, axis=-1, keepdims=True)
        - normed * jnp.mean(grad * normed, axis=-1, keepdims=True)
    )
    return factor * inner


def contract_rows(left, right):
    return lax.dot_general(
        left, right, (((0,), (0,)), ((), ())), preferred_element_type=jnp.float32
    )


def contract_cols(left, right):
    return lax.dot_general(
        left, right, (((1,), (1,)), ((), ())), preferred_element_type=jnp.float32
    )


def score_block(query_block, keys, seg_block, seg_ids):
    scores = jnp.einsum(
        "qhe,khe->hqk", query_block, keys, preferred_element_type=jnp.float32
    ) * HD ** (-0.5)
    same = seg_block[:, None] == seg_ids[None, :]
    return jnp.where(same[None], scores, -1e30)


def attention_forward(query, keys, values, seg_ids):
    length = query.shape[0]
    block = min(512, length)
    outs = []
    totals = []
    for offset in range(0, length, block):
        scores = score_block(
            query[offset : offset + block], keys, seg_ids[offset : offset + block], seg_ids
        )
        peak = jnp.max(scores, axis=-1, keepdims=True)
        denom = jnp.sum(jnp.exp(scores - peak), axis=-1, keepdims=True)
        log_total = peak + jnp.log(denom)
        probs = jnp.exp(scores - log_total).astype(jnp.bfloat16)
        outs.append(jnp.einsum("hqk,khe->qhe", probs, values, preferred_element_type=jnp.float32))
        totals.append(log_total)
    return (jnp.concatenate(outs, axis=0), totals)


def attention_backward(query, keys, values, seg_ids, totals, d_attn):
    length = query.shape[0]
    block = min(512, length)
    scale = HD ** (-0.5)
    d_keys = jnp.zeros(keys.shape, jnp.float32)
    d_values = jnp.zeros(values.shape, jnp.float32)
    d_queries = []
    for number, offset in enumerate(range(0, length, block)):
        query_block = query[offset : offset + block]
        scores = score_block(query_block, keys, seg_ids[offset : offset + block], seg_ids)
        probs = jnp.exp(scores - totals[number])
        grad_block = d_attn[offset : offset + block]
        d_values = d_values + jnp.einsum(
            "hqk,qhe->khe",
            probs.astype(jnp.bfloat16),
            grad_block,
            preferred_element_type=jnp.float32,
        )
        d_probs = jnp.einsum("qhe,khe->hqk", grad_block, values, preferred_element_type=jnp.float32)
        d_scores = (probs * (d_probs - jnp.sum(probs * d_probs, axis=-1, keepdims=True))).astype(
            jnp.bfloat16
        )
        d_queries.append(
            jnp.einsum("hqk,khe->qhe", d_scores, keys, preferred_element_type=jnp.float32) * scale
        )
        d_keys = (
            d_keys
            + jnp.einsum("hqk,qhe->khe", d_scores, query_block, preferred_element_type=jnp.float32)
            * scale
        )
    stacked = jnp.stack([jnp.concatenate(d_queries, axis=0), d_keys, d_values], axis=2)
    return stacked.astype(jnp.bfloat16).reshape(length, -1)


def body(
    tokens,
    time_embed,
    segments,
    micro_order,
    head_mask,
    group_mask,
    keep_route,
    w_qkv,
    w_proj,
    w_fc1,
    w_fc2,
    w_ada,
    b_ada,
    cotangent,
):
    micro = tokens.shape[0]
    local_rows = tokens.shape[1]
    length = segments.shape[1]
    heads_here = head_mask.shape[1]
    segs = time_embed.shape[1]
    tensor_index = lax.axis_index("tensor")
    chooser = (micro_order[:, None] == jnp.arange(micro, dtype=jnp.int32)[None, :]).astype(
        jnp.float32
    )
    head_sel = jnp.dot(chooser, head_mask.astype(jnp.float32), precision=HIGH)
    group_sel = jnp.repeat(
        jnp.dot(chooser, group_mask.astype(jnp.float32), precision=HIGH), FF // GROUPS, axis=1
    )
    keep_float = keep_route.astype(jnp.float32)

    def reduce_grads(grad_qkv, grad_proj, grad_fc1, grad_fc2, grad_ada):
        return (
            lax.psum_scatter(
                grad_qkv.astype(jnp.bfloat16), "dp", scatter_dimension=0, tiled=True
            ).astype(jnp.float32),
            lax.psum_scatter(
                grad_proj.astype(jnp.bfloat16), "dp", scatter_dimension=0, tiled=True
            ).astype(jnp.float32),
            lax.psum_scatter(
                grad_fc1.astype(jnp.bfloat16), "dp", scatter_dimension=0, tiled=True
            ).astype(jnp.float32),
            lax.psum_scatter(
                grad_fc2.astype(jnp.bfloat16), "dp", scatter_dimension=0, tiled=True
            ).astype(jnp.float32),
            lax.psum_scatter(
                grad_ada.astype(jnp.bfloat16), "dp", scatter_dimension=0, tiled=True
            ).astype(jnp.float32),
        )

    shard_shapes = [w.shape for w in (w_qkv, w_proj, w_fc1, w_fc2, w_ada)]
    start_acc = tuple((jnp.zeros(shape, jnp.float32) for shape in shard_shapes))

    def slot_step(carry, items):
        acc, bias_acc = carry
        slot_tokens, slot_grad, seg_ids, embed, hmask, gcols, keepf = items
        full = (
            lax.all_gather(w_qkv, "dp", axis=0, tiled=True),
            lax.all_gather(w_proj, "dp", axis=0, tiled=True),
            lax.all_gather(w_fc1, "dp", axis=0, tiled=True),
            lax.all_gather(w_fc2, "dp", axis=0, tiled=True),
            lax.all_gather(w_ada, "dp", axis=0, tiled=True),
        )
        full_qkv, full_proj, full_fc1, full_fc2, full_ada = full
        seg_local = lax.dynamic_slice_in_dim(seg_ids, tensor_index * local_rows, local_rows)
        scond = jax.nn.silu(embed.astype(jnp.float32)).astype(jnp.bfloat16)
        part_mods = jnp.dot(scond, full_ada, preferred_element_type=jnp.float32) + b_ada[None, :]
        mods = lax.all_gather(part_mods, "tensor", axis=1, tiled=True)
        onehot = (seg_local[:, None] == jnp.arange(segs, dtype=jnp.int32)[None, :]).astype(
            jnp.float32
        )
        modtok = jnp.dot(onehot, mods, precision=HIGH)
        shift1, scale1, gate1, shift2, scale2, gate2 = jnp.split(modtok, 6, axis=1)
        token_vals = slot_tokens.astype(jnp.float32)
        normed1, factor1 = layer_norm(token_vals)
        h_first = lax.all_gather(
            (normed1 * (1.0 + scale1) + shift1).astype(jnp.bfloat16), "tensor", axis=0, tiled=True
        )
        packed = jnp.dot(h_first, full_qkv, preferred_element_type=jnp.float32).astype(jnp.bfloat16)
        packed = packed.reshape(length, heads_here, 3, HD)
        query = packed[:, :, 0]
        keys = packed[:, :, 1]
        values = packed[:, :, 2]
        outs, totals = attention_forward(query, keys, values, seg_ids)
        attn = (outs * hmask[None, :, None]).astype(jnp.bfloat16).reshape(length, heads_here * HD)
        branch = lax.psum_scatter(
            contract_cols(attn, full_proj).astype(jnp.bfloat16),
            "tensor",
            scatter_dimension=0,
            tiled=True,
        ).astype(jnp.float32)
        first = token_vals + gate1 * branch
        normed2, factor2 = layer_norm(first)
        h_second = lax.all_gather(
            (normed2 * (1.0 + scale2) + shift2).astype(jnp.bfloat16), "tensor", axis=0, tiled=True
        )
        upward = jnp.dot(h_second, full_fc1, preferred_element_type=jnp.float32)
        gelu_val, gelu_pull = jax.vjp(lambda inner: jax.nn.gelu(inner, approximate=True), upward)
        act = (gelu_val * gcols[None, :]).astype(jnp.bfloat16)
        mlp = lax.psum_scatter(
            contract_cols(act, full_fc2).astype(jnp.bfloat16),
            "tensor",
            scatter_dimension=0,
            tiled=True,
        ).astype(jnp.float32)
        keep_col = keepf[:, None]
        result = (first + gate2 * keep_col * mlp).astype(jnp.bfloat16)
        grad_out = slot_grad.astype(jnp.float32)
        d_mlp = lax.all_gather(
            (gate2 * keep_col * grad_out).astype(jnp.bfloat16), "tensor", axis=0, tiled=True
        )
        grad_fc2 = contract_rows(d_mlp, act)
        d_act = jnp.dot(d_mlp, full_fc2, preferred_element_type=jnp.float32)
        d_up = gelu_pull(d_act * gcols[None, :])[0].astype(jnp.bfloat16)
        grad_fc1 = contract_rows(h_second, d_up)
        d_second = lax.psum_scatter(
            contract_cols(d_up, full_fc1).astype(jnp.bfloat16),
            "tensor",
            scatter_dimension=0,
            tiled=True,
        ).astype(jnp.float32)
        d_first = grad_out + norm_back(d_second * (1.0 + scale2), normed2, factor2)
        d_branch = lax.all_gather(
            (gate1 * d_first).astype(jnp.bfloat16), "tensor", axis=0, tiled=True
        )
        grad_proj = contract_rows(d_branch, attn)
        d_attn = jnp.dot(d_branch, full_proj, preferred_element_type=jnp.float32).astype(
            jnp.bfloat16
        )
        d_attn = d_attn.reshape(length, heads_here, HD) * hmask[None, :, None].astype(jnp.bfloat16)
        d_packed = attention_backward(query, keys, values, seg_ids, totals, d_attn)
        grad_qkv = contract_rows(h_first, d_packed)
        d_h_first = lax.psum_scatter(
            contract_cols(d_packed, full_qkv).astype(jnp.bfloat16),
            "tensor",
            scatter_dimension=0,
            tiled=True,
        ).astype(jnp.float32)
        d_input = d_first + norm_back(d_h_first * (1.0 + scale1), normed1, factor1)
        d_modtok = jnp.concatenate(
            [
                d_h_first,
                d_h_first * normed1,
                d_first * branch,
                d_second,
                d_second * normed2,
                grad_out * keep_col * mlp,
            ],
            axis=1,
        )
        part_dmods = lax.dot_general(onehot, d_modtok, (((0,), (0,)), ((), ())), precision=HIGH)
        d_mods = lax.psum_scatter(
            part_dmods.astype(jnp.bfloat16), "tensor", scatter_dimension=1, tiled=True
        ).astype(jnp.float32)
        grad_ada = jnp.dot(scond.astype(jnp.float32).T, d_mods, precision=HIGH)
        bias_acc = bias_acc + jnp.sum(d_mods, axis=0)
        parts = reduce_grads(grad_qkv, grad_proj, grad_fc1, grad_fc2, grad_ada)
        acc = tuple((held + piece for held, piece in zip(acc, parts)))
        return ((acc, bias_acc), (result, d_input.astype(jnp.bfloat16)))

    start_bias = jnp.zeros(b_ada.shape, jnp.float32)
    (acc, bias_acc), (results, d_tokens) = lax.scan(
        slot_step,
        (start_acc, start_bias),
        (tokens, cotangent, segments, time_embed, head_sel, group_sel, keep_float),
    )
    g_bias = lax.psum(bias_acc, "dp")
    return (results, d_tokens, acc[0], acc[1], acc[2], acc[3], acc[4], g_bias)


AX = ("dp", "tensor")


def route(value, where):
    return lax.ppermute(value, AX, [(d * 4 + t, where(d, t)) for d in range(8) for t in range(4)])


def sibling(value):
    return route(value, lambda d, t: (d ^ 1) * 4 + t)


def over_x(value):
    return route(value, lambda d, t: (d ^ 2) * 4 + t)


def over_y(value):
    return route(value, lambda d, t: (d ^ 4) * 4 + t)


def deal_to(step):
    def where(d, t):
        slot = (t % 2 + step) % 2
        return ((d // 2) * 2 + t // 2) * 4 + 2 * (d % 2) + slot

    return where


def deal_back(step):
    forward = deal_to(step)
    back = {forward(d, t): d * 4 + t for d in range(8) for t in range(4)}
    return lambda d, t: back[d * 4 + t]


def pick(value, index):
    return lax.dynamic_index_in_dim(value, index, 0, keepdims=False)


def order(flag, first, second, axis=0):
    swapped = flag == 1
    return jnp.concatenate(
        [jnp.where(swapped, second, first), jnp.where(swapped, first, second)], axis=axis
    )


def undeal(value, odd):
    parts = [route(pick(value, (odd + step) % 2), deal_back(step)) for step in range(2)]
    return order(odd, parts[0][None], parts[1][None])


def scatter_grad(grad, core, chip):
    rows = grad.shape[1] // 8
    blocks = grad.reshape(2, 4, 2, rows, grad.shape[2]).transpose(1, 0, 2, 3, 4)
    own = pick(blocks, chip)
    to_x = pick(blocks, chip ^ 1)
    to_y = pick(blocks, chip ^ 2)
    far = pick(blocks, chip ^ 3)
    add = lambda one, two: (one.astype(jnp.float32) + two.astype(jnp.float32)).astype(jnp.bfloat16)
    via_x = over_x(far[0])
    via_y = over_y(far[1])
    got_y = over_y(jnp.stack([add(to_y[0], via_x), to_y[1]]))
    got_x = over_x(jnp.stack([to_x[0], add(to_x[1], via_y)]))
    total = (
        own.astype(jnp.float32) + got_x.astype(jnp.float32) + got_y.astype(jnp.float32)
    ).astype(jnp.bfloat16)
    total = total.transpose(1, 0, 2, 3)
    mine = pick(total, core)
    other = sibling(pick(total, 1 - core))
    lines = order(core, mine, other)
    return lax.psum_scatter(lines, "tensor", scatter_dimension=0, tiled=False).astype(jnp.float32)


MESH = pl.DeviceIdType.MESH
ANY = pl.BlockSpec(memory_space=pl.ANY)
DMA = pltpu.SemaphoreType.DMA


class Place:
    def __init__(self):
        self.dp = lax.axis_index("dp")
        self.line = lax.axis_index("tensor")
        self.core = self.dp % 2
        self.base = self.dp - self.core
        self.half = self.line // 2
        x, y = (self.dp // 2) % 2, self.dp // 4
        self.dp_x = self.dp + 2 * (1 - 2 * x)
        self.dp_y = self.dp + 4 * (1 - 2 * y)
        self.base_x = self.dp_x - self.core
        self.base_y = self.dp_y - self.core
        self.base_far = self.base_x + self.base_y - self.base

    def barrier(self):
        bar = pltpu.get_barrier_semaphore()
        spot = self.core * 4 + self.line
        for step in range(1, 8):
            other = (spot + step) % 8
            pl.semaphore_signal(
                bar,
                inc=1,
                device_id=(self.base + other // 4, other % 4),
                device_id_type=MESH,
            )
        for near in (self.dp_x, self.dp_y):
            pl.semaphore_signal(bar, inc=1, device_id=(near, self.line), device_id_type=MESH)
        pl.semaphore_wait(bar, 9)


def remote(src, dst, send, recv, dp, line):
    return pltpu.make_async_remote_copy(
        src_ref=src,
        dst_ref=dst,
        send_sem=send,
        recv_sem=recv,
        device_id=(dp, line),
        device_id_type=MESH,
    )


def move(src, dst, send, recv, dp, line, here):
    @pl.when(here)
    def _():
        pltpu.make_async_copy(src, dst, recv).start()

    @pl.when(jnp.logical_not(here))
    def _():
        remote(src, dst, send, recv, dp, line).start()


def gather_kernel(
    wh, w1, w2, tok, cot, weights, x_out, g_out, zs, zr, fs, xs, xr, ys, yr, ds, dr, ts, tr
):
    at = Place()
    dp, line, core, half = at.dp, at.line, at.core, at.half
    units = (wh, w1, w2)
    lane = line % 2
    at.barrier()

    def deal(kind, start):
        src, dst = ((tok, x_out), (cot, g_out))[kind]
        for slot in range(2):
            there = 2 * core + slot
            here = jnp.logical_and(half == core, there == line)
            send, recv = ts.at[kind, slot], tr.at[kind, lane]
            if start:
                move(src.at[slot], dst.at[lane], send, recv, at.base + half, there, here)
            else:

                @pl.when(jnp.logical_not(here))
                def _():
                    remote(
                        src.at[slot], dst.at[lane], send, recv, at.base + half, there
                    ).wait_send()

    def deal_arrive(kind):
        src, dst = ((tok, x_out), (cot, g_out))[kind]
        for block in range(2):
            pltpu.make_async_copy(src.at[0], dst.at[block], tr.at[kind, block]).wait()

    def source(u, start):
        dst = weights.at[u, lane, dp]
        recv = zr.at[u, lane, core]
        home = at.base + half
        if start:
            move(units[u], dst, zs.at[u, 0], recv, home, line, half == core)
        else:

            @pl.when(half != core)
            def _():
                remote(units[u], dst, zs.at[u, 0], recv, home, line).wait_send()

        for which, step in ((1, 1), (2, -1)):
            inside = line < 3 if step == 1 else line > 0

            @pl.when(inside)
            def _():
                copy = remote(units[u], dst, zs.at[u, which], recv, home, line + step)
                copy.start() if start else copy.wait_send()

    first = jnp.where(core == 0, jnp.where(line == 0, 0, 1), jnp.where(line == 3, 1, 0))

    def z_stage(u, k, other, start):
        zi = first if k == 0 else 1 - first
        origin = 2 * core + zi
        ref = weights.at[u, zi, at.base + other]
        if start:
            pltpu.make_async_copy(units[u], ref, zr.at[u, zi, other]).wait()
        up = jnp.logical_and(origin < line, line < 3)
        down = jnp.logical_and(origin > line, line > 0)
        for go, step in ((up, 1), (down, -1)):

            @pl.when(go)
            def _():
                copy = remote(
                    ref, ref, fs.at[u, zi, other], zr.at[u, zi, other], dp, line + step
                )
                copy.start() if start else copy.wait_send()

        for near, send, recv in ((at.dp_x, xs, xr), (at.dp_y, ys, yr)):
            copy = remote(ref, ref, send.at[u, zi, other], recv.at[u, zi, other], near, line)
            copy.start() if start else copy.wait_send()

    def far_stage(u, zi, other, start):
        base, recv = ((at.base_x, xr), (at.base_y, yr))[zi]
        near = (at.dp_y, at.dp_x)[zi]
        ref = weights.at[u, zi, base + other]
        if start:
            pltpu.make_async_copy(units[u], ref, recv.at[u, zi, other]).wait()
        copy = remote(ref, ref, ds.at[u, zi, other], dr.at[u, zi, other], near, line)
        copy.start() if start else copy.wait_send()

    def last_stage(u, zi, other):
        base, recv = ((at.base_y, yr), (at.base_x, xr))[zi]
        ref = weights.at[u, zi, base + other]
        pltpu.make_async_copy(units[u], ref, recv.at[u, zi, other]).wait()
        ref = weights.at[u, zi, at.base_far + other]
        pltpu.make_async_copy(units[u], ref, dr.at[u, zi, other]).wait()

    deal(0, True)
    source(0, True)
    for u in range(3):
        for k in range(2):
            for other in range(2):
                z_stage(u, k, other, True)
        if u < 2:
            source(u + 1, True)
        if u == 0:
            deal(1, True)
        for other in range(2):
            for zi in range(2):
                far_stage(u, zi, other, True)
    for u in range(3):
        source(u, False)
        for k in range(2):
            for other in range(2):
                z_stage(u, k, other, False)
                far_stage(u, k, other, False)
                last_stage(u, k, other)
    for kind in range(2):
        deal(kind, False)
        deal_arrive(kind)


def gather_all(wh, w1, w2, tok, cot):
    rows, cols = w1.shape
    item = jax.ShapeDtypeStruct(tok.shape, tok.dtype)
    return pl.pallas_call(
        gather_kernel,
        out_shape=(jax.ShapeDtypeStruct((3, 2, 8, rows, cols), w1.dtype), item, item),
        in_specs=[ANY] * 5,
        out_specs=(ANY,) * 3,
        scratch_shapes=[
            DMA((3, 3)),
            DMA((3, 2, 2)),
            DMA((3, 2, 2)),
            DMA((3, 2, 2)),
            DMA((3, 2, 2)),
            DMA((3, 2, 2)),
            DMA((3, 2, 2)),
            DMA((3, 2, 2)),
            DMA((3, 2, 2)),
            DMA((2, 2)),
            DMA((2, 2)),
        ],
        compiler_params=pltpu.CompilerParams(collective_id=0, has_side_effects=True),
    )(wh, w1, w2, tok, cot)


def fast_body(
    tokens,
    time_embed,
    segments,
    micro_order,
    head_mask,
    group_mask,
    keep_route,
    w_qkv,
    w_proj,
    w_fc1,
    w_fc2,
    w_ada,
    b_ada,
    cotangent,
):
    dp = lax.axis_index("dp")
    line = lax.axis_index("tensor")
    core = dp % 2
    chip = dp // 2
    odd = line % 2
    owner = line // 2
    segs = time_embed.shape[1]
    part = tokens.shape[1]
    width = tokens.shape[2]
    length = segments.shape[1]
    qcols = w_qkv.shape[1]
    heads_here = head_mask.shape[1]

    hsel = head_mask[micro_order]
    gsel = group_mask[micro_order]
    packed_meta = jnp.concatenate([hsel, gsel, keep_route], axis=1)
    meta = lax.all_gather(packed_meta, "tensor", axis=0, tiled=False)
    meta_other, seg_other = sibling(meta), sibling(segments)
    meta = pick(jnp.where(core == owner, meta, meta_other).transpose(1, 0, 2), odd)
    seg_ids = pick(jnp.where(core == owner, segments, seg_other), odd)
    hmask = lax.dynamic_slice_in_dim(meta[:, :heads_here], 2 * core, 2).astype(jnp.float32)
    gmask = lax.dynamic_slice_in_dim(meta[:, heads_here : 2 * heads_here], 2 * core, 2)
    gcols = jnp.repeat(gmask.astype(jnp.float32), FF // GROUPS, axis=1)
    keepf = lax.dynamic_slice_in_dim(meta[:, 2 * heads_here :], 2 * core, 2).astype(jnp.float32)
    keep_col = keepf[:, :, None]

    te_all = lax.all_gather(time_embed, "dp", axis=0, tiled=True).reshape(-1, width)
    scond = jax.nn.silu(te_all.astype(jnp.float32)).astype(jnp.bfloat16)
    scond_rows = lax.dynamic_slice_in_dim(scond, dp * w_ada.shape[0], w_ada.shape[0], axis=1)
    part_mods = jnp.dot(scond_rows, w_ada, preferred_element_type=jnp.float32)
    my_mods = lax.psum_scatter(part_mods, "dp", scatter_dimension=0, tiled=True) + b_ada[None, :]
    line_mods = lax.all_gather(my_mods, "tensor", axis=1, tiled=True)
    other_mods = sibling(line_mods)
    mods = pick(jnp.where(core == owner, line_mods, other_mods).reshape(2, segs, -1), odd)
    block_item = lax.dynamic_slice_in_dim(seg_ids[:: length // 4], 2 * core, 2)
    modtok = mods[block_item][:, None, :]
    shift1, scale1, gate1, shift2, scale2, gate2 = jnp.split(modtok, 6, axis=2)

    whead = jnp.concatenate([w_qkv, w_proj], axis=1)
    weights, dealt, dealt_grad = gather_all(whead, w_fc1, w_fc2, tokens, cotangent)
    weights = weights.reshape(3, 2, width, w_fc1.shape[1])
    full_qkv = weights[0, :, :, :qcols]
    full_proj = weights[0, :, :, qcols:]
    full_fc1 = weights[1]
    full_fc2 = weights[2]
    token_vals = dealt.astype(jnp.float32)
    grad_out = dealt_grad.astype(jnp.float32)

    def share(value):
        rows = value.astype(jnp.bfloat16).reshape(2 * part, width)
        return order(core, rows, sibling(rows))

    def collect(partial):
        theirs = lax.dynamic_slice_in_dim(partial, (1 - core) * 2 * part, 2 * part)
        mine = lax.dynamic_slice_in_dim(partial, core * 2 * part, 2 * part)
        got = sibling(theirs.astype(jnp.bfloat16)).astype(jnp.float32)
        return (mine + got).reshape(2, part, width)

    d_mlp = share(gate2 * keep_col * grad_out)
    normed1, factor1 = layer_norm(token_vals)
    h_first = share(normed1 * (1.0 + scale1) + shift1)
    packed = jnp.einsum("rd,zdc->rzc", h_first, full_qkv, preferred_element_type=jnp.float32)
    packed = packed.astype(jnp.bfloat16).reshape(length, 2 * heads_here, 3, HD)
    query, keys, values = packed[:, :, 0], packed[:, :, 1], packed[:, :, 2]
    outs, totals = attention_forward(query, keys, values, seg_ids)
    hm = hmask.reshape(-1)[None, :, None]
    attn = (outs * hm).astype(jnp.bfloat16).reshape(length, 2, heads_here * HD)
    branch = collect(
        jnp.einsum("rzk,zok->ro", attn, full_proj, preferred_element_type=jnp.float32)
    )
    first = token_vals + gate1 * branch
    normed2, factor2 = layer_norm(first)
    h_second = share(normed2 * (1.0 + scale2) + shift2)
    upward = jnp.einsum("rd,zdu->zru", h_second, full_fc1, preferred_element_type=jnp.float32)
    gelu_val, gelu_pull = jax.vjp(lambda inner: jax.nn.gelu(inner, approximate=True), upward)
    act = (gelu_val * gcols[:, None, :]).astype(jnp.bfloat16)
    mlp = collect(jnp.einsum("zru,zou->ro", act, full_fc2, preferred_element_type=jnp.float32))
    result = (first + gate2 * keep_col * mlp).astype(jnp.bfloat16)

    grad_fc2 = jnp.einsum("ro,zru->zou", d_mlp, act, preferred_element_type=jnp.float32)
    g_fc2 = scatter_grad(grad_fc2.astype(jnp.bfloat16), core, chip)
    d_act = jnp.einsum("ro,zou->zru", d_mlp, full_fc2, preferred_element_type=jnp.float32)
    d_up = gelu_pull(d_act * gcols[:, None, :])[0].astype(jnp.bfloat16)
    grad_fc1 = jnp.einsum("rd,zru->zdu", h_second, d_up, preferred_element_type=jnp.float32)
    g_fc1 = scatter_grad(grad_fc1.astype(jnp.bfloat16), core, chip)
    d_second = collect(
        jnp.einsum("zru,zdu->rd", d_up, full_fc1, preferred_element_type=jnp.float32)
    )
    d_first = grad_out + norm_back(d_second * (1.0 + scale2), normed2, factor2)
    d_branch = share(gate1 * d_first)
    grad_proj = jnp.einsum("ro,rzk->zok", d_branch, attn, preferred_element_type=jnp.float32)
    d_attn = jnp.einsum("ro,zok->rzk", d_branch, full_proj, preferred_element_type=jnp.float32)
    d_attn = d_attn.astype(jnp.bfloat16).reshape(length, 2 * heads_here, HD)
    d_attn = d_attn * hm.astype(jnp.bfloat16)
    d_packed = attention_backward(query, keys, values, seg_ids, totals, d_attn)
    d_packed = d_packed.reshape(length, 2, qcols)
    grad_qkv = jnp.einsum("rd,rzc->zdc", h_first, d_packed, preferred_element_type=jnp.float32)
    grad_head = jnp.concatenate([grad_qkv, grad_proj], axis=2).astype(jnp.bfloat16)
    g_head = scatter_grad(grad_head, core, chip)
    d_h_first = collect(
        jnp.einsum("rzc,zdc->rd", d_packed, full_qkv, preferred_element_type=jnp.float32)
    )
    d_input = d_first + norm_back(d_h_first * (1.0 + scale1), normed1, factor1)

    sums = jnp.concatenate(
        [
            jnp.sum(v, axis=1)
            for v in (
                d_h_first,
                d_h_first * normed1,
                d_first * branch,
                d_second,
                d_second * normed2,
                grad_out * keep_col * mlp,
            )
        ],
        axis=1,
    )
    onehot = (block_item[None, :] == jnp.arange(segs, dtype=jnp.int32)[:, None]).astype(jnp.float32)
    d_mods = jnp.sum(onehot[:, :, None] * sums[None], axis=1)
    cols = b_ada.shape[0]
    d_lines = lax.all_to_all(
        d_mods.reshape(segs, -1, cols).transpose(1, 0, 2), "tensor", 0, 0, tiled=False
    )
    d_all = lax.all_gather(d_lines, "dp", axis=0, tiled=False)
    d_all = d_all.reshape(-1, 2, *d_lines.shape).sum(axis=1).reshape(-1, cols)
    g_ada = jnp.dot(scond_rows.astype(jnp.float32).T, d_all, precision=HIGH)
    g_bias = jnp.sum(d_all, axis=0)

    return (
        undeal(result, odd),
        undeal(d_input.astype(jnp.bfloat16), odd),
        g_head[:, :qcols],
        g_head[:, qcols:],
        g_fc1,
        g_fc2,
        g_ada,
        g_bias,
    )


def solution(mesh):
    placed = (
        P("dp", "tensor", None),
        P("dp", None, None),
        P("dp", None),
        P("dp"),
        P("dp", "tensor"),
        P("dp", "tensor"),
        P("dp", "tensor"),
        P("dp", "tensor"),
        P("dp", "tensor"),
        P("dp", "tensor"),
        P("dp", "tensor"),
        P("dp", "tensor"),
        P("tensor"),
        P("dp", "tensor", None),
    )
    return jax.shard_map(
        fast_body if mesh.shape["dp"] == 8 and mesh.shape["tensor"] == 4 else body,
        mesh=mesh,
        in_specs=placed,
        out_specs=(
            P("dp", "tensor", None),
            P("dp", "tensor", None),
            P("dp", "tensor"),
            P("dp", "tensor"),
            P("dp", "tensor"),
            P("dp", "tensor"),
            P("dp", "tensor"),
            P("tensor"),
        ),
        check_vma=False,
    )
```

```python
import jax
import jax.numpy as jnp
from jax import lax
from jax.experimental import pallas as pl
from jax.experimental.pallas import tpu as pltpu
from jax.sharding import PartitionSpec as P

HD = 72
FF = 4608
GROUPS = 16


EPSILON = 1e-06
HIGH = lax.Precision.HIGHEST


def layer_norm(values):
    middle = jnp.mean(values, axis=-1, keepdims=True)
    centred = values - middle
    spread = jnp.mean(centred * centred, axis=-1, keepdims=True)
    factor = lax.rsqrt(spread + EPSILON)
    return (centred * factor, factor)


def norm_back(grad, normed, factor):
    inner = (
        grad
        - jnp.mean(grad, axis=-1, keepdims=True)
        - normed * jnp.mean(grad * normed, axis=-1, keepdims=True)
    )
    return factor * inner


def contract_rows(left, right):
    return lax.dot_general(
        left, right, (((0,), (0,)), ((), ())), preferred_element_type=jnp.float32
    )


def contract_cols(left, right):
    return lax.dot_general(
        left, right, (((1,), (1,)), ((), ())), preferred_element_type=jnp.float32
    )


def score_block(query_block, keys, seg_block, seg_ids):
    scores = jnp.einsum(
        "qhe,khe->hqk", query_block, keys, preferred_element_type=jnp.float32
    ) * HD ** (-0.5)
    same = seg_block[:, None] == seg_ids[None, :]
    return jnp.where(same[None], scores, -1e30)


def attention_forward(query, keys, values, seg_ids):
    length = query.shape[0]
    block = min(512, length)
    outs = []
    totals = []
    for offset in range(0, length, block):
        scores = score_block(
            query[offset : offset + block], keys, seg_ids[offset : offset + block], seg_ids
        )
        peak = jnp.max(scores, axis=-1, keepdims=True)
        denom = jnp.sum(jnp.exp(scores - peak), axis=-1, keepdims=True)
        log_total = peak + jnp.log(denom)
        probs = jnp.exp(scores - log_total).astype(jnp.bfloat16)
        outs.append(jnp.einsum("hqk,khe->qhe", probs, values, preferred_element_type=jnp.float32))
        totals.append(log_total)
    return (jnp.concatenate(outs, axis=0), totals)


def attention_backward(query, keys, values, seg_ids, totals, d_attn):
    length = query.shape[0]
    block = min(512, length)
    scale = HD ** (-0.5)
    d_keys = jnp.zeros(keys.shape, jnp.float32)
    d_values = jnp.zeros(values.shape, jnp.float32)
    d_queries = []
    for number, offset in enumerate(range(0, length, block)):
        query_block = query[offset : offset + block]
        scores = score_block(query_block, keys, seg_ids[offset : offset + block], seg_ids)
        probs = jnp.exp(scores - totals[number])
        grad_block = d_attn[offset : offset + block]
        d_values = d_values + jnp.einsum(
            "hqk,qhe->khe",
            probs.astype(jnp.bfloat16),
            grad_block,
            preferred_element_type=jnp.float32,
        )
        d_probs = jnp.einsum("qhe,khe->hqk", grad_block, values, preferred_element_type=jnp.float32)
        d_scores = (probs * (d_probs - jnp.sum(probs * d_probs, axis=-1, keepdims=True))).astype(
            jnp.bfloat16
        )
        d_queries.append(
            jnp.einsum("hqk,khe->qhe", d_scores, keys, preferred_element_type=jnp.float32) * scale
        )
        d_keys = (
            d_keys
            + jnp.einsum("hqk,qhe->khe", d_scores, query_block, preferred_element_type=jnp.float32)
            * scale
        )
    stacked = jnp.stack([jnp.concatenate(d_queries, axis=0), d_keys, d_values], axis=2)
    return stacked.astype(jnp.bfloat16).reshape(length, -1)


def body(
    tokens,
    time_embed,
    segments,
    micro_order,
    head_mask,
    group_mask,
    keep_route,
    w_qkv,
    w_proj,
    w_fc1,
    w_fc2,
    w_ada,
    b_ada,
    cotangent,
):
    micro = tokens.shape[0]
    local_rows = tokens.shape[1]
    length = segments.shape[1]
    heads_here = head_mask.shape[1]
    segs = time_embed.shape[1]
    tensor_index = lax.axis_index("tensor")
    chooser = (micro_order[:, None] == jnp.arange(micro, dtype=jnp.int32)[None, :]).astype(
        jnp.float32
    )
    head_sel = jnp.dot(chooser, head_mask.astype(jnp.float32), precision=HIGH)
    group_sel = jnp.repeat(
        jnp.dot(chooser, group_mask.astype(jnp.float32), precision=HIGH), FF // GROUPS, axis=1
    )
    keep_float = keep_route.astype(jnp.float32)

    def reduce_grads(grad_qkv, grad_proj, grad_fc1, grad_fc2, grad_ada):
        return (
            lax.psum_scatter(
                grad_qkv.astype(jnp.bfloat16), "dp", scatter_dimension=0, tiled=True
            ).astype(jnp.float32),
            lax.psum_scatter(
                grad_proj.astype(jnp.bfloat16), "dp", scatter_dimension=0, tiled=True
            ).astype(jnp.float32),
            lax.psum_scatter(
                grad_fc1.astype(jnp.bfloat16), "dp", scatter_dimension=0, tiled=True
            ).astype(jnp.float32),
            lax.psum_scatter(
                grad_fc2.astype(jnp.bfloat16), "dp", scatter_dimension=0, tiled=True
            ).astype(jnp.float32),
            lax.psum_scatter(
                grad_ada.astype(jnp.bfloat16), "dp", scatter_dimension=0, tiled=True
            ).astype(jnp.float32),
        )

    shard_shapes = [w.shape for w in (w_qkv, w_proj, w_fc1, w_fc2, w_ada)]
    start_acc = tuple((jnp.zeros(shape, jnp.float32) for shape in shard_shapes))

    def slot_step(carry, items):
        acc, bias_acc = carry
        slot_tokens, slot_grad, seg_ids, embed, hmask, gcols, keepf = items
        full = (
            lax.all_gather(w_qkv, "dp", axis=0, tiled=True),
            lax.all_gather(w_proj, "dp", axis=0, tiled=True),
            lax.all_gather(w_fc1, "dp", axis=0, tiled=True),
            lax.all_gather(w_fc2, "dp", axis=0, tiled=True),
            lax.all_gather(w_ada, "dp", axis=0, tiled=True),
        )
        full_qkv, full_proj, full_fc1, full_fc2, full_ada = full
        seg_local = lax.dynamic_slice_in_dim(seg_ids, tensor_index * local_rows, local_rows)
        scond = jax.nn.silu(embed.astype(jnp.float32)).astype(jnp.bfloat16)
        part_mods = jnp.dot(scond, full_ada, preferred_element_type=jnp.float32) + b_ada[None, :]
        mods = lax.all_gather(part_mods, "tensor", axis=1, tiled=True)
        onehot = (seg_local[:, None] == jnp.arange(segs, dtype=jnp.int32)[None, :]).astype(
            jnp.float32
        )
        modtok = jnp.dot(onehot, mods, precision=HIGH)
        shift1, scale1, gate1, shift2, scale2, gate2 = jnp.split(modtok, 6, axis=1)
        token_vals = slot_tokens.astype(jnp.float32)
        normed1, factor1 = layer_norm(token_vals)
        h_first = lax.all_gather(
            (normed1 * (1.0 + scale1) + shift1).astype(jnp.bfloat16), "tensor", axis=0, tiled=True
        )
        packed = jnp.dot(h_first, full_qkv, preferred_element_type=jnp.float32).astype(jnp.bfloat16)
        packed = packed.reshape(length, heads_here, 3, HD)
        query = packed[:, :, 0]
        keys = packed[:, :, 1]
        values = packed[:, :, 2]
        outs, totals = attention_forward(query, keys, values, seg_ids)
        attn = (outs * hmask[None, :, None]).astype(jnp.bfloat16).reshape(length, heads_here * HD)
        branch = lax.psum_scatter(
            contract_cols(attn, full_proj).astype(jnp.bfloat16),
            "tensor",
            scatter_dimension=0,
            tiled=True,
        ).astype(jnp.float32)
        first = token_vals + gate1 * branch
        normed2, factor2 = layer_norm(first)
        h_second = lax.all_gather(
            (normed2 * (1.0 + scale2) + shift2).astype(jnp.bfloat16), "tensor", axis=0, tiled=True
        )
        upward = jnp.dot(h_second, full_fc1, preferred_element_type=jnp.float32)
        gelu_val, gelu_pull = jax.vjp(lambda inner: jax.nn.gelu(inner, approximate=True), upward)
        act = (gelu_val * gcols[None, :]).astype(jnp.bfloat16)
        mlp = lax.psum_scatter(
            contract_cols(act, full_fc2).astype(jnp.bfloat16),
            "tensor",
            scatter_dimension=0,
            tiled=True,
        ).astype(jnp.float32)
        keep_col = keepf[:, None]
        result = (first + gate2 * keep_col * mlp).astype(jnp.bfloat16)
        grad_out = slot_grad.astype(jnp.float32)
        d_mlp = lax.all_gather(
            (gate2 * keep_col * grad_out).astype(jnp.bfloat16), "tensor", axis=0, tiled=True
        )
        grad_fc2 = contract_rows(d_mlp, act)
        d_act = jnp.dot(d_mlp, full_fc2, preferred_element_type=jnp.float32)
        d_up = gelu_pull(d_act * gcols[None, :])[0].astype(jnp.bfloat16)
        grad_fc1 = contract_rows(h_second, d_up)
        d_second = lax.psum_scatter(
            contract_cols(d_up, full_fc1).astype(jnp.bfloat16),
            "tensor",
            scatter_dimension=0,
            tiled=True,
        ).astype(jnp.float32)
        d_first = grad_out + norm_back(d_second * (1.0 + scale2), normed2, factor2)
        d_branch = lax.all_gather(
            (gate1 * d_first).astype(jnp.bfloat16), "tensor", axis=0, tiled=True
        )
        grad_proj = contract_rows(d_branch, attn)
        d_attn = jnp.dot(d_branch, full_proj, preferred_element_type=jnp.float32).astype(
            jnp.bfloat16
        )
        d_attn = d_attn.reshape(length, heads_here, HD) * hmask[None, :, None].astype(jnp.bfloat16)
        d_packed = attention_backward(query, keys, values, seg_ids, totals, d_attn)
        grad_qkv = contract_rows(h_first, d_packed)
        d_h_first = lax.psum_scatter(
            contract_cols(d_packed, full_qkv).astype(jnp.bfloat16),
            "tensor",
            scatter_dimension=0,
            tiled=True,
        ).astype(jnp.float32)
        d_input = d_first + norm_back(d_h_first * (1.0 + scale1), normed1, factor1)
        d_modtok = jnp.concatenate(
            [
                d_h_first,
                d_h_first * normed1,
                d_first * branch,
                d_second,
                d_second * normed2,
                grad_out * keep_col * mlp,
            ],
            axis=1,
        )
        part_dmods = lax.dot_general(onehot, d_modtok, (((0,), (0,)), ((), ())), precision=HIGH)
        d_mods = lax.psum_scatter(
            part_dmods.astype(jnp.bfloat16), "tensor", scatter_dimension=1, tiled=True
        ).astype(jnp.float32)
        grad_ada = jnp.dot(scond.astype(jnp.float32).T, d_mods, precision=HIGH)
        bias_acc = bias_acc + jnp.sum(d_mods, axis=0)
        parts = reduce_grads(grad_qkv, grad_proj, grad_fc1, grad_fc2, grad_ada)
        acc = tuple((held + piece for held, piece in zip(acc, parts)))
        return ((acc, bias_acc), (result, d_input.astype(jnp.bfloat16)))

    start_bias = jnp.zeros(b_ada.shape, jnp.float32)
    (acc, bias_acc), (results, d_tokens) = lax.scan(
        slot_step,
        (start_acc, start_bias),
        (tokens, cotangent, segments, time_embed, head_sel, group_sel, keep_float),
    )
    g_bias = lax.psum(bias_acc, "dp")
    return (results, d_tokens, acc[0], acc[1], acc[2], acc[3], acc[4], g_bias)


AX = ("dp", "tensor")


def route(value, where):
    return lax.ppermute(value, AX, [(d * 4 + t, where(d, t)) for d in range(8) for t in range(4)])


def sibling(value):
    return route(value, lambda d, t: (d ^ 1) * 4 + t)


def over_x(value):
    return route(value, lambda d, t: (d ^ 2) * 4 + t)


def over_y(value):
    return route(value, lambda d, t: (d ^ 4) * 4 + t)


def deal_to(step):
    def where(d, t):
        slot = (t % 2 + step) % 2
        return ((d // 2) * 2 + t // 2) * 4 + 2 * (d % 2) + slot

    return where


def deal_back(step):
    forward = deal_to(step)
    back = {forward(d, t): d * 4 + t for d in range(8) for t in range(4)}
    return lambda d, t: back[d * 4 + t]


def pick(value, index):
    return lax.dynamic_index_in_dim(value, index, 0, keepdims=False)


def order(flag, first, second, axis=0):
    swapped = flag == 1
    return jnp.concatenate(
        [jnp.where(swapped, second, first), jnp.where(swapped, first, second)], axis=axis
    )


def undeal(value, odd):
    parts = [route(pick(value, (odd + step) % 2), deal_back(step)) for step in range(2)]
    return order(odd, parts[0][None], parts[1][None])


def scatter_grad(grad, core, chip):
    rows = grad.shape[1] // 8
    blocks = grad.reshape(2, 4, 2, rows, grad.shape[2]).transpose(1, 0, 2, 3, 4)
    own = pick(blocks, chip)
    to_x = pick(blocks, chip ^ 1)
    to_y = pick(blocks, chip ^ 2)
    far = pick(blocks, chip ^ 3)
    add = lambda one, two: (one.astype(jnp.float32) + two.astype(jnp.float32)).astype(jnp.bfloat16)
    via_x = over_x(far[0])
    via_y = over_y(far[1])
    got_y = over_y(jnp.stack([add(to_y[0], via_x), to_y[1]]))
    got_x = over_x(jnp.stack([to_x[0], add(to_x[1], via_y)]))
    total = (
        own.astype(jnp.float32) + got_x.astype(jnp.float32) + got_y.astype(jnp.float32)
    ).astype(jnp.bfloat16)
    total = total.transpose(1, 0, 2, 3)
    mine = pick(total, core)
    other = sibling(pick(total, 1 - core))
    lines = order(core, mine, other)
    return lax.psum_scatter(lines, "tensor", scatter_dimension=0, tiled=False).astype(jnp.float32)


MESH = pl.DeviceIdType.MESH
ANY = pl.BlockSpec(memory_space=pl.ANY)
DMA = pltpu.SemaphoreType.DMA


class Place:
    def __init__(self):
        self.dp = lax.axis_index("dp")
        self.line = lax.axis_index("tensor")
        self.core = self.dp % 2
        self.base = self.dp - self.core
        self.half = self.line // 2
        x, y = (self.dp // 2) % 2, self.dp // 4
        self.dp_x = self.dp + 2 * (1 - 2 * x)
        self.dp_y = self.dp + 4 * (1 - 2 * y)
        self.base_x = self.dp_x - self.core
        self.base_y = self.dp_y - self.core
        self.base_far = self.base_x + self.base_y - self.base

    def barrier(self):
        bar = pltpu.get_barrier_semaphore()
        spot = self.core * 4 + self.line
        for step in range(1, 8):
            other = (spot + step) % 8
            pl.semaphore_signal(
                bar,
                inc=1,
                device_id=(self.base + other // 4, other % 4),
                device_id_type=MESH,
            )
        for near in (self.dp_x, self.dp_y):
            pl.semaphore_signal(bar, inc=1, device_id=(near, self.line), device_id_type=MESH)
        pl.semaphore_wait(bar, 9)


def remote(src, dst, send, recv, dp, line):
    return pltpu.make_async_remote_copy(
        src_ref=src,
        dst_ref=dst,
        send_sem=send,
        recv_sem=recv,
        device_id=(dp, line),
        device_id_type=MESH,
    )


def move(src, dst, send, recv, dp, line, here):
    @pl.when(here)
    def _():
        pltpu.make_async_copy(src, dst, recv).start()

    @pl.when(jnp.logical_not(here))
    def _():
        remote(src, dst, send, recv, dp, line).start()


LOG2E = 1.4426950408889634
LOW = jnp.bfloat16
F32 = jnp.float32
SHADE = -1e30


def dot_nn(left, right):
    return jnp.dot(left, right, preferred_element_type=F32)


def dot_nt(left, right):
    return lax.dot_general(left, right, (((1,), (1,)), ((), ())), preferred_element_type=F32)


def dot_tn(left, right):
    return lax.dot_general(left, right, (((0,), (0,)), ((), ())), preferred_element_type=F32)


def lanes(rows):
    return lax.broadcasted_iota(jnp.int32, (rows, 128), 1)


def window(value, start):
    tile, rest = start // 128, start % 128
    here = value[:, 128 * tile : 128 * tile + 128]
    if rest == 0:
        return here
    here = pltpu.roll(here, 128 - rest, 1)
    if rest + HD <= 128:
        return here
    after = pltpu.roll(value[:, 128 * tile + 128 : 128 * tile + 256], 128 - rest, 1)
    return jnp.where(lanes(value.shape[0]) < 128 - rest, here, after)


def pack(parts, start, tiles):
    rows = parts[0].shape[0]
    lane = lanes(rows)
    out = []
    for tile in range(tiles):
        total = jnp.zeros((rows, 128), F32)
        for number, part in enumerate(parts):
            low = start + HD * number - 128 * tile
            if low >= 128 or low + HD <= 0:
                continue
            moved = pltpu.roll(part, low % 128, 1) if low % 128 else part
            inside = jnp.logical_and(lane >= low, lane < low + HD)
            total = jnp.where(inside, moved, total)
        out.append(total)
    return out


def front_kernel(
    hmask,
    wh,
    w1,
    w2,
    tok,
    cot,
    mod,
    feat,
    weights,
    head_out,
    x_out,
    g_out,
    h1_out,
    qkv_out,
    stat_out,
    att_out,
    x1_out,
    br_out,
    h2_out,
    xt,
    w0,
    h1,
    qkv,
    obuf,
    stat,
    att,
    sb,
    rb,
    br,
    x1,
    h2,
    zs,
    zr,
    fs,
    ns,
    nr,
    ds,
    dr,
    ts,
    tr,
    es,
    er,
    ls,
):
    at = Place()
    dp, line, core, half = at.dp, at.line, at.core, at.half
    units = (wh, w1, w2)
    lane = line % 2
    rows_u = w1.shape[0]
    sib = at.base + 1 - core
    at.barrier()

    def spot(u, zi, row):
        if isinstance(u, int) and u == 0:
            return w0.at[zi, pl.ds(pl.multiple_of(row * rows_u, 16), rows_u)]
        return weights.at[u - 1, zi, row]

    def deal(kind, start):
        src, dst = ((tok, xt), (cot, g_out))[kind]
        for slot in range(2):
            there = 2 * core + slot
            here = jnp.logical_and(half == core, there == line)
            send, recv = ts.at[kind, slot], tr.at[kind, lane]
            if start:
                move(src.at[slot], dst.at[lane], send, recv, at.base + half, there, here)
            else:

                @pl.when(jnp.logical_not(here))
                def _():
                    remote(
                        src.at[slot], dst.at[lane], send, recv, at.base + half, there
                    ).wait_send()

    def deal_arrive(kind):
        src, dst = ((tok, xt), (cot, g_out))[kind]
        for block in range(2):
            pltpu.make_async_copy(src.at[0], dst.at[block], tr.at[kind, block]).wait()

    def source(u, start):
        dst = spot(u, lane, dp)
        recv = zr.at[u, lane, core]
        home = at.base + half
        if start:
            move(units[u], dst, zs.at[u, 0], recv, home, line, half == core)
        else:

            @pl.when(half != core)
            def _():
                remote(units[u], dst, zs.at[u, 0], recv, home, line).wait_send()

        for which, step in ((1, 1), (2, -1)):
            inside = line < 3 if step == 1 else line > 0

            @pl.when(inside)
            def _():
                copy = remote(units[u], dst, zs.at[u, which], recv, home, line + step)
                copy.start() if start else copy.wait_send()

    first = jnp.where(core == 0, jnp.where(line == 0, 0, 1), jnp.where(line == 3, 1, 0))

    def z_stage(u, k, other, start):
        zi = first + k - 2 * first * k
        origin = 2 * core + zi
        ref = spot(u, zi, at.base + other)
        if start:
            pltpu.make_async_copy(w1, ref, zr.at[u, zi, other]).wait()
        up = jnp.logical_and(origin < line, line < 3)
        down = jnp.logical_and(origin > line, line > 0)
        for go, step in ((up, 1), (down, -1)):

            @pl.when(go)
            def _():
                copy = remote(
                    ref, ref, fs.at[u, zi, other], zr.at[u, zi, other], dp, line + step
                )
                copy.start() if start else copy.wait_send()

        for which, near in ((0, at.dp_x), (1, at.dp_y)):
            copy = remote(
                ref, ref, ns.at[which, u, zi, other], nr.at[which, u, zi, other], near, line
            )
            copy.start() if start else copy.wait_send()

    def far_stage(u, zi, other, start):
        base = at.base_x + zi * (at.base_y - at.base_x)
        near = at.dp_y + zi * (at.dp_x - at.dp_y)
        ref = spot(u, zi, base + other)
        if start:
            pltpu.make_async_copy(w1, ref, nr.at[zi, u, zi, other]).wait()
        copy = remote(ref, ref, ds.at[u, zi, other], dr.at[u, zi, other], near, line)
        copy.start() if start else copy.wait_send()

    def last_stage(u, zi, other):
        base = at.base_y + zi * (at.base_x - at.base_y)
        ref = spot(u, zi, base + other)
        pltpu.make_async_copy(w1, ref, nr.at[1 - zi, u, zi, other]).wait()
        ref = spot(u, zi, at.base_far + other)
        pltpu.make_async_copy(w1, ref, dr.at[u, zi, other]).wait()

    def pump(number):
        u = 1 + number // 8
        k, other = (number % 4) // 2, number % 2

        @pl.when(number % 8 < 4)
        def _():
            z_stage(u, k, other, True)

        @pl.when(number % 8 >= 4)
        def _():
            far_stage(u, k, other, True)

    def keep(src, dst, number):
        return pltpu.make_async_copy(src, dst, ls.at[number])

    deal(0, True)
    source(0, True)
    for k in range(2):
        for other in range(2):
            z_stage(0, k, other, True)
    source(1, True)
    deal(1, True)

    def exchange(src, dst, number):
        return remote(src, dst, es.at[number], er.at[number], sib, line)

    deal_arrive(0)
    keep(xt, x_out, 0).start()

    for block in range(2):
        shift, scale = mod[block, 0:1, :], 1.0 + mod[block, 1:2, :]

        def norm_first(step, _):
            at_row = pl.ds(pl.multiple_of(step * 128, 128), 128)
            normed, _f = layer_norm(xt[block, at_row, :].astype(F32))
            to_row = pl.ds(pl.multiple_of(block * 256 + step * 128, 128), 128)
            h1[core, to_row, :] = (normed * scale + shift).astype(LOW)
            return 0

        lax.fori_loop(0, 2, norm_first, 0)
        part = h1.at[core, pl.ds(block * 256, 256)]
        exchange(part, part, block).start()
    for zi in range(2):
        for other in range(2):
            far_stage(0, zi, other, True)
    source(2, True)
    for zi in range(2):
        for other in range(2):
            last_stage(0, zi, other)
    keep(w0, head_out, 1).start()

    def project(step, _):
        @pl.when(step >= 2)
        def _():
            part = h1.at[1 - core, pl.ds(pl.multiple_of((step - 2) * 256, 256), 256)]
            pltpu.make_async_copy(part, part, er.at[step - 2]).wait()

        pump(step)
        tile = (2 * core + step) % 4
        rows = h1[tile // 2, pl.ds(pl.multiple_of((tile % 2) * 256, 256), 256), :]
        to_row = pl.ds(pl.multiple_of(tile * 256, 256), 256)
        narrow = lanes(256) < HD
        fills = (feat[0, pl.ds(tile, 1), :], feat[1, pl.ds(tile, 1), :], jnp.zeros((1, 128), F32))
        for zi in range(2):
            value = dot_nn(rows, w0[zi, :, 0:896])
            for number in range(12):
                head, part = zi * 4 + number // 3, number % 3
                piece = jnp.where(narrow, window(value, HD * number), fills[part])
                qkv[head, part, to_row, :] = piece.astype(LOW)
        return 0

    lax.fori_loop(0, 4, project, 0)
    keep(h1, h1_out, 2).start()
    keep(qkv, qkv_out, 3).start()

    factor = HD ** (-0.5) * LOG2E

    def attend(head, _):
        pump(4 + head)
        gain = hmask[head]

        def tile_step(tile, _):
            rows = pl.ds(pl.multiple_of(tile * 256, 256), 256)
            scores = dot_nt(qkv[head, 0, rows, :], qkv[head, 1])
            peak = jnp.max(scores, axis=1, keepdims=True)
            power = jnp.exp2((scores - peak) * factor)
            total = jnp.sum(power, axis=1, keepdims=True)
            probs = (power * (1.0 / total)).astype(LOW)
            obuf[head, rows, :] = (dot_nn(probs, qkv[head, 2]) * gain).astype(LOW)
            level = peak * factor + jnp.log2(total)
            stat[rows, :] = jnp.where(lanes(256) == head, level, stat[rows, :])
            return 0

        lax.fori_loop(0, 4, tile_step, 0)
        return 0

    lax.fori_loop(0, 8, attend, 0)
    keep(stat, stat_out, 4).start()

    def lay(step, _):
        rows = pl.ds(pl.multiple_of(step * 128, 128), 128)
        for zi in range(2):
            parts = [obuf[zi * 4 + n, rows, :].astype(F32) for n in range(4)]
            for tile, value in enumerate(pack(parts, 96, 3)):
                att[zi, rows, 128 * tile : 128 * tile + 128] = value.astype(LOW)
        return 0

    lax.fori_loop(0, 8, lay, 0)
    keep(att, att_out, 5).start()

    for step in range(4):
        tile = (2 * (1 - core) + step) % 4
        rows = pl.ds(pl.multiple_of(tile * 256, 256), 256)
        value = dot_nt(att[0, rows, :], w0[0, :, 768:1152])
        value = value + dot_nt(att[1, rows, :], w0[1, :, 768:1152])
        if step < 2:
            sb[step] = value.astype(LOW)
            exchange(sb.at[step], rb.at[step], 2 + step).start()
        else:
            br[step - 2] = value
    for block in range(2):
        exchange(sb.at[block], rb.at[block], 2 + block).wait_recv()
        gate = mod[block, 2:3, :]
        shift, scale = mod[block, 3:4, :], 1.0 + mod[block, 4:5, :]

        def norm_second(step, _):
            at_row = pl.ds(pl.multiple_of(step * 128, 128), 128)
            branch = br[block, at_row, :] + rb[block, at_row, :].astype(F32)
            br[block, at_row, :] = branch
            value = xt[block, at_row, :].astype(F32) + gate * branch
            x1[block, at_row, :] = value
            normed, _f = layer_norm(value)
            to_row = pl.ds(pl.multiple_of(block * 256 + step * 128, 128), 128)
            h2[core, to_row, :] = (normed * scale + shift).astype(LOW)
            return 0

        lax.fori_loop(0, 2, norm_second, 0)
        part = h2.at[core, pl.ds(block * 256, 256)]
        exchange(part, part, 4 + block).start()
    keep(x1, x1_out, 6).start()
    keep(br, br_out, 7).start()

    def drain(number, _):
        pump(number)
        return 0

    lax.fori_loop(12, 16, drain, 0)
    for block in range(2):
        part = h2.at[1 - core, pl.ds(block * 256, 256)]
        pltpu.make_async_copy(part, part, er.at[4 + block]).wait()
    keep(h2, h2_out, 8).start()

    for u in range(3):
        source(u, False)
        for k in range(2):
            for other in range(2):
                z_stage(u, k, other, False)
                far_stage(u, k, other, False)
                if u:
                    last_stage(u, k, other)
    for kind in range(2):
        deal(kind, False)
    deal_arrive(1)
    for block in range(2):
        own1 = h1.at[core, pl.ds(block * 256, 256)]
        own2 = h2.at[core, pl.ds(block * 256, 256)]
        exchange(own1, own1, block).wait_send()
        exchange(sb.at[block], rb.at[block], 2 + block).wait_send()
        exchange(own2, own2, 4 + block).wait_send()
    pairs = (
        (xt, x_out),
        (w0, head_out),
        (h1, h1_out),
        (qkv, qkv_out),
        (stat, stat_out),
        (att, att_out),
        (x1, x1_out),
        (br, br_out),
        (h2, h2_out),
    )
    for number, (src, dst) in enumerate(pairs):
        keep(src, dst, number).wait()


def run_front(hmask, wh, w1, w2, tok, cot, mod, feat):
    rows, cols = w1.shape
    part = tok.shape[1]
    length = 4 * part
    shape = jax.ShapeDtypeStruct
    vmem = pl.BlockSpec(memory_space=pltpu.VMEM)
    outs = (
        shape((2, 2, 8, rows, cols), LOW),
        shape((2, 8 * rows, cols), LOW),
        shape(tok.shape, LOW),
        shape(tok.shape, LOW),
        shape((2, 2 * part, cols), LOW),
        shape((8, 3, length, 128), LOW),
        shape((length, 128), F32),
        shape((2, length, 384), LOW),
        shape((2, part, cols), F32),
        shape((2, part, cols), F32),
        shape((2, 2 * part, cols), LOW),
    )
    three = DMA((3, 2, 2))
    return pl.pallas_call(
        front_kernel,
        out_shape=outs,
        in_specs=[pl.BlockSpec(memory_space=pltpu.SMEM)] + [ANY] * 5 + [vmem, vmem],
        out_specs=(ANY,) * len(outs),
        scratch_shapes=[
            pltpu.VMEM(tok.shape, LOW),
            pltpu.VMEM((2, 8 * rows, cols), LOW),
            pltpu.VMEM((2, 2 * part, cols), LOW),
            pltpu.VMEM((8, 3, length, 128), LOW),
            pltpu.VMEM((8, length, 128), LOW),
            pltpu.VMEM((length, 128), F32),
            pltpu.VMEM((2, length, 384), LOW),
            pltpu.VMEM((2, part, cols), LOW),
            pltpu.VMEM((2, part, cols), LOW),
            pltpu.VMEM((2, part, cols), F32),
            pltpu.VMEM((2, part, cols), F32),
            pltpu.VMEM((2, 2 * part, cols), LOW),
            DMA((3, 3)),
            three,
            three,
            DMA((2, 3, 2, 2)),
            DMA((2, 3, 2, 2)),
            three,
            three,
            DMA((2, 2)),
            DMA((2, 2)),
            DMA((6,)),
            DMA((6,)),
            DMA((9,)),
        ],
        compiler_params=pltpu.CompilerParams(
            collective_id=0, has_side_effects=True, vmem_limit_bytes=58 << 20
        ),
    )(hmask, wh, w1, w2, tok, cot, mod, feat)


def fast_body(
    tokens,
    time_embed,
    segments,
    micro_order,
    head_mask,
    group_mask,
    keep_route,
    w_qkv,
    w_proj,
    w_fc1,
    w_fc2,
    w_ada,
    b_ada,
    cotangent,
):
    dp = lax.axis_index("dp")
    line = lax.axis_index("tensor")
    core = dp % 2
    chip = dp // 2
    odd = line % 2
    owner = line // 2
    segs = time_embed.shape[1]
    part = tokens.shape[1]
    width = tokens.shape[2]
    length = segments.shape[1]
    qcols = w_qkv.shape[1]
    heads_here = head_mask.shape[1]

    hsel = head_mask[micro_order]
    gsel = group_mask[micro_order]
    packed_meta = jnp.concatenate([hsel, gsel, keep_route], axis=1)
    meta = lax.all_gather(packed_meta, "tensor", axis=0, tiled=False)
    meta_other, seg_other = sibling(meta), sibling(segments)
    meta = pick(jnp.where(core == owner, meta, meta_other).transpose(1, 0, 2), odd)
    seg_ids = pick(jnp.where(core == owner, segments, seg_other), odd)
    hmask = lax.dynamic_slice_in_dim(meta[:, :heads_here], 2 * core, 2).astype(jnp.float32)
    gmask = lax.dynamic_slice_in_dim(meta[:, heads_here : 2 * heads_here], 2 * core, 2)
    gcols = jnp.repeat(gmask.astype(jnp.float32), FF // GROUPS, axis=1)
    keepf = lax.dynamic_slice_in_dim(meta[:, 2 * heads_here :], 2 * core, 2).astype(jnp.float32)
    keep_col = keepf[:, :, None]

    te_all = lax.all_gather(time_embed, "dp", axis=0, tiled=True).reshape(-1, width)
    scond = jax.nn.silu(te_all.astype(jnp.float32)).astype(jnp.bfloat16)
    scond_rows = lax.dynamic_slice_in_dim(scond, dp * w_ada.shape[0], w_ada.shape[0], axis=1)
    part_mods = jnp.dot(scond_rows, w_ada, preferred_element_type=jnp.float32)
    my_mods = lax.psum_scatter(part_mods, "dp", scatter_dimension=0, tiled=True) + b_ada[None, :]
    line_mods = lax.all_gather(my_mods, "tensor", axis=1, tiled=True)
    other_mods = sibling(line_mods)
    mods = pick(jnp.where(core == owner, line_mods, other_mods).reshape(2, segs, -1), odd)
    block_item = lax.dynamic_slice_in_dim(seg_ids[:: length // 4], 2 * core, 2)
    modtok = mods[block_item][:, None, :]
    shift1, scale1, gate1, shift2, scale2, gate2 = jnp.split(modtok, 6, axis=2)

    whead = jnp.concatenate([w_qkv, w_proj], axis=1)
    mod = jnp.pad(mods[block_item].reshape(2, 6, width), ((0, 0), (0, 2), (0, 0)))
    items = seg_ids[:: length // 4]
    spots = jnp.arange(128, dtype=jnp.int32)[None, :] - HD
    same = (items[:, None] == spots).astype(jnp.float32)
    inside = jnp.logical_and(spots >= 0, spots < segs)
    feat = jnp.stack([jnp.where(inside, SHADE * (1.0 - same), 0.0), same])
    (
        weights,
        head_w,
        dealt,
        dealt_grad,
        h_first,
        qkv,
        stat,
        att,
        first,
        branch,
        h_second,
    ) = run_front(hmask.reshape(-1), whead, w_fc1, w_fc2, tokens, cotangent, mod, feat)
    weights = weights.reshape(2, 2, width, w_fc1.shape[1])
    full_qkv = head_w[:, :, :qcols]
    full_proj = head_w[:, :, qcols:]
    full_fc1 = weights[0]
    full_fc2 = weights[1]
    token_vals = dealt.astype(jnp.float32)
    grad_out = dealt_grad.astype(jnp.float32)
    h_first = h_first.reshape(length, width)
    h_second = h_second.reshape(length, width)

    def share(value):
        rows = value.astype(jnp.bfloat16).reshape(2 * part, width)
        return order(core, rows, sibling(rows))

    def collect(partial):
        theirs = lax.dynamic_slice_in_dim(partial, (1 - core) * 2 * part, 2 * part)
        mine = lax.dynamic_slice_in_dim(partial, core * 2 * part, 2 * part)
        got = sibling(theirs.astype(jnp.bfloat16)).astype(jnp.float32)
        return (mine + got).reshape(2, part, width)

    d_mlp = share(gate2 * keep_col * grad_out)
    normed1, factor1 = layer_norm(token_vals)
    hm = hmask.reshape(-1)[None, :, None]
    query, keys, values = (qkv[:, j, :, :HD].transpose(1, 0, 2) for j in range(3))
    level = stat[:, :8].T[:, :, None] * (1.0 / LOG2E)
    totals = [level[:, :512], level[:, 512:]]
    attn = att[:, :, 96:].transpose(1, 0, 2)
    normed2, factor2 = layer_norm(first)
    upward = jnp.einsum("rd,zdu->zru", h_second, full_fc1, preferred_element_type=jnp.float32)
    gelu_val, gelu_pull = jax.vjp(lambda inner: jax.nn.gelu(inner, approximate=True), upward)
    act = (gelu_val * gcols[:, None, :]).astype(jnp.bfloat16)
    mlp = collect(jnp.einsum("zru,zou->ro", act, full_fc2, preferred_element_type=jnp.float32))
    result = (first + gate2 * keep_col * mlp).astype(jnp.bfloat16)

    grad_fc2 = jnp.einsum("ro,zru->zou", d_mlp, act, preferred_element_type=jnp.float32)
    g_fc2 = scatter_grad(grad_fc2.astype(jnp.bfloat16), core, chip)
    d_act = jnp.einsum("ro,zou->zru", d_mlp, full_fc2, preferred_element_type=jnp.float32)
    d_up = gelu_pull(d_act * gcols[:, None, :])[0].astype(jnp.bfloat16)
    grad_fc1 = jnp.einsum("rd,zru->zdu", h_second, d_up, preferred_element_type=jnp.float32)
    g_fc1 = scatter_grad(grad_fc1.astype(jnp.bfloat16), core, chip)
    d_second = collect(
        jnp.einsum("zru,zdu->rd", d_up, full_fc1, preferred_element_type=jnp.float32)
    )
    d_first = grad_out + norm_back(d_second * (1.0 + scale2), normed2, factor2)
    d_branch = share(gate1 * d_first)
    grad_proj = jnp.einsum("ro,rzk->zok", d_branch, attn, preferred_element_type=jnp.float32)
    d_attn = jnp.einsum("ro,zok->rzk", d_branch, full_proj, preferred_element_type=jnp.float32)
    d_attn = d_attn.astype(jnp.bfloat16).reshape(length, 2 * heads_here, HD)
    d_attn = d_attn * hm.astype(jnp.bfloat16)
    d_packed = attention_backward(query, keys, values, seg_ids, totals, d_attn)
    d_packed = d_packed.reshape(length, 2, qcols)
    grad_qkv = jnp.einsum("rd,rzc->zdc", h_first, d_packed, preferred_element_type=jnp.float32)
    grad_head = jnp.concatenate([grad_qkv, grad_proj], axis=2).astype(jnp.bfloat16)
    g_head = scatter_grad(grad_head, core, chip)
    d_h_first = collect(
        jnp.einsum("rzc,zdc->rd", d_packed, full_qkv, preferred_element_type=jnp.float32)
    )
    d_input = d_first + norm_back(d_h_first * (1.0 + scale1), normed1, factor1)

    sums = jnp.concatenate(
        [
            jnp.sum(v, axis=1)
            for v in (
                d_h_first,
                d_h_first * normed1,
                d_first * branch,
                d_second,
                d_second * normed2,
                grad_out * keep_col * mlp,
            )
        ],
        axis=1,
    )
    onehot = (block_item[None, :] == jnp.arange(segs, dtype=jnp.int32)[:, None]).astype(jnp.float32)
    d_mods = jnp.sum(onehot[:, :, None] * sums[None], axis=1)
    cols = b_ada.shape[0]
    d_lines = lax.all_to_all(
        d_mods.reshape(segs, -1, cols).transpose(1, 0, 2), "tensor", 0, 0, tiled=False
    )
    d_all = lax.all_gather(d_lines, "dp", axis=0, tiled=False)
    d_all = d_all.reshape(-1, 2, *d_lines.shape).sum(axis=1).reshape(-1, cols)
    g_ada = jnp.dot(scond_rows.astype(jnp.float32).T, d_all, precision=HIGH)
    g_bias = jnp.sum(d_all, axis=0)

    return (
        undeal(result, odd),
        undeal(d_input.astype(jnp.bfloat16), odd),
        g_head[:, :qcols],
        g_head[:, qcols:],
        g_fc1,
        g_fc2,
        g_ada,
        g_bias,
    )


def solution(mesh):
    placed = (
        P("dp", "tensor", None),
        P("dp", None, None),
        P("dp", None),
        P("dp"),
        P("dp", "tensor"),
        P("dp", "tensor"),
        P("dp", "tensor"),
        P("dp", "tensor"),
        P("dp", "tensor"),
        P("dp", "tensor"),
        P("dp", "tensor"),
        P("dp", "tensor"),
        P("tensor"),
        P("dp", "tensor", None),
    )
    return jax.shard_map(
        fast_body if mesh.shape["dp"] == 8 and mesh.shape["tensor"] == 4 else body,
        mesh=mesh,
        in_specs=placed,
        out_specs=(
            P("dp", "tensor", None),
            P("dp", "tensor", None),
            P("dp", "tensor"),
            P("dp", "tensor"),
            P("dp", "tensor"),
            P("dp", "tensor"),
            P("dp", "tensor"),
            P("tensor"),
        ),
        check_vma=False,
    )
```

```python
import jax
import jax.numpy as jnp
from jax import lax
from jax.experimental import pallas as pl
from jax.experimental.pallas import tpu as pltpu
from jax.sharding import PartitionSpec as P

HD = 72
FF = 4608
GROUPS = 16


EPSILON = 1e-06
HIGH = lax.Precision.HIGHEST


def layer_norm(values):
    middle = jnp.mean(values, axis=-1, keepdims=True)
    centred = values - middle
    spread = jnp.mean(centred * centred, axis=-1, keepdims=True)
    factor = lax.rsqrt(spread + EPSILON)
    return (centred * factor, factor)


def norm_back(grad, normed, factor):
    inner = (
        grad
        - jnp.mean(grad, axis=-1, keepdims=True)
        - normed * jnp.mean(grad * normed, axis=-1, keepdims=True)
    )
    return factor * inner


def contract_rows(left, right):
    return lax.dot_general(
        left, right, (((0,), (0,)), ((), ())), preferred_element_type=jnp.float32
    )


def contract_cols(left, right):
    return lax.dot_general(
        left, right, (((1,), (1,)), ((), ())), preferred_element_type=jnp.float32
    )


def score_block(query_block, keys, seg_block, seg_ids):
    scores = jnp.einsum(
        "qhe,khe->hqk", query_block, keys, preferred_element_type=jnp.float32
    ) * HD ** (-0.5)
    same = seg_block[:, None] == seg_ids[None, :]
    return jnp.where(same[None], scores, -1e30)


def attention_forward(query, keys, values, seg_ids):
    length = query.shape[0]
    block = min(512, length)
    outs = []
    totals = []
    for offset in range(0, length, block):
        scores = score_block(
            query[offset : offset + block], keys, seg_ids[offset : offset + block], seg_ids
        )
        peak = jnp.max(scores, axis=-1, keepdims=True)
        denom = jnp.sum(jnp.exp(scores - peak), axis=-1, keepdims=True)
        log_total = peak + jnp.log(denom)
        probs = jnp.exp(scores - log_total).astype(jnp.bfloat16)
        outs.append(jnp.einsum("hqk,khe->qhe", probs, values, preferred_element_type=jnp.float32))
        totals.append(log_total)
    return (jnp.concatenate(outs, axis=0), totals)


def attention_backward(query, keys, values, seg_ids, totals, d_attn):
    length = query.shape[0]
    block = min(512, length)
    scale = HD ** (-0.5)
    d_keys = jnp.zeros(keys.shape, jnp.float32)
    d_values = jnp.zeros(values.shape, jnp.float32)
    d_queries = []
    for number, offset in enumerate(range(0, length, block)):
        query_block = query[offset : offset + block]
        scores = score_block(query_block, keys, seg_ids[offset : offset + block], seg_ids)
        probs = jnp.exp(scores - totals[number])
        grad_block = d_attn[offset : offset + block]
        d_values = d_values + jnp.einsum(
            "hqk,qhe->khe",
            probs.astype(jnp.bfloat16),
            grad_block,
            preferred_element_type=jnp.float32,
        )
        d_probs = jnp.einsum("qhe,khe->hqk", grad_block, values, preferred_element_type=jnp.float32)
        d_scores = (probs * (d_probs - jnp.sum(probs * d_probs, axis=-1, keepdims=True))).astype(
            jnp.bfloat16
        )
        d_queries.append(
            jnp.einsum("hqk,khe->qhe", d_scores, keys, preferred_element_type=jnp.float32) * scale
        )
        d_keys = (
            d_keys
            + jnp.einsum("hqk,qhe->khe", d_scores, query_block, preferred_element_type=jnp.float32)
            * scale
        )
    stacked = jnp.stack([jnp.concatenate(d_queries, axis=0), d_keys, d_values], axis=2)
    return stacked.astype(jnp.bfloat16).reshape(length, -1)


def body(
    tokens,
    time_embed,
    segments,
    micro_order,
    head_mask,
    group_mask,
    keep_route,
    w_qkv,
    w_proj,
    w_fc1,
    w_fc2,
    w_ada,
    b_ada,
    cotangent,
):
    micro = tokens.shape[0]
    local_rows = tokens.shape[1]
    length = segments.shape[1]
    heads_here = head_mask.shape[1]
    segs = time_embed.shape[1]
    tensor_index = lax.axis_index("tensor")
    chooser = (micro_order[:, None] == jnp.arange(micro, dtype=jnp.int32)[None, :]).astype(
        jnp.float32
    )
    head_sel = jnp.dot(chooser, head_mask.astype(jnp.float32), precision=HIGH)
    group_sel = jnp.repeat(
        jnp.dot(chooser, group_mask.astype(jnp.float32), precision=HIGH), FF // GROUPS, axis=1
    )
    keep_float = keep_route.astype(jnp.float32)

    def reduce_grads(grad_qkv, grad_proj, grad_fc1, grad_fc2, grad_ada):
        return (
            lax.psum_scatter(
                grad_qkv.astype(jnp.bfloat16), "dp", scatter_dimension=0, tiled=True
            ).astype(jnp.float32),
            lax.psum_scatter(
                grad_proj.astype(jnp.bfloat16), "dp", scatter_dimension=0, tiled=True
            ).astype(jnp.float32),
            lax.psum_scatter(
                grad_fc1.astype(jnp.bfloat16), "dp", scatter_dimension=0, tiled=True
            ).astype(jnp.float32),
            lax.psum_scatter(
                grad_fc2.astype(jnp.bfloat16), "dp", scatter_dimension=0, tiled=True
            ).astype(jnp.float32),
            lax.psum_scatter(
                grad_ada.astype(jnp.bfloat16), "dp", scatter_dimension=0, tiled=True
            ).astype(jnp.float32),
        )

    shard_shapes = [w.shape for w in (w_qkv, w_proj, w_fc1, w_fc2, w_ada)]
    start_acc = tuple((jnp.zeros(shape, jnp.float32) for shape in shard_shapes))

    def slot_step(carry, items):
        acc, bias_acc = carry
        slot_tokens, slot_grad, seg_ids, embed, hmask, gcols, keepf = items
        full = (
            lax.all_gather(w_qkv, "dp", axis=0, tiled=True),
            lax.all_gather(w_proj, "dp", axis=0, tiled=True),
            lax.all_gather(w_fc1, "dp", axis=0, tiled=True),
            lax.all_gather(w_fc2, "dp", axis=0, tiled=True),
            lax.all_gather(w_ada, "dp", axis=0, tiled=True),
        )
        full_qkv, full_proj, full_fc1, full_fc2, full_ada = full
        seg_local = lax.dynamic_slice_in_dim(seg_ids, tensor_index * local_rows, local_rows)
        scond = jax.nn.silu(embed.astype(jnp.float32)).astype(jnp.bfloat16)
        part_mods = jnp.dot(scond, full_ada, preferred_element_type=jnp.float32) + b_ada[None, :]
        mods = lax.all_gather(part_mods, "tensor", axis=1, tiled=True)
        onehot = (seg_local[:, None] == jnp.arange(segs, dtype=jnp.int32)[None, :]).astype(
            jnp.float32
        )
        modtok = jnp.dot(onehot, mods, precision=HIGH)
        shift1, scale1, gate1, shift2, scale2, gate2 = jnp.split(modtok, 6, axis=1)
        token_vals = slot_tokens.astype(jnp.float32)
        normed1, factor1 = layer_norm(token_vals)
        h_first = lax.all_gather(
            (normed1 * (1.0 + scale1) + shift1).astype(jnp.bfloat16), "tensor", axis=0, tiled=True
        )
        packed = jnp.dot(h_first, full_qkv, preferred_element_type=jnp.float32).astype(jnp.bfloat16)
        packed = packed.reshape(length, heads_here, 3, HD)
        query = packed[:, :, 0]
        keys = packed[:, :, 1]
        values = packed[:, :, 2]
        outs, totals = attention_forward(query, keys, values, seg_ids)
        attn = (outs * hmask[None, :, None]).astype(jnp.bfloat16).reshape(length, heads_here * HD)
        branch = lax.psum_scatter(
            contract_cols(attn, full_proj).astype(jnp.bfloat16),
            "tensor",
            scatter_dimension=0,
            tiled=True,
        ).astype(jnp.float32)
        first = token_vals + gate1 * branch
        normed2, factor2 = layer_norm(first)
        h_second = lax.all_gather(
            (normed2 * (1.0 + scale2) + shift2).astype(jnp.bfloat16), "tensor", axis=0, tiled=True
        )
        upward = jnp.dot(h_second, full_fc1, preferred_element_type=jnp.float32)
        gelu_val, gelu_pull = jax.vjp(lambda inner: jax.nn.gelu(inner, approximate=True), upward)
        act = (gelu_val * gcols[None, :]).astype(jnp.bfloat16)
        mlp = lax.psum_scatter(
            contract_cols(act, full_fc2).astype(jnp.bfloat16),
            "tensor",
            scatter_dimension=0,
            tiled=True,
        ).astype(jnp.float32)
        keep_col = keepf[:, None]
        result = (first + gate2 * keep_col * mlp).astype(jnp.bfloat16)
        grad_out = slot_grad.astype(jnp.float32)
        d_mlp = lax.all_gather(
            (gate2 * keep_col * grad_out).astype(jnp.bfloat16), "tensor", axis=0, tiled=True
        )
        grad_fc2 = contract_rows(d_mlp, act)
        d_act = jnp.dot(d_mlp, full_fc2, preferred_element_type=jnp.float32)
        d_up = gelu_pull(d_act * gcols[None, :])[0].astype(jnp.bfloat16)
        grad_fc1 = contract_rows(h_second, d_up)
        d_second = lax.psum_scatter(
            contract_cols(d_up, full_fc1).astype(jnp.bfloat16),
            "tensor",
            scatter_dimension=0,
            tiled=True,
        ).astype(jnp.float32)
        d_first = grad_out + norm_back(d_second * (1.0 + scale2), normed2, factor2)
        d_branch = lax.all_gather(
            (gate1 * d_first).astype(jnp.bfloat16), "tensor", axis=0, tiled=True
        )
        grad_proj = contract_rows(d_branch, attn)
        d_attn = jnp.dot(d_branch, full_proj, preferred_element_type=jnp.float32).astype(
            jnp.bfloat16
        )
        d_attn = d_attn.reshape(length, heads_here, HD) * hmask[None, :, None].astype(jnp.bfloat16)
        d_packed = attention_backward(query, keys, values, seg_ids, totals, d_attn)
        grad_qkv = contract_rows(h_first, d_packed)
        d_h_first = lax.psum_scatter(
            contract_cols(d_packed, full_qkv).astype(jnp.bfloat16),
            "tensor",
            scatter_dimension=0,
            tiled=True,
        ).astype(jnp.float32)
        d_input = d_first + norm_back(d_h_first * (1.0 + scale1), normed1, factor1)
        d_modtok = jnp.concatenate(
            [
                d_h_first,
                d_h_first * normed1,
                d_first * branch,
                d_second,
                d_second * normed2,
                grad_out * keep_col * mlp,
            ],
            axis=1,
        )
        part_dmods = lax.dot_general(onehot, d_modtok, (((0,), (0,)), ((), ())), precision=HIGH)
        d_mods = lax.psum_scatter(
            part_dmods.astype(jnp.bfloat16), "tensor", scatter_dimension=1, tiled=True
        ).astype(jnp.float32)
        grad_ada = jnp.dot(scond.astype(jnp.float32).T, d_mods, precision=HIGH)
        bias_acc = bias_acc + jnp.sum(d_mods, axis=0)
        parts = reduce_grads(grad_qkv, grad_proj, grad_fc1, grad_fc2, grad_ada)
        acc = tuple((held + piece for held, piece in zip(acc, parts)))
        return ((acc, bias_acc), (result, d_input.astype(jnp.bfloat16)))

    start_bias = jnp.zeros(b_ada.shape, jnp.float32)
    (acc, bias_acc), (results, d_tokens) = lax.scan(
        slot_step,
        (start_acc, start_bias),
        (tokens, cotangent, segments, time_embed, head_sel, group_sel, keep_float),
    )
    g_bias = lax.psum(bias_acc, "dp")
    return (results, d_tokens, acc[0], acc[1], acc[2], acc[3], acc[4], g_bias)


AX = ("dp", "tensor")


def route(value, where):
    return lax.ppermute(value, AX, [(d * 4 + t, where(d, t)) for d in range(8) for t in range(4)])


def sibling(value):
    return route(value, lambda d, t: (d ^ 1) * 4 + t)


def pick(value, index):
    return lax.dynamic_index_in_dim(value, index, 0, keepdims=False)


def order(flag, first, second, axis=0):
    swapped = flag == 1
    return jnp.concatenate(
        [jnp.where(swapped, second, first), jnp.where(swapped, first, second)], axis=axis
    )


MESH = pl.DeviceIdType.MESH
ANY = pl.BlockSpec(memory_space=pl.ANY)
DMA = pltpu.SemaphoreType.DMA


class Place:
    def __init__(self):
        self.dp = lax.axis_index("dp")
        self.line = lax.axis_index("tensor")
        self.core = self.dp % 2
        self.base = self.dp - self.core
        self.half = self.line // 2
        x, y = (self.dp // 2) % 2, self.dp // 4
        self.dp_x = self.dp + 2 * (1 - 2 * x)
        self.dp_y = self.dp + 4 * (1 - 2 * y)
        self.base_x = self.dp_x - self.core
        self.base_y = self.dp_y - self.core
        self.base_far = self.base_x + self.base_y - self.base

    def barrier(self):
        bar = pltpu.get_barrier_semaphore()
        spot = self.core * 4 + self.line
        for step in range(1, 8):
            other = (spot + step) % 8
            pl.semaphore_signal(
                bar,
                inc=1,
                device_id=(self.base + other // 4, other % 4),
                device_id_type=MESH,
            )
        for near in (self.dp_x, self.dp_y):
            pl.semaphore_signal(bar, inc=1, device_id=(near, self.line), device_id_type=MESH)
        pl.semaphore_wait(bar, 9)


def remote(src, dst, send, recv, dp, line):
    return pltpu.make_async_remote_copy(
        src_ref=src,
        dst_ref=dst,
        send_sem=send,
        recv_sem=recv,
        device_id=(dp, line),
        device_id_type=MESH,
    )


def move(src, dst, send, recv, dp, line, here):
    @pl.when(here)
    def _():
        pltpu.make_async_copy(src, dst, recv).start()

    @pl.when(jnp.logical_not(here))
    def _():
        remote(src, dst, send, recv, dp, line).start()


LOG2E = 1.4426950408889634
LOW = jnp.bfloat16
F32 = jnp.float32
SHADE = -1e30


def dot_nn(left, right):
    return jnp.dot(left, right, preferred_element_type=F32)


def dot_nt(left, right):
    return lax.dot_general(left, right, (((1,), (1,)), ((), ())), preferred_element_type=F32)


def dot_tn(left, right):
    return lax.dot_general(left, right, (((0,), (0,)), ((), ())), preferred_element_type=F32)


def lanes(rows):
    return lax.broadcasted_iota(jnp.int32, (rows, 128), 1)


def window(value, start):
    tile, rest = start // 128, start % 128
    here = value[:, 128 * tile : 128 * tile + 128]
    if rest == 0:
        return here
    here = pltpu.roll(here, 128 - rest, 1)
    if rest + HD <= 128:
        return here
    after = pltpu.roll(value[:, 128 * tile + 128 : 128 * tile + 256], 128 - rest, 1)
    return jnp.where(lanes(value.shape[0]) < 128 - rest, here, after)


def pack(parts, start, tiles):
    rows = parts[0].shape[0]
    lane = lanes(rows)
    out = []
    for tile in range(tiles):
        total = jnp.zeros((rows, 128), F32)
        for number, part in enumerate(parts):
            low = start + HD * number - 128 * tile
            if low >= 128 or low + HD <= 0:
                continue
            moved = pltpu.roll(part, low % 128, 1) if low % 128 else part
            inside = jnp.logical_and(lane >= low, lane < low + HD)
            total = jnp.where(inside, moved, total)
        out.append(total)
    return out


def front_kernel(
    hmask,
    wh,
    w1,
    w2,
    tok,
    cot,
    mod,
    feat,
    weights,
    head_out,
    x_out,
    g_out,
    h1_out,
    qkv_out,
    stat_out,
    att_out,
    x1_out,
    br_out,
    h2_out,
    xt,
    w0,
    h1,
    qkv,
    obuf,
    stat,
    att,
    sb,
    rb,
    br,
    x1,
    h2,
    zs,
    zr,
    fs,
    ns,
    nr,
    ds,
    dr,
    ts,
    tr,
    es,
    er,
    ls,
):
    at = Place()
    dp, line, core, half = at.dp, at.line, at.core, at.half
    units = (wh, w1, w2)
    lane = line % 2
    rows_u = w1.shape[0]
    sib = at.base + 1 - core
    at.barrier()

    def spot(u, zi, row):
        if isinstance(u, int) and u == 0:
            return w0.at[zi, pl.ds(pl.multiple_of(row * rows_u, 16), rows_u)]
        return weights.at[u - 1, zi, row]

    def deal(kind, start):
        src, dst = ((tok, xt), (cot, g_out))[kind]
        for slot in range(2):
            there = 2 * core + slot
            here = jnp.logical_and(half == core, there == line)
            send, recv = ts.at[kind, slot], tr.at[kind, lane]
            if start:
                move(src.at[slot], dst.at[lane], send, recv, at.base + half, there, here)
            else:

                @pl.when(jnp.logical_not(here))
                def _():
                    remote(
                        src.at[slot], dst.at[lane], send, recv, at.base + half, there
                    ).wait_send()

    def deal_arrive(kind):
        src, dst = ((tok, xt), (cot, g_out))[kind]
        for block in range(2):
            pltpu.make_async_copy(src.at[0], dst.at[block], tr.at[kind, block]).wait()

    def source(u, start):
        dst = spot(u, lane, dp)
        recv = zr.at[u, lane, core]
        home = at.base + half
        if start:
            move(units[u], dst, zs.at[u, 0], recv, home, line, half == core)
        else:

            @pl.when(half != core)
            def _():
                remote(units[u], dst, zs.at[u, 0], recv, home, line).wait_send()

        for which, step in ((1, 1), (2, -1)):
            inside = line < 3 if step == 1 else line > 0

            @pl.when(inside)
            def _():
                copy = remote(units[u], dst, zs.at[u, which], recv, home, line + step)
                copy.start() if start else copy.wait_send()

    first = jnp.where(core == 0, jnp.where(line == 0, 0, 1), jnp.where(line == 3, 1, 0))

    def z_stage(u, k, other, start):
        zi = first + k - 2 * first * k
        origin = 2 * core + zi
        ref = spot(u, zi, at.base + other)
        if start:
            pltpu.make_async_copy(w1, ref, zr.at[u, zi, other]).wait()
        up = jnp.logical_and(origin < line, line < 3)
        down = jnp.logical_and(origin > line, line > 0)
        for go, step in ((up, 1), (down, -1)):

            @pl.when(go)
            def _():
                copy = remote(
                    ref, ref, fs.at[u, zi, other], zr.at[u, zi, other], dp, line + step
                )
                copy.start() if start else copy.wait_send()

        for which, near in ((0, at.dp_x), (1, at.dp_y)):
            copy = remote(
                ref, ref, ns.at[which, u, zi, other], nr.at[which, u, zi, other], near, line
            )
            copy.start() if start else copy.wait_send()

    def far_stage(u, zi, other, start):
        base = at.base_x + zi * (at.base_y - at.base_x)
        near = at.dp_y + zi * (at.dp_x - at.dp_y)
        ref = spot(u, zi, base + other)
        if start:
            pltpu.make_async_copy(w1, ref, nr.at[zi, u, zi, other]).wait()
        copy = remote(ref, ref, ds.at[u, zi, other], dr.at[u, zi, other], near, line)
        copy.start() if start else copy.wait_send()

    def last_stage(u, zi, other):
        base = at.base_y + zi * (at.base_x - at.base_y)
        ref = spot(u, zi, base + other)
        pltpu.make_async_copy(w1, ref, nr.at[1 - zi, u, zi, other]).wait()
        ref = spot(u, zi, at.base_far + other)
        pltpu.make_async_copy(w1, ref, dr.at[u, zi, other]).wait()

    def pump(number):
        u = 1 + number // 8
        k, other = (number % 4) // 2, number % 2

        @pl.when(number % 8 < 4)
        def _():
            z_stage(u, k, other, True)

        @pl.when(number % 8 >= 4)
        def _():
            far_stage(u, k, other, True)

    def keep(src, dst, number):
        return pltpu.make_async_copy(src, dst, ls.at[number])

    deal(0, True)
    source(0, True)
    for k in range(2):
        for other in range(2):
            z_stage(0, k, other, True)
    source(1, True)
    deal(1, True)

    def exchange(src, dst, number):
        return remote(src, dst, es.at[number], er.at[number], sib, line)

    deal_arrive(0)
    keep(xt, x_out, 0).start()

    for block in range(2):
        shift, scale = mod[block, 0:1, :], 1.0 + mod[block, 1:2, :]

        def norm_first(step, _):
            at_row = pl.ds(pl.multiple_of(step * 128, 128), 128)
            normed, _f = layer_norm(xt[block, at_row, :].astype(F32))
            to_row = pl.ds(pl.multiple_of(block * 256 + step * 128, 128), 128)
            h1[core, to_row, :] = (normed * scale + shift).astype(LOW)
            return 0

        lax.fori_loop(0, 2, norm_first, 0)
        part = h1.at[core, pl.ds(block * 256, 256)]
        exchange(part, part, block).start()
    for zi in range(2):
        for other in range(2):
            far_stage(0, zi, other, True)
    source(2, True)
    for zi in range(2):
        for other in range(2):
            last_stage(0, zi, other)
    keep(w0, head_out, 1).start()

    def project(step, _):
        @pl.when(step >= 2)
        def _():
            part = h1.at[1 - core, pl.ds(pl.multiple_of((step - 2) * 256, 256), 256)]
            pltpu.make_async_copy(part, part, er.at[step - 2]).wait()

        pump(step)
        tile = (2 * core + step) % 4
        rows = h1[tile // 2, pl.ds(pl.multiple_of((tile % 2) * 256, 256), 256), :]
        to_row = pl.ds(pl.multiple_of(tile * 256, 256), 256)
        narrow = lanes(256) < HD
        fills = (feat[0, pl.ds(tile, 1), :], feat[1, pl.ds(tile, 1), :], jnp.zeros((1, 128), F32))
        for zi in range(2):
            value = dot_nn(rows, w0[zi, :, 0:896])
            for number in range(12):
                head, part = zi * 4 + number // 3, number % 3
                piece = jnp.where(narrow, window(value, HD * number), fills[part])
                qkv[head, part, to_row, :] = piece.astype(LOW)
        return 0

    lax.fori_loop(0, 4, project, 0)
    keep(h1, h1_out, 2).start()
    keep(qkv, qkv_out, 3).start()

    factor = HD ** (-0.5) * LOG2E

    def attend(head, _):
        pump(4 + head)
        gain = hmask[head]

        def tile_step(tile, _):
            rows = pl.ds(pl.multiple_of(tile * 256, 256), 256)
            scores = dot_nt(qkv[head, 0, rows, :], qkv[head, 1])
            peak = jnp.max(scores, axis=1, keepdims=True)
            power = jnp.exp2((scores - peak) * factor)
            total = jnp.sum(power, axis=1, keepdims=True)
            probs = (power * (1.0 / total)).astype(LOW)
            obuf[head, rows, :] = (dot_nn(probs, qkv[head, 2]) * gain).astype(LOW)
            level = peak * factor + jnp.log2(total)
            stat[rows, :] = jnp.where(lanes(256) == head, level, stat[rows, :])
            return 0

        lax.fori_loop(0, 4, tile_step, 0)
        return 0

    lax.fori_loop(0, 8, attend, 0)
    keep(stat, stat_out, 4).start()

    def lay(step, _):
        rows = pl.ds(pl.multiple_of(step * 128, 128), 128)
        for zi in range(2):
            parts = [obuf[zi * 4 + n, rows, :].astype(F32) for n in range(4)]
            for tile, value in enumerate(pack(parts, 96, 3)):
                att[zi, rows, 128 * tile : 128 * tile + 128] = value.astype(LOW)
        return 0

    lax.fori_loop(0, 8, lay, 0)
    keep(att, att_out, 5).start()

    for step in range(4):
        tile = (2 * (1 - core) + step) % 4
        rows = pl.ds(pl.multiple_of(tile * 256, 256), 256)
        value = dot_nt(att[0, rows, :], w0[0, :, 768:1152])
        value = value + dot_nt(att[1, rows, :], w0[1, :, 768:1152])
        if step < 2:
            sb[step] = value.astype(LOW)
            exchange(sb.at[step], rb.at[step], 2 + step).start()
        else:
            br[step - 2] = value
    for block in range(2):
        exchange(sb.at[block], rb.at[block], 2 + block).wait_recv()
        gate = mod[block, 2:3, :]
        shift, scale = mod[block, 3:4, :], 1.0 + mod[block, 4:5, :]

        def norm_second(step, _):
            at_row = pl.ds(pl.multiple_of(step * 128, 128), 128)
            branch = br[block, at_row, :] + rb[block, at_row, :].astype(F32)
            br[block, at_row, :] = branch
            value = xt[block, at_row, :].astype(F32) + gate * branch
            x1[block, at_row, :] = value
            normed, _f = layer_norm(value)
            to_row = pl.ds(pl.multiple_of(block * 256 + step * 128, 128), 128)
            h2[core, to_row, :] = (normed * scale + shift).astype(LOW)
            return 0

        lax.fori_loop(0, 2, norm_second, 0)
        part = h2.at[core, pl.ds(block * 256, 256)]
        exchange(part, part, 4 + block).start()
    keep(x1, x1_out, 6).start()
    keep(br, br_out, 7).start()

    def drain(number, _):
        pump(number)
        return 0

    lax.fori_loop(12, 16, drain, 0)
    for block in range(2):
        part = h2.at[1 - core, pl.ds(block * 256, 256)]
        pltpu.make_async_copy(part, part, er.at[4 + block]).wait()
    keep(h2, h2_out, 8).start()

    for u in range(3):
        source(u, False)
        for k in range(2):
            for other in range(2):
                z_stage(u, k, other, False)
                far_stage(u, k, other, False)
                if u:
                    last_stage(u, k, other)
    for kind in range(2):
        deal(kind, False)
    deal_arrive(1)
    for block in range(2):
        own1 = h1.at[core, pl.ds(block * 256, 256)]
        own2 = h2.at[core, pl.ds(block * 256, 256)]
        exchange(own1, own1, block).wait_send()
        exchange(sb.at[block], rb.at[block], 2 + block).wait_send()
        exchange(own2, own2, 4 + block).wait_send()
    pairs = (
        (xt, x_out),
        (w0, head_out),
        (h1, h1_out),
        (qkv, qkv_out),
        (stat, stat_out),
        (att, att_out),
        (x1, x1_out),
        (br, br_out),
        (h2, h2_out),
    )
    for number, (src, dst) in enumerate(pairs):
        keep(src, dst, number).wait()


def run_front(hmask, wh, w1, w2, tok, cot, mod, feat):
    rows, cols = w1.shape
    part = tok.shape[1]
    length = 4 * part
    shape = jax.ShapeDtypeStruct
    vmem = pl.BlockSpec(memory_space=pltpu.VMEM)
    outs = (
        shape((2, 2, 8, rows, cols), LOW),
        shape((2, 8 * rows, cols), LOW),
        shape(tok.shape, LOW),
        shape(tok.shape, LOW),
        shape((2, 2 * part, cols), LOW),
        shape((8, 3, length, 128), LOW),
        shape((length, 128), F32),
        shape((2, length, 384), LOW),
        shape((2, part, cols), F32),
        shape((2, part, cols), F32),
        shape((2, 2 * part, cols), LOW),
    )
    three = DMA((3, 2, 2))
    return pl.pallas_call(
        front_kernel,
        out_shape=outs,
        in_specs=[pl.BlockSpec(memory_space=pltpu.SMEM)] + [ANY] * 5 + [vmem, vmem],
        out_specs=(ANY,) * len(outs),
        scratch_shapes=[
            pltpu.VMEM(tok.shape, LOW),
            pltpu.VMEM((2, 8 * rows, cols), LOW),
            pltpu.VMEM((2, 2 * part, cols), LOW),
            pltpu.VMEM((8, 3, length, 128), LOW),
            pltpu.VMEM((8, length, 128), LOW),
            pltpu.VMEM((length, 128), F32),
            pltpu.VMEM((2, length, 384), LOW),
            pltpu.VMEM((2, part, cols), LOW),
            pltpu.VMEM((2, part, cols), LOW),
            pltpu.VMEM((2, part, cols), F32),
            pltpu.VMEM((2, part, cols), F32),
            pltpu.VMEM((2, 2 * part, cols), LOW),
            DMA((3, 3)),
            three,
            three,
            DMA((2, 3, 2, 2)),
            DMA((2, 3, 2, 2)),
            three,
            three,
            DMA((2, 2)),
            DMA((2, 2)),
            DMA((6,)),
            DMA((6,)),
            DMA((9,)),
        ],
        compiler_params=pltpu.CompilerParams(
            collective_id=0, has_side_effects=True, vmem_limit_bytes=58 << 20
        ),
    )(hmask, wh, w1, w2, tok, cot, mod, feat)


def back_kernel(
    hmask,
    gfc,
    dh2_send,
    mlp_send,
    dh2_own,
    mlp_own,
    x1_in,
    br_in,
    x_in,
    g_in,
    h1_in,
    qkv_in,
    stat_in,
    att_in,
    head_in,
    mod,
    keep_col,
    out_tok,
    out_dtok,
    out_grad,
    rz,
    sums,
    w0,
    h1,
    qkv,
    stat,
    dpk,
    db,
    do,
    g0,
    dfirst,
    xb,
    yb,
    gb,
    xt,
    sb,
    rb,
    rm,
    ob,
    acc,
    r1,
    rn,
    stage,
    fin,
    s1s,
    s1r,
    nss,
    nsr,
    rls,
    zss,
    zsr,
    es,
    er,
    ts,
    tr,
    ls,
    gs,
):
    at = Place()
    dp, line, core, half = at.dp, at.line, at.core, at.half
    lane = line % 2
    rows_u = out_grad.shape[1]
    sib = at.base + 1 - core
    scale_q = HD ** (-0.5)
    factor = HD ** (-0.5) * LOG2E

    def load(src, dst, number):
        return pltpu.make_async_copy(src, dst, ls.at[number])

    load(head_in, w0, 0).start()
    load(qkv_in, qkv, 1).start()
    load(stat_in, stat, 2).start()
    load(att_in, dpk.at[:, :, 0:384], 3).start()
    load(h1_in, h1, 4).start()
    at.barrier()

    def exchange(src, dst, number):
        return remote(src, dst, es.at[number], er.at[number], sib, line)

    def grad_ref(u, zi, row):
        if isinstance(u, int) and u == 0:
            return g0.at[zi, pl.ds(pl.multiple_of(row * rows_u, 16), rows_u)]
        return gfc.at[u - 1, zi, row]

    def base_of(which):
        return at.base_x + which * (at.base_y - at.base_x)

    def near_of(which):
        return at.dp_x + which * (at.dp_y - at.dp_x)

    def far_send(u, zi, o):
        return remote(
            grad_ref(u, zi, at.base_far + o),
            r1.at[u, zi, o],
            s1s.at[u, zi, o],
            s1r.at[u, zi, o],
            near_of(zi),
            line,
        )

    def plain_send(u, zi, o):
        return remote(
            grad_ref(u, zi, base_of(zi) + o),
            rn.at[zi, u, zi, o],
            nss.at[zi, u, zi, o],
            nsr.at[zi, u, zi, o],
            near_of(zi),
            line,
        )

    def relay_send(u, zi, o):
        return remote(
            r1.at[u, zi, o],
            rn.at[1 - zi, u, zi, o],
            nss.at[1 - zi, u, zi, o],
            nsr.at[1 - zi, u, zi, o],
            near_of(1 - zi),
            line,
        )

    def fetch(u, zi, row, slot):
        if isinstance(u, int) and u == 0:
            return grad_ref(u, zi, row), None
        copy = pltpu.make_async_copy(grad_ref(u, zi, row), stage.at[slot], gs.at[slot])
        copy.start()
        return stage.at[slot], copy

    def relay(u, zi, o):
        ref, copy = fetch(u, zi, base_of(1 - zi) + o, 0)
        far_send(u, zi, o).wait_recv()
        if copy is not None:
            copy.wait()
        r1[u, zi, o] = (r1[u, zi, o].astype(F32) + ref[...].astype(F32)).astype(LOW)
        relay_send(u, zi, o).start()

    def settle(u, zi, o, start):
        here = jnp.logical_and(core == o, line == 2 * core + zi)
        src, dst = rn.at[0, u, zi, o], rz.at[u, line]
        send, recv = zss.at[u, zi, o], zsr.at[u, line]
        if not start:

            @pl.when(jnp.logical_not(here))
            def _():
                remote(src, dst, send, recv, at.base + o, 2 * core + zi).wait_send()

            return
        ref, copy = fetch(u, zi, at.base + o, 1)
        for which in range(2):
            there = rn.at[which, u, zi, o]
            pltpu.make_async_copy(there, there, nsr.at[which, u, zi, o]).wait()
        if copy is not None:
            copy.wait()
        total = rn[0, u, zi, o].astype(F32) + rn[1, u, zi, o].astype(F32)
        rn[0, u, zi, o] = (total + ref[...].astype(F32)).astype(LOW)
        move(src, dst, send, recv, at.base + o, 2 * core + zi, here)

    def finish(u):
        for source in range(4):
            ref = rz.at[u, source]
            pltpu.make_async_copy(ref, ref, zsr.at[u, source]).wait()
        for source in range(4):
            pltpu.make_async_copy(rz.at[u, source], stage.at[source], gs.at[source]).start()
        for source in range(4):
            pltpu.make_async_copy(rz.at[u, source], stage.at[source], gs.at[source]).wait()
        total = stage[0].astype(F32) + stage[1].astype(F32)
        fin[...] = total + (stage[2].astype(F32) + stage[3].astype(F32))
        copy = pltpu.make_async_copy(fin, out_grad.at[u], gs.at[0])
        copy.start()
        copy.wait()

    def pump(number):
        index = number % 8
        u, zi, o = 1 + index // 4, (index // 2) % 2, index % 2

        @pl.when(number < 8)
        def _():
            relay(u, zi, o)

        @pl.when(number >= 8)
        def _():
            settle(u, zi, o, True)

    def give_back(block, kind, start):
        dst = (out_tok, out_dtok)[kind].at[lane]
        there = 2 * core + block
        here = jnp.logical_and(half == core, there == line)
        send, recv = ts.at[kind, block], tr.at[kind, lane]
        if start:
            move(ob.at[block], dst, send, recv, at.base + half, there, here)
        else:

            @pl.when(here)
            def _():
                pltpu.make_async_copy(ob.at[block], dst, recv).wait()

            @pl.when(jnp.logical_not(here))
            def _():
                remote(ob.at[block], dst, send, recv, at.base + half, there).wait_send()

    for block in range(2):
        exchange(dh2_send.at[block], rb.at[block], block).start()
        exchange(mlp_send.at[block], rm.at[block], 2 + block).start()
    for u in (1, 2):
        for zi in range(2):
            for o in range(2):
                far_send(u, zi, o).start()
        for zi in range(2):
            for o in range(2):
                plain_send(u, zi, o).start()

    for block in range(2):
        copies = (
            load(x1_in.at[block], xb.at[0], 5),
            load(br_in.at[block], xb.at[1], 6),
            load(dh2_own.at[block], yb.at[0], 7),
            load(mlp_own.at[block], yb.at[1], 8),
            load(g_in.at[block], gb, 9),
        )
        for copy in copies:
            copy.start()
        for copy in copies:
            copy.wait()
        exchange(dh2_send.at[block], rb.at[block], block).wait_recv()
        exchange(mlp_send.at[block], rm.at[block], 2 + block).wait_recv()
        gate1, scale2 = mod[block, 2:3, :], 1.0 + mod[block, 4:5, :]
        gate2 = mod[block, 5:6, :]

        def norm_second(step, sums_now):
            at_row = pl.ds(pl.multiple_of(step * 128, 128), 128)
            grad = gb[at_row, :].astype(F32)
            first = xb[0, at_row, :]
            d_second = yb[0, at_row, :] + rb[block, at_row, :].astype(F32)
            kept = keep_col[block, at_row, :] * (
                yb[1, at_row, :] + rm[block, at_row, :].astype(F32)
            )
            ob[block, at_row, :] = (first + gate2 * kept).astype(LOW)
            normed, spread = layer_norm(first)
            d_first = grad + norm_back(d_second * scale2, normed, spread)
            dfirst[block, at_row, :] = d_first
            to_row = pl.ds(pl.multiple_of(block * 256 + step * 128, 128), 128)
            db[core, to_row, :] = (gate1 * d_first).astype(LOW)
            terms = (d_first * xb[1, at_row, :], d_second, d_second * normed, grad * kept)
            return tuple(
                now + jnp.sum(term, axis=0, keepdims=True) for now, term in zip(sums_now, terms)
            )

        zero = jnp.zeros((1, gb.shape[1]), F32)
        totals = lax.fori_loop(0, 2, norm_second, (zero,) * 4)
        for place, value in zip((2, 3, 4, 5), totals):
            sums[block, place : place + 1, :] = value
        part = db.at[core, pl.ds(block * 256, 256)]
        exchange(part, part, 4 + block).start()
        give_back(block, 0, True)

    for number in range(4):
        load((head_in, qkv_in, stat_in, att_in)[number], (w0, qkv, stat, dpk.at[:, :, 0:384])[number], number).wait()
    pump(jnp.int32(0))
    pump(jnp.int32(1))

    def to_heads(step, _):
        @pl.when(step >= 2)
        def _():
            part = db.at[1 - core, pl.ds(pl.multiple_of((step - 2) * 256, 256), 256)]
            pltpu.make_async_copy(part, part, er.at[4 + step - 2]).wait()

        tile = (2 * core + step) % 4
        rows = db[tile // 2, pl.ds(pl.multiple_of((tile % 2) * 256, 256), 256), :]
        to_row = pl.ds(pl.multiple_of(tile * 256, 256), 256)
        narrow = lanes(256) < HD
        for zi in range(2):
            value = dot_nn(rows, w0[zi, :, 768:1152])
            for number in range(4):
                piece = jnp.where(narrow, window(value, 96 + HD * number), 0.0)
                head = zi * 4 + number
                do[head, to_row, :] = (piece * hmask[head]).astype(LOW)
        return 0

    lax.fori_loop(0, 4, to_heads, 0)
    pump(jnp.int32(2))
    pump(jnp.int32(3))
    length = stat.shape[0]
    mid = length // 2
    for zi in range(2):
        for tile in range(3):
            cols = slice(384 * tile, 384 * tile + 384)
            value = dot_tn(db[0, :, cols], dpk[zi, 0:mid, 0:384])
            value = value + dot_tn(db[1, :, cols], dpk[zi, mid:length, 0:384])
            g0[zi, cols, 768:1152] = value.astype(LOW)

    def attend(head, _):
        pump(4 + head)
        acc[...] = jnp.zeros_like(acc)

        def tile_step(tile, _):
            rows = pl.ds(pl.multiple_of(tile * 256, 256), 256)
            query, grad = qkv[head, 0, rows, :], do[head, rows, :]
            level = jnp.sum(jnp.where(lanes(256) == head, stat[rows, :], 0.0), axis=1, keepdims=True)
            probs = jnp.exp2(dot_nt(query, qkv[head, 1]) * factor - level)
            d_probs = dot_nt(grad, qkv[head, 2])
            inner = jnp.sum(probs * d_probs, axis=1, keepdims=True)
            d_scores = (probs * (d_probs - inner)).astype(LOW)
            acc[0] += dot_tn(d_scores, query)
            acc[1] += dot_tn(probs.astype(LOW), grad)
            qkv[head, 0, rows, :] = (dot_nn(d_scores, qkv[head, 1]) * scale_q).astype(LOW)
            return 0

        lax.fori_loop(0, 4, tile_step, 0)
        qkv[head, 1] = (acc[0] * scale_q).astype(LOW)
        qkv[head, 2] = acc[1].astype(LOW)
        return 0

    lax.fori_loop(0, 8, attend, 0)

    def lay(step, _):
        rows = pl.ds(pl.multiple_of(step * 128, 128), 128)
        for zi in range(2):
            parts = [
                jnp.where(lanes(128) < HD, qkv[zi * 4 + n // 3, n % 3, rows, :].astype(F32), 0.0)
                for n in range(12)
            ]
            for tile, value in enumerate(pack(parts, 0, 7)):
                dpk[zi, rows, 128 * tile : 128 * tile + 128] = value.astype(LOW)
        return 0

    lax.fori_loop(0, 8, lay, 0)
    load(h1_in, h1, 4).wait()
    for zi in range(2):
        for tile in range(3):
            cols = slice(384 * tile, 384 * tile + 384)
            value = dot_tn(h1[0, :, cols], dpk[zi, 0:mid, :])
            value = value + dot_tn(h1[1, :, cols], dpk[zi, mid:length, :])
            g0[zi, cols, 0:768] = value[:, 0:768].astype(LOW)
            both = value[:, 768:896] + g0[zi, cols, 768:896].astype(F32)
            g0[zi, cols, 768:896] = both.astype(LOW)
    for zi in range(2):
        for o in range(2):
            far_send(0, zi, o).start()
    for zi in range(2):
        for o in range(2):
            plain_send(0, zi, o).start()

    for block in range(2):
        load(x_in.at[block], xt.at[block], 5 + block).start()
    for step in range(4):
        tile = (2 * (1 - core) + step) % 4
        rows = pl.ds(pl.multiple_of(tile * 256, 256), 256)
        value = dot_nt(dpk[0, rows, :], w0[0, :, 0:896])
        value = value + dot_nt(dpk[1, rows, :], w0[1, :, 0:896])
        if step < 2:
            sb[step] = value.astype(LOW)
            exchange(sb.at[step], rb.at[step], 6 + step).start()
        else:
            yb[step - 2] = value
    for block in range(2):
        give_back(block, 0, False)
        load(x_in.at[block], xt.at[block], 5 + block).wait()
        exchange(sb.at[block], rb.at[block], 6 + block).wait_recv()
        scale1 = 1.0 + mod[block, 1:2, :]

        def norm_first(step, sums_now):
            at_row = pl.ds(pl.multiple_of(step * 128, 128), 128)
            d_norm = yb[block, at_row, :] + rb[block, at_row, :].astype(F32)
            normed, spread = layer_norm(xt[block, at_row, :].astype(F32))
            d_input = dfirst[block, at_row, :] + norm_back(d_norm * scale1, normed, spread)
            ob[block, at_row, :] = d_input.astype(LOW)
            terms = (d_norm, d_norm * normed)
            return tuple(
                now + jnp.sum(term, axis=0, keepdims=True) for now, term in zip(sums_now, terms)
            )

        zero = jnp.zeros((1, gb.shape[1]), F32)
        totals = lax.fori_loop(0, 2, norm_first, (zero,) * 2)
        for place, value in zip((0, 1), totals):
            sums[block, place : place + 1, :] = value
        sums[block, 6:8, :] = jnp.zeros((2, gb.shape[1]), F32)
        give_back(block, 1, True)

    def drain(number, _):
        pump(number)
        return 0

    lax.fori_loop(12, 16, drain, 0)
    for zi in range(2):
        for o in range(2):
            relay(0, zi, o)
    finish(1)
    finish(2)
    for zi in range(2):
        for o in range(2):
            settle(0, zi, o, True)
    finish(0)

    for u in range(3):
        for zi in range(2):
            for o in range(2):
                far_send(u, zi, o).wait_send()
                plain_send(u, zi, o).wait_send()
                relay_send(u, zi, o).wait_send()
                settle(u, zi, o, False)
    for block in range(2):
        give_back(block, 1, False)
        exchange(dh2_send.at[block], rb.at[block], block).wait_send()
        exchange(mlp_send.at[block], rm.at[block], 2 + block).wait_send()
        part = db.at[core, pl.ds(block * 256, 256)]
        exchange(part, part, 4 + block).wait_send()
        exchange(sb.at[block], rb.at[block], 6 + block).wait_send()
    for kind in range(2):
        dst = (out_tok, out_dtok)[kind]
        for slot in range(2):
            source = 2 * core + slot
            here = jnp.logical_and(source == line, half == core)

            @pl.when(jnp.logical_not(here))
            def _():
                pltpu.make_async_copy(dst.at[slot], dst.at[slot], tr.at[kind, slot]).wait()


def run_back(hmask, gfc, *rest):
    ins = (hmask, gfc) + rest
    rows, cols = gfc.shape[3:]
    part = rest[0].shape[1]
    length = 4 * part
    shape = jax.ShapeDtypeStruct
    vmem = pl.BlockSpec(memory_space=pltpu.VMEM)
    outs = (
        shape((2, part, cols), LOW),
        shape((2, part, cols), LOW),
        shape((3, rows, cols), F32),
        shape((3, 4, rows, cols), LOW),
        shape((2, 8, cols), F32),
    )
    three = DMA((3, 2, 2))
    return pl.pallas_call(
        back_kernel,
        out_shape=outs,
        in_specs=[pl.BlockSpec(memory_space=pltpu.SMEM)] + [ANY] * 14 + [vmem] * 2,
        out_specs=(ANY,) * 4 + (vmem,),
        scratch_shapes=[
            pltpu.VMEM((2, 8 * rows, cols), LOW),
            pltpu.VMEM((2, 2 * part, cols), LOW),
            pltpu.VMEM((8, 3, length, 128), LOW),
            pltpu.VMEM((length, 128), F32),
            pltpu.VMEM((2, length, 896), LOW),
            pltpu.VMEM((2, 2 * part, cols), LOW),
            pltpu.VMEM((8, length, 128), LOW),
            pltpu.VMEM((2, 8 * rows, cols), LOW),
            pltpu.VMEM((2, part, cols), F32),
            pltpu.VMEM((2, part, cols), F32),
            pltpu.VMEM((2, part, cols), F32),
            pltpu.VMEM((part, cols), LOW),
            pltpu.VMEM((2, part, cols), LOW),
            pltpu.VMEM((2, part, cols), LOW),
            pltpu.VMEM((2, part, cols), LOW),
            pltpu.VMEM((2, part, cols), LOW),
            pltpu.VMEM((2, part, cols), LOW),
            pltpu.VMEM((2, length, 128), F32),
            pltpu.VMEM((3, 2, 2, rows, cols), LOW),
            pltpu.VMEM((2, 3, 2, 2, rows, cols), LOW),
            pltpu.VMEM((4, rows, cols), LOW),
            pltpu.VMEM((rows, cols), F32),
            three,
            three,
            DMA((2, 3, 2, 2)),
            DMA((2, 3, 2, 2)),
            three,
            three,
            DMA((3, 4)),
            DMA((8,)),
            DMA((8,)),
            DMA((2, 2)),
            DMA((2, 2)),
            DMA((10,)),
            DMA((4,)),
        ],
        compiler_params=pltpu.CompilerParams(
            collective_id=1, has_side_effects=True, vmem_limit_bytes=63 << 20
        ),
    )(*ins)


def fast_body(
    tokens,
    time_embed,
    segments,
    micro_order,
    head_mask,
    group_mask,
    keep_route,
    w_qkv,
    w_proj,
    w_fc1,
    w_fc2,
    w_ada,
    b_ada,
    cotangent,
):
    dp = lax.axis_index("dp")
    line = lax.axis_index("tensor")
    core = dp % 2
    chip = dp // 2
    odd = line % 2
    owner = line // 2
    segs = time_embed.shape[1]
    part = tokens.shape[1]
    width = tokens.shape[2]
    length = segments.shape[1]
    qcols = w_qkv.shape[1]
    heads_here = head_mask.shape[1]

    hsel = head_mask[micro_order]
    gsel = group_mask[micro_order]
    packed_meta = jnp.concatenate([hsel, gsel, keep_route], axis=1)
    meta = lax.all_gather(packed_meta, "tensor", axis=0, tiled=False)
    meta_other, seg_other = sibling(meta), sibling(segments)
    meta = pick(jnp.where(core == owner, meta, meta_other).transpose(1, 0, 2), odd)
    seg_ids = pick(jnp.where(core == owner, segments, seg_other), odd)
    hmask = lax.dynamic_slice_in_dim(meta[:, :heads_here], 2 * core, 2).astype(jnp.float32)
    gmask = lax.dynamic_slice_in_dim(meta[:, heads_here : 2 * heads_here], 2 * core, 2)
    gcols = jnp.repeat(gmask.astype(jnp.float32), FF // GROUPS, axis=1)
    keepf = lax.dynamic_slice_in_dim(meta[:, 2 * heads_here :], 2 * core, 2).astype(jnp.float32)
    keep_col = keepf[:, :, None]

    te_all = lax.all_gather(time_embed, "dp", axis=0, tiled=True).reshape(-1, width)
    scond = jax.nn.silu(te_all.astype(jnp.float32)).astype(jnp.bfloat16)
    scond_rows = lax.dynamic_slice_in_dim(scond, dp * w_ada.shape[0], w_ada.shape[0], axis=1)
    part_mods = jnp.dot(scond_rows, w_ada, preferred_element_type=jnp.float32)
    my_mods = lax.psum_scatter(part_mods, "dp", scatter_dimension=0, tiled=True) + b_ada[None, :]
    line_mods = lax.all_gather(my_mods, "tensor", axis=1, tiled=True)
    other_mods = sibling(line_mods)
    mods = pick(jnp.where(core == owner, line_mods, other_mods).reshape(2, segs, -1), odd)
    block_item = lax.dynamic_slice_in_dim(seg_ids[:: length // 4], 2 * core, 2)
    modtok = mods[block_item][:, None, :]
    shift1, scale1, gate1, shift2, scale2, gate2 = jnp.split(modtok, 6, axis=2)

    whead = jnp.concatenate([w_qkv, w_proj], axis=1)
    mod = jnp.pad(mods[block_item].reshape(2, 6, width), ((0, 0), (0, 2), (0, 0)))
    items = seg_ids[:: length // 4]
    spots = jnp.arange(128, dtype=jnp.int32)[None, :] - HD
    same = (items[:, None] == spots).astype(jnp.float32)
    inside = jnp.logical_and(spots >= 0, spots < segs)
    feat = jnp.stack([jnp.where(inside, SHADE * (1.0 - same), 0.0), same])
    (
        weights,
        head_w,
        dealt,
        dealt_grad,
        h_first,
        qkv,
        stat,
        att,
        first,
        branch,
        h_second,
    ) = run_front(hmask.reshape(-1), whead, w_fc1, w_fc2, tokens, cotangent, mod, feat)
    weights = weights.reshape(2, 2, width, w_fc1.shape[1])
    full_qkv = head_w[:, :, :qcols]
    full_proj = head_w[:, :, qcols:]
    full_fc1 = weights[0]
    full_fc2 = weights[1]
    grad_out = dealt_grad.astype(jnp.float32)
    h_second = h_second.reshape(length, width)

    def share(value):
        rows = value.astype(jnp.bfloat16).reshape(2 * part, width)
        return order(core, rows, sibling(rows))

    d_mlp = share(gate2 * keep_col * grad_out)
    upward = jnp.einsum("rd,zdu->zru", h_second, full_fc1, preferred_element_type=jnp.float32)
    gelu_val, gelu_pull = jax.vjp(lambda inner: jax.nn.gelu(inner, approximate=True), upward)
    act = (gelu_val * gcols[:, None, :]).astype(jnp.bfloat16)
    def halves(partial):
        theirs = lax.dynamic_slice_in_dim(partial, (1 - core) * 2 * part, 2 * part)
        mine = lax.dynamic_slice_in_dim(partial, core * 2 * part, 2 * part)
        shape = (2, part, width)
        return theirs.astype(jnp.bfloat16).reshape(shape), mine.reshape(shape)

    mlp_send, mlp_own = halves(
        jnp.einsum("zru,zou->ro", act, full_fc2, preferred_element_type=jnp.float32)
    )
    grad_fc2 = jnp.einsum("ro,zru->zou", d_mlp, act, preferred_element_type=jnp.float32)
    d_act = jnp.einsum("ro,zou->zru", d_mlp, full_fc2, preferred_element_type=jnp.float32)
    d_up = gelu_pull(d_act * gcols[:, None, :])[0].astype(jnp.bfloat16)
    grad_fc1 = jnp.einsum("rd,zru->zdu", h_second, d_up, preferred_element_type=jnp.float32)
    dh2_send, dh2_own = halves(
        jnp.einsum("zru,zdu->rd", d_up, full_fc1, preferred_element_type=jnp.float32)
    )
    gfc = jnp.stack([grad_fc1, grad_fc2]).astype(jnp.bfloat16)
    gfc = gfc.reshape(2, 2, 8, width // 8, width)
    result, d_input, grads, _, sums = run_back(
        hmask.reshape(-1),
        gfc,
        dh2_send,
        mlp_send,
        dh2_own,
        mlp_own,
        first,
        branch,
        dealt,
        dealt_grad,
        h_first,
        qkv,
        stat,
        att,
        head_w,
        mod,
        keep_col,
    )
    sums = sums[:, :6].reshape(2, -1)
    onehot = (block_item[None, :] == jnp.arange(segs, dtype=jnp.int32)[:, None]).astype(jnp.float32)
    d_mods = jnp.sum(onehot[:, :, None] * sums[None], axis=1)
    cols = b_ada.shape[0]
    d_lines = lax.all_to_all(
        d_mods.reshape(segs, -1, cols).transpose(1, 0, 2), "tensor", 0, 0, tiled=False
    )
    d_all = lax.all_gather(d_lines, "dp", axis=0, tiled=False)
    d_all = d_all.reshape(-1, 2, *d_lines.shape).sum(axis=1).reshape(-1, cols)
    g_ada = jnp.dot(scond_rows.astype(jnp.float32).T, d_all, precision=HIGH)
    g_bias = jnp.sum(d_all, axis=0)

    return (
        result,
        d_input,
        grads[0, :, :qcols],
        grads[0, :, qcols:],
        grads[1],
        grads[2],
        g_ada,
        g_bias,
    )


def solution(mesh):
    placed = (
        P("dp", "tensor", None),
        P("dp", None, None),
        P("dp", None),
        P("dp"),
        P("dp", "tensor"),
        P("dp", "tensor"),
        P("dp", "tensor"),
        P("dp", "tensor"),
        P("dp", "tensor"),
        P("dp", "tensor"),
        P("dp", "tensor"),
        P("dp", "tensor"),
        P("tensor"),
        P("dp", "tensor", None),
    )
    return jax.shard_map(
        fast_body if mesh.shape["dp"] == 8 and mesh.shape["tensor"] == 4 else body,
        mesh=mesh,
        in_specs=placed,
        out_specs=(
            P("dp", "tensor", None),
            P("dp", "tensor", None),
            P("dp", "tensor"),
            P("dp", "tensor"),
            P("dp", "tensor"),
            P("dp", "tensor"),
            P("dp", "tensor"),
            P("tensor"),
        ),
        check_vma=False,
    )
```

```python
import jax
import jax.numpy as jnp
from jax import lax
from jax.experimental import pallas as pl
from jax.experimental.pallas import tpu as pltpu
from jax.sharding import PartitionSpec as P

HD = 72
FF = 4608
GROUPS = 16


EPSILON = 1e-06
HIGH = lax.Precision.HIGHEST


def layer_norm(values):
    middle = jnp.mean(values, axis=-1, keepdims=True)
    centred = values - middle
    spread = jnp.mean(centred * centred, axis=-1, keepdims=True)
    factor = lax.rsqrt(spread + EPSILON)
    return (centred * factor, factor)


def norm_back(grad, normed, factor):
    inner = (
        grad
        - jnp.mean(grad, axis=-1, keepdims=True)
        - normed * jnp.mean(grad * normed, axis=-1, keepdims=True)
    )
    return factor * inner


def contract_rows(left, right):
    return lax.dot_general(
        left, right, (((0,), (0,)), ((), ())), preferred_element_type=jnp.float32
    )


def contract_cols(left, right):
    return lax.dot_general(
        left, right, (((1,), (1,)), ((), ())), preferred_element_type=jnp.float32
    )


def score_block(query_block, keys, seg_block, seg_ids):
    scores = jnp.einsum(
        "qhe,khe->hqk", query_block, keys, preferred_element_type=jnp.float32
    ) * HD ** (-0.5)
    same = seg_block[:, None] == seg_ids[None, :]
    return jnp.where(same[None], scores, -1e30)


def attention_forward(query, keys, values, seg_ids):
    length = query.shape[0]
    block = min(512, length)
    outs = []
    totals = []
    for offset in range(0, length, block):
        scores = score_block(
            query[offset : offset + block], keys, seg_ids[offset : offset + block], seg_ids
        )
        peak = jnp.max(scores, axis=-1, keepdims=True)
        denom = jnp.sum(jnp.exp(scores - peak), axis=-1, keepdims=True)
        log_total = peak + jnp.log(denom)
        probs = jnp.exp(scores - log_total).astype(jnp.bfloat16)
        outs.append(jnp.einsum("hqk,khe->qhe", probs, values, preferred_element_type=jnp.float32))
        totals.append(log_total)
    return (jnp.concatenate(outs, axis=0), totals)


def attention_backward(query, keys, values, seg_ids, totals, d_attn):
    length = query.shape[0]
    block = min(512, length)
    scale = HD ** (-0.5)
    d_keys = jnp.zeros(keys.shape, jnp.float32)
    d_values = jnp.zeros(values.shape, jnp.float32)
    d_queries = []
    for number, offset in enumerate(range(0, length, block)):
        query_block = query[offset : offset + block]
        scores = score_block(query_block, keys, seg_ids[offset : offset + block], seg_ids)
        probs = jnp.exp(scores - totals[number])
        grad_block = d_attn[offset : offset + block]
        d_values = d_values + jnp.einsum(
            "hqk,qhe->khe",
            probs.astype(jnp.bfloat16),
            grad_block,
            preferred_element_type=jnp.float32,
        )
        d_probs = jnp.einsum("qhe,khe->hqk", grad_block, values, preferred_element_type=jnp.float32)
        d_scores = (probs * (d_probs - jnp.sum(probs * d_probs, axis=-1, keepdims=True))).astype(
            jnp.bfloat16
        )
        d_queries.append(
            jnp.einsum("hqk,khe->qhe", d_scores, keys, preferred_element_type=jnp.float32) * scale
        )
        d_keys = (
            d_keys
            + jnp.einsum("hqk,qhe->khe", d_scores, query_block, preferred_element_type=jnp.float32)
            * scale
        )
    stacked = jnp.stack([jnp.concatenate(d_queries, axis=0), d_keys, d_values], axis=2)
    return stacked.astype(jnp.bfloat16).reshape(length, -1)


def body(
    tokens,
    time_embed,
    segments,
    micro_order,
    head_mask,
    group_mask,
    keep_route,
    w_qkv,
    w_proj,
    w_fc1,
    w_fc2,
    w_ada,
    b_ada,
    cotangent,
):
    micro = tokens.shape[0]
    local_rows = tokens.shape[1]
    length = segments.shape[1]
    heads_here = head_mask.shape[1]
    segs = time_embed.shape[1]
    tensor_index = lax.axis_index("tensor")
    chooser = (micro_order[:, None] == jnp.arange(micro, dtype=jnp.int32)[None, :]).astype(
        jnp.float32
    )
    head_sel = jnp.dot(chooser, head_mask.astype(jnp.float32), precision=HIGH)
    group_sel = jnp.repeat(
        jnp.dot(chooser, group_mask.astype(jnp.float32), precision=HIGH), FF // GROUPS, axis=1
    )
    keep_float = keep_route.astype(jnp.float32)

    def reduce_grads(grad_qkv, grad_proj, grad_fc1, grad_fc2, grad_ada):
        return (
            lax.psum_scatter(
                grad_qkv.astype(jnp.bfloat16), "dp", scatter_dimension=0, tiled=True
            ).astype(jnp.float32),
            lax.psum_scatter(
                grad_proj.astype(jnp.bfloat16), "dp", scatter_dimension=0, tiled=True
            ).astype(jnp.float32),
            lax.psum_scatter(
                grad_fc1.astype(jnp.bfloat16), "dp", scatter_dimension=0, tiled=True
            ).astype(jnp.float32),
            lax.psum_scatter(
                grad_fc2.astype(jnp.bfloat16), "dp", scatter_dimension=0, tiled=True
            ).astype(jnp.float32),
            lax.psum_scatter(
                grad_ada.astype(jnp.bfloat16), "dp", scatter_dimension=0, tiled=True
            ).astype(jnp.float32),
        )

    shard_shapes = [w.shape for w in (w_qkv, w_proj, w_fc1, w_fc2, w_ada)]
    start_acc = tuple((jnp.zeros(shape, jnp.float32) for shape in shard_shapes))

    def slot_step(carry, items):
        acc, bias_acc = carry
        slot_tokens, slot_grad, seg_ids, embed, hmask, gcols, keepf = items
        full = (
            lax.all_gather(w_qkv, "dp", axis=0, tiled=True),
            lax.all_gather(w_proj, "dp", axis=0, tiled=True),
            lax.all_gather(w_fc1, "dp", axis=0, tiled=True),
            lax.all_gather(w_fc2, "dp", axis=0, tiled=True),
            lax.all_gather(w_ada, "dp", axis=0, tiled=True),
        )
        full_qkv, full_proj, full_fc1, full_fc2, full_ada = full
        seg_local = lax.dynamic_slice_in_dim(seg_ids, tensor_index * local_rows, local_rows)
        scond = jax.nn.silu(embed.astype(jnp.float32)).astype(jnp.bfloat16)
        part_mods = jnp.dot(scond, full_ada, preferred_element_type=jnp.float32) + b_ada[None, :]
        mods = lax.all_gather(part_mods, "tensor", axis=1, tiled=True)
        onehot = (seg_local[:, None] == jnp.arange(segs, dtype=jnp.int32)[None, :]).astype(
            jnp.float32
        )
        modtok = jnp.dot(onehot, mods, precision=HIGH)
        shift1, scale1, gate1, shift2, scale2, gate2 = jnp.split(modtok, 6, axis=1)
        token_vals = slot_tokens.astype(jnp.float32)
        normed1, factor1 = layer_norm(token_vals)
        h_first = lax.all_gather(
            (normed1 * (1.0 + scale1) + shift1).astype(jnp.bfloat16), "tensor", axis=0, tiled=True
        )
        packed = jnp.dot(h_first, full_qkv, preferred_element_type=jnp.float32).astype(jnp.bfloat16)
        packed = packed.reshape(length, heads_here, 3, HD)
        query = packed[:, :, 0]
        keys = packed[:, :, 1]
        values = packed[:, :, 2]
        outs, totals = attention_forward(query, keys, values, seg_ids)
        attn = (outs * hmask[None, :, None]).astype(jnp.bfloat16).reshape(length, heads_here * HD)
        branch = lax.psum_scatter(
            contract_cols(attn, full_proj).astype(jnp.bfloat16),
            "tensor",
            scatter_dimension=0,
            tiled=True,
        ).astype(jnp.float32)
        first = token_vals + gate1 * branch
        normed2, factor2 = layer_norm(first)
        h_second = lax.all_gather(
            (normed2 * (1.0 + scale2) + shift2).astype(jnp.bfloat16), "tensor", axis=0, tiled=True
        )
        upward = jnp.dot(h_second, full_fc1, preferred_element_type=jnp.float32)
        gelu_val, gelu_pull = jax.vjp(lambda inner: jax.nn.gelu(inner, approximate=True), upward)
        act = (gelu_val * gcols[None, :]).astype(jnp.bfloat16)
        mlp = lax.psum_scatter(
            contract_cols(act, full_fc2).astype(jnp.bfloat16),
            "tensor",
            scatter_dimension=0,
            tiled=True,
        ).astype(jnp.float32)
        keep_col = keepf[:, None]
        result = (first + gate2 * keep_col * mlp).astype(jnp.bfloat16)
        grad_out = slot_grad.astype(jnp.float32)
        d_mlp = lax.all_gather(
            (gate2 * keep_col * grad_out).astype(jnp.bfloat16), "tensor", axis=0, tiled=True
        )
        grad_fc2 = contract_rows(d_mlp, act)
        d_act = jnp.dot(d_mlp, full_fc2, preferred_element_type=jnp.float32)
        d_up = gelu_pull(d_act * gcols[None, :])[0].astype(jnp.bfloat16)
        grad_fc1 = contract_rows(h_second, d_up)
        d_second = lax.psum_scatter(
            contract_cols(d_up, full_fc1).astype(jnp.bfloat16),
            "tensor",
            scatter_dimension=0,
            tiled=True,
        ).astype(jnp.float32)
        d_first = grad_out + norm_back(d_second * (1.0 + scale2), normed2, factor2)
        d_branch = lax.all_gather(
            (gate1 * d_first).astype(jnp.bfloat16), "tensor", axis=0, tiled=True
        )
        grad_proj = contract_rows(d_branch, attn)
        d_attn = jnp.dot(d_branch, full_proj, preferred_element_type=jnp.float32).astype(
            jnp.bfloat16
        )
        d_attn = d_attn.reshape(length, heads_here, HD) * hmask[None, :, None].astype(jnp.bfloat16)
        d_packed = attention_backward(query, keys, values, seg_ids, totals, d_attn)
        grad_qkv = contract_rows(h_first, d_packed)
        d_h_first = lax.psum_scatter(
            contract_cols(d_packed, full_qkv).astype(jnp.bfloat16),
            "tensor",
            scatter_dimension=0,
            tiled=True,
        ).astype(jnp.float32)
        d_input = d_first + norm_back(d_h_first * (1.0 + scale1), normed1, factor1)
        d_modtok = jnp.concatenate(
            [
                d_h_first,
                d_h_first * normed1,
                d_first * branch,
                d_second,
                d_second * normed2,
                grad_out * keep_col * mlp,
            ],
            axis=1,
        )
        part_dmods = lax.dot_general(onehot, d_modtok, (((0,), (0,)), ((), ())), precision=HIGH)
        d_mods = lax.psum_scatter(
            part_dmods.astype(jnp.bfloat16), "tensor", scatter_dimension=1, tiled=True
        ).astype(jnp.float32)
        grad_ada = jnp.dot(scond.astype(jnp.float32).T, d_mods, precision=HIGH)
        bias_acc = bias_acc + jnp.sum(d_mods, axis=0)
        parts = reduce_grads(grad_qkv, grad_proj, grad_fc1, grad_fc2, grad_ada)
        acc = tuple((held + piece for held, piece in zip(acc, parts)))
        return ((acc, bias_acc), (result, d_input.astype(jnp.bfloat16)))

    start_bias = jnp.zeros(b_ada.shape, jnp.float32)
    (acc, bias_acc), (results, d_tokens) = lax.scan(
        slot_step,
        (start_acc, start_bias),
        (tokens, cotangent, segments, time_embed, head_sel, group_sel, keep_float),
    )
    g_bias = lax.psum(bias_acc, "dp")
    return (results, d_tokens, acc[0], acc[1], acc[2], acc[3], acc[4], g_bias)


MESH = pl.DeviceIdType.MESH
ANY = pl.BlockSpec(memory_space=pl.ANY)
DMA = pltpu.SemaphoreType.DMA


class Place:
    def __init__(self):
        self.dp = lax.axis_index("dp")
        self.line = lax.axis_index("tensor")
        self.core = self.dp % 2
        self.base = self.dp - self.core
        self.half = self.line // 2
        x, y = (self.dp // 2) % 2, self.dp // 4
        self.dp_x = self.dp + 2 * (1 - 2 * x)
        self.dp_y = self.dp + 4 * (1 - 2 * y)
        self.base_x = self.dp_x - self.core
        self.base_y = self.dp_y - self.core
        self.base_far = self.base_x + self.base_y - self.base

    def barrier(self):
        bar = pltpu.get_barrier_semaphore()
        spot = self.core * 4 + self.line
        for step in range(1, 8):
            other = (spot + step) % 8
            pl.semaphore_signal(
                bar,
                inc=1,
                device_id=(self.base + other // 4, other % 4),
                device_id_type=MESH,
            )
        for step in range(1, 8):
            other = (self.dp + step) % 8
            pl.semaphore_signal(bar, inc=1, device_id=(other, self.line), device_id_type=MESH)
        pl.semaphore_wait(bar, 14)


def remote(src, dst, send, recv, dp, line):
    return pltpu.make_async_remote_copy(
        src_ref=src,
        dst_ref=dst,
        send_sem=send,
        recv_sem=recv,
        device_id=(dp, line),
        device_id_type=MESH,
    )


def move(src, dst, send, recv, dp, line, here):
    @pl.when(here)
    def _():
        pltpu.make_async_copy(src, dst, recv).start()

    @pl.when(jnp.logical_not(here))
    def _():
        remote(src, dst, send, recv, dp, line).start()


LOG2E = 1.4426950408889634
LOW = jnp.bfloat16
F32 = jnp.float32
SHADE = -1e30


def dot_nn(left, right):
    return jnp.dot(left, right, preferred_element_type=F32)


def dot_nt(left, right):
    return lax.dot_general(left, right, (((1,), (1,)), ((), ())), preferred_element_type=F32)


def dot_tn(left, right):
    return lax.dot_general(left, right, (((0,), (0,)), ((), ())), preferred_element_type=F32)


def lanes(rows):
    return lax.broadcasted_iota(jnp.int32, (rows, 128), 1)


def window(value, start):
    tile, rest = start // 128, start % 128
    here = value[:, 128 * tile : 128 * tile + 128]
    if rest == 0:
        return here
    here = pltpu.roll(here, 128 - rest, 1)
    if rest + HD <= 128:
        return here
    after = pltpu.roll(value[:, 128 * tile + 128 : 128 * tile + 256], 128 - rest, 1)
    return jnp.where(lanes(value.shape[0]) < 128 - rest, here, after)


def pack(parts, start, tiles):
    rows = parts[0].shape[0]
    lane = lanes(rows)
    out = []
    for tile in range(tiles):
        total = jnp.zeros((rows, 128), F32)
        for number, part in enumerate(parts):
            low = start + HD * number - 128 * tile
            if low >= 128 or low + HD <= 0:
                continue
            moved = pltpu.roll(part, low % 128, 1) if low % 128 else part
            inside = jnp.logical_and(lane >= low, lane < low + HD)
            total = jnp.where(inside, moved, total)
        out.append(total)
    return out


def turned(value, tile):
    start = 128 * tile
    stop = min(start + 128, value.shape[1])
    part = value[:, start:stop]
    if stop - start < 128:
        part = jnp.concatenate([part, jnp.zeros((part.shape[0], 64), F32)], axis=1)
    return pltpu.roll(part, 64, 1)


def to_blocks(even, odd):
    low = lanes(even.shape[0]) < 64
    turn = [turned(odd, tile) for tile in range(14)]
    tail = jnp.concatenate([even[:, 1664:1728], jnp.zeros((even.shape[0], 64), F32)], axis=1)
    one = [even[:, 0:1152]]
    two = [even[:, 1152:1664], jnp.where(low, tail, turn[0])]
    two += [jnp.where(low, turn[t], turn[t + 1]) for t in range(4)]
    three = [jnp.where(low, turn[t], turn[t + 1]) for t in range(4, 13)]
    return [jnp.concatenate(parts, axis=1) for parts in (one, two, three)]


def to_chunks(one, two, three):
    low = lanes(one.shape[0]) < 64
    even = jnp.concatenate([one, two[:, 0:576]], axis=1)
    turn = [turned(two, tile) for tile in range(4, 9)] + [turned(three, t) for t in range(9)]
    odd = [jnp.where(low, turn[t], turn[t + 1]) for t in range(13)]
    return even, jnp.concatenate(odd + [turn[13][:, 0:64]], axis=1)


def front_kernel(
    wh,
    w1,
    w2,
    tok,
    cot,
    meta,
    te,
    wa,
    ba,
    weights,
    head_out,
    x_out,
    g_out,
    h1_out,
    qkv_out,
    stat_out,
    att_out,
    x1_out,
    br_out,
    h2_out,
    dm_out,
    cond,
    mod,
    gains,
    groups,
    kept,
    select,
    xt,
    w0,
    h1,
    qkv,
    obuf,
    stat,
    att,
    sb,
    rb,
    br,
    x1,
    h2,
    ct,
    dm,
    mt,
    te_all,
    pb,
    pr,
    mine,
    mr,
    feat,
    zs,
    zr,
    fs,
    ns,
    nr,
    ds,
    dr,
    ts,
    tr,
    es,
    er,
    ls,
    ms,
    mrs,
    tes,
    ter,
    pbs,
    pbr,
    mms,
    mmr,
):
    at = Place()
    dp, line, core, half = at.dp, at.line, at.core, at.half
    units = (wh, w1, w2)
    lane = line % 2
    rows_u = w1.shape[0]
    sib = at.base + 1 - core
    at.barrier()

    def spot(u, zi, row):
        if isinstance(u, int) and u == 0:
            return w0.at[zi, pl.ds(pl.multiple_of(row * rows_u, 16), rows_u)]
        return weights.at[u - 1, zi, row]

    def deal(kind, start):
        src, dst = ((tok, xt), (cot, ct))[kind]
        for slot in range(2):
            there = 2 * core + slot
            here = jnp.logical_and(half == core, there == line)
            send, recv = ts.at[kind, slot], tr.at[kind, lane]
            if start:
                move(src.at[slot], dst.at[lane], send, recv, at.base + half, there, here)
            else:

                @pl.when(jnp.logical_not(here))
                def _():
                    remote(
                        src.at[slot], dst.at[lane], send, recv, at.base + half, there
                    ).wait_send()

    def deal_arrive(kind):
        src, dst = ((tok, xt), (cot, ct))[kind]
        for block in range(2):
            pltpu.make_async_copy(src.at[0], dst.at[block], tr.at[kind, block]).wait()

    def source(u, start):
        dst = spot(u, lane, dp)
        recv = zr.at[u, lane, core]
        home = at.base + half
        if start:
            move(units[u], dst, zs.at[u, 0], recv, home, line, half == core)
        else:

            @pl.when(half != core)
            def _():
                remote(units[u], dst, zs.at[u, 0], recv, home, line).wait_send()

        for which, step in ((1, 1), (2, -1)):
            inside = line < 3 if step == 1 else line > 0

            @pl.when(inside)
            def _():
                copy = remote(units[u], dst, zs.at[u, which], recv, home, line + step)
                copy.start() if start else copy.wait_send()

    first = jnp.where(core == 0, jnp.where(line == 0, 0, 1), jnp.where(line == 3, 1, 0))

    def z_stage(u, k, other, start):
        zi = first + k - 2 * first * k
        origin = 2 * core + zi
        ref = spot(u, zi, at.base + other)
        if start:
            pltpu.make_async_copy(w1, ref, zr.at[u, zi, other]).wait()
        up = jnp.logical_and(origin < line, line < 3)
        down = jnp.logical_and(origin > line, line > 0)
        for go, step in ((up, 1), (down, -1)):

            @pl.when(go)
            def _():
                copy = remote(
                    ref, ref, fs.at[u, zi, other], zr.at[u, zi, other], dp, line + step
                )
                copy.start() if start else copy.wait_send()

        for which, near in ((0, at.dp_x), (1, at.dp_y)):
            copy = remote(
                ref, ref, ns.at[which, u, zi, other], nr.at[which, u, zi, other], near, line
            )
            copy.start() if start else copy.wait_send()

    def far_stage(u, zi, other, start):
        base = at.base_x + zi * (at.base_y - at.base_x)
        near = at.dp_y + zi * (at.dp_x - at.dp_y)
        ref = spot(u, zi, base + other)
        if start:
            pltpu.make_async_copy(w1, ref, nr.at[zi, u, zi, other]).wait()
        copy = remote(ref, ref, ds.at[u, zi, other], dr.at[u, zi, other], near, line)
        copy.start() if start else copy.wait_send()

    def last_stage(u, zi, other):
        base = at.base_y + zi * (at.base_x - at.base_y)
        ref = spot(u, zi, base + other)
        pltpu.make_async_copy(w1, ref, nr.at[1 - zi, u, zi, other]).wait()
        ref = spot(u, zi, at.base_far + other)
        pltpu.make_async_copy(w1, ref, dr.at[u, zi, other]).wait()

    def pump(number):
        u = 1 + number // 8
        k, other = (number % 4) // 2, number % 2

        @pl.when(number % 8 < 4)
        def _():
            z_stage(u, k, other, True)

        @pl.when(number % 8 >= 4)
        def _():
            far_stage(u, k, other, True)

    def keep(src, dst, number):
        return pltpu.make_async_copy(src, dst, ls.at[number])

    def each_column(start):
        for step in range(1, 8):
            other = (core * 4 + line + step) % 8
            copy = remote(
                meta, mt.at[core * 4 + line], ms.at[step], mrs.at[core * 4 + line],
                at.base + other // 4, other % 4,
            )
            copy.start() if start else copy.wait_send()

    def each_row(src, dst, send, recv, start, pieces):
        for step in range(1, 8):
            other = (dp + step) % 8
            part = src.at[other] if pieces else src
            copy = remote(part, dst.at[dp], send.at[step], recv.at[dp], other, line)
            copy.start() if start else copy.wait_send()

    def row_arrive(dst, recv):
        for step in range(1, 8):
            other = (dp + step) % 8
            pltpu.make_async_copy(dst.at[other], dst.at[other], recv.at[other]).wait()

    each_row(te, te_all, tes, ter, True, True)
    each_column(True)
    te_all[dp] = te[dp]
    mt[core * 4 + line] = meta[...]

    deal(0, True)
    source(0, True)
    row_arrive(te_all, ter)
    for number in range(8):
        spread = te_all[number]
        cond[8 * number : 8 * number + 8, :] = spread * (1.0 / (1.0 + jnp.exp(-spread)))
    value = dot_nn(cond[...].astype(LOW), wa[...])
    for number in range(8):
        pb[number] = value[8 * number : 8 * number + 8, :]
    each_row(pb, pr, pbs, pbr, True, True)
    pr[dp] = pb[dp]
    for other in range(2):
        z_stage(0, 0, other, True)
    row_arrive(pr, pbr)
    total = ba[...] + pr[0]
    for number in range(1, 8):
        total = total + pr[number]
    mine[...] = total

    def each_slot(start):
        for slot in range(2):
            there = 2 * core + slot
            for to in range(2):
                here = jnp.logical_and(core == to, there == line)
                send, recv = mms.at[slot, to], mmr.at[line]
                if start:
                    move(mine, mr.at[line], send, recv, at.base + to, there, here)
                else:

                    @pl.when(jnp.logical_not(here))
                    def _():
                        remote(mine, mr.at[line], send, recv, at.base + to, there).wait_send()

    each_slot(True)
    for other in range(2):
        z_stage(0, 1, other, True)
    source(1, True)
    deal(1, True)

    for step in range(1, 8):
        other = (core * 4 + line + step) % 8
        pltpu.make_async_copy(meta, mt.at[other], mrs.at[other]).wait()
    one_row = lanes(1)
    spots = (one_row - HD).astype(F32)
    inside = jnp.logical_and(one_row >= HD, one_row < HD + 4)

    def lane_of(row, place):
        return jnp.sum(jnp.where(one_row == place, row, 0.0), axis=1, keepdims=True)

    for zi in range(2):
        info = mt[half * 4 + 2 * core + zi, pl.ds(4 + lane, 1), :]
        for number in range(4):
            head = zi * 4 + number
            gains[head : head + 1, :] = jnp.broadcast_to(lane_of(info, number), (1, 128))
            groups[head : head + 1, :] = jnp.broadcast_to(lane_of(info, 4 + number), (1, 128))
    info = mt[half * 4 + line, pl.ds(4 + lane, 1), :]
    for tile in range(4):
        same = jnp.where(spots == lane_of(info, 8 + tile), 1.0, 0.0)
        feat[0, tile : tile + 1, :] = jnp.where(inside, SHADE * (1.0 - same), 0.0)
        feat[1, tile : tile + 1, :] = jnp.where(inside, same, 0.0)
    row_ids = lax.broadcasted_iota(jnp.int32, (8, 128), 0)
    diagonal = lax.broadcasted_iota(jnp.int32, (128, 128), 0) == lanes(128)
    for block in range(2):
        item = jnp.sum(
            jnp.where(one_row == 8 + 2 * core + block, info, 0.0), axis=1, keepdims=True
        )
        hit = row_ids.astype(F32) == item + (4 * lane).astype(F32)
        select[block] = jnp.where(hit, 1.0, 0.0)
        for number in range(2):
            row = mt[half * 4 + 2 * core + block, pl.ds(2 * lane + number, 1), :]
            column = jnp.sum(jnp.where(diagonal, row, 0.0), axis=1, keepdims=True)
            kept[block, 128 * number : 128 * number + 128, :] = jnp.broadcast_to(column, (128, 128))
    for source_line in range(4):
        pltpu.make_async_copy(mine, mr.at[source_line], mmr.at[source_line]).wait()
    for block in range(2):
        weight = select[block][:, 0:1]
        rows = [jnp.sum(weight * mr[n], axis=0, keepdims=True) for n in range(4)]
        pieces = to_blocks(rows[0], rows[1]) + to_blocks(rows[2], rows[3])
        for number, piece in enumerate(pieces):
            mod[block, number : number + 1, :] = piece
        mod[block, 6:8, :] = jnp.zeros((2, mod.shape[2]), F32)

    def exchange(src, dst, number):
        return remote(src, dst, es.at[number], er.at[number], sib, line)

    deal_arrive(0)
    keep(xt, x_out, 0).start()

    for block in range(2):
        shift, scale = mod[block, 0:1, :], 1.0 + mod[block, 1:2, :]

        def norm_first(step, _):
            at_row = pl.ds(pl.multiple_of(step * 128, 128), 128)
            normed, _f = layer_norm(xt[block, at_row, :].astype(F32))
            to_row = pl.ds(pl.multiple_of(block * 256 + step * 128, 128), 128)
            h1[core, to_row, :] = (normed * scale + shift).astype(LOW)
            return 0

        lax.fori_loop(0, 2, norm_first, 0)
        part = h1.at[core, pl.ds(block * 256, 256)]
        exchange(part, part, block).start()
    for zi in range(2):
        for other in range(2):
            far_stage(0, zi, other, True)
    source(2, True)
    for zi in range(2):
        for other in range(2):
            last_stage(0, zi, other)
    keep(w0, head_out, 1).start()

    def project(step, _):
        @pl.when(step >= 2)
        def _():
            part = h1.at[1 - core, pl.ds(pl.multiple_of((step - 2) * 256, 256), 256)]
            pltpu.make_async_copy(part, part, er.at[step - 2]).wait()

        pump(step)
        tile = (2 * core + step) % 4
        rows = h1[tile // 2, pl.ds(pl.multiple_of((tile % 2) * 256, 256), 256), :]
        to_row = pl.ds(pl.multiple_of(tile * 256, 256), 256)
        narrow = lanes(256) < HD
        fills = (feat[0, pl.ds(tile, 1), :], feat[1, pl.ds(tile, 1), :], jnp.zeros((1, 128), F32))
        for zi in range(2):
            value = dot_nn(rows, w0[zi, :, 0:896])
            for number in range(12):
                head, part = zi * 4 + number // 3, number % 3
                piece = jnp.where(narrow, window(value, HD * number), fills[part])
                qkv[head, part, to_row, :] = piece.astype(LOW)
        return 0

    lax.fori_loop(0, 4, project, 0)
    keep(h1, h1_out, 2).start()
    keep(qkv, qkv_out, 3).start()

    factor = HD ** (-0.5) * LOG2E

    def attend(head, _):
        pump(4 + head)
        gain = gains[pl.ds(head, 1), :]

        def tile_step(tile, _):
            rows = pl.ds(pl.multiple_of(tile * 256, 256), 256)
            scores = dot_nt(qkv[head, 0, rows, :], qkv[head, 1])
            peak = jnp.max(scores, axis=1, keepdims=True)
            power = jnp.exp2((scores - peak) * factor)
            total = jnp.sum(power, axis=1, keepdims=True)
            probs = (power * (1.0 / total)).astype(LOW)
            obuf[head, rows, :] = (dot_nn(probs, qkv[head, 2]) * gain).astype(LOW)
            level = peak * factor + jnp.log2(total)
            stat[rows, :] = jnp.where(lanes(256) == head, level, stat[rows, :])
            return 0

        lax.fori_loop(0, 4, tile_step, 0)
        return 0

    lax.fori_loop(0, 8, attend, 0)
    keep(stat, stat_out, 4).start()

    def lay(step, _):
        rows = pl.ds(pl.multiple_of(step * 128, 128), 128)
        for zi in range(2):
            parts = [obuf[zi * 4 + n, rows, :].astype(F32) for n in range(4)]
            for tile, value in enumerate(pack(parts, 96, 3)):
                att[zi, rows, 128 * tile : 128 * tile + 128] = value.astype(LOW)
        return 0

    lax.fori_loop(0, 8, lay, 0)
    keep(att, att_out, 5).start()

    for step in range(4):
        tile = (2 * (1 - core) + step) % 4
        rows = pl.ds(pl.multiple_of(tile * 256, 256), 256)
        value = dot_nt(att[0, rows, :], w0[0, :, 768:1152])
        value = value + dot_nt(att[1, rows, :], w0[1, :, 768:1152])
        if step < 2:
            sb[step] = value.astype(LOW)
            exchange(sb.at[step], rb.at[step], 2 + step).start()
        else:
            br[step - 2] = value
    for block in range(2):
        exchange(sb.at[block], rb.at[block], 2 + block).wait_recv()
        gate = mod[block, 2:3, :]
        shift, scale = mod[block, 3:4, :], 1.0 + mod[block, 4:5, :]

        def norm_second(step, _):
            at_row = pl.ds(pl.multiple_of(step * 128, 128), 128)
            branch = br[block, at_row, :] + rb[block, at_row, :].astype(F32)
            br[block, at_row, :] = branch
            value = xt[block, at_row, :].astype(F32) + gate * branch
            x1[block, at_row, :] = value
            normed, _f = layer_norm(value)
            to_row = pl.ds(pl.multiple_of(block * 256 + step * 128, 128), 128)
            h2[core, to_row, :] = (normed * scale + shift).astype(LOW)
            return 0

        lax.fori_loop(0, 2, norm_second, 0)
        part = h2.at[core, pl.ds(block * 256, 256)]
        exchange(part, part, 4 + block).start()
    keep(x1, x1_out, 6).start()
    keep(br, br_out, 7).start()

    deal_arrive(1)
    keep(ct, g_out, 9).start()
    for block in range(2):
        gate2 = mod[block, 5:6, :]

        def grad_rows(step, _):
            at_row = pl.ds(pl.multiple_of(step * 128, 128), 128)
            value = gate2 * kept[block, at_row, 0:1] * ct[block, at_row, :].astype(F32)
            to_row = pl.ds(pl.multiple_of(block * 256 + step * 128, 128), 128)
            dm[core, to_row, :] = value.astype(LOW)
            return 0

        lax.fori_loop(0, 2, grad_rows, 0)
        part = dm.at[core, pl.ds(block * 256, 256)]
        exchange(part, part, 6 + block).start()

    def drain(number, _):
        pump(number)
        return 0

    lax.fori_loop(12, 16, drain, 0)
    for block in range(2):
        part = h2.at[1 - core, pl.ds(block * 256, 256)]
        pltpu.make_async_copy(part, part, er.at[4 + block]).wait()
    keep(h2, h2_out, 8).start()
    for block in range(2):
        part = dm.at[1 - core, pl.ds(block * 256, 256)]
        pltpu.make_async_copy(part, part, er.at[6 + block]).wait()
    keep(dm, dm_out, 10).start()

    for u in range(3):
        source(u, False)
        for k in range(2):
            for other in range(2):
                z_stage(u, k, other, False)
                far_stage(u, k, other, False)
                if u:
                    last_stage(u, k, other)
    for kind in range(2):
        deal(kind, False)
    each_column(False)
    each_row(te, te_all, tes, ter, False, True)
    each_row(pb, pr, pbs, pbr, False, True)
    each_slot(False)
    for block in range(2):
        own1 = h1.at[core, pl.ds(block * 256, 256)]
        own2 = h2.at[core, pl.ds(block * 256, 256)]
        exchange(own1, own1, block).wait_send()
        exchange(sb.at[block], rb.at[block], 2 + block).wait_send()
        exchange(own2, own2, 4 + block).wait_send()
        own3 = dm.at[core, pl.ds(block * 256, 256)]
        exchange(own3, own3, 6 + block).wait_send()
    pairs = (
        (xt, x_out),
        (w0, head_out),
        (h1, h1_out),
        (qkv, qkv_out),
        (stat, stat_out),
        (att, att_out),
        (x1, x1_out),
        (br, br_out),
        (h2, h2_out),
        (ct, g_out),
        (dm, dm_out),
    )
    for number, (src, dst) in enumerate(pairs):
        keep(src, dst, number).wait()


def run_front(wh, w1, w2, tok, cot, meta, te, wa, ba):
    rows, cols = w1.shape
    part = tok.shape[1]
    length = 4 * part
    shape = jax.ShapeDtypeStruct
    vmem = pl.BlockSpec(memory_space=pltpu.VMEM)
    shared = shape((2, 2 * part, cols), LOW)
    single = shape((2, part, cols), F32)
    outs = (
        shape((2, 2, 8, rows, cols), LOW),
        shape((2, 8 * rows, cols), LOW),
        shape(tok.shape, LOW),
        shape(tok.shape, LOW),
        shared,
        shape((8, 3, length, 128), LOW),
        shape((length, 128), F32),
        shape((2, length, 384), LOW),
        single,
        single,
        shared,
        shared,
    )
    small = (
        shape((64, rows), F32),
        shape((2, 8, cols), F32),
        shape((8, 128), F32),
        shape((8, 128), F32),
        shape((2, part, 128), F32),
        shape((2, 8, 128), F32),
    )
    three = DMA((3, 2, 2))
    return pl.pallas_call(
        front_kernel,
        out_shape=outs + small,
        in_specs=[ANY] * 5 + [vmem] * 4,
        out_specs=(ANY,) * len(outs) + (vmem,) * len(small),
        scratch_shapes=[
            pltpu.VMEM(tok.shape, LOW),
            pltpu.VMEM((2, 8 * rows, cols), LOW),
            pltpu.VMEM((2, 2 * part, cols), LOW),
            pltpu.VMEM((8, 3, length, 128), LOW),
            pltpu.VMEM((8, length, 128), LOW),
            pltpu.VMEM((length, 128), F32),
            pltpu.VMEM((2, length, 384), LOW),
            pltpu.VMEM((2, part, cols), LOW),
            pltpu.VMEM((2, part, cols), LOW),
            pltpu.VMEM((2, part, cols), F32),
            pltpu.VMEM((2, part, cols), F32),
            pltpu.VMEM((2, 2 * part, cols), LOW),
            pltpu.VMEM(tok.shape, LOW),
            pltpu.VMEM((2, 2 * part, cols), LOW),
            pltpu.VMEM((8, 8, 128), F32),
            pltpu.VMEM((8, 8, rows), F32),
            pltpu.VMEM((8, 8, wa.shape[1]), F32),
            pltpu.VMEM((8, 8, wa.shape[1]), F32),
            pltpu.VMEM((8, wa.shape[1]), F32),
            pltpu.VMEM((4, 8, wa.shape[1]), F32),
            pltpu.VMEM((2, 8, 128), F32),
            DMA((3, 3)),
            three,
            three,
            DMA((2, 3, 2, 2)),
            DMA((2, 3, 2, 2)),
            three,
            three,
            DMA((2, 2)),
            DMA((2, 2)),
            DMA((8,)),
            DMA((8,)),
            DMA((11,)),
            DMA((8,)),
            DMA((8,)),
            DMA((8,)),
            DMA((8,)),
            DMA((8,)),
            DMA((8,)),
            DMA((2, 2)),
            DMA((4,)),
        ],
        compiler_params=pltpu.CompilerParams(
            collective_id=0, has_side_effects=True, vmem_limit_bytes=60 << 20
        ),
    )(wh, w1, w2, tok, cot, meta, te, wa, ba)


def back_kernel(
    gfc,
    dh2_send,
    mlp_send,
    dh2_own,
    mlp_own,
    x1_in,
    br_in,
    x_in,
    g_in,
    h1_in,
    qkv_in,
    stat_in,
    att_in,
    head_in,
    mod,
    gains,
    keep_col,
    select,
    cond,
    out_tok,
    out_dtok,
    out_grad,
    rz,
    g_ada,
    g_bias,
    sums,
    w0,
    h1,
    qkv,
    stat,
    dpk,
    db,
    do,
    g0,
    dfirst,
    xb,
    yb,
    gb,
    xt,
    sb,
    rb,
    rm,
    ob,
    acc,
    r1,
    rn,
    stage,
    fin,
    dc,
    nr,
    da,
    s1s,
    s1r,
    nss,
    nsr,
    rls,
    zss,
    zsr,
    es,
    er,
    ts,
    tr,
    ls,
    gs,
    dcs,
    dcr,
    das,
    dar,
):
    at = Place()
    dp, line, core, half = at.dp, at.line, at.core, at.half
    lane = line % 2
    rows_u = out_grad.shape[1]
    sib = at.base + 1 - core
    scale_q = HD ** (-0.5)
    factor = HD ** (-0.5) * LOG2E

    def load(src, dst, number):
        return pltpu.make_async_copy(src, dst, ls.at[number])

    load(head_in, w0, 0).start()
    load(qkv_in, qkv, 1).start()
    load(stat_in, stat, 2).start()
    load(att_in, dpk.at[:, :, 0:384], 3).start()
    load(h1_in, h1, 4).start()
    at.barrier()

    def exchange(src, dst, number):
        return remote(src, dst, es.at[number], er.at[number], sib, line)

    def grad_ref(u, zi, row):
        if isinstance(u, int) and u == 0:
            return g0.at[zi, pl.ds(pl.multiple_of(row * rows_u, 16), rows_u)]
        return gfc.at[u - 1, zi, row]

    def base_of(which):
        return at.base_x + which * (at.base_y - at.base_x)

    def near_of(which):
        return at.dp_x + which * (at.dp_y - at.dp_x)

    def far_send(u, zi, o):
        return remote(
            grad_ref(u, zi, at.base_far + o),
            r1.at[u, zi, o],
            s1s.at[u, zi, o],
            s1r.at[u, zi, o],
            near_of(zi),
            line,
        )

    def plain_send(u, zi, o):
        return remote(
            grad_ref(u, zi, base_of(zi) + o),
            rn.at[zi, u, zi, o],
            nss.at[zi, u, zi, o],
            nsr.at[zi, u, zi, o],
            near_of(zi),
            line,
        )

    def relay_send(u, zi, o):
        return remote(
            r1.at[u, zi, o],
            rn.at[1 - zi, u, zi, o],
            nss.at[1 - zi, u, zi, o],
            nsr.at[1 - zi, u, zi, o],
            near_of(1 - zi),
            line,
        )

    def fetch(u, zi, row, slot):
        if isinstance(u, int) and u == 0:
            return grad_ref(u, zi, row), None
        copy = pltpu.make_async_copy(grad_ref(u, zi, row), stage.at[slot], gs.at[slot])
        copy.start()
        return stage.at[slot], copy

    def relay(u, zi, o):
        ref, copy = fetch(u, zi, base_of(1 - zi) + o, 0)
        far_send(u, zi, o).wait_recv()
        if copy is not None:
            copy.wait()
        r1[u, zi, o] = (r1[u, zi, o].astype(F32) + ref[...].astype(F32)).astype(LOW)
        relay_send(u, zi, o).start()

    def settle(u, zi, o, start):
        here = jnp.logical_and(core == o, line == 2 * core + zi)
        src, dst = rn.at[0, u, zi, o], rz.at[u, line]
        send, recv = zss.at[u, zi, o], zsr.at[u, line]
        if not start:

            @pl.when(jnp.logical_not(here))
            def _():
                remote(src, dst, send, recv, at.base + o, 2 * core + zi).wait_send()

            return
        ref, copy = fetch(u, zi, at.base + o, 1)
        for which in range(2):
            there = rn.at[which, u, zi, o]
            pltpu.make_async_copy(there, there, nsr.at[which, u, zi, o]).wait()
        if copy is not None:
            copy.wait()
        total = rn[0, u, zi, o].astype(F32) + rn[1, u, zi, o].astype(F32)
        rn[0, u, zi, o] = (total + ref[...].astype(F32)).astype(LOW)
        move(src, dst, send, recv, at.base + o, 2 * core + zi, here)

    def finish(u):
        for source in range(4):
            ref = rz.at[u, source]
            pltpu.make_async_copy(ref, ref, zsr.at[u, source]).wait()
        for source in range(4):
            pltpu.make_async_copy(rz.at[u, source], stage.at[source], gs.at[source]).start()
        for source in range(4):
            pltpu.make_async_copy(rz.at[u, source], stage.at[source], gs.at[source]).wait()
        total = stage[0].astype(F32) + stage[1].astype(F32)
        fin[...] = total + (stage[2].astype(F32) + stage[3].astype(F32))
        copy = pltpu.make_async_copy(fin, out_grad.at[u], gs.at[0])
        copy.start()
        copy.wait()

    def pump(number):
        index = number % 8
        u, zi, o = 1 + index // 4, (index // 2) % 2, index % 2

        @pl.when(number < 8)
        def _():
            relay(u, zi, o)

        @pl.when(number >= 8)
        def _():
            settle(u, zi, o, True)

    def give_back(block, kind, start):
        dst = (out_tok, out_dtok)[kind].at[lane]
        there = 2 * core + block
        here = jnp.logical_and(half == core, there == line)
        send, recv = ts.at[kind, block], tr.at[kind, lane]
        if start:
            move(ob.at[block], dst, send, recv, at.base + half, there, here)
        else:

            @pl.when(here)
            def _():
                pltpu.make_async_copy(ob.at[block], dst, recv).wait()

            @pl.when(jnp.logical_not(here))
            def _():
                remote(ob.at[block], dst, send, recv, at.base + half, there).wait_send()

    for block in range(2):
        exchange(dh2_send.at[block], rb.at[block], block).start()
        exchange(mlp_send.at[block], rm.at[block], 2 + block).start()
    for u in (1, 2):
        for zi in range(2):
            for o in range(2):
                far_send(u, zi, o).start()
        for zi in range(2):
            for o in range(2):
                plain_send(u, zi, o).start()

    for block in range(2):
        copies = (
            load(x1_in.at[block], xb.at[0], 5),
            load(br_in.at[block], xb.at[1], 6),
            load(dh2_own.at[block], yb.at[0], 7),
            load(mlp_own.at[block], yb.at[1], 8),
            load(g_in.at[block], gb, 9),
        )
        for copy in copies:
            copy.start()
        for copy in copies:
            copy.wait()
        exchange(dh2_send.at[block], rb.at[block], block).wait_recv()
        exchange(mlp_send.at[block], rm.at[block], 2 + block).wait_recv()
        gate1, scale2 = mod[block, 2:3, :], 1.0 + mod[block, 4:5, :]
        gate2 = mod[block, 5:6, :]

        def norm_second(step, sums_now):
            at_row = pl.ds(pl.multiple_of(step * 128, 128), 128)
            grad = gb[at_row, :].astype(F32)
            first = xb[0, at_row, :]
            d_second = yb[0, at_row, :] + rb[block, at_row, :].astype(F32)
            kept = keep_col[block, at_row, 0:1] * (
                yb[1, at_row, :] + rm[block, at_row, :].astype(F32)
            )
            ob[block, at_row, :] = (first + gate2 * kept).astype(LOW)
            normed, spread = layer_norm(first)
            d_first = grad + norm_back(d_second * scale2, normed, spread)
            dfirst[block, at_row, :] = d_first
            to_row = pl.ds(pl.multiple_of(block * 256 + step * 128, 128), 128)
            db[core, to_row, :] = (gate1 * d_first).astype(LOW)
            terms = (d_first * xb[1, at_row, :], d_second, d_second * normed, grad * kept)
            return tuple(
                now + jnp.sum(term, axis=0, keepdims=True) for now, term in zip(sums_now, terms)
            )

        zero = jnp.zeros((1, gb.shape[1]), F32)
        totals = lax.fori_loop(0, 2, norm_second, (zero,) * 4)
        for place, value in zip((2, 3, 4, 5), totals):
            sums[block, place : place + 1, :] = value
        part = db.at[core, pl.ds(block * 256, 256)]
        exchange(part, part, 4 + block).start()
        give_back(block, 0, True)

    for number in range(4):
        load((head_in, qkv_in, stat_in, att_in)[number], (w0, qkv, stat, dpk.at[:, :, 0:384])[number], number).wait()
    pump(jnp.int32(0))
    pump(jnp.int32(1))

    def to_heads(step, _):
        @pl.when(step >= 2)
        def _():
            part = db.at[1 - core, pl.ds(pl.multiple_of((step - 2) * 256, 256), 256)]
            pltpu.make_async_copy(part, part, er.at[4 + step - 2]).wait()

        tile = (2 * core + step) % 4
        rows = db[tile // 2, pl.ds(pl.multiple_of((tile % 2) * 256, 256), 256), :]
        to_row = pl.ds(pl.multiple_of(tile * 256, 256), 256)
        narrow = lanes(256) < HD
        for zi in range(2):
            value = dot_nn(rows, w0[zi, :, 768:1152])
            for number in range(4):
                piece = jnp.where(narrow, window(value, 96 + HD * number), 0.0)
                head = zi * 4 + number
                do[head, to_row, :] = (piece * gains[head : head + 1, :]).astype(LOW)
        return 0

    lax.fori_loop(0, 4, to_heads, 0)
    pump(jnp.int32(2))
    pump(jnp.int32(3))
    length = stat.shape[0]
    mid = length // 2
    for zi in range(2):
        for tile in range(3):
            cols = slice(384 * tile, 384 * tile + 384)
            value = dot_tn(db[0, :, cols], dpk[zi, 0:mid, 0:384])
            value = value + dot_tn(db[1, :, cols], dpk[zi, mid:length, 0:384])
            g0[zi, cols, 768:1152] = value.astype(LOW)

    def attend(head, _):
        pump(4 + head)
        acc[...] = jnp.zeros_like(acc)

        def tile_step(tile, _):
            rows = pl.ds(pl.multiple_of(tile * 256, 256), 256)
            query, grad = qkv[head, 0, rows, :], do[head, rows, :]
            level = jnp.sum(jnp.where(lanes(256) == head, stat[rows, :], 0.0), axis=1, keepdims=True)
            probs = jnp.exp2(dot_nt(query, qkv[head, 1]) * factor - level)
            d_probs = dot_nt(grad, qkv[head, 2])
            inner = jnp.sum(probs * d_probs, axis=1, keepdims=True)
            d_scores = (probs * (d_probs - inner)).astype(LOW)
            acc[0] += dot_tn(d_scores, query)
            acc[1] += dot_tn(probs.astype(LOW), grad)
            qkv[head, 0, rows, :] = (dot_nn(d_scores, qkv[head, 1]) * scale_q).astype(LOW)
            return 0

        lax.fori_loop(0, 4, tile_step, 0)
        qkv[head, 1] = (acc[0] * scale_q).astype(LOW)
        qkv[head, 2] = acc[1].astype(LOW)
        return 0

    lax.fori_loop(0, 8, attend, 0)

    def lay(step, _):
        rows = pl.ds(pl.multiple_of(step * 128, 128), 128)
        for zi in range(2):
            parts = [
                jnp.where(lanes(128) < HD, qkv[zi * 4 + n // 3, n % 3, rows, :].astype(F32), 0.0)
                for n in range(12)
            ]
            for tile, value in enumerate(pack(parts, 0, 7)):
                dpk[zi, rows, 128 * tile : 128 * tile + 128] = value.astype(LOW)
        return 0

    lax.fori_loop(0, 8, lay, 0)
    load(h1_in, h1, 4).wait()
    for zi in range(2):
        for tile in range(3):
            cols = slice(384 * tile, 384 * tile + 384)
            value = dot_tn(h1[0, :, cols], dpk[zi, 0:mid, :])
            value = value + dot_tn(h1[1, :, cols], dpk[zi, mid:length, :])
            g0[zi, cols, 0:768] = value[:, 0:768].astype(LOW)
            both = value[:, 768:896] + g0[zi, cols, 768:896].astype(F32)
            g0[zi, cols, 768:896] = both.astype(LOW)
    for zi in range(2):
        for o in range(2):
            far_send(0, zi, o).start()
    for zi in range(2):
        for o in range(2):
            plain_send(0, zi, o).start()

    for block in range(2):
        load(x_in.at[block], xt.at[block], 5 + block).start()
    for step in range(4):
        tile = (2 * (1 - core) + step) % 4
        rows = pl.ds(pl.multiple_of(tile * 256, 256), 256)
        value = dot_nt(dpk[0, rows, :], w0[0, :, 0:896])
        value = value + dot_nt(dpk[1, rows, :], w0[1, :, 0:896])
        if step < 2:
            sb[step] = value.astype(LOW)
            exchange(sb.at[step], rb.at[step], 6 + step).start()
        else:
            yb[step - 2] = value
    for block in range(2):
        give_back(block, 0, False)
        load(x_in.at[block], xt.at[block], 5 + block).wait()
        exchange(sb.at[block], rb.at[block], 6 + block).wait_recv()
        scale1 = 1.0 + mod[block, 1:2, :]

        def norm_first(step, sums_now):
            at_row = pl.ds(pl.multiple_of(step * 128, 128), 128)
            d_norm = yb[block, at_row, :] + rb[block, at_row, :].astype(F32)
            normed, spread = layer_norm(xt[block, at_row, :].astype(F32))
            d_input = dfirst[block, at_row, :] + norm_back(d_norm * scale1, normed, spread)
            ob[block, at_row, :] = d_input.astype(LOW)
            terms = (d_norm, d_norm * normed)
            return tuple(
                now + jnp.sum(term, axis=0, keepdims=True) for now, term in zip(sums_now, terms)
            )

        zero = jnp.zeros((1, gb.shape[1]), F32)
        totals = lax.fori_loop(0, 2, norm_first, (zero,) * 2)
        for place, value in zip((0, 1), totals):
            sums[block, place : place + 1, :] = value
        give_back(block, 1, True)

    blocks = []
    for number in range(6):
        value = select[0][:, 0:1] * sums[0, number : number + 1, :]
        blocks.append(value + select[1][:, 0:1] * sums[1, number : number + 1, :])
    chunks = to_chunks(*blocks[0:3]) + to_chunks(*blocks[3:6])
    for number in range(4):
        dc[number] = chunks[number]

    def each_chunk(start):
        for number in range(4):
            here = jnp.logical_and(half == core, line == number)
            dst, send, recv = nr.at[lane, core], dcs.at[number], dcr.at[lane, core]
            if start:
                move(dc.at[number], dst, send, recv, at.base + half, number, here)
            else:

                @pl.when(jnp.logical_not(here))
                def _():
                    remote(dc.at[number], dst, send, recv, at.base + half, number).wait_send()

    def each_row(start):
        for step in range(1, 8):
            other = (dp + step) % 8
            copy = remote(da.at[dp], da.at[dp], das.at[step], dar.at[dp], other, line)
            copy.start() if start else copy.wait_send()

    each_chunk(True)

    def drain(number, _):
        pump(number)
        return 0

    lax.fori_loop(12, 16, drain, 0)
    for zi in range(2):
        for o in range(2):
            pltpu.make_async_copy(dc.at[0], nr.at[zi, o], dcr.at[zi, o]).wait()
    da[dp] = (nr[0, 0] + nr[0, 1]) + (nr[1, 0] + nr[1, 1])
    each_row(True)
    for zi in range(2):
        for o in range(2):
            relay(0, zi, o)
    finish(1)
    finish(2)
    for zi in range(2):
        for o in range(2):
            settle(0, zi, o, True)
    for step in range(1, 8):
        other = (dp + step) % 8
        pltpu.make_async_copy(da.at[other], da.at[other], dar.at[other]).wait()
    value = jnp.concatenate([da[n] for n in range(8)], axis=0)
    g_bias[...] = jnp.sum(value, axis=0, keepdims=True)
    g_ada[...] = lax.dot_general(
        cond[...].astype(LOW).astype(F32), value, (((0,), (0,)), ((), ())), precision=HIGH, preferred_element_type=F32
    )
    finish(0)

    each_chunk(False)
    each_row(False)
    for u in range(3):
        for zi in range(2):
            for o in range(2):
                far_send(u, zi, o).wait_send()
                plain_send(u, zi, o).wait_send()
                relay_send(u, zi, o).wait_send()
                settle(u, zi, o, False)
    for block in range(2):
        give_back(block, 1, False)
        exchange(dh2_send.at[block], rb.at[block], block).wait_send()
        exchange(mlp_send.at[block], rm.at[block], 2 + block).wait_send()
        part = db.at[core, pl.ds(block * 256, 256)]
        exchange(part, part, 4 + block).wait_send()
        exchange(sb.at[block], rb.at[block], 6 + block).wait_send()
    for kind in range(2):
        dst = (out_tok, out_dtok)[kind]
        for slot in range(2):
            source = 2 * core + slot
            here = jnp.logical_and(source == line, half == core)

            @pl.when(jnp.logical_not(here))
            def _():
                pltpu.make_async_copy(dst.at[slot], dst.at[slot], tr.at[kind, slot]).wait()


def run_back(gfc, *rest):
    rows, cols = gfc.shape[3:]
    part = rest[0].shape[1]
    length = 4 * part
    chunk = 6 * cols // 4
    shape = jax.ShapeDtypeStruct
    vmem = pl.BlockSpec(memory_space=pltpu.VMEM)
    outs = (
        shape((2, part, cols), LOW),
        shape((2, part, cols), LOW),
        shape((3, rows, cols), F32),
        shape((3, 4, rows, cols), LOW),
        shape((rows, chunk), F32),
        shape((1, chunk), F32),
    )
    three = DMA((3, 2, 2))
    return pl.pallas_call(
        back_kernel,
        out_shape=outs,
        in_specs=[ANY] * 14 + [vmem] * 5,
        out_specs=(ANY,) * 4 + (vmem,) * 2,
        scratch_shapes=[
            pltpu.VMEM((2, 8, cols), F32),
            pltpu.VMEM((2, 8 * rows, cols), LOW),
            pltpu.VMEM((2, 2 * part, cols), LOW),
            pltpu.VMEM((8, 3, length, 128), LOW),
            pltpu.VMEM((length, 128), F32),
            pltpu.VMEM((2, length, 896), LOW),
            pltpu.VMEM((2, 2 * part, cols), LOW),
            pltpu.VMEM((8, length, 128), LOW),
            pltpu.VMEM((2, 8 * rows, cols), LOW),
            pltpu.VMEM((2, part, cols), F32),
            pltpu.VMEM((2, part, cols), F32),
            pltpu.VMEM((2, part, cols), F32),
            pltpu.VMEM((part, cols), LOW),
            pltpu.VMEM((2, part, cols), LOW),
            pltpu.VMEM((2, part, cols), LOW),
            pltpu.VMEM((2, part, cols), LOW),
            pltpu.VMEM((2, part, cols), LOW),
            pltpu.VMEM((2, part, cols), LOW),
            pltpu.VMEM((2, length, 128), F32),
            pltpu.VMEM((3, 2, 2, rows, cols), LOW),
            pltpu.VMEM((2, 3, 2, 2, rows, cols), LOW),
            pltpu.VMEM((4, rows, cols), LOW),
            pltpu.VMEM((rows, cols), F32),
            pltpu.VMEM((4, 8, chunk), F32),
            pltpu.VMEM((2, 2, 8, chunk), F32),
            pltpu.VMEM((8, 8, chunk), F32),
            three,
            three,
            DMA((2, 3, 2, 2)),
            DMA((2, 3, 2, 2)),
            three,
            three,
            DMA((3, 4)),
            DMA((8,)),
            DMA((8,)),
            DMA((2, 2)),
            DMA((2, 2)),
            DMA((10,)),
            DMA((4,)),
            DMA((4,)),
            DMA((2, 2)),
            DMA((8,)),
            DMA((8,)),
        ],
        compiler_params=pltpu.CompilerParams(
            collective_id=1, has_side_effects=True, vmem_limit_bytes=63 << 20
        ),
    )(gfc, *rest)


def fast_body(
    tokens,
    time_embed,
    segments,
    micro_order,
    head_mask,
    group_mask,
    keep_route,
    w_qkv,
    w_proj,
    w_fc1,
    w_fc2,
    w_ada,
    b_ada,
    cotangent,
):
    dp = lax.axis_index("dp")
    line = lax.axis_index("tensor")
    core = dp % 2
    chip = dp // 2
    odd = line % 2
    owner = line // 2
    segs = time_embed.shape[1]
    part = tokens.shape[1]
    width = tokens.shape[2]
    length = segments.shape[1]
    qcols = w_qkv.shape[1]
    heads_here = head_mask.shape[1]

    lines = jnp.concatenate(
        [
            head_mask[micro_order],
            group_mask[micro_order],
            segments[:, :: length // 4],
            jnp.zeros((2, 116), jnp.int32),
        ],
        axis=1,
    )
    meta = jnp.concatenate(
        [keep_route.reshape(4, 128), lines, jnp.zeros((2, 128), jnp.int32)], axis=0
    ).astype(jnp.float32)
    te = time_embed.reshape(8, 8, width // 8).transpose(1, 0, 2).astype(jnp.float32)
    whead = jnp.concatenate([w_qkv, w_proj], axis=1)
    (
        weights,
        head_w,
        dealt,
        dealt_grad,
        h_first,
        qkv,
        stat,
        att,
        first,
        branch,
        h_second,
        d_mlp,
        cond,
        mod,
        gains,
        groups,
        kept,
        select,
    ) = run_front(
        whead, w_fc1, w_fc2, tokens, cotangent, meta, te, w_ada, b_ada[None, :]
    )
    weights = weights.reshape(2, 2, width, w_fc1.shape[1])
    full_fc1 = weights[0]
    full_fc2 = weights[1]
    h_second = h_second.reshape(length, width)
    d_mlp = d_mlp.reshape(length, width)
    gcols = jnp.repeat(groups[:, 0], FF // GROUPS).reshape(2, -1)

    upward = jnp.einsum("rd,zdu->zru", h_second, full_fc1, preferred_element_type=jnp.float32)
    gelu_val, gelu_pull = jax.vjp(lambda inner: jax.nn.gelu(inner, approximate=True), upward)
    act = (gelu_val * gcols[:, None, :]).astype(jnp.bfloat16)
    def halves(partial):
        theirs = lax.dynamic_slice_in_dim(partial, (1 - core) * 2 * part, 2 * part)
        mine = lax.dynamic_slice_in_dim(partial, core * 2 * part, 2 * part)
        shape = (2, part, width)
        return theirs.astype(jnp.bfloat16).reshape(shape), mine.reshape(shape)

    mlp_send, mlp_own = halves(
        jnp.einsum("zru,zou->ro", act, full_fc2, preferred_element_type=jnp.float32)
    )
    grad_fc2 = jnp.einsum("ro,zru->zou", d_mlp, act, preferred_element_type=jnp.float32)
    d_act = jnp.einsum("ro,zou->zru", d_mlp, full_fc2, preferred_element_type=jnp.float32)
    d_up = gelu_pull(d_act * gcols[:, None, :])[0].astype(jnp.bfloat16)
    grad_fc1 = jnp.einsum("rd,zru->zdu", h_second, d_up, preferred_element_type=jnp.float32)
    dh2_send, dh2_own = halves(
        jnp.einsum("zru,zdu->rd", d_up, full_fc1, preferred_element_type=jnp.float32)
    )
    gfc = jnp.stack([grad_fc1, grad_fc2]).astype(jnp.bfloat16)
    gfc = gfc.reshape(2, 2, 8, width // 8, width)
    result, d_input, grads, _, g_ada, g_bias = run_back(
        gfc,
        dh2_send,
        mlp_send,
        dh2_own,
        mlp_own,
        first,
        branch,
        dealt,
        dealt_grad,
        h_first,
        qkv,
        stat,
        att,
        head_w,
        mod,
        gains,
        kept,
        select,
        cond,
    )
    return (
        result,
        d_input,
        grads[0, :, :qcols],
        grads[0, :, qcols:],
        grads[1],
        grads[2],
        g_ada,
        g_bias[0],
    )


def solution(mesh):
    placed = (
        P("dp", "tensor", None),
        P("dp", None, None),
        P("dp", None),
        P("dp"),
        P("dp", "tensor"),
        P("dp", "tensor"),
        P("dp", "tensor"),
        P("dp", "tensor"),
        P("dp", "tensor"),
        P("dp", "tensor"),
        P("dp", "tensor"),
        P("dp", "tensor"),
        P("tensor"),
        P("dp", "tensor", None),
    )
    return jax.shard_map(
        fast_body if mesh.shape["dp"] == 8 and mesh.shape["tensor"] == 4 else body,
        mesh=mesh,
        in_specs=placed,
        out_specs=(
            P("dp", "tensor", None),
            P("dp", "tensor", None),
            P("dp", "tensor"),
            P("dp", "tensor"),
            P("dp", "tensor"),
            P("dp", "tensor"),
            P("dp", "tensor"),
            P("tensor"),
        ),
        check_vma=False,
    )
```

```python
import jax
import jax.numpy as jnp
from jax import lax
from jax.experimental import pallas as pl
from jax.experimental.pallas import tpu as pltpu
from jax.sharding import PartitionSpec as P

HD = 72
FF = 4608
GROUPS = 16


EPSILON = 1e-06
HIGH = lax.Precision.HIGHEST


def layer_norm(values):
    middle = jnp.mean(values, axis=-1, keepdims=True)
    centred = values - middle
    spread = jnp.mean(centred * centred, axis=-1, keepdims=True)
    factor = lax.rsqrt(spread + EPSILON)
    return (centred * factor, factor)


def norm_back(grad, normed, factor):
    inner = (
        grad
        - jnp.mean(grad, axis=-1, keepdims=True)
        - normed * jnp.mean(grad * normed, axis=-1, keepdims=True)
    )
    return factor * inner


def contract_rows(left, right):
    return lax.dot_general(
        left, right, (((0,), (0,)), ((), ())), preferred_element_type=jnp.float32
    )


def contract_cols(left, right):
    return lax.dot_general(
        left, right, (((1,), (1,)), ((), ())), preferred_element_type=jnp.float32
    )


def score_block(query_block, keys, seg_block, seg_ids):
    scores = jnp.einsum(
        "qhe,khe->hqk", query_block, keys, preferred_element_type=jnp.float32
    ) * HD ** (-0.5)
    same = seg_block[:, None] == seg_ids[None, :]
    return jnp.where(same[None], scores, -1e30)


def attention_forward(query, keys, values, seg_ids):
    length = query.shape[0]
    block = min(512, length)
    outs = []
    totals = []
    for offset in range(0, length, block):
        scores = score_block(
            query[offset : offset + block], keys, seg_ids[offset : offset + block], seg_ids
        )
        peak = jnp.max(scores, axis=-1, keepdims=True)
        denom = jnp.sum(jnp.exp(scores - peak), axis=-1, keepdims=True)
        log_total = peak + jnp.log(denom)
        probs = jnp.exp(scores - log_total).astype(jnp.bfloat16)
        outs.append(jnp.einsum("hqk,khe->qhe", probs, values, preferred_element_type=jnp.float32))
        totals.append(log_total)
    return (jnp.concatenate(outs, axis=0), totals)


def attention_backward(query, keys, values, seg_ids, totals, d_attn):
    length = query.shape[0]
    block = min(512, length)
    scale = HD ** (-0.5)
    d_keys = jnp.zeros(keys.shape, jnp.float32)
    d_values = jnp.zeros(values.shape, jnp.float32)
    d_queries = []
    for number, offset in enumerate(range(0, length, block)):
        query_block = query[offset : offset + block]
        scores = score_block(query_block, keys, seg_ids[offset : offset + block], seg_ids)
        probs = jnp.exp(scores - totals[number])
        grad_block = d_attn[offset : offset + block]
        d_values = d_values + jnp.einsum(
            "hqk,qhe->khe",
            probs.astype(jnp.bfloat16),
            grad_block,
            preferred_element_type=jnp.float32,
        )
        d_probs = jnp.einsum("qhe,khe->hqk", grad_block, values, preferred_element_type=jnp.float32)
        d_scores = (probs * (d_probs - jnp.sum(probs * d_probs, axis=-1, keepdims=True))).astype(
            jnp.bfloat16
        )
        d_queries.append(
            jnp.einsum("hqk,khe->qhe", d_scores, keys, preferred_element_type=jnp.float32) * scale
        )
        d_keys = (
            d_keys
            + jnp.einsum("hqk,qhe->khe", d_scores, query_block, preferred_element_type=jnp.float32)
            * scale
        )
    stacked = jnp.stack([jnp.concatenate(d_queries, axis=0), d_keys, d_values], axis=2)
    return stacked.astype(jnp.bfloat16).reshape(length, -1)


def body(
    tokens,
    time_embed,
    segments,
    micro_order,
    head_mask,
    group_mask,
    keep_route,
    w_qkv,
    w_proj,
    w_fc1,
    w_fc2,
    w_ada,
    b_ada,
    cotangent,
):
    micro = tokens.shape[0]
    local_rows = tokens.shape[1]
    length = segments.shape[1]
    heads_here = head_mask.shape[1]
    segs = time_embed.shape[1]
    tensor_index = lax.axis_index("tensor")
    chooser = (micro_order[:, None] == jnp.arange(micro, dtype=jnp.int32)[None, :]).astype(
        jnp.float32
    )
    head_sel = jnp.dot(chooser, head_mask.astype(jnp.float32), precision=HIGH)
    group_sel = jnp.repeat(
        jnp.dot(chooser, group_mask.astype(jnp.float32), precision=HIGH), FF // GROUPS, axis=1
    )
    keep_float = keep_route.astype(jnp.float32)

    def reduce_grads(grad_qkv, grad_proj, grad_fc1, grad_fc2, grad_ada):
        return (
            lax.psum_scatter(
                grad_qkv.astype(jnp.bfloat16), "dp", scatter_dimension=0, tiled=True
            ).astype(jnp.float32),
            lax.psum_scatter(
                grad_proj.astype(jnp.bfloat16), "dp", scatter_dimension=0, tiled=True
            ).astype(jnp.float32),
            lax.psum_scatter(
                grad_fc1.astype(jnp.bfloat16), "dp", scatter_dimension=0, tiled=True
            ).astype(jnp.float32),
            lax.psum_scatter(
                grad_fc2.astype(jnp.bfloat16), "dp", scatter_dimension=0, tiled=True
            ).astype(jnp.float32),
            lax.psum_scatter(
                grad_ada.astype(jnp.bfloat16), "dp", scatter_dimension=0, tiled=True
            ).astype(jnp.float32),
        )

    shard_shapes = [w.shape for w in (w_qkv, w_proj, w_fc1, w_fc2, w_ada)]
    start_acc = tuple((jnp.zeros(shape, jnp.float32) for shape in shard_shapes))

    def slot_step(carry, items):
        acc, bias_acc = carry
        slot_tokens, slot_grad, seg_ids, embed, hmask, gcols, keepf = items
        full = (
            lax.all_gather(w_qkv, "dp", axis=0, tiled=True),
            lax.all_gather(w_proj, "dp", axis=0, tiled=True),
            lax.all_gather(w_fc1, "dp", axis=0, tiled=True),
            lax.all_gather(w_fc2, "dp", axis=0, tiled=True),
            lax.all_gather(w_ada, "dp", axis=0, tiled=True),
        )
        full_qkv, full_proj, full_fc1, full_fc2, full_ada = full
        seg_local = lax.dynamic_slice_in_dim(seg_ids, tensor_index * local_rows, local_rows)
        scond = jax.nn.silu(embed.astype(jnp.float32)).astype(jnp.bfloat16)
        part_mods = jnp.dot(scond, full_ada, preferred_element_type=jnp.float32) + b_ada[None, :]
        mods = lax.all_gather(part_mods, "tensor", axis=1, tiled=True)
        onehot = (seg_local[:, None] == jnp.arange(segs, dtype=jnp.int32)[None, :]).astype(
            jnp.float32
        )
        modtok = jnp.dot(onehot, mods, precision=HIGH)
        shift1, scale1, gate1, shift2, scale2, gate2 = jnp.split(modtok, 6, axis=1)
        token_vals = slot_tokens.astype(jnp.float32)
        normed1, factor1 = layer_norm(token_vals)
        h_first = lax.all_gather(
            (normed1 * (1.0 + scale1) + shift1).astype(jnp.bfloat16), "tensor", axis=0, tiled=True
        )
        packed = jnp.dot(h_first, full_qkv, preferred_element_type=jnp.float32).astype(jnp.bfloat16)
        packed = packed.reshape(length, heads_here, 3, HD)
        query = packed[:, :, 0]
        keys = packed[:, :, 1]
        values = packed[:, :, 2]
        outs, totals = attention_forward(query, keys, values, seg_ids)
        attn = (outs * hmask[None, :, None]).astype(jnp.bfloat16).reshape(length, heads_here * HD)
        branch = lax.psum_scatter(
            contract_cols(attn, full_proj).astype(jnp.bfloat16),
            "tensor",
            scatter_dimension=0,
            tiled=True,
        ).astype(jnp.float32)
        first = token_vals + gate1 * branch
        normed2, factor2 = layer_norm(first)
        h_second = lax.all_gather(
            (normed2 * (1.0 + scale2) + shift2).astype(jnp.bfloat16), "tensor", axis=0, tiled=True
        )
        upward = jnp.dot(h_second, full_fc1, preferred_element_type=jnp.float32)
        gelu_val, gelu_pull = jax.vjp(lambda inner: jax.nn.gelu(inner, approximate=True), upward)
        act = (gelu_val * gcols[None, :]).astype(jnp.bfloat16)
        mlp = lax.psum_scatter(
            contract_cols(act, full_fc2).astype(jnp.bfloat16),
            "tensor",
            scatter_dimension=0,
            tiled=True,
        ).astype(jnp.float32)
        keep_col = keepf[:, None]
        result = (first + gate2 * keep_col * mlp).astype(jnp.bfloat16)
        grad_out = slot_grad.astype(jnp.float32)
        d_mlp = lax.all_gather(
            (gate2 * keep_col * grad_out).astype(jnp.bfloat16), "tensor", axis=0, tiled=True
        )
        grad_fc2 = contract_rows(d_mlp, act)
        d_act = jnp.dot(d_mlp, full_fc2, preferred_element_type=jnp.float32)
        d_up = gelu_pull(d_act * gcols[None, :])[0].astype(jnp.bfloat16)
        grad_fc1 = contract_rows(h_second, d_up)
        d_second = lax.psum_scatter(
            contract_cols(d_up, full_fc1).astype(jnp.bfloat16),
            "tensor",
            scatter_dimension=0,
            tiled=True,
        ).astype(jnp.float32)
        d_first = grad_out + norm_back(d_second * (1.0 + scale2), normed2, factor2)
        d_branch = lax.all_gather(
            (gate1 * d_first).astype(jnp.bfloat16), "tensor", axis=0, tiled=True
        )
        grad_proj = contract_rows(d_branch, attn)
        d_attn = jnp.dot(d_branch, full_proj, preferred_element_type=jnp.float32).astype(
            jnp.bfloat16
        )
        d_attn = d_attn.reshape(length, heads_here, HD) * hmask[None, :, None].astype(jnp.bfloat16)
        d_packed = attention_backward(query, keys, values, seg_ids, totals, d_attn)
        grad_qkv = contract_rows(h_first, d_packed)
        d_h_first = lax.psum_scatter(
            contract_cols(d_packed, full_qkv).astype(jnp.bfloat16),
            "tensor",
            scatter_dimension=0,
            tiled=True,
        ).astype(jnp.float32)
        d_input = d_first + norm_back(d_h_first * (1.0 + scale1), normed1, factor1)
        d_modtok = jnp.concatenate(
            [
                d_h_first,
                d_h_first * normed1,
                d_first * branch,
                d_second,
                d_second * normed2,
                grad_out * keep_col * mlp,
            ],
            axis=1,
        )
        part_dmods = lax.dot_general(onehot, d_modtok, (((0,), (0,)), ((), ())), precision=HIGH)
        d_mods = lax.psum_scatter(
            part_dmods.astype(jnp.bfloat16), "tensor", scatter_dimension=1, tiled=True
        ).astype(jnp.float32)
        grad_ada = jnp.dot(scond.astype(jnp.float32).T, d_mods, precision=HIGH)
        bias_acc = bias_acc + jnp.sum(d_mods, axis=0)
        parts = reduce_grads(grad_qkv, grad_proj, grad_fc1, grad_fc2, grad_ada)
        acc = tuple((held + piece for held, piece in zip(acc, parts)))
        return ((acc, bias_acc), (result, d_input.astype(jnp.bfloat16)))

    start_bias = jnp.zeros(b_ada.shape, jnp.float32)
    (acc, bias_acc), (results, d_tokens) = lax.scan(
        slot_step,
        (start_acc, start_bias),
        (tokens, cotangent, segments, time_embed, head_sel, group_sel, keep_float),
    )
    g_bias = lax.psum(bias_acc, "dp")
    return (results, d_tokens, acc[0], acc[1], acc[2], acc[3], acc[4], g_bias)


MESH = pl.DeviceIdType.MESH
ANY = pl.BlockSpec(memory_space=pl.ANY)
DMA = pltpu.SemaphoreType.DMA


class Place:
    def __init__(self):
        self.dp = lax.axis_index("dp")
        self.line = lax.axis_index("tensor")
        self.core = self.dp % 2
        self.base = self.dp - self.core
        self.half = self.line // 2
        x, y = (self.dp // 2) % 2, self.dp // 4
        self.dp_x = self.dp + 2 * (1 - 2 * x)
        self.dp_y = self.dp + 4 * (1 - 2 * y)
        self.base_x = self.dp_x - self.core
        self.base_y = self.dp_y - self.core
        self.base_far = self.base_x + self.base_y - self.base

    def barrier(self):
        bar = pltpu.get_barrier_semaphore()
        spot = self.core * 4 + self.line
        for step in range(1, 8):
            other = (spot + step) % 8
            pl.semaphore_signal(
                bar,
                inc=1,
                device_id=(self.base + other // 4, other % 4),
                device_id_type=MESH,
            )
        for step in range(1, 8):
            other = (self.dp + step) % 8
            pl.semaphore_signal(bar, inc=1, device_id=(other, self.line), device_id_type=MESH)
        pl.semaphore_wait(bar, 14)


def remote(src, dst, send, recv, dp, line):
    return pltpu.make_async_remote_copy(
        src_ref=src,
        dst_ref=dst,
        send_sem=send,
        recv_sem=recv,
        device_id=(dp, line),
        device_id_type=MESH,
    )


def move(src, dst, send, recv, dp, line, here):
    @pl.when(here)
    def _():
        pltpu.make_async_copy(src, dst, recv).start()

    @pl.when(jnp.logical_not(here))
    def _():
        remote(src, dst, send, recv, dp, line).start()


LOG2E = 1.4426950408889634
LOW = jnp.bfloat16
F32 = jnp.float32
SHADE = -1e30


def dot_nn(left, right):
    return jnp.dot(left, right, preferred_element_type=F32)


def dot_nt(left, right):
    return lax.dot_general(left, right, (((1,), (1,)), ((), ())), preferred_element_type=F32)


def dot_tn(left, right):
    return lax.dot_general(left, right, (((0,), (0,)), ((), ())), preferred_element_type=F32)


def lanes(rows):
    return lax.broadcasted_iota(jnp.int32, (rows, 128), 1)


def window(value, start):
    tile, rest = start // 128, start % 128
    here = value[:, 128 * tile : 128 * tile + 128]
    if rest == 0:
        return here
    here = pltpu.roll(here, 128 - rest, 1)
    if rest + HD <= 128:
        return here
    after = pltpu.roll(value[:, 128 * tile + 128 : 128 * tile + 256], 128 - rest, 1)
    return jnp.where(lanes(value.shape[0]) < 128 - rest, here, after)


def pack(parts, start, tiles):
    rows = parts[0].shape[0]
    lane = lanes(rows)
    out = []
    for tile in range(tiles):
        total = jnp.zeros((rows, 128), F32)
        for number, part in enumerate(parts):
            low = start + HD * number - 128 * tile
            if low >= 128 or low + HD <= 0:
                continue
            moved = pltpu.roll(part, low % 128, 1) if low % 128 else part
            inside = jnp.logical_and(lane >= low, lane < low + HD)
            total = jnp.where(inside, moved, total)
        out.append(total)
    return out


def turned(value, tile):
    start = 128 * tile
    stop = min(start + 128, value.shape[1])
    part = value[:, start:stop]
    if stop - start < 128:
        part = jnp.concatenate([part, jnp.zeros((part.shape[0], 64), F32)], axis=1)
    return pltpu.roll(part, 64, 1)


def to_blocks(even, odd):
    low = lanes(even.shape[0]) < 64
    turn = [turned(odd, tile) for tile in range(14)]
    tail = jnp.concatenate([even[:, 1664:1728], jnp.zeros((even.shape[0], 64), F32)], axis=1)
    one = [even[:, 0:1152]]
    two = [even[:, 1152:1664], jnp.where(low, tail, turn[0])]
    two += [jnp.where(low, turn[t], turn[t + 1]) for t in range(4)]
    three = [jnp.where(low, turn[t], turn[t + 1]) for t in range(4, 13)]
    return [jnp.concatenate(parts, axis=1) for parts in (one, two, three)]


def to_chunks(one, two, three):
    low = lanes(one.shape[0]) < 64
    even = jnp.concatenate([one, two[:, 0:576]], axis=1)
    turn = [turned(two, tile) for tile in range(4, 9)] + [turned(three, t) for t in range(9)]
    odd = [jnp.where(low, turn[t], turn[t + 1]) for t in range(13)]
    return even, jnp.concatenate(odd + [turn[13][:, 0:64]], axis=1)


def front_kernel(
    wh,
    w1,
    w2,
    tok,
    cot,
    meta,
    te,
    wa,
    ba,
    weights,
    w1_out,
    head_out,
    x_out,
    g_out,
    h1_out,
    qkv_out,
    stat_out,
    att_out,
    x1_out,
    br_out,
    h2_out,
    dm_out,
    act_out,
    gp_out,
    cond,
    mod,
    gains,
    groups,
    kept,
    select,
    xt,
    w0,
    h1,
    qkv,
    obuf,
    stat,
    att,
    sb,
    rb,
    br,
    x1,
    h2,
    ct,
    dm,
    w1v,
    act,
    gp,
    gc,
    mt,
    te_all,
    pb,
    pr,
    mine,
    mr,
    feat,
    zs,
    zr,
    fs,
    ns,
    nr,
    ds,
    dr,
    ts,
    tr,
    es,
    er,
    ls,
    ms,
    mrs,
    tes,
    ter,
    pbs,
    pbr,
    mms,
    mmr,
):
    at = Place()
    dp, line, core, half = at.dp, at.line, at.core, at.half
    units = (wh, w1, w2)
    lane = line % 2
    rows_u = w1.shape[0]
    sib = at.base + 1 - core
    at.barrier()

    def spot(u, zi, row):
        if u < 2:
            return (w0, w1v)[u].at[zi, pl.ds(pl.multiple_of(row * rows_u, 16), rows_u)]
        return weights.at[zi, row]

    def deal(kind, start):
        src, dst = ((tok, xt), (cot, ct))[kind]
        for slot in range(2):
            there = 2 * core + slot
            here = jnp.logical_and(half == core, there == line)
            send, recv = ts.at[kind, slot], tr.at[kind, lane]
            if start:
                move(src.at[slot], dst.at[lane], send, recv, at.base + half, there, here)
            else:

                @pl.when(jnp.logical_not(here))
                def _():
                    remote(
                        src.at[slot], dst.at[lane], send, recv, at.base + half, there
                    ).wait_send()

    def deal_arrive(kind):
        src, dst = ((tok, xt), (cot, ct))[kind]
        for block in range(2):
            pltpu.make_async_copy(src.at[0], dst.at[block], tr.at[kind, block]).wait()

    def source(u, start):
        dst = spot(u, lane, dp)
        recv = zr.at[u, lane, core]
        home = at.base + half
        if start:
            move(units[u], dst, zs.at[u, 0], recv, home, line, half == core)
        else:

            @pl.when(half != core)
            def _():
                remote(units[u], dst, zs.at[u, 0], recv, home, line).wait_send()

        for which, step in ((1, 1), (2, -1)):
            inside = line < 3 if step == 1 else line > 0

            @pl.when(inside)
            def _():
                copy = remote(units[u], dst, zs.at[u, which], recv, home, line + step)
                copy.start() if start else copy.wait_send()

    first = jnp.where(core == 0, jnp.where(line == 0, 0, 1), jnp.where(line == 3, 1, 0))

    def z_stage(u, k, other, start):
        zi = first + k - 2 * first * k
        origin = 2 * core + zi
        ref = spot(u, zi, at.base + other)
        if start:
            pltpu.make_async_copy(w1, ref, zr.at[u, zi, other]).wait()
        up = jnp.logical_and(origin < line, line < 3)
        down = jnp.logical_and(origin > line, line > 0)
        for go, step in ((up, 1), (down, -1)):

            @pl.when(go)
            def _():
                copy = remote(
                    ref, ref, fs.at[u, zi, other], zr.at[u, zi, other], dp, line + step
                )
                copy.start() if start else copy.wait_send()

        for which, near in ((0, at.dp_x), (1, at.dp_y)):
            copy = remote(
                ref, ref, ns.at[which, u, zi, other], nr.at[which, u, zi, other], near, line
            )
            copy.start() if start else copy.wait_send()

    def far_stage(u, zi, other, start):
        base = at.base_x + zi * (at.base_y - at.base_x)
        near = at.dp_y + zi * (at.dp_x - at.dp_y)
        ref = spot(u, zi, base + other)
        if start:
            pltpu.make_async_copy(w1, ref, nr.at[zi, u, zi, other]).wait()
        copy = remote(ref, ref, ds.at[u, zi, other], dr.at[u, zi, other], near, line)
        copy.start() if start else copy.wait_send()

    def last_stage(u, zi, other):
        base = at.base_y + zi * (at.base_x - at.base_y)
        ref = spot(u, zi, base + other)
        pltpu.make_async_copy(w1, ref, nr.at[1 - zi, u, zi, other]).wait()
        ref = spot(u, zi, at.base_far + other)
        pltpu.make_async_copy(w1, ref, dr.at[u, zi, other]).wait()

    def pump(number):
        k, other = (number % 4) // 2, number % 2
        for quarter in range(4):
            u, stage = 1 + quarter // 2, (z_stage, far_stage)[quarter % 2]

            @pl.when(number // 4 == quarter)
            def _():
                stage(u, k, other, True)

    def keep(src, dst, number):
        return pltpu.make_async_copy(src, dst, ls.at[number])

    def each_column(start):
        for step in range(1, 8):
            other = (core * 4 + line + step) % 8
            copy = remote(
                meta, mt.at[core * 4 + line], ms.at[step], mrs.at[core * 4 + line],
                at.base + other // 4, other % 4,
            )
            copy.start() if start else copy.wait_send()

    def each_row(src, dst, send, recv, start, pieces):
        for step in range(1, 8):
            other = (dp + step) % 8
            part = src.at[other] if pieces else src
            copy = remote(part, dst.at[dp], send.at[step], recv.at[dp], other, line)
            copy.start() if start else copy.wait_send()

    def row_arrive(dst, recv):
        for step in range(1, 8):
            other = (dp + step) % 8
            pltpu.make_async_copy(dst.at[other], dst.at[other], recv.at[other]).wait()

    each_row(te, te_all, tes, ter, True, True)
    each_column(True)
    te_all[dp] = te[dp]
    mt[core * 4 + line] = meta[...]

    deal(0, True)
    source(0, True)
    row_arrive(te_all, ter)
    for number in range(8):
        spread = te_all[number]
        cond[8 * number : 8 * number + 8, :] = spread * (1.0 / (1.0 + jnp.exp(-spread)))
    value = dot_nn(cond[...].astype(LOW), wa[...])
    for number in range(8):
        pb[number] = value[8 * number : 8 * number + 8, :]
    each_row(pb, pr, pbs, pbr, True, True)
    pr[dp] = pb[dp]
    for other in range(2):
        z_stage(0, 0, other, True)
    row_arrive(pr, pbr)
    total = ba[...] + pr[0]
    for number in range(1, 8):
        total = total + pr[number]
    mine[...] = total

    def each_slot(start):
        for slot in range(2):
            there = 2 * core + slot
            for to in range(2):
                here = jnp.logical_and(core == to, there == line)
                send, recv = mms.at[slot, to], mmr.at[line]
                if start:
                    move(mine, mr.at[line], send, recv, at.base + to, there, here)
                else:

                    @pl.when(jnp.logical_not(here))
                    def _():
                        remote(mine, mr.at[line], send, recv, at.base + to, there).wait_send()

    each_slot(True)
    for other in range(2):
        z_stage(0, 1, other, True)
    source(1, True)
    deal(1, True)

    for step in range(1, 8):
        other = (core * 4 + line + step) % 8
        pltpu.make_async_copy(meta, mt.at[other], mrs.at[other]).wait()
    one_row = lanes(1)
    spots = (one_row - HD).astype(F32)
    inside = jnp.logical_and(one_row >= HD, one_row < HD + 4)

    def lane_of(row, place):
        return jnp.sum(jnp.where(one_row == place, row, 0.0), axis=1, keepdims=True)

    for zi in range(2):
        info = mt[half * 4 + 2 * core + zi, pl.ds(4 + lane, 1), :]
        for number in range(4):
            head = zi * 4 + number
            gains[head : head + 1, :] = jnp.broadcast_to(lane_of(info, number), (1, 128))
            groups[head : head + 1, :] = jnp.broadcast_to(lane_of(info, 4 + number), (1, 128))
    unit = lax.broadcasted_iota(jnp.int32, (1, gc.shape[1]), 1) // (gc.shape[1] // 4)
    for zi in range(2):
        row = jnp.zeros((1, gc.shape[1]), F32)
        for number in range(4):
            head = zi * 4 + number
            row = jnp.where(unit == number, groups[head : head + 1, 0:1], row)
        gc[8 * zi : 8 * zi + 8, :] = jnp.broadcast_to(row, (8, gc.shape[1]))
    info = mt[half * 4 + line, pl.ds(4 + lane, 1), :]
    for tile in range(4):
        same = jnp.where(spots == lane_of(info, 8 + tile), 1.0, 0.0)
        feat[0, tile : tile + 1, :] = jnp.where(inside, SHADE * (1.0 - same), 0.0)
        feat[1, tile : tile + 1, :] = jnp.where(inside, same, 0.0)
    row_ids = lax.broadcasted_iota(jnp.int32, (8, 128), 0)
    diagonal = lax.broadcasted_iota(jnp.int32, (128, 128), 0) == lanes(128)
    for block in range(2):
        item = jnp.sum(
            jnp.where(one_row == 8 + 2 * core + block, info, 0.0), axis=1, keepdims=True
        )
        hit = row_ids.astype(F32) == item + (4 * lane).astype(F32)
        select[block] = jnp.where(hit, 1.0, 0.0)
        for number in range(2):
            row = mt[half * 4 + 2 * core + block, pl.ds(2 * lane + number, 1), :]
            column = jnp.sum(jnp.where(diagonal, row, 0.0), axis=1, keepdims=True)
            kept[block, 128 * number : 128 * number + 128, :] = jnp.broadcast_to(column, (128, 128))
    for source_line in range(4):
        pltpu.make_async_copy(mine, mr.at[source_line], mmr.at[source_line]).wait()
    for block in range(2):
        weight = select[block][:, 0:1]
        rows = [jnp.sum(weight * mr[n], axis=0, keepdims=True) for n in range(4)]
        pieces = to_blocks(rows[0], rows[1]) + to_blocks(rows[2], rows[3])
        for number, piece in enumerate(pieces):
            mod[block, number : number + 1, :] = piece
        mod[block, 6:8, :] = jnp.zeros((2, mod.shape[2]), F32)

    def exchange(src, dst, number):
        return remote(src, dst, es.at[number], er.at[number], sib, line)

    deal_arrive(0)
    keep(xt, x_out, 0).start()

    for block in range(2):
        shift, scale = mod[block, 0:1, :], 1.0 + mod[block, 1:2, :]

        def norm_first(step, _):
            at_row = pl.ds(pl.multiple_of(step * 128, 128), 128)
            normed, _f = layer_norm(xt[block, at_row, :].astype(F32))
            to_row = pl.ds(pl.multiple_of(block * 256 + step * 128, 128), 128)
            h1[core, to_row, :] = (normed * scale + shift).astype(LOW)
            return 0

        lax.fori_loop(0, 2, norm_first, 0)
        part = h1.at[core, pl.ds(block * 256, 256)]
        exchange(part, part, block).start()
    for zi in range(2):
        for other in range(2):
            far_stage(0, zi, other, True)
    source(2, True)
    for zi in range(2):
        for other in range(2):
            last_stage(0, zi, other)
    keep(w0, head_out, 1).start()

    def project(step, _):
        @pl.when(step >= 2)
        def _():
            part = h1.at[1 - core, pl.ds(pl.multiple_of((step - 2) * 256, 256), 256)]
            pltpu.make_async_copy(part, part, er.at[step - 2]).wait()

        pump(step)
        tile = (2 * core + step) % 4
        rows = h1[tile // 2, pl.ds(pl.multiple_of((tile % 2) * 256, 256), 256), :]
        to_row = pl.ds(pl.multiple_of(tile * 256, 256), 256)
        narrow = lanes(256) < HD
        fills = (feat[0, pl.ds(tile, 1), :], feat[1, pl.ds(tile, 1), :], jnp.zeros((1, 128), F32))
        for zi in range(2):
            value = dot_nn(rows, w0[zi, :, 0:896])
            for number in range(12):
                head, part = zi * 4 + number // 3, number % 3
                piece = jnp.where(narrow, window(value, HD * number), fills[part])
                qkv[head, part, to_row, :] = piece.astype(LOW)
        return 0

    lax.fori_loop(0, 4, project, 0)
    keep(h1, h1_out, 2).start()
    keep(qkv, qkv_out, 3).start()

    factor = HD ** (-0.5) * LOG2E

    def attend(head, _):
        pump(4 + head)
        gain = gains[pl.ds(head, 1), :]

        def tile_step(tile, _):
            rows = pl.ds(pl.multiple_of(tile * 256, 256), 256)
            scores = dot_nt(qkv[head, 0, rows, :], qkv[head, 1])
            peak = jnp.max(scores, axis=1, keepdims=True)
            power = jnp.exp2((scores - peak) * factor)
            total = jnp.sum(power, axis=1, keepdims=True)
            probs = (power * (1.0 / total)).astype(LOW)
            obuf[head, rows, :] = (dot_nn(probs, qkv[head, 2]) * gain).astype(LOW)
            level = peak * factor + jnp.log2(total)
            stat[rows, :] = jnp.where(lanes(256) == head, level, stat[rows, :])
            return 0

        lax.fori_loop(0, 4, tile_step, 0)
        return 0

    lax.fori_loop(0, 8, attend, 0)
    keep(stat, stat_out, 4).start()

    def lay(step, _):
        rows = pl.ds(pl.multiple_of(step * 128, 128), 128)
        for zi in range(2):
            parts = [obuf[zi * 4 + n, rows, :].astype(F32) for n in range(4)]
            for tile, value in enumerate(pack(parts, 96, 3)):
                att[zi, rows, 128 * tile : 128 * tile + 128] = value.astype(LOW)
        return 0

    lax.fori_loop(0, 8, lay, 0)
    keep(att, att_out, 5).start()

    for step in range(4):
        tile = (2 * (1 - core) + step) % 4
        rows = pl.ds(pl.multiple_of(tile * 256, 256), 256)
        value = dot_nt(att[0, rows, :], w0[0, :, 768:1152])
        value = value + dot_nt(att[1, rows, :], w0[1, :, 768:1152])
        if step < 2:
            sb[step] = value.astype(LOW)
            exchange(sb.at[step], rb.at[step], 2 + step).start()
        else:
            br[step - 2] = value
    for block in range(2):
        exchange(sb.at[block], rb.at[block], 2 + block).wait_recv()
        gate = mod[block, 2:3, :]
        shift, scale = mod[block, 3:4, :], 1.0 + mod[block, 4:5, :]

        def norm_second(step, _):
            at_row = pl.ds(pl.multiple_of(step * 128, 128), 128)
            branch = br[block, at_row, :] + rb[block, at_row, :].astype(F32)
            br[block, at_row, :] = branch
            value = xt[block, at_row, :].astype(F32) + gate * branch
            x1[block, at_row, :] = value
            normed, _f = layer_norm(value)
            to_row = pl.ds(pl.multiple_of(block * 256 + step * 128, 128), 128)
            h2[core, to_row, :] = (normed * scale + shift).astype(LOW)
            return 0

        lax.fori_loop(0, 2, norm_second, 0)
        part = h2.at[core, pl.ds(block * 256, 256)]
        exchange(part, part, 4 + block).start()
    keep(x1, x1_out, 6).start()
    keep(br, br_out, 7).start()

    deal_arrive(1)
    keep(ct, g_out, 9).start()
    for block in range(2):
        gate2 = mod[block, 5:6, :]

        def grad_rows(step, _):
            at_row = pl.ds(pl.multiple_of(step * 128, 128), 128)
            value = gate2 * kept[block, at_row, 0:1] * ct[block, at_row, :].astype(F32)
            to_row = pl.ds(pl.multiple_of(block * 256 + step * 128, 128), 128)
            dm[core, to_row, :] = value.astype(LOW)
            return 0

        lax.fori_loop(0, 2, grad_rows, 0)
        part = dm.at[core, pl.ds(block * 256, 256)]
        exchange(part, part, 6 + block).start()

    for block in range(2):
        part = h2.at[1 - core, pl.ds(block * 256, 256)]
        pltpu.make_async_copy(part, part, er.at[4 + block]).wait()
    keep(h2, h2_out, 8).start()
    for block in range(2):
        part = dm.at[1 - core, pl.ds(block * 256, 256)]
        pltpu.make_async_copy(part, part, er.at[6 + block]).wait()
    keep(dm, dm_out, 10).start()

    for zi in range(2):
        for other in range(2):
            last_stage(1, zi, other)
    keep(w1v, w1_out, 11).start()
    ratio = (2.0 / 3.141592653589793) ** 0.5

    def widen(step, _):
        tile, zi = (2 * core + step // 2) % 4, step % 2
        rows = h2[tile // 2, pl.ds(pl.multiple_of((tile % 2) * 256, 256), 256), :]
        value = dot_nn(rows, w1v[zi])
        mask = gc[pl.ds(pl.multiple_of(8 * zi, 8), 8), :][0:1, :]
        square = value * value
        bend = jnp.tanh(ratio * (value + 0.044715 * (value * square)))
        grown = 0.5 * (1.0 + bend)
        slope = grown + 0.5 * value * (1.0 - bend * bend) * (
            ratio * (1.0 + (3.0 * 0.044715) * square)
        )
        to_row = pl.ds(pl.multiple_of(tile * 256, 256), 256)
        act[zi, to_row, :] = (value * grown * mask).astype(LOW)
        gp[zi, to_row, :] = (slope * mask).astype(LOW)

        @pl.when(step % 2 == 1)
        def _():
            pump(12 + step // 2)

        return 0

    lax.fori_loop(0, 8, widen, 0)
    keep(act, act_out, 12).start()
    keep(gp, gp_out, 13).start()

    for u in range(3):
        source(u, False)
        for k in range(2):
            for other in range(2):
                z_stage(u, k, other, False)
                far_stage(u, k, other, False)
                if u == 2:
                    last_stage(u, k, other)
    for kind in range(2):
        deal(kind, False)
    each_column(False)
    each_row(te, te_all, tes, ter, False, True)
    each_row(pb, pr, pbs, pbr, False, True)
    each_slot(False)
    for block in range(2):
        own1 = h1.at[core, pl.ds(block * 256, 256)]
        own2 = h2.at[core, pl.ds(block * 256, 256)]
        exchange(own1, own1, block).wait_send()
        exchange(sb.at[block], rb.at[block], 2 + block).wait_send()
        exchange(own2, own2, 4 + block).wait_send()
        own3 = dm.at[core, pl.ds(block * 256, 256)]
        exchange(own3, own3, 6 + block).wait_send()
    pairs = (
        (xt, x_out),
        (w0, head_out),
        (h1, h1_out),
        (qkv, qkv_out),
        (stat, stat_out),
        (att, att_out),
        (x1, x1_out),
        (br, br_out),
        (h2, h2_out),
        (ct, g_out),
        (dm, dm_out),
        (w1v, w1_out),
        (act, act_out),
        (gp, gp_out),
    )
    for number, (src, dst) in enumerate(pairs):
        keep(src, dst, number).wait()


def run_front(wh, w1, w2, tok, cot, meta, te, wa, ba):
    rows, cols = w1.shape
    part = tok.shape[1]
    length = 4 * part
    shape = jax.ShapeDtypeStruct
    vmem = pl.BlockSpec(memory_space=pltpu.VMEM)
    shared = shape((2, 2 * part, cols), LOW)
    single = shape((2, part, cols), F32)
    outs = (
        shape((2, 8, rows, cols), LOW),
        shape((2, 8 * rows, cols), LOW),
        shape((2, 8 * rows, cols), LOW),
        shape(tok.shape, LOW),
        shape(tok.shape, LOW),
        shared,
        shape((8, 3, length, 128), LOW),
        shape((length, 128), F32),
        shape((2, length, 384), LOW),
        single,
        single,
        shared,
        shared,
        shape((2, length, cols), LOW),
        shape((2, length, cols), LOW),
    )
    small = (
        shape((64, rows), F32),
        shape((2, 8, cols), F32),
        shape((8, 128), F32),
        shape((8, 128), F32),
        shape((2, part, 128), F32),
        shape((2, 8, 128), F32),
    )
    three = DMA((3, 2, 2))
    return pl.pallas_call(
        front_kernel,
        out_shape=outs + small,
        in_specs=[ANY] * 5 + [vmem] * 4,
        out_specs=(ANY,) * len(outs) + (vmem,) * len(small),
        scratch_shapes=[
            pltpu.VMEM(tok.shape, LOW),
            pltpu.VMEM((2, 8 * rows, cols), LOW),
            pltpu.VMEM((2, 2 * part, cols), LOW),
            pltpu.VMEM((8, 3, length, 128), LOW),
            pltpu.VMEM((8, length, 128), LOW),
            pltpu.VMEM((length, 128), F32),
            pltpu.VMEM((2, length, 384), LOW),
            pltpu.VMEM((2, part, cols), LOW),
            pltpu.VMEM((2, part, cols), LOW),
            pltpu.VMEM((2, part, cols), F32),
            pltpu.VMEM((2, part, cols), F32),
            pltpu.VMEM((2, 2 * part, cols), LOW),
            pltpu.VMEM(tok.shape, LOW),
            pltpu.VMEM((2, 2 * part, cols), LOW),
            pltpu.VMEM((2, 8 * rows, cols), LOW),
            pltpu.VMEM((2, length, cols), LOW),
            pltpu.VMEM((2, length, cols), LOW),
            pltpu.VMEM((16, cols), F32),
            pltpu.VMEM((8, 8, 128), F32),
            pltpu.VMEM((8, 8, rows), F32),
            pltpu.VMEM((8, 8, wa.shape[1]), F32),
            pltpu.VMEM((8, 8, wa.shape[1]), F32),
            pltpu.VMEM((8, wa.shape[1]), F32),
            pltpu.VMEM((4, 8, wa.shape[1]), F32),
            pltpu.VMEM((2, 8, 128), F32),
            DMA((3, 3)),
            three,
            three,
            DMA((2, 3, 2, 2)),
            DMA((2, 3, 2, 2)),
            three,
            three,
            DMA((2, 2)),
            DMA((2, 2)),
            DMA((8,)),
            DMA((8,)),
            DMA((14,)),
            DMA((8,)),
            DMA((8,)),
            DMA((8,)),
            DMA((8,)),
            DMA((8,)),
            DMA((8,)),
            DMA((2, 2)),
            DMA((4,)),
        ],
        compiler_params=pltpu.CompilerParams(
            collective_id=0, has_side_effects=True, vmem_limit_bytes=60 << 20
        ),
    )(wh, w1, w2, tok, cot, meta, te, wa, ba)


def back_kernel(
    act_in,
    gp_in,
    dm_in,
    h2_in,
    w1_in,
    w2_in,
    x1_in,
    br_in,
    x_in,
    g_in,
    h1_in,
    qkv_in,
    stat_in,
    att_in,
    head_in,
    mod,
    gains,
    keep_col,
    select,
    cond,
    out_tok,
    out_dtok,
    rz,
    gfc,
    g_ada,
    g_bias,
    sums,
    db,
    yb,
    zb,
    sb,
    sm,
    rb,
    rm,
    ob,
    r1,
    rn,
    stage,
    dc,
    nr,
    da,
    s1s,
    s1r,
    nss,
    nsr,
    zss,
    zsr,
    es,
    er,
    ts,
    tr,
    ls,
    gs,
    dcs,
    dcr,
    das,
    dar,
):
    at = Place()
    dp, line, core, half = at.dp, at.line, at.core, at.half
    lane = line % 2
    rows_u = stage.shape[1]
    local = {}
    sib = at.base + 1 - core
    scale_q = HD ** (-0.5)
    factor = HD ** (-0.5) * LOG2E

    def load(src, dst, number):
        return pltpu.make_async_copy(src, dst, ls.at[number])

    def exchange(src, dst, number):
        return remote(src, dst, es.at[number], er.at[number], sib, line)

    def grad_ref(u, zi, row):
        here = pl.ds(pl.multiple_of(row * rows_u, 16), rows_u)
        if isinstance(u, int) and u == 0:
            return local["g0"].at[zi, here]
        return gfc.at[u - 1, zi, here]

    def base_of(which):
        return at.base_x + which * (at.base_y - at.base_x)

    def near_of(which):
        return at.dp_x + which * (at.dp_y - at.dp_x)

    def far_send(u, zi, o):
        return remote(
            grad_ref(u, zi, at.base_far + o),
            r1.at[u, zi, o],
            s1s.at[u, zi, o],
            s1r.at[u, zi, o],
            near_of(zi),
            line,
        )

    def plain_send(u, zi, o):
        return remote(
            grad_ref(u, zi, base_of(zi) + o),
            rn.at[zi, u, zi, o],
            nss.at[zi, u, zi, o],
            nsr.at[zi, u, zi, o],
            near_of(zi),
            line,
        )

    def relay_send(u, zi, o):
        return remote(
            r1.at[u, zi, o],
            rn.at[1 - zi, u, zi, o],
            nss.at[1 - zi, u, zi, o],
            nsr.at[1 - zi, u, zi, o],
            near_of(1 - zi),
            line,
        )

    def fetch(u, zi, row, slot):
        if isinstance(u, int) and u == 0:
            return grad_ref(u, zi, row), None
        copy = pltpu.make_async_copy(grad_ref(u, zi, row), stage.at[slot], gs.at[slot])
        copy.start()
        return stage.at[slot], copy

    def relay(u, zi, o):
        ref, copy = fetch(u, zi, base_of(1 - zi) + o, 0)
        far_send(u, zi, o).wait_recv()
        if copy is not None:
            copy.wait()
        r1[u, zi, o] = (r1[u, zi, o].astype(F32) + ref[...].astype(F32)).astype(LOW)
        relay_send(u, zi, o).start()

    def settle(u, zi, o, start):
        here = jnp.logical_and(core == o, line == 2 * core + zi)
        src, dst = rn.at[0, u, zi, o], rz.at[u, line]
        send, recv = zss.at[u, zi, o], zsr.at[u, line]
        if not start:

            @pl.when(jnp.logical_not(here))
            def _():
                remote(src, dst, send, recv, at.base + o, 2 * core + zi).wait_send()

            return
        ref, copy = fetch(u, zi, at.base + o, 1)
        for which in range(2):
            there = rn.at[which, u, zi, o]
            pltpu.make_async_copy(there, there, nsr.at[which, u, zi, o]).wait()
        if copy is not None:
            copy.wait()
        total = rn[0, u, zi, o].astype(F32) + rn[1, u, zi, o].astype(F32)
        rn[0, u, zi, o] = (total + ref[...].astype(F32)).astype(LOW)
        move(src, dst, send, recv, at.base + o, 2 * core + zi, here)

    def finish(u):
        for source in range(4):
            ref = rz.at[u, source]
            pltpu.make_async_copy(ref, ref, zsr.at[u, source]).wait()

    def pump(number):
        index = number % 8
        u, zi, o = 2 - index // 4, (index // 2) % 2, index % 2

        @pl.when(number < 8)
        def _():
            relay(u, zi, o)

        @pl.when(number >= 8)
        def _():
            settle(u, zi, o, True)

    def give_back(block, kind, start):
        dst = (out_tok, out_dtok)[kind].at[lane]
        there = 2 * core + block
        here = jnp.logical_and(half == core, there == line)
        send, recv = ts.at[kind, block], tr.at[kind, lane]
        if start:
            move(ob.at[block], dst, send, recv, at.base + half, there, here)
        else:

            @pl.when(here)
            def _():
                pltpu.make_async_copy(ob.at[block], dst, recv).wait()

            @pl.when(jnp.logical_not(here))
            def _():
                remote(ob.at[block], dst, send, recv, at.base + half, there).wait_send()

    def mlp_phase(act, gp, w1v, w2v, dm, h2, gst):
        pairs = ((dm_in, dm), (act_in, act), (w2_in, w2v), (gp_in, gp), (h2_in, h2), (w1_in, w1v))
        copies = [load(src, dst, number) for number, (src, dst) in enumerate(pairs)]
        for copy in copies:
            copy.start()
        at.barrier()
        length = act.shape[1]
        mid = length // 2

        def weight_grad(u, left, right):
            def column_half(zi, _):
                def piece(tile, _):
                    cols = pl.ds(pl.multiple_of(384 * tile, 128), 384)
                    value = dot_tn(left[0, :, cols], right[zi, 0:mid, :])
                    value = value + dot_tn(left[1, :, cols], right[zi, mid:length, :])
                    gst[tile] = value.astype(LOW)
                    rows = pl.ds(pl.multiple_of(384 * tile, 128), 384)
                    pltpu.make_async_copy(gst.at[tile], gfc.at[u - 1, zi, rows], gs.at[tile]).start()
                    return 0

                lax.fori_loop(0, 3, piece, 0)
                for tile in range(3):
                    rows = pl.ds(384 * tile, 384)
                    pltpu.make_async_copy(gst.at[tile], gfc.at[u - 1, zi, rows], gs.at[tile]).wait()
                for o in range(2):
                    far_send(u, zi, o).start()
                for o in range(2):
                    plain_send(u, zi, o).start()
                return 0

            lax.fori_loop(0, 2, column_half, 0)

        copies[0].wait()
        copies[1].wait()
        weight_grad(2, dm, act)
        copies[2].wait()
        copies[3].wait()

        def down(step, _):
            tile, zi = step // 2, step % 2
            rows = dm[tile // 2, pl.ds(pl.multiple_of((tile % 2) * 256, 256), 256), :]
            to_row = pl.ds(pl.multiple_of(tile * 256, 256), 256)
            value = dot_nn(rows, w2v[zi]) * gp[zi, to_row, :].astype(F32)
            gp[zi, to_row, :] = value.astype(LOW)
            return 0

        lax.fori_loop(0, 8, down, 0)
        copies[4].wait()
        weight_grad(1, h2, gp)
        copies[5].wait()

        def partial(left, right, send, recv, own, number):
            def part(step, _):
                tile = (2 * (1 - core) + step) % 4
                rows = pl.ds(pl.multiple_of(tile * 256, 256), 256)
                value = dot_nt(left[0, rows, :], right[0])
                value = value + dot_nt(left[1, rows, :], right[1])

                @pl.when(step < 2)
                def _():
                    send[step] = value.astype(LOW)
                    exchange(send.at[step], recv.at[step], number + step).start()

                @pl.when(step >= 2)
                def _():
                    own[step - 2] = value

                return 0

            lax.fori_loop(0, 4, part, 0)

        partial(gp, w1v, sb, rb, yb, 0)
        partial(act, w2v, sm, rm, zb, 2)

    cols = gfc.shape[3]
    length = stat_in.shape[0]
    mid = length // 2
    pl.run_scoped(
        mlp_phase,
        pltpu.VMEM((2, length, cols), LOW),
        pltpu.VMEM((2, length, cols), LOW),
        pltpu.VMEM((2, 8 * rows_u, cols), LOW),
        pltpu.VMEM((2, 8 * rows_u, cols), LOW),
        pltpu.VMEM((2, mid, cols), LOW),
        pltpu.VMEM((2, mid, cols), LOW),
        pltpu.VMEM((3, 384, cols), LOW),
    )
    for number in range(4):
        pump(jnp.int32(number))

    def attention_phase(w0, h1, qkv, stat, dpk, do, g0, xb, gb, xt, acc):
        local["g0"] = g0
        pairs = (
            (head_in, w0),
            (qkv_in, qkv),
            (stat_in, stat),
            (att_in, dpk.at[:, :, 0:384]),
            (h1_in, h1),
        )
        early = [load(src, dst, number) for number, (src, dst) in enumerate(pairs)]
        for copy in early:
            copy.start()
        for block in range(2):
            copies = (
                load(x1_in.at[block], xb.at[0], 5),
                load(br_in.at[block], xb.at[1], 6),
                load(g_in.at[block], gb, 7),
            )
            for copy in copies:
                copy.start()
            for copy in copies:
                copy.wait()
            exchange(sb.at[block], rb.at[block], block).wait_recv()
            exchange(sm.at[block], rm.at[block], 2 + block).wait_recv()
            gate1, scale2 = mod[block, 2:3, :], 1.0 + mod[block, 4:5, :]
            gate2 = mod[block, 5:6, :]

            def norm_second(step, sums_now):
                at_row = pl.ds(pl.multiple_of(step * 128, 128), 128)
                grad = gb[at_row, :].astype(F32)
                first = xb[0, at_row, :]
                d_second = yb[block, at_row, :] + rb[block, at_row, :].astype(F32)
                kept = keep_col[block, at_row, 0:1] * (
                    zb[block, at_row, :] + rm[block, at_row, :].astype(F32)
                )
                ob[block, at_row, :] = (first + gate2 * kept).astype(LOW)
                normed, spread = layer_norm(first)
                d_first = grad + norm_back(d_second * scale2, normed, spread)
                yb[block, at_row, :] = d_first
                to_row = pl.ds(pl.multiple_of(block * 256 + step * 128, 128), 128)
                db[core, to_row, :] = (gate1 * d_first).astype(LOW)
                terms = (d_first * xb[1, at_row, :], d_second, d_second * normed, grad * kept)
                return tuple(
                    now + jnp.sum(term, axis=0, keepdims=True) for now, term in zip(sums_now, terms)
                )

            zero = jnp.zeros((1, gb.shape[1]), F32)
            totals = lax.fori_loop(0, 2, norm_second, (zero,) * 4)
            for place, value in zip((2, 3, 4, 5), totals):
                sums[block, place : place + 1, :] = value
            part = db.at[core, pl.ds(block * 256, 256)]
            exchange(part, part, 4 + block).start()
            give_back(block, 0, True)

        for copy in early[0:4]:
            copy.wait()

        def to_heads(step, _):
            @pl.when(step >= 2)
            def _():
                part = db.at[1 - core, pl.ds(pl.multiple_of((step - 2) * 256, 256), 256)]
                pltpu.make_async_copy(part, part, er.at[4 + step - 2]).wait()

            tile = (2 * core + step) % 4
            rows = db[tile // 2, pl.ds(pl.multiple_of((tile % 2) * 256, 256), 256), :]
            to_row = pl.ds(pl.multiple_of(tile * 256, 256), 256)
            narrow = lanes(256) < HD
            for zi in range(2):
                value = dot_nn(rows, w0[zi, :, 768:1152])
                for number in range(4):
                    piece = jnp.where(narrow, window(value, 96 + HD * number), 0.0)
                    head = zi * 4 + number
                    do[head, to_row, :] = (piece * gains[head : head + 1, :]).astype(LOW)
            return 0

        lax.fori_loop(0, 4, to_heads, 0)
        for zi in range(2):
            for tile in range(3):
                cols = slice(384 * tile, 384 * tile + 384)
                value = dot_tn(db[0, :, cols], dpk[zi, 0:mid, 0:384])
                value = value + dot_tn(db[1, :, cols], dpk[zi, mid:length, 0:384])
                g0[zi, cols, 768:1152] = value.astype(LOW)

        def attend(head, _):
            pump(4 + head)
            acc[...] = jnp.zeros_like(acc)

            def tile_step(tile, _):
                rows = pl.ds(pl.multiple_of(tile * 256, 256), 256)
                query, grad = qkv[head, 0, rows, :], do[head, rows, :]
                level = jnp.sum(jnp.where(lanes(256) == head, stat[rows, :], 0.0), axis=1, keepdims=True)
                probs = jnp.exp2(dot_nt(query, qkv[head, 1]) * factor - level)
                d_probs = dot_nt(grad, qkv[head, 2])
                inner = jnp.sum(probs * d_probs, axis=1, keepdims=True)
                d_scores = (probs * (d_probs - inner)).astype(LOW)
                acc[0] += dot_tn(d_scores, query)
                acc[1] += dot_tn(probs.astype(LOW), grad)
                qkv[head, 0, rows, :] = (dot_nn(d_scores, qkv[head, 1]) * scale_q).astype(LOW)
                return 0

            lax.fori_loop(0, 4, tile_step, 0)
            qkv[head, 1] = (acc[0] * scale_q).astype(LOW)
            qkv[head, 2] = acc[1].astype(LOW)
            return 0

        lax.fori_loop(0, 8, attend, 0)

        def lay(step, _):
            rows = pl.ds(pl.multiple_of(step * 128, 128), 128)
            for zi in range(2):
                parts = [
                    jnp.where(lanes(128) < HD, qkv[zi * 4 + n // 3, n % 3, rows, :].astype(F32), 0.0)
                    for n in range(12)
                ]
                for tile, value in enumerate(pack(parts, 0, 7)):
                    dpk[zi, rows, 128 * tile : 128 * tile + 128] = value.astype(LOW)
            return 0

        lax.fori_loop(0, 8, lay, 0)
        early[4].wait()
        for zi in range(2):
            for tile in range(3):
                cols = slice(384 * tile, 384 * tile + 384)
                value = dot_tn(h1[0, :, cols], dpk[zi, 0:mid, :])
                value = value + dot_tn(h1[1, :, cols], dpk[zi, mid:length, :])
                g0[zi, cols, 0:768] = value[:, 0:768].astype(LOW)
                both = value[:, 768:896] + g0[zi, cols, 768:896].astype(F32)
                g0[zi, cols, 768:896] = both.astype(LOW)
        for zi in range(2):
            for o in range(2):
                far_send(0, zi, o).start()
        for zi in range(2):
            for o in range(2):
                plain_send(0, zi, o).start()

        for block in range(2):
            load(x_in.at[block], xt.at[block], 5 + block).start()
        for block in range(2):
            exchange(sb.at[block], rb.at[block], block).wait_send()
        for step in range(4):
            tile = (2 * (1 - core) + step) % 4
            rows = pl.ds(pl.multiple_of(tile * 256, 256), 256)
            value = dot_nt(dpk[0, rows, :], w0[0, :, 0:896])
            value = value + dot_nt(dpk[1, rows, :], w0[1, :, 0:896])
            if step < 2:
                sb[step] = value.astype(LOW)
                exchange(sb.at[step], rb.at[step], 6 + step).start()
            else:
                zb[step - 2] = value
        for block in range(2):
            give_back(block, 0, False)
            load(x_in.at[block], xt.at[block], 5 + block).wait()
            exchange(sb.at[block], rb.at[block], 6 + block).wait_recv()
            scale1 = 1.0 + mod[block, 1:2, :]

            def norm_first(step, sums_now):
                at_row = pl.ds(pl.multiple_of(step * 128, 128), 128)
                d_norm = zb[block, at_row, :] + rb[block, at_row, :].astype(F32)
                normed, spread = layer_norm(xt[block, at_row, :].astype(F32))
                d_input = yb[block, at_row, :] + norm_back(d_norm * scale1, normed, spread)
                ob[block, at_row, :] = d_input.astype(LOW)
                terms = (d_norm, d_norm * normed)
                return tuple(
                    now + jnp.sum(term, axis=0, keepdims=True) for now, term in zip(sums_now, terms)
                )

            zero = jnp.zeros((1, gb.shape[1]), F32)
            totals = lax.fori_loop(0, 2, norm_first, (zero,) * 2)
            for place, value in zip((0, 1), totals):
                sums[block, place : place + 1, :] = value
            give_back(block, 1, True)

        blocks = []
        for number in range(6):
            value = select[0][:, 0:1] * sums[0, number : number + 1, :]
            blocks.append(value + select[1][:, 0:1] * sums[1, number : number + 1, :])
        chunks = to_chunks(*blocks[0:3]) + to_chunks(*blocks[3:6])
        for number in range(4):
            dc[number] = chunks[number]

        def each_chunk(start):
            for number in range(4):
                here = jnp.logical_and(half == core, line == number)
                dst, send, recv = nr.at[lane, core], dcs.at[number], dcr.at[lane, core]
                if start:
                    move(dc.at[number], dst, send, recv, at.base + half, number, here)
                else:

                    @pl.when(jnp.logical_not(here))
                    def _():
                        remote(dc.at[number], dst, send, recv, at.base + half, number).wait_send()

        def each_row(start):
            for step in range(1, 8):
                other = (dp + step) % 8
                copy = remote(da.at[dp], da.at[dp], das.at[step], dar.at[dp], other, line)
                copy.start() if start else copy.wait_send()

        each_chunk(True)

        def drain(number, _):
            pump(number)
            return 0

        lax.fori_loop(12, 16, drain, 0)
        for zi in range(2):
            for o in range(2):
                pltpu.make_async_copy(dc.at[0], nr.at[zi, o], dcr.at[zi, o]).wait()
        da[dp] = (nr[0, 0] + nr[0, 1]) + (nr[1, 0] + nr[1, 1])
        each_row(True)
        for zi in range(2):
            for o in range(2):
                relay(0, zi, o)
        for zi in range(2):
            for o in range(2):
                settle(0, zi, o, True)
        for step in range(1, 8):
            other = (dp + step) % 8
            pltpu.make_async_copy(da.at[other], da.at[other], dar.at[other]).wait()
        value = jnp.concatenate([da[n] for n in range(8)], axis=0)
        g_bias[...] = jnp.sum(value, axis=0, keepdims=True)
        g_ada[...] = lax.dot_general(
            cond[...].astype(LOW).astype(F32), value, (((0,), (0,)), ((), ())), precision=HIGH, preferred_element_type=F32
        )
        for u in range(3):
            finish(u)

        each_chunk(False)
        each_row(False)
        for u in range(3):
            for zi in range(2):
                for o in range(2):
                    far_send(u, zi, o).wait_send()
                    plain_send(u, zi, o).wait_send()
                    relay_send(u, zi, o).wait_send()
                    settle(u, zi, o, False)
        for block in range(2):
            give_back(block, 1, False)
            exchange(sm.at[block], rm.at[block], 2 + block).wait_send()
            part = db.at[core, pl.ds(block * 256, 256)]
            exchange(part, part, 4 + block).wait_send()
            exchange(sb.at[block], rb.at[block], 6 + block).wait_send()
        for kind in range(2):
            dst = (out_tok, out_dtok)[kind]
            for slot in range(2):
                source = 2 * core + slot
                here = jnp.logical_and(source == line, half == core)

                @pl.when(jnp.logical_not(here))
                def _():
                    pltpu.make_async_copy(dst.at[slot], dst.at[slot], tr.at[kind, slot]).wait()

    pl.run_scoped(
        attention_phase,
        pltpu.VMEM((2, 8 * rows_u, cols), LOW),
        pltpu.VMEM((2, mid, cols), LOW),
        pltpu.VMEM((8, 3, length, 128), LOW),
        pltpu.VMEM((length, 128), F32),
        pltpu.VMEM((2, length, 896), LOW),
        pltpu.VMEM((8, length, 128), LOW),
        pltpu.VMEM((2, 8 * rows_u, cols), LOW),
        pltpu.VMEM((2, mid // 2, cols), F32),
        pltpu.VMEM((mid // 2, cols), LOW),
        pltpu.VMEM((2, mid // 2, cols), LOW),
        pltpu.VMEM((2, length, 128), F32),
    )


def run_back(*args):
    rows, part = args[-1].shape[1], args[6].shape[1]
    length, cols = args[0].shape[1:]
    chunk = 6 * cols // 4
    shape = jax.ShapeDtypeStruct
    vmem = pl.BlockSpec(memory_space=pltpu.VMEM)
    outs = (
        shape((2, part, cols), LOW),
        shape((2, part, cols), LOW),
        shape((3, 4, rows, cols), LOW),
        shape((2, 2, 8 * rows, cols), LOW),
        shape((rows, chunk), F32),
        shape((1, chunk), F32),
    )
    three = DMA((3, 2, 2))
    low = pltpu.VMEM((2, part, cols), LOW)
    return pl.pallas_call(
        back_kernel,
        out_shape=outs,
        in_specs=[ANY] * 15 + [vmem] * 5,
        out_specs=(ANY,) * 4 + (vmem,) * 2,
        scratch_shapes=[
            pltpu.VMEM((2, 8, cols), F32),
            pltpu.VMEM((2, 2 * part, cols), LOW),
            pltpu.VMEM((2, part, cols), F32),
            pltpu.VMEM((2, part, cols), F32),
            low,
            low,
            low,
            low,
            low,
            pltpu.VMEM((3, 2, 2, rows, cols), LOW),
            pltpu.VMEM((2, 3, 2, 2, rows, cols), LOW),
            pltpu.VMEM((2, rows, cols), LOW),
            pltpu.VMEM((4, 8, chunk), F32),
            pltpu.VMEM((2, 2, 8, chunk), F32),
            pltpu.VMEM((8, 8, chunk), F32),
            three,
            three,
            DMA((2, 3, 2, 2)),
            DMA((2, 3, 2, 2)),
            three,
            DMA((3, 4)),
            DMA((8,)),
            DMA((8,)),
            DMA((2, 2)),
            DMA((2, 2)),
            DMA((8,)),
            DMA((3,)),
            DMA((4,)),
            DMA((2, 2)),
            DMA((8,)),
            DMA((8,)),
        ],
        compiler_params=pltpu.CompilerParams(
            collective_id=1, has_side_effects=True, vmem_limit_bytes=63 << 20
        ),
    )(*args)


def fast_body(
    tokens,
    time_embed,
    segments,
    micro_order,
    head_mask,
    group_mask,
    keep_route,
    w_qkv,
    w_proj,
    w_fc1,
    w_fc2,
    w_ada,
    b_ada,
    cotangent,
):
    width = tokens.shape[2]
    length = segments.shape[1]
    qcols = w_qkv.shape[1]
    swap = micro_order[:, None] == 1

    lines = jnp.concatenate(
        [
            jnp.where(swap, head_mask[1:2], head_mask[0:1]),
            jnp.where(swap, group_mask[1:2], group_mask[0:1]),
            segments[:, :: length // 4],
            jnp.zeros((2, 116), jnp.int32),
        ],
        axis=1,
    )
    meta = jnp.concatenate(
        [keep_route.reshape(4, 128), lines, jnp.zeros((2, 128), jnp.int32)], axis=0
    ).astype(jnp.float32)
    te = time_embed.reshape(8, 8, width // 8).transpose(1, 0, 2).astype(jnp.float32)
    whead = jnp.concatenate([w_qkv, w_proj], axis=1)
    (
        full_fc2,
        full_fc1,
        head_w,
        dealt,
        dealt_grad,
        h_first,
        qkv,
        stat,
        att,
        first,
        branch,
        h_second,
        d_mlp,
        act,
        slope,
        cond,
        mod,
        gains,
        _,
        kept,
        select,
    ) = run_front(whead, w_fc1, w_fc2, tokens, cotangent, meta, te, w_ada, b_ada[None, :])
    result, d_input, grads, _, g_ada, g_bias = run_back(
        act,
        slope,
        d_mlp,
        h_second,
        full_fc1,
        full_fc2.reshape(full_fc1.shape),
        first,
        branch,
        dealt,
        dealt_grad,
        h_first,
        qkv,
        stat,
        att,
        head_w,
        mod,
        gains,
        kept,
        select,
        cond,
    )
    total = jnp.sum(grads.astype(jnp.float32), axis=1)
    return (
        result,
        d_input,
        total[0, :, :qcols],
        total[0, :, qcols:],
        total[1],
        total[2],
        g_ada,
        g_bias[0],
    )


def solution(mesh):
    placed = (
        P("dp", "tensor", None),
        P("dp", None, None),
        P("dp", None),
        P("dp"),
        P("dp", "tensor"),
        P("dp", "tensor"),
        P("dp", "tensor"),
        P("dp", "tensor"),
        P("dp", "tensor"),
        P("dp", "tensor"),
        P("dp", "tensor"),
        P("dp", "tensor"),
        P("tensor"),
        P("dp", "tensor", None),
    )
    return jax.shard_map(
        fast_body if mesh.shape["dp"] == 8 and mesh.shape["tensor"] == 4 else body,
        mesh=mesh,
        in_specs=placed,
        out_specs=(
            P("dp", "tensor", None),
            P("dp", "tensor", None),
            P("dp", "tensor"),
            P("dp", "tensor"),
            P("dp", "tensor"),
            P("dp", "tensor"),
            P("dp", "tensor"),
            P("tensor"),
        ),
        check_vma=False,
    )
```

```python
import jax
import jax.numpy as jnp
from jax import lax
from jax.experimental import pallas as pl
from jax.experimental.pallas import tpu as pltpu
from jax.sharding import PartitionSpec as P

HD = 72
FF = 4608
GROUPS = 16


EPSILON = 1e-06
HIGH = lax.Precision.HIGHEST


def layer_norm(values):
    middle = jnp.mean(values, axis=-1, keepdims=True)
    centred = values - middle
    spread = jnp.mean(centred * centred, axis=-1, keepdims=True)
    factor = lax.rsqrt(spread + EPSILON)
    return (centred * factor, factor)


def norm_back(grad, normed, factor):
    inner = (
        grad
        - jnp.mean(grad, axis=-1, keepdims=True)
        - normed * jnp.mean(grad * normed, axis=-1, keepdims=True)
    )
    return factor * inner


def contract_rows(left, right):
    return lax.dot_general(
        left, right, (((0,), (0,)), ((), ())), preferred_element_type=jnp.float32
    )


def contract_cols(left, right):
    return lax.dot_general(
        left, right, (((1,), (1,)), ((), ())), preferred_element_type=jnp.float32
    )


def score_block(query_block, keys, seg_block, seg_ids):
    scores = jnp.einsum(
        "qhe,khe->hqk", query_block, keys, preferred_element_type=jnp.float32
    ) * HD ** (-0.5)
    same = seg_block[:, None] == seg_ids[None, :]
    return jnp.where(same[None], scores, -1e30)


def attention_forward(query, keys, values, seg_ids):
    length = query.shape[0]
    block = min(512, length)
    outs = []
    totals = []
    for offset in range(0, length, block):
        scores = score_block(
            query[offset : offset + block], keys, seg_ids[offset : offset + block], seg_ids
        )
        peak = jnp.max(scores, axis=-1, keepdims=True)
        denom = jnp.sum(jnp.exp(scores - peak), axis=-1, keepdims=True)
        log_total = peak + jnp.log(denom)
        probs = jnp.exp(scores - log_total).astype(jnp.bfloat16)
        outs.append(jnp.einsum("hqk,khe->qhe", probs, values, preferred_element_type=jnp.float32))
        totals.append(log_total)
    return (jnp.concatenate(outs, axis=0), totals)


def attention_backward(query, keys, values, seg_ids, totals, d_attn):
    length = query.shape[0]
    block = min(512, length)
    scale = HD ** (-0.5)
    d_keys = jnp.zeros(keys.shape, jnp.float32)
    d_values = jnp.zeros(values.shape, jnp.float32)
    d_queries = []
    for number, offset in enumerate(range(0, length, block)):
        query_block = query[offset : offset + block]
        scores = score_block(query_block, keys, seg_ids[offset : offset + block], seg_ids)
        probs = jnp.exp(scores - totals[number])
        grad_block = d_attn[offset : offset + block]
        d_values = d_values + jnp.einsum(
            "hqk,qhe->khe",
            probs.astype(jnp.bfloat16),
            grad_block,
            preferred_element_type=jnp.float32,
        )
        d_probs = jnp.einsum("qhe,khe->hqk", grad_block, values, preferred_element_type=jnp.float32)
        d_scores = (probs * (d_probs - jnp.sum(probs * d_probs, axis=-1, keepdims=True))).astype(
            jnp.bfloat16
        )
        d_queries.append(
            jnp.einsum("hqk,khe->qhe", d_scores, keys, preferred_element_type=jnp.float32) * scale
        )
        d_keys = (
            d_keys
            + jnp.einsum("hqk,qhe->khe", d_scores, query_block, preferred_element_type=jnp.float32)
            * scale
        )
    stacked = jnp.stack([jnp.concatenate(d_queries, axis=0), d_keys, d_values], axis=2)
    return stacked.astype(jnp.bfloat16).reshape(length, -1)


def body(
    tokens,
    time_embed,
    segments,
    micro_order,
    head_mask,
    group_mask,
    keep_route,
    w_qkv,
    w_proj,
    w_fc1,
    w_fc2,
    w_ada,
    b_ada,
    cotangent,
):
    micro = tokens.shape[0]
    local_rows = tokens.shape[1]
    length = segments.shape[1]
    heads_here = head_mask.shape[1]
    segs = time_embed.shape[1]
    tensor_index = lax.axis_index("tensor")
    chooser = (micro_order[:, None] == jnp.arange(micro, dtype=jnp.int32)[None, :]).astype(
        jnp.float32
    )
    head_sel = jnp.dot(chooser, head_mask.astype(jnp.float32), precision=HIGH)
    group_sel = jnp.repeat(
        jnp.dot(chooser, group_mask.astype(jnp.float32), precision=HIGH), FF // GROUPS, axis=1
    )
    keep_float = keep_route.astype(jnp.float32)

    def reduce_grads(grad_qkv, grad_proj, grad_fc1, grad_fc2, grad_ada):
        return (
            lax.psum_scatter(
                grad_qkv.astype(jnp.bfloat16), "dp", scatter_dimension=0, tiled=True
            ).astype(jnp.float32),
            lax.psum_scatter(
                grad_proj.astype(jnp.bfloat16), "dp", scatter_dimension=0, tiled=True
            ).astype(jnp.float32),
            lax.psum_scatter(
                grad_fc1.astype(jnp.bfloat16), "dp", scatter_dimension=0, tiled=True
            ).astype(jnp.float32),
            lax.psum_scatter(
                grad_fc2.astype(jnp.bfloat16), "dp", scatter_dimension=0, tiled=True
            ).astype(jnp.float32),
            lax.psum_scatter(
                grad_ada.astype(jnp.bfloat16), "dp", scatter_dimension=0, tiled=True
            ).astype(jnp.float32),
        )

    shard_shapes = [w.shape for w in (w_qkv, w_proj, w_fc1, w_fc2, w_ada)]
    start_acc = tuple((jnp.zeros(shape, jnp.float32) for shape in shard_shapes))

    def slot_step(carry, items):
        acc, bias_acc = carry
        slot_tokens, slot_grad, seg_ids, embed, hmask, gcols, keepf = items
        full = (
            lax.all_gather(w_qkv, "dp", axis=0, tiled=True),
            lax.all_gather(w_proj, "dp", axis=0, tiled=True),
            lax.all_gather(w_fc1, "dp", axis=0, tiled=True),
            lax.all_gather(w_fc2, "dp", axis=0, tiled=True),
            lax.all_gather(w_ada, "dp", axis=0, tiled=True),
        )
        full_qkv, full_proj, full_fc1, full_fc2, full_ada = full
        seg_local = lax.dynamic_slice_in_dim(seg_ids, tensor_index * local_rows, local_rows)
        scond = jax.nn.silu(embed.astype(jnp.float32)).astype(jnp.bfloat16)
        part_mods = jnp.dot(scond, full_ada, preferred_element_type=jnp.float32) + b_ada[None, :]
        mods = lax.all_gather(part_mods, "tensor", axis=1, tiled=True)
        onehot = (seg_local[:, None] == jnp.arange(segs, dtype=jnp.int32)[None, :]).astype(
            jnp.float32
        )
        modtok = jnp.dot(onehot, mods, precision=HIGH)
        shift1, scale1, gate1, shift2, scale2, gate2 = jnp.split(modtok, 6, axis=1)
        token_vals = slot_tokens.astype(jnp.float32)
        normed1, factor1 = layer_norm(token_vals)
        h_first = lax.all_gather(
            (normed1 * (1.0 + scale1) + shift1).astype(jnp.bfloat16), "tensor", axis=0, tiled=True
        )
        packed = jnp.dot(h_first, full_qkv, preferred_element_type=jnp.float32).astype(jnp.bfloat16)
        packed = packed.reshape(length, heads_here, 3, HD)
        query = packed[:, :, 0]
        keys = packed[:, :, 1]
        values = packed[:, :, 2]
        outs, totals = attention_forward(query, keys, values, seg_ids)
        attn = (outs * hmask[None, :, None]).astype(jnp.bfloat16).reshape(length, heads_here * HD)
        branch = lax.psum_scatter(
            contract_cols(attn, full_proj).astype(jnp.bfloat16),
            "tensor",
            scatter_dimension=0,
            tiled=True,
        ).astype(jnp.float32)
        first = token_vals + gate1 * branch
        normed2, factor2 = layer_norm(first)
        h_second = lax.all_gather(
            (normed2 * (1.0 + scale2) + shift2).astype(jnp.bfloat16), "tensor", axis=0, tiled=True
        )
        upward = jnp.dot(h_second, full_fc1, preferred_element_type=jnp.float32)
        gelu_val, gelu_pull = jax.vjp(lambda inner: jax.nn.gelu(inner, approximate=True), upward)
        act = (gelu_val * gcols[None, :]).astype(jnp.bfloat16)
        mlp = lax.psum_scatter(
            contract_cols(act, full_fc2).astype(jnp.bfloat16),
            "tensor",
            scatter_dimension=0,
            tiled=True,
        ).astype(jnp.float32)
        keep_col = keepf[:, None]
        result = (first + gate2 * keep_col * mlp).astype(jnp.bfloat16)
        grad_out = slot_grad.astype(jnp.float32)
        d_mlp = lax.all_gather(
            (gate2 * keep_col * grad_out).astype(jnp.bfloat16), "tensor", axis=0, tiled=True
        )
        grad_fc2 = contract_rows(d_mlp, act)
        d_act = jnp.dot(d_mlp, full_fc2, preferred_element_type=jnp.float32)
        d_up = gelu_pull(d_act * gcols[None, :])[0].astype(jnp.bfloat16)
        grad_fc1 = contract_rows(h_second, d_up)
        d_second = lax.psum_scatter(
            contract_cols(d_up, full_fc1).astype(jnp.bfloat16),
            "tensor",
            scatter_dimension=0,
            tiled=True,
        ).astype(jnp.float32)
        d_first = grad_out + norm_back(d_second * (1.0 + scale2), normed2, factor2)
        d_branch = lax.all_gather(
            (gate1 * d_first).astype(jnp.bfloat16), "tensor", axis=0, tiled=True
        )
        grad_proj = contract_rows(d_branch, attn)
        d_attn = jnp.dot(d_branch, full_proj, preferred_element_type=jnp.float32).astype(
            jnp.bfloat16
        )
        d_attn = d_attn.reshape(length, heads_here, HD) * hmask[None, :, None].astype(jnp.bfloat16)
        d_packed = attention_backward(query, keys, values, seg_ids, totals, d_attn)
        grad_qkv = contract_rows(h_first, d_packed)
        d_h_first = lax.psum_scatter(
            contract_cols(d_packed, full_qkv).astype(jnp.bfloat16),
            "tensor",
            scatter_dimension=0,
            tiled=True,
        ).astype(jnp.float32)
        d_input = d_first + norm_back(d_h_first * (1.0 + scale1), normed1, factor1)
        d_modtok = jnp.concatenate(
            [
                d_h_first,
                d_h_first * normed1,
                d_first * branch,
                d_second,
                d_second * normed2,
                grad_out * keep_col * mlp,
            ],
            axis=1,
        )
        part_dmods = lax.dot_general(onehot, d_modtok, (((0,), (0,)), ((), ())), precision=HIGH)
        d_mods = lax.psum_scatter(
            part_dmods.astype(jnp.bfloat16), "tensor", scatter_dimension=1, tiled=True
        ).astype(jnp.float32)
        grad_ada = jnp.dot(scond.astype(jnp.float32).T, d_mods, precision=HIGH)
        bias_acc = bias_acc + jnp.sum(d_mods, axis=0)
        parts = reduce_grads(grad_qkv, grad_proj, grad_fc1, grad_fc2, grad_ada)
        acc = tuple((held + piece for held, piece in zip(acc, parts)))
        return ((acc, bias_acc), (result, d_input.astype(jnp.bfloat16)))

    start_bias = jnp.zeros(b_ada.shape, jnp.float32)
    (acc, bias_acc), (results, d_tokens) = lax.scan(
        slot_step,
        (start_acc, start_bias),
        (tokens, cotangent, segments, time_embed, head_sel, group_sel, keep_float),
    )
    g_bias = lax.psum(bias_acc, "dp")
    return (results, d_tokens, acc[0], acc[1], acc[2], acc[3], acc[4], g_bias)


MESH = pl.DeviceIdType.MESH
ANY = pl.BlockSpec(memory_space=pl.ANY)
DMA = pltpu.SemaphoreType.DMA


class Place:
    def __init__(self):
        self.dp = lax.axis_index("dp")
        self.line = lax.axis_index("tensor")
        self.core = self.dp % 2
        self.base = self.dp - self.core
        self.half = self.line // 2
        x, y = (self.dp // 2) % 2, self.dp // 4
        self.dp_x = self.dp + 2 * (1 - 2 * x)
        self.dp_y = self.dp + 4 * (1 - 2 * y)
        self.base_x = self.dp_x - self.core
        self.base_y = self.dp_y - self.core
        self.base_far = self.base_x + self.base_y - self.base

    def barrier(self):
        bar = pltpu.get_barrier_semaphore()
        spot = self.core * 4 + self.line
        for step in range(1, 8):
            other = (spot + step) % 8
            pl.semaphore_signal(
                bar,
                inc=1,
                device_id=(self.base + other // 4, other % 4),
                device_id_type=MESH,
            )
        for step in range(1, 8):
            other = (self.dp + step) % 8
            pl.semaphore_signal(bar, inc=1, device_id=(other, self.line), device_id_type=MESH)
        pl.semaphore_wait(bar, 14)


def remote(src, dst, send, recv, dp, line):
    return pltpu.make_async_remote_copy(
        src_ref=src,
        dst_ref=dst,
        send_sem=send,
        recv_sem=recv,
        device_id=(dp, line),
        device_id_type=MESH,
    )


def move(src, dst, send, recv, dp, line, here):
    @pl.when(here)
    def _():
        pltpu.make_async_copy(src, dst, recv).start()

    @pl.when(jnp.logical_not(here))
    def _():
        remote(src, dst, send, recv, dp, line).start()


LOG2E = 1.4426950408889634
LOW = jnp.bfloat16
F32 = jnp.float32
SHADE = -1e30


def dot_nn(left, right):
    return jnp.dot(left, right, preferred_element_type=F32)


def dot_nt(left, right):
    return lax.dot_general(left, right, (((1,), (1,)), ((), ())), preferred_element_type=F32)


def dot_tn(left, right):
    return lax.dot_general(left, right, (((0,), (0,)), ((), ())), preferred_element_type=F32)


def lanes(rows):
    return lax.broadcasted_iota(jnp.int32, (rows, 128), 1)


def window(value, start):
    tile, rest = start // 128, start % 128
    here = value[:, 128 * tile : 128 * tile + 128]
    if rest == 0:
        return here
    here = pltpu.roll(here, 128 - rest, 1)
    if rest + HD <= 128:
        return here
    after = pltpu.roll(value[:, 128 * tile + 128 : 128 * tile + 256], 128 - rest, 1)
    return jnp.where(lanes(value.shape[0]) < 128 - rest, here, after)


def pack(parts, start, tiles):
    rows = parts[0].shape[0]
    lane = lanes(rows)
    out = []
    for tile in range(tiles):
        total = jnp.zeros((rows, 128), F32)
        for number, part in enumerate(parts):
            low = start + HD * number - 128 * tile
            if low >= 128 or low + HD <= 0:
                continue
            moved = pltpu.roll(part, low % 128, 1) if low % 128 else part
            inside = jnp.logical_and(lane >= low, lane < low + HD)
            total = jnp.where(inside, moved, total)
        out.append(total)
    return out


def turned(value, tile):
    start = 128 * tile
    stop = min(start + 128, value.shape[1])
    part = value[:, start:stop]
    if stop - start < 128:
        part = jnp.concatenate([part, jnp.zeros((part.shape[0], 64), F32)], axis=1)
    return pltpu.roll(part, 64, 1)


def to_blocks(even, odd):
    low = lanes(even.shape[0]) < 64
    turn = [turned(odd, tile) for tile in range(14)]
    tail = jnp.concatenate([even[:, 1664:1728], jnp.zeros((even.shape[0], 64), F32)], axis=1)
    one = [even[:, 0:1152]]
    two = [even[:, 1152:1664], jnp.where(low, tail, turn[0])]
    two += [jnp.where(low, turn[t], turn[t + 1]) for t in range(4)]
    three = [jnp.where(low, turn[t], turn[t + 1]) for t in range(4, 13)]
    return [jnp.concatenate(parts, axis=1) for parts in (one, two, three)]


def to_chunks(one, two, three):
    low = lanes(one.shape[0]) < 64
    even = jnp.concatenate([one, two[:, 0:576]], axis=1)
    turn = [turned(two, tile) for tile in range(4, 9)] + [turned(three, t) for t in range(9)]
    odd = [jnp.where(low, turn[t], turn[t + 1]) for t in range(13)]
    return even, jnp.concatenate(odd + [turn[13][:, 0:64]], axis=1)


def front_kernel(
    wh,
    w1,
    w2,
    tok,
    cot,
    meta,
    te,
    wa,
    ba,
    weights,
    w1_out,
    head_out,
    x_out,
    g_out,
    h1_out,
    qkv_out,
    pt_out,
    att_out,
    x1_out,
    br_out,
    h2_out,
    dm_out,
    act_out,
    gp_out,
    gf_out,
    cond,
    mod,
    gains,
    groups,
    kept,
    select,
    xt,
    w0,
    h1,
    qkv,
    obuf,
    pt,
    gst,
    att,
    sb,
    rb,
    br,
    x1,
    h2,
    ct,
    dm,
    w1v,
    act,
    gp,
    gc,
    mt,
    te_all,
    pb,
    pr,
    mine,
    mr,
    feat,
    zs,
    zr,
    fs,
    ns,
    nr,
    ds,
    dr,
    ts,
    tr,
    es,
    er,
    ls,
    ps,
    gs,
    ms,
    mrs,
    tes,
    ter,
    pbs,
    pbr,
    mms,
    mmr,
):
    at = Place()
    dp, line, core, half = at.dp, at.line, at.core, at.half
    units = (wh, w1, w2)
    lane = line % 2
    rows_u = w1.shape[0]
    sib = at.base + 1 - core
    at.barrier()

    def spot(u, zi, row):
        if u < 2:
            return (w0, w1v)[u].at[zi, pl.ds(pl.multiple_of(row * rows_u, 16), rows_u)]
        return weights.at[zi, row]

    def deal(kind, start):
        src, dst = ((tok, xt), (cot, ct))[kind]
        for slot in range(2):
            there = 2 * core + slot
            here = jnp.logical_and(half == core, there == line)
            send, recv = ts.at[kind, slot], tr.at[kind, lane]
            if start:
                move(src.at[slot], dst.at[lane], send, recv, at.base + half, there, here)
            else:

                @pl.when(jnp.logical_not(here))
                def _():
                    remote(
                        src.at[slot], dst.at[lane], send, recv, at.base + half, there
                    ).wait_send()

    def deal_arrive(kind):
        src, dst = ((tok, xt), (cot, ct))[kind]
        for block in range(2):
            pltpu.make_async_copy(src.at[0], dst.at[block], tr.at[kind, block]).wait()

    def source(u, start):
        dst = spot(u, lane, dp)
        recv = zr.at[u, lane, core]
        home = at.base + half
        if start:
            move(units[u], dst, zs.at[u, 0], recv, home, line, half == core)
        else:

            @pl.when(half != core)
            def _():
                remote(units[u], dst, zs.at[u, 0], recv, home, line).wait_send()

        for which, step in ((1, 1), (2, -1)):
            inside = line < 3 if step == 1 else line > 0

            @pl.when(inside)
            def _():
                copy = remote(units[u], dst, zs.at[u, which], recv, home, line + step)
                copy.start() if start else copy.wait_send()

    first = jnp.where(core == 0, jnp.where(line == 0, 0, 1), jnp.where(line == 3, 1, 0))

    def z_stage(u, k, other, start):
        zi = first + k - 2 * first * k
        origin = 2 * core + zi
        ref = spot(u, zi, at.base + other)
        if start:
            pltpu.make_async_copy(w1, ref, zr.at[u, zi, other]).wait()
        up = jnp.logical_and(origin < line, line < 3)
        down = jnp.logical_and(origin > line, line > 0)
        for go, step in ((up, 1), (down, -1)):

            @pl.when(go)
            def _():
                copy = remote(
                    ref, ref, fs.at[u, zi, other], zr.at[u, zi, other], dp, line + step
                )
                copy.start() if start else copy.wait_send()

        for which, near in ((0, at.dp_x), (1, at.dp_y)):
            copy = remote(
                ref, ref, ns.at[which, u, zi, other], nr.at[which, u, zi, other], near, line
            )
            copy.start() if start else copy.wait_send()

    def far_stage(u, zi, other, start):
        base = at.base_x + other * (at.base_y - at.base_x)
        near = at.dp_y + other * (at.dp_x - at.dp_y)
        ref = spot(u, zi, base + other)
        if start:
            pltpu.make_async_copy(w1, ref, nr.at[other, u, zi, other]).wait()
        copy = remote(ref, ref, ds.at[u, zi, other], dr.at[u, zi, other], near, line)
        copy.start() if start else copy.wait_send()

    def last_stage(u, zi, other):
        base = at.base_y + other * (at.base_x - at.base_y)
        ref = spot(u, zi, base + other)
        pltpu.make_async_copy(w1, ref, nr.at[1 - other, u, zi, other]).wait()
        ref = spot(u, zi, at.base_far + other)
        pltpu.make_async_copy(w1, ref, dr.at[u, zi, other]).wait()

    def pump(number):
        k, other = (number % 4) // 2, number % 2
        for quarter in range(4):
            u, stage = 1 + quarter // 2, (z_stage, far_stage)[quarter % 2]

            @pl.when(number // 4 == quarter)
            def _():
                stage(u, k, other, True)

    def keep(src, dst, number):
        return pltpu.make_async_copy(src, dst, ls.at[number])

    def each_column(start):
        for step in range(1, 8):
            other = (core * 4 + line + step) % 8
            copy = remote(
                meta, mt.at[core * 4 + line], ms.at[step], mrs.at[core * 4 + line],
                at.base + other // 4, other % 4,
            )
            copy.start() if start else copy.wait_send()

    def each_row(src, dst, send, recv, start, pieces):
        for step in range(1, 8):
            other = (dp + step) % 8
            part = src.at[other] if pieces else src
            copy = remote(part, dst.at[dp], send.at[step], recv.at[dp], other, line)
            copy.start() if start else copy.wait_send()

    def row_arrive(dst, recv):
        for step in range(1, 8):
            other = (dp + step) % 8
            pltpu.make_async_copy(dst.at[other], dst.at[other], recv.at[other]).wait()

    each_row(te, te_all, tes, ter, True, True)
    each_column(True)
    te_all[dp] = te[dp]
    mt[core * 4 + line] = meta[...]

    deal(0, True)
    source(0, True)
    row_arrive(te_all, ter)
    for number in range(8):
        spread = te_all[number]
        cond[8 * number : 8 * number + 8, :] = spread * (1.0 / (1.0 + jnp.exp(-spread)))
    value = dot_nn(cond[...].astype(LOW), wa[...])
    for number in range(8):
        pb[number] = value[8 * number : 8 * number + 8, :]
    each_row(pb, pr, pbs, pbr, True, True)
    pr[dp] = pb[dp]
    for other in range(2):
        z_stage(0, 0, other, True)
    row_arrive(pr, pbr)
    total = ba[...] + pr[0]
    for number in range(1, 8):
        total = total + pr[number]
    mine[...] = total

    def each_slot(start):
        for slot in range(2):
            there = 2 * core + slot
            for to in range(2):
                here = jnp.logical_and(core == to, there == line)
                send, recv = mms.at[slot, to], mmr.at[line]
                if start:
                    move(mine, mr.at[line], send, recv, at.base + to, there, here)
                else:

                    @pl.when(jnp.logical_not(here))
                    def _():
                        remote(mine, mr.at[line], send, recv, at.base + to, there).wait_send()

    each_slot(True)
    for other in range(2):
        z_stage(0, 1, other, True)
    source(1, True)
    deal(1, True)

    for step in range(1, 8):
        other = (core * 4 + line + step) % 8
        pltpu.make_async_copy(meta, mt.at[other], mrs.at[other]).wait()
    one_row = lanes(1)
    spots = (one_row - HD).astype(F32)
    inside = jnp.logical_and(one_row >= HD, one_row < HD + 4)

    def lane_of(row, place):
        return jnp.sum(jnp.where(one_row == place, row, 0.0), axis=1, keepdims=True)

    for zi in range(2):
        info = mt[half * 4 + 2 * core + zi, pl.ds(4 + lane, 1), :]
        for number in range(4):
            head = zi * 4 + number
            gains[head : head + 1, :] = jnp.broadcast_to(lane_of(info, number), (1, 128))
            groups[head : head + 1, :] = jnp.broadcast_to(lane_of(info, 4 + number), (1, 128))
    unit = lax.broadcasted_iota(jnp.int32, (1, gc.shape[1]), 1) // (gc.shape[1] // 4)
    for zi in range(2):
        row = jnp.zeros((1, gc.shape[1]), F32)
        for number in range(4):
            head = zi * 4 + number
            row = jnp.where(unit == number, groups[head : head + 1, 0:1], row)
        gc[8 * zi : 8 * zi + 8, :] = jnp.broadcast_to(row, (8, gc.shape[1]))
    info = mt[half * 4 + line, pl.ds(4 + lane, 1), :]
    for tile in range(4):
        same = jnp.where(spots == lane_of(info, 8 + tile), 1.0, 0.0)
        feat[0, tile : tile + 1, :] = jnp.where(inside, SHADE * (1.0 - same), 0.0)
        feat[1, tile : tile + 1, :] = jnp.where(inside, same, 0.0)
    row_ids = lax.broadcasted_iota(jnp.int32, (8, 128), 0)
    diagonal = lax.broadcasted_iota(jnp.int32, (128, 128), 0) == lanes(128)
    for block in range(2):
        item = jnp.sum(
            jnp.where(one_row == 8 + 2 * core + block, info, 0.0), axis=1, keepdims=True
        )
        hit = row_ids.astype(F32) == item + (4 * lane).astype(F32)
        select[block] = jnp.where(hit, 1.0, 0.0)
        for number in range(2):
            row = mt[half * 4 + 2 * core + block, pl.ds(2 * lane + number, 1), :]
            column = jnp.sum(jnp.where(diagonal, row, 0.0), axis=1, keepdims=True)
            kept[block, 128 * number : 128 * number + 128, :] = jnp.broadcast_to(column, (128, 128))
    for source_line in range(4):
        pltpu.make_async_copy(mine, mr.at[source_line], mmr.at[source_line]).wait()
    for block in range(2):
        weight = select[block][:, 0:1]
        rows = [jnp.sum(weight * mr[n], axis=0, keepdims=True) for n in range(4)]
        pieces = to_blocks(rows[0], rows[1]) + to_blocks(rows[2], rows[3])
        for number, piece in enumerate(pieces):
            mod[block, number : number + 1, :] = piece
        mod[block, 6:8, :] = jnp.zeros((2, mod.shape[2]), F32)

    def exchange(src, dst, number):
        return remote(src, dst, es.at[number], er.at[number], sib, line)

    deal_arrive(0)
    keep(xt, x_out, 0).start()

    for block in range(2):
        shift, scale = mod[block, 0:1, :], 1.0 + mod[block, 1:2, :]

        def norm_first(step, _):
            at_row = pl.ds(pl.multiple_of(step * 128, 128), 128)
            normed, _f = layer_norm(xt[block, at_row, :].astype(F32))
            to_row = pl.ds(pl.multiple_of(block * 256 + step * 128, 128), 128)
            h1[core, to_row, :] = (normed * scale + shift).astype(LOW)
            return 0

        lax.fori_loop(0, 2, norm_first, 0)
        part = h1.at[core, pl.ds(block * 256, 256)]
        exchange(part, part, block).start()
    for zi in range(2):
        for other in range(2):
            far_stage(0, zi, other, True)
    source(2, True)
    for zi in range(2):
        for other in range(2):
            last_stage(0, zi, other)
    keep(w0, head_out, 1).start()

    def project(step, _):
        @pl.when(step >= 2)
        def _():
            part = h1.at[1 - core, pl.ds(pl.multiple_of((step - 2) * 256, 256), 256)]
            pltpu.make_async_copy(part, part, er.at[step - 2]).wait()

        pump(step)
        tile = (2 * core + step) % 4
        rows = h1[tile // 2, pl.ds(pl.multiple_of((tile % 2) * 256, 256), 256), :]
        to_row = pl.ds(pl.multiple_of(tile * 256, 256), 256)
        narrow = lanes(256) < HD
        fills = (feat[0, pl.ds(tile, 1), :], feat[1, pl.ds(tile, 1), :], jnp.zeros((1, 128), F32))
        for zi in range(2):
            value = dot_nn(rows, w0[zi, :, 0:896])
            for number in range(12):
                head, part = zi * 4 + number // 3, number % 3
                piece = jnp.where(narrow, window(value, HD * number), fills[part])
                qkv[head, part, to_row, :] = piece.astype(LOW)
        return 0

    lax.fori_loop(0, 4, project, 0)
    keep(h1, h1_out, 2).start()
    keep(qkv, qkv_out, 3).start()

    factor = HD ** (-0.5) * LOG2E

    def attend(head, _):
        pump(4 + head)
        gain = gains[pl.ds(head, 1), :]

        def tile_step(tile, _):
            rows = pl.ds(pl.multiple_of(tile * 256, 256), 256)
            number = 4 * head + tile
            slot = number % 2
            scores = dot_nt(qkv[head, 1], qkv[head, 0, rows, :])
            peak = jnp.max(scores, axis=0, keepdims=True)
            power = jnp.exp2((scores - peak) * factor)
            total = jnp.sum(power, axis=0, keepdims=True)
            probs = (power * (1.0 / total)).astype(LOW)
            obuf[head, rows, :] = (dot_tn(probs, qkv[head, 2]) * gain).astype(LOW)

            @pl.when(number >= 2)
            def _():
                pltpu.make_async_copy(pt.at[slot], pt_out.at[number - 2], ps.at[slot]).wait()

            pt[slot] = probs
            pltpu.make_async_copy(pt.at[slot], pt_out.at[number], ps.at[slot]).start()
            return 0

        lax.fori_loop(0, 4, tile_step, 0)
        return 0

    lax.fori_loop(0, 8, attend, 0)

    def lay(step, _):
        rows = pl.ds(pl.multiple_of(step * 128, 128), 128)
        for zi in range(2):
            parts = [obuf[zi * 4 + n, rows, :].astype(F32) for n in range(4)]
            for tile, value in enumerate(pack(parts, 96, 3)):
                att[zi, rows, 128 * tile : 128 * tile + 128] = value.astype(LOW)
        return 0

    lax.fori_loop(0, 8, lay, 0)
    keep(att, att_out, 5).start()

    for step in range(4):
        tile = (2 * (1 - core) + step) % 4
        rows = pl.ds(pl.multiple_of(tile * 256, 256), 256)
        value = dot_nt(att[0, rows, :], w0[0, :, 768:1152])
        value = value + dot_nt(att[1, rows, :], w0[1, :, 768:1152])
        if step < 2:
            sb[step] = value.astype(LOW)
            exchange(sb.at[step], rb.at[step], 2 + step).start()
        else:
            br[step - 2] = value
    for block in range(2):
        exchange(sb.at[block], rb.at[block], 2 + block).wait_recv()
        gate = mod[block, 2:3, :]
        shift, scale = mod[block, 3:4, :], 1.0 + mod[block, 4:5, :]

        def norm_second(step, _):
            at_row = pl.ds(pl.multiple_of(step * 128, 128), 128)
            branch = br[block, at_row, :] + rb[block, at_row, :].astype(F32)
            br[block, at_row, :] = branch
            value = xt[block, at_row, :].astype(F32) + gate * branch
            x1[block, at_row, :] = value
            normed, _f = layer_norm(value)
            to_row = pl.ds(pl.multiple_of(block * 256 + step * 128, 128), 128)
            h2[core, to_row, :] = (normed * scale + shift).astype(LOW)
            return 0

        lax.fori_loop(0, 2, norm_second, 0)
        part = h2.at[core, pl.ds(block * 256, 256)]
        exchange(part, part, 4 + block).start()
    keep(x1, x1_out, 6).start()
    keep(br, br_out, 7).start()

    deal_arrive(1)
    keep(ct, g_out, 9).start()
    for block in range(2):
        gate2 = mod[block, 5:6, :]

        def grad_rows(step, _):
            at_row = pl.ds(pl.multiple_of(step * 128, 128), 128)
            value = gate2 * kept[block, at_row, 0:1] * ct[block, at_row, :].astype(F32)
            to_row = pl.ds(pl.multiple_of(block * 256 + step * 128, 128), 128)
            dm[core, to_row, :] = value.astype(LOW)
            return 0

        lax.fori_loop(0, 2, grad_rows, 0)
        part = dm.at[core, pl.ds(block * 256, 256)]
        exchange(part, part, 6 + block).start()

    for block in range(2):
        part = h2.at[1 - core, pl.ds(block * 256, 256)]
        pltpu.make_async_copy(part, part, er.at[4 + block]).wait()
    keep(h2, h2_out, 8).start()
    for block in range(2):
        part = dm.at[1 - core, pl.ds(block * 256, 256)]
        pltpu.make_async_copy(part, part, er.at[6 + block]).wait()
    keep(dm, dm_out, 10).start()

    for zi in range(2):
        for other in range(2):
            last_stage(1, zi, other)
    keep(w1v, w1_out, 11).start()
    ratio = (2.0 / 3.141592653589793) ** 0.5

    def widen(step, _):
        tile, zi = (2 * core + step // 2) % 4, step % 2
        rows = h2[tile // 2, pl.ds(pl.multiple_of((tile % 2) * 256, 256), 256), :]
        value = dot_nn(rows, w1v[zi])
        mask = gc[pl.ds(pl.multiple_of(8 * zi, 8), 8), :][0:1, :]
        square = value * value
        bend = jnp.tanh(ratio * (value + 0.044715 * (value * square)))
        grown = 0.5 * (1.0 + bend)
        slope = grown + 0.5 * value * (1.0 - bend * bend) * (
            ratio * (1.0 + (3.0 * 0.044715) * square)
        )
        to_row = pl.ds(pl.multiple_of(tile * 256, 256), 256)
        act[zi, to_row, :] = (value * grown * mask).astype(LOW)
        gp[zi, to_row, :] = (slope * mask).astype(LOW)

        @pl.when(step % 2 == 1)
        def _():
            pump(12 + step // 2)

        return 0

    lax.fori_loop(0, 8, widen, 0)
    keep(act, act_out, 12).start()
    keep(gp, gp_out, 13).start()

    def grad_piece(number):
        rows = pl.ds(384 * (number % 3), 384)
        if not isinstance(number, int):
            rows = pl.ds(pl.multiple_of(384 * (number % 3), 128), 384)
        return gf_out.at[number // 3, rows]

    def fc2_grad(number, _):
        zi, slot = number // 3, number % 3
        some = pl.ds(pl.multiple_of(384 * slot, 128), 384)
        value = dot_tn(dm[0, :, some], act[zi, 0:512, :])
        value = value + dot_tn(dm[1, :, some], act[zi, 512:1024, :])

        @pl.when(number >= 3)
        def _():
            pltpu.make_async_copy(gst.at[slot], grad_piece(number - 3), gs.at[slot]).wait()

        gst[slot] = value.astype(LOW)
        pltpu.make_async_copy(gst.at[slot], grad_piece(number), gs.at[slot]).start()
        return 0

    lax.fori_loop(0, 6, fc2_grad, 0)

    for u in range(3):
        source(u, False)
        for k in range(2):
            for other in range(2):
                z_stage(u, k, other, False)
                far_stage(u, k, other, False)
                if u == 2:
                    last_stage(u, k, other)
    for kind in range(2):
        deal(kind, False)
    each_column(False)
    each_row(te, te_all, tes, ter, False, True)
    each_row(pb, pr, pbs, pbr, False, True)
    each_slot(False)
    for block in range(2):
        own1 = h1.at[core, pl.ds(block * 256, 256)]
        own2 = h2.at[core, pl.ds(block * 256, 256)]
        exchange(own1, own1, block).wait_send()
        exchange(sb.at[block], rb.at[block], 2 + block).wait_send()
        exchange(own2, own2, 4 + block).wait_send()
        own3 = dm.at[core, pl.ds(block * 256, 256)]
        exchange(own3, own3, 6 + block).wait_send()
    pairs = (
        (xt, x_out),
        (w0, head_out),
        (h1, h1_out),
        (qkv, qkv_out),
        (None, None),
        (att, att_out),
        (x1, x1_out),
        (br, br_out),
        (h2, h2_out),
        (ct, g_out),
        (dm, dm_out),
        (w1v, w1_out),
        (act, act_out),
        (gp, gp_out),
    )
    for number, (src, dst) in enumerate(pairs):
        if number != 4:
            keep(src, dst, number).wait()
    for slot in range(2):
        pltpu.make_async_copy(pt.at[slot], pt_out.at[30 + slot], ps.at[slot]).wait()
    for slot in range(3):
        pltpu.make_async_copy(gst.at[slot], grad_piece(3 + slot), gs.at[slot]).wait()


def run_front(wh, w1, w2, tok, cot, meta, te, wa, ba):
    rows, cols = w1.shape
    part = tok.shape[1]
    length = 4 * part
    shape = jax.ShapeDtypeStruct
    vmem = pl.BlockSpec(memory_space=pltpu.VMEM)
    shared = shape((2, 2 * part, cols), LOW)
    single = shape((2, part, cols), F32)
    outs = (
        shape((2, 8, rows, cols), LOW),
        shape((2, 8 * rows, cols), LOW),
        shape((2, 8 * rows, cols), LOW),
        shape(tok.shape, LOW),
        shape(tok.shape, LOW),
        shared,
        shape((8, 3, length, 128), LOW),
        shape((32, length, part), LOW),
        shape((2, length, 384), LOW),
        single,
        single,
        shared,
        shared,
        shape((2, length, cols), LOW),
        shape((2, length, cols), LOW),
        shape((2, 8 * rows, cols), LOW),
    )
    small = (
        shape((64, rows), F32),
        shape((2, 8, cols), F32),
        shape((8, 128), F32),
        shape((8, 128), F32),
        shape((2, part, 128), F32),
        shape((2, 8, 128), F32),
    )
    three = DMA((3, 2, 2))
    return pl.pallas_call(
        front_kernel,
        out_shape=outs + small,
        in_specs=[ANY] * 5 + [vmem] * 4,
        out_specs=(ANY,) * len(outs) + (vmem,) * len(small),
        scratch_shapes=[
            pltpu.VMEM(tok.shape, LOW),
            pltpu.VMEM((2, 8 * rows, cols), LOW),
            pltpu.VMEM((2, 2 * part, cols), LOW),
            pltpu.VMEM((8, 3, length, 128), LOW),
            pltpu.VMEM((8, length, 128), LOW),
            pltpu.VMEM((2, length, part), LOW),
            pltpu.VMEM((3, 384, cols), LOW),
            pltpu.VMEM((2, length, 384), LOW),
            pltpu.VMEM((2, part, cols), LOW),
            pltpu.VMEM((2, part, cols), LOW),
            pltpu.VMEM((2, part, cols), F32),
            pltpu.VMEM((2, part, cols), F32),
            pltpu.VMEM((2, 2 * part, cols), LOW),
            pltpu.VMEM(tok.shape, LOW),
            pltpu.VMEM((2, 2 * part, cols), LOW),
            pltpu.VMEM((2, 8 * rows, cols), LOW),
            pltpu.VMEM((2, length, cols), LOW),
            pltpu.VMEM((2, length, cols), LOW),
            pltpu.VMEM((16, cols), F32),
            pltpu.VMEM((8, 8, 128), F32),
            pltpu.VMEM((8, 8, rows), F32),
            pltpu.VMEM((8, 8, wa.shape[1]), F32),
            pltpu.VMEM((8, 8, wa.shape[1]), F32),
            pltpu.VMEM((8, wa.shape[1]), F32),
            pltpu.VMEM((4, 8, wa.shape[1]), F32),
            pltpu.VMEM((2, 8, 128), F32),
            DMA((3, 3)),
            three,
            three,
            DMA((2, 3, 2, 2)),
            DMA((2, 3, 2, 2)),
            three,
            three,
            DMA((2, 2)),
            DMA((2, 2)),
            DMA((8,)),
            DMA((8,)),
            DMA((14,)),
            DMA((2,)),
            DMA((3,)),
            DMA((8,)),
            DMA((8,)),
            DMA((8,)),
            DMA((8,)),
            DMA((8,)),
            DMA((8,)),
            DMA((2, 2)),
            DMA((4,)),
        ],
        compiler_params=pltpu.CompilerParams(
            collective_id=0, has_side_effects=True, vmem_limit_bytes=60 << 20
        ),
    )(wh, w1, w2, tok, cot, meta, te, wa, ba)


def back_kernel(
    act_in,
    gp_in,
    dm_in,
    h2_in,
    w1_in,
    w2_in,
    gf_in,
    x1_in,
    br_in,
    x_in,
    g_in,
    h1_in,
    qkv_in,
    pt_in,
    att_in,
    head_in,
    mod,
    gains,
    keep_col,
    select,
    cond,
    out_tok,
    out_dtok,
    rz,
    gf1,
    g_ada,
    g_bias,
    sums,
    db,
    yb,
    zb,
    sb,
    sm,
    rb,
    rm,
    ob,
    r1,
    rn,
    stage,
    dc,
    nr,
    da,
    s1s,
    s1r,
    nss,
    nsr,
    zss,
    zsr,
    es,
    er,
    ts,
    tr,
    ls,
    gs,
    ps,
    dcs,
    dcr,
    das,
    dar,
):
    at = Place()
    dp, line, core, half = at.dp, at.line, at.core, at.half
    lane = line % 2
    rows_u = stage.shape[1]
    local = {}
    sib = at.base + 1 - core
    scale_q = HD ** (-0.5)
    factor = HD ** (-0.5) * LOG2E

    def load(src, dst, number):
        return pltpu.make_async_copy(src, dst, ls.at[number])

    def exchange(src, dst, number):
        return remote(src, dst, es.at[number], er.at[number], sib, line)

    def grad_ref(u, zi, row):
        here = pl.ds(pl.multiple_of(row * rows_u, 16), rows_u)
        return (local.get("g0"), gf1, gf_in)[u].at[zi, here]

    def base_of(which):
        return at.base_x + which * (at.base_y - at.base_x)

    def near_of(which):
        return at.dp_x + which * (at.dp_y - at.dp_x)

    def far_send(u, zi, o):
        return remote(
            grad_ref(u, zi, at.base_far + o),
            r1.at[u, zi, o],
            s1s.at[u, zi, o],
            s1r.at[u, zi, o],
            near_of(o),
            line,
        )

    def plain_send(u, zi, o):
        return remote(
            grad_ref(u, zi, base_of(o) + o),
            rn.at[o, u, zi, o],
            nss.at[o, u, zi, o],
            nsr.at[o, u, zi, o],
            near_of(o),
            line,
        )

    def relay_send(u, zi, o):
        return remote(
            r1.at[u, zi, o],
            rn.at[1 - o, u, zi, o],
            nss.at[1 - o, u, zi, o],
            nsr.at[1 - o, u, zi, o],
            near_of(1 - o),
            line,
        )

    def fetch(u, zi, o, which):
        row = (base_of(1 - o), at.base)[which] + o
        slot = 2 * which + o
        return pltpu.make_async_copy(grad_ref(u, zi, row), stage.at[slot], gs.at[slot])

    def own_term(u, zi, o, which):
        if u == 0:
            return grad_ref(u, zi, (base_of(1 - o), at.base)[which] + o)
        return stage.at[2 * which + o]

    def relay(u, zi, o):
        far_send(u, zi, o).wait_recv()
        if u:
            fetch(u, zi, o, 0).wait()
        ref = own_term(u, zi, o, 0)
        r1[u, zi, o] = (r1[u, zi, o].astype(F32) + ref[...].astype(F32)).astype(LOW)
        relay_send(u, zi, o).start()

    def settle(u, zi, o, start):
        here = jnp.logical_and(core == o, line == 2 * core + zi)
        src, dst = rn.at[0, u, zi, o], rz.at[u, line]
        send, recv = zss.at[u, zi, o], zsr.at[u, line]
        if not start:

            @pl.when(jnp.logical_not(here))
            def _():
                remote(src, dst, send, recv, at.base + o, 2 * core + zi).wait_send()

            return
        for which in range(2):
            there = rn.at[which, u, zi, o]
            pltpu.make_async_copy(there, there, nsr.at[which, u, zi, o]).wait()
        if u:
            fetch(u, zi, o, 1).wait()
        ref = own_term(u, zi, o, 1)
        total = rn[0, u, zi, o].astype(F32) + rn[1, u, zi, o].astype(F32)
        rn[0, u, zi, o] = (total + ref[...].astype(F32)).astype(LOW)
        move(src, dst, send, recv, at.base + o, 2 * core + zi, here)

    def finish(u):
        for source in range(4):
            ref = rz.at[u, source]
            pltpu.make_async_copy(ref, ref, zsr.at[u, source]).wait()

    def fetch_pair(u, zi, which):
        for o in range(2):
            fetch(u, zi, o, which).start()

    def relay_pair(u, zi):
        for o in range(2):
            relay(u, zi, o)

    def settle_pair(u, zi):
        for o in range(2):
            settle(u, zi, o, True)

    def give_back(block, kind, start):
        dst = (out_tok, out_dtok)[kind].at[lane]
        there = 2 * core + block
        here = jnp.logical_and(half == core, there == line)
        send, recv = ts.at[kind, block], tr.at[kind, lane]
        if start:
            move(ob.at[block], dst, send, recv, at.base + half, there, here)
        else:

            @pl.when(here)
            def _():
                pltpu.make_async_copy(ob.at[block], dst, recv).wait()

            @pl.when(jnp.logical_not(here))
            def _():
                remote(ob.at[block], dst, send, recv, at.base + half, there).wait_send()

    def mlp_phase(act, gp, w1v, w2v, dm, h2, gst):
        pairs = ((dm_in, dm), (w2_in, w2v), (gp_in, gp), (h2_in, h2), (w1_in, w1v), (act_in, act))
        copies = [load(src, dst, number) for number, (src, dst) in enumerate(pairs)]
        for copy in copies:
            copy.start()
        at.barrier()
        for zi in range(2):
            for o in range(2):
                far_send(2, zi, o).start()
            for o in range(2):
                plain_send(2, zi, o).start()
        length = act.shape[1]
        mid = length // 2

        def weight_grad(u, left, right):
            def column_half(zi, _):
                def piece(tile, _):
                    cols = pl.ds(pl.multiple_of(384 * tile, 128), 384)
                    value = dot_tn(left[0, :, cols], right[zi, 0:mid, :])
                    value = value + dot_tn(left[1, :, cols], right[zi, mid:length, :])
                    gst[tile] = value.astype(LOW)
                    rows = pl.ds(pl.multiple_of(384 * tile, 128), 384)
                    pltpu.make_async_copy(gst.at[tile], gf1.at[zi, rows], gs.at[tile]).start()
                    return 0

                lax.fori_loop(0, 3, piece, 0)
                for tile in range(3):
                    rows = pl.ds(384 * tile, 384)
                    pltpu.make_async_copy(gst.at[tile], gf1.at[zi, rows], gs.at[tile]).wait()
                for o in range(2):
                    far_send(u, zi, o).start()
                for o in range(2):
                    plain_send(u, zi, o).start()
                return 0

            lax.fori_loop(0, 2, column_half, 0)

        for copy in copies[0:3]:
            copy.wait()

        def down(step, _):
            tile, zi = step // 2, step % 2
            rows = dm[tile // 2, pl.ds(pl.multiple_of((tile % 2) * 256, 256), 256), :]
            to_row = pl.ds(pl.multiple_of(tile * 256, 256), 256)
            value = dot_nn(rows, w2v[zi]) * gp[zi, to_row, :].astype(F32)
            gp[zi, to_row, :] = value.astype(LOW)
            return 0

        lax.fori_loop(0, 8, down, 0)
        def partial(left, right, send, recv, own, number):
            def part(step, _):
                tile = (2 * (1 - core) + step) % 4
                rows = pl.ds(pl.multiple_of(tile * 256, 256), 256)
                value = dot_nt(left[0, rows, :], right[0])
                value = value + dot_nt(left[1, rows, :], right[1])

                @pl.when(step < 2)
                def _():
                    send[step] = value.astype(LOW)
                    exchange(send.at[step], recv.at[step], number + step).start()

                @pl.when(step >= 2)
                def _():
                    own[step - 2] = value

                return 0

            lax.fori_loop(0, 4, part, 0)

        for copy in copies[3:6]:
            copy.wait()
        partial(gp, w1v, sb, rb, yb, 0)
        weight_grad(1, h2, gp)
        fetch_pair(2, 0, 0)
        partial(act, w2v, sm, rm, zb, 2)
        relay_pair(2, 0)
        fetch_pair(2, 1, 0)

    cols = gf1.shape[2]
    length = act_in.shape[1]
    mid = length // 2
    pl.run_scoped(
        mlp_phase,
        pltpu.VMEM((2, length, cols), LOW),
        pltpu.VMEM((2, length, cols), LOW),
        pltpu.VMEM((2, 8 * rows_u, cols), LOW),
        pltpu.VMEM((2, 8 * rows_u, cols), LOW),
        pltpu.VMEM((2, mid, cols), LOW),
        pltpu.VMEM((2, mid, cols), LOW),
        pltpu.VMEM((3, 384, cols), LOW),
    )
    def attention_phase(w0, h1, qkv, pt, dpk, do, g0, xb, gb, acc):
        local["g0"] = g0
        pairs = (
            (head_in, w0),
            (qkv_in, qkv),
            (att_in, dpk.at[:, :, 0:384]),
            (h1_in, h1),
        )
        early = [load(src, dst, number) for number, (src, dst) in enumerate(pairs)]
        for copy in early:
            copy.start()

        def probs_in(number):
            slot = number % 2
            return pltpu.make_async_copy(pt_in.at[number], pt.at[slot], ps.at[slot])

        probs_in(0).start()

        for block in range(2):
            copies = (
                load(x1_in.at[block], xb.at[0], 5),
                load(br_in.at[block], xb.at[1], 6),
                load(g_in.at[block], gb, 7),
            )
            for copy in copies:
                copy.start()
            for copy in copies:
                copy.wait()
            exchange(sb.at[block], rb.at[block], block).wait_recv()
            exchange(sm.at[block], rm.at[block], 2 + block).wait_recv()
            gate1, scale2 = mod[block, 2:3, :], 1.0 + mod[block, 4:5, :]
            gate2 = mod[block, 5:6, :]

            def norm_second(step, sums_now):
                at_row = pl.ds(pl.multiple_of(step * 128, 128), 128)
                grad = gb[at_row, :].astype(F32)
                first = xb[0, at_row, :]
                d_second = yb[block, at_row, :] + rb[block, at_row, :].astype(F32)
                kept = keep_col[block, at_row, 0:1] * (
                    zb[block, at_row, :] + rm[block, at_row, :].astype(F32)
                )
                ob[block, at_row, :] = (first + gate2 * kept).astype(LOW)
                normed, spread = layer_norm(first)
                d_first = grad + norm_back(d_second * scale2, normed, spread)
                yb[block, at_row, :] = d_first
                to_row = pl.ds(pl.multiple_of(block * 256 + step * 128, 128), 128)
                db[core, to_row, :] = (gate1 * d_first).astype(LOW)
                terms = (d_first * xb[1, at_row, :], d_second, d_second * normed, grad * kept)
                return tuple(
                    now + jnp.sum(term, axis=0, keepdims=True) for now, term in zip(sums_now, terms)
                )

            zero = jnp.zeros((1, gb.shape[1]), F32)
            totals = lax.fori_loop(0, 2, norm_second, (zero,) * 4)
            for place, value in zip((2, 3, 4, 5), totals):
                sums[block, place : place + 1, :] = value
            part = db.at[core, pl.ds(block * 256, 256)]
            exchange(part, part, 4 + block).start()
            give_back(block, 0, True)

        for copy in early[0:3]:
            copy.wait()

        relay_pair(2, 1)
        fetch_pair(1, 0, 0)
        fetch_pair(2, 0, 1)

        def to_heads(step, _):
            @pl.when(step >= 2)
            def _():
                part = db.at[1 - core, pl.ds(pl.multiple_of((step - 2) * 256, 256), 256)]
                pltpu.make_async_copy(part, part, er.at[4 + step - 2]).wait()

            tile = (2 * core + step) % 4
            rows = db[tile // 2, pl.ds(pl.multiple_of((tile % 2) * 256, 256), 256), :]
            to_row = pl.ds(pl.multiple_of(tile * 256, 256), 256)
            narrow = lanes(256) < HD
            for zi in range(2):
                value = dot_nn(rows, w0[zi, :, 768:1152])
                for number in range(4):
                    piece = jnp.where(narrow, window(value, 96 + HD * number), 0.0)
                    head = zi * 4 + number
                    do[head, to_row, :] = (piece * gains[head : head + 1, :]).astype(LOW)
            return 0

        lax.fori_loop(0, 4, to_heads, 0)
        def proj_grad(number, _):
            zi, tile = number // 3, number % 3
            some = pl.ds(pl.multiple_of(384 * tile, 128), 384)
            value = dot_tn(db[0, :, some], dpk[zi, 0:mid, 0:384])
            value = value + dot_tn(db[1, :, some], dpk[zi, mid:length, 0:384])
            g0[zi, some, 768:1152] = value.astype(LOW)
            return 0

        lax.fori_loop(0, 6, proj_grad, 0)

        def attend(head, _):
            step_of = (
                lambda: (relay_pair(1, 0), fetch_pair(1, 1, 0)),
                lambda: relay_pair(1, 1),
                lambda: (settle_pair(2, 0), fetch_pair(2, 1, 1)),
                lambda: (settle_pair(2, 1), fetch_pair(1, 0, 1)),
                lambda: None,
                lambda: (settle_pair(1, 0), fetch_pair(1, 1, 1)),
                lambda: None,
                lambda: settle_pair(1, 1),
            )
            for place, task in enumerate(step_of):

                @pl.when(head == place)
                def _():
                    task()

            acc[...] = jnp.zeros_like(acc)

            def tile_step(tile, _):
                number = 4 * head + tile
                rows = pl.ds(pl.multiple_of(tile * 256, 256), 256)

                @pl.when(number < 31)
                def _():
                    probs_in(number + 1).start()

                probs_in(number).wait()
                grad = do[head, rows, :]
                probs = pt[number % 2]
                acc[1] += dot_nn(probs, grad)
                d_probs = dot_nt(qkv[head, 2], grad)
                wide = probs.astype(F32)
                inner = jnp.sum(wide * d_probs, axis=0, keepdims=True)
                d_scores = (wide * (d_probs - inner)).astype(LOW)
                acc[0] += dot_nn(d_scores, qkv[head, 0, rows, :])
                qkv[head, 0, rows, :] = (dot_tn(d_scores, qkv[head, 1]) * scale_q).astype(LOW)
                return 0

            lax.fori_loop(0, 4, tile_step, 0)
            qkv[head, 1] = (acc[0] * scale_q).astype(LOW)
            qkv[head, 2] = acc[1].astype(LOW)
            return 0

        early[3].wait()

        def column_half(zi, _):
            def one_head(number, _):
                return attend(4 * zi + number, 0)

            lax.fori_loop(0, 4, one_head, 0)

            def lay(step, _):
                rows = pl.ds(pl.multiple_of(step * 128, 128), 128)
                narrow = lanes(128) < HD
                parts = [
                    jnp.where(narrow, qkv[zi * 4 + n // 3, n % 3, rows, :].astype(F32), 0.0)
                    for n in range(12)
                ]
                for tile, value in enumerate(pack(parts, 0, 7)):
                    dpk[zi, rows, 128 * tile : 128 * tile + 128] = value.astype(LOW)
                return 0

            lax.fori_loop(0, 8, lay, 0)

            def head_grad(tile, _):
                some = pl.ds(pl.multiple_of(384 * tile, 128), 384)
                value = dot_tn(h1[0, :, some], dpk[zi, 0:mid, :])
                value = value + dot_tn(h1[1, :, some], dpk[zi, mid:length, :])
                g0[zi, some, 0:768] = value[:, 0:768].astype(LOW)
                both = value[:, 768:896] + g0[zi, some, 768:896].astype(F32)
                g0[zi, some, 768:896] = both.astype(LOW)
                return 0

            lax.fori_loop(0, 3, head_grad, 0)
            for o in range(2):
                far_send(0, zi, o).start()
            for o in range(2):
                plain_send(0, zi, o).start()
            return 0

        lax.fori_loop(0, 2, column_half, 0)

        for block in range(2):
            load(x_in.at[block], rm.at[block], 5 + block).start()
        for block in range(2):
            exchange(sb.at[block], rb.at[block], block).wait_send()
        for step in range(4):
            tile = (2 * (1 - core) + step) % 4
            rows = pl.ds(pl.multiple_of(tile * 256, 256), 256)
            value = dot_nt(dpk[0, rows, :], w0[0, :, 0:896])
            value = value + dot_nt(dpk[1, rows, :], w0[1, :, 0:896])
            if step < 2:
                sb[step] = value.astype(LOW)
                exchange(sb.at[step], rb.at[step], 6 + step).start()
            else:
                zb[step - 2] = value
            if step == 1:
                relay_pair(0, 0)
        relay_pair(0, 1)
        settle_pair(0, 0)
        for block in range(2):
            give_back(block, 0, False)
            load(x_in.at[block], rm.at[block], 5 + block).wait()
            exchange(sb.at[block], rb.at[block], 6 + block).wait_recv()
            scale1 = 1.0 + mod[block, 1:2, :]

            def norm_first(step, sums_now):
                at_row = pl.ds(pl.multiple_of(step * 128, 128), 128)
                d_norm = zb[block, at_row, :] + rb[block, at_row, :].astype(F32)
                normed, spread = layer_norm(rm[block, at_row, :].astype(F32))
                d_input = yb[block, at_row, :] + norm_back(d_norm * scale1, normed, spread)
                ob[block, at_row, :] = d_input.astype(LOW)
                terms = (d_norm, d_norm * normed)
                return tuple(
                    now + jnp.sum(term, axis=0, keepdims=True) for now, term in zip(sums_now, terms)
                )

            zero = jnp.zeros((1, gb.shape[1]), F32)
            totals = lax.fori_loop(0, 2, norm_first, (zero,) * 2)
            for place, value in zip((0, 1), totals):
                sums[block, place : place + 1, :] = value
            give_back(block, 1, True)

        blocks = []
        for number in range(6):
            value = select[0][:, 0:1] * sums[0, number : number + 1, :]
            blocks.append(value + select[1][:, 0:1] * sums[1, number : number + 1, :])
        chunks = to_chunks(*blocks[0:3]) + to_chunks(*blocks[3:6])
        for number in range(4):
            dc[number] = chunks[number]

        def each_chunk(start):
            for number in range(4):
                here = jnp.logical_and(half == core, line == number)
                dst, send, recv = nr.at[lane, core], dcs.at[number], dcr.at[lane, core]
                if start:
                    move(dc.at[number], dst, send, recv, at.base + half, number, here)
                else:

                    @pl.when(jnp.logical_not(here))
                    def _():
                        remote(dc.at[number], dst, send, recv, at.base + half, number).wait_send()

        def each_row(start):
            for step in range(1, 8):
                other = (dp + step) % 8
                copy = remote(da.at[dp], da.at[dp], das.at[step], dar.at[dp], other, line)
                copy.start() if start else copy.wait_send()

        each_chunk(True)

        for o in range(2):
            settle(0, 1, o, True)
        for zi in range(2):
            for o in range(2):
                pltpu.make_async_copy(dc.at[0], nr.at[zi, o], dcr.at[zi, o]).wait()
        da[dp] = (nr[0, 0] + nr[0, 1]) + (nr[1, 0] + nr[1, 1])
        each_row(True)
        for step in range(1, 8):
            other = (dp + step) % 8
            pltpu.make_async_copy(da.at[other], da.at[other], dar.at[other]).wait()
        value = jnp.concatenate([da[n] for n in range(8)], axis=0)
        g_bias[...] = jnp.sum(value, axis=0, keepdims=True)
        g_ada[...] = lax.dot_general(
            cond[...].astype(LOW).astype(F32), value, (((0,), (0,)), ((), ())), precision=HIGH, preferred_element_type=F32
        )
        for u in range(3):
            finish(u)

        each_chunk(False)
        each_row(False)
        for u in range(3):
            for zi in range(2):
                for o in range(2):
                    far_send(u, zi, o).wait_send()
                    plain_send(u, zi, o).wait_send()
                    relay_send(u, zi, o).wait_send()
                    settle(u, zi, o, False)
        for block in range(2):
            give_back(block, 1, False)
            exchange(sm.at[block], rm.at[block], 2 + block).wait_send()
            part = db.at[core, pl.ds(block * 256, 256)]
            exchange(part, part, 4 + block).wait_send()
            exchange(sb.at[block], rb.at[block], 6 + block).wait_send()
        for kind in range(2):
            dst = (out_tok, out_dtok)[kind]
            for slot in range(2):
                source = 2 * core + slot
                here = jnp.logical_and(source == line, half == core)

                @pl.when(jnp.logical_not(here))
                def _():
                    pltpu.make_async_copy(dst.at[slot], dst.at[slot], tr.at[kind, slot]).wait()

    pl.run_scoped(
        attention_phase,
        pltpu.VMEM((2, 8 * rows_u, cols), LOW),
        pltpu.VMEM((2, mid, cols), LOW),
        pltpu.VMEM((8, 3, length, 128), LOW),
        pltpu.VMEM((2, length, mid // 2), LOW),
        pltpu.VMEM((2, length, 896), LOW),
        pltpu.VMEM((8, length, 128), LOW),
        pltpu.VMEM((2, 8 * rows_u, cols), LOW),
        pltpu.VMEM((2, mid // 2, cols), F32),
        pltpu.VMEM((mid // 2, cols), LOW),
        pltpu.VMEM((2, length, 128), F32),
    )


def run_back(*args):
    rows, part = args[-1].shape[1], args[7].shape[1]
    length, cols = args[0].shape[1:]
    chunk = 6 * cols // 4
    shape = jax.ShapeDtypeStruct
    vmem = pl.BlockSpec(memory_space=pltpu.VMEM)
    outs = (
        shape((2, part, cols), LOW),
        shape((2, part, cols), LOW),
        shape((3, 4, rows, cols), LOW),
        shape((2, 8 * rows, cols), LOW),
        shape((rows, chunk), F32),
        shape((1, chunk), F32),
    )
    three = DMA((3, 2, 2))
    low = pltpu.VMEM((2, part, cols), LOW)
    return pl.pallas_call(
        back_kernel,
        out_shape=outs,
        in_specs=[ANY] * 16 + [vmem] * 5,
        out_specs=(ANY,) * 4 + (vmem,) * 2,
        scratch_shapes=[
            pltpu.VMEM((2, 8, cols), F32),
            pltpu.VMEM((2, 2 * part, cols), LOW),
            pltpu.VMEM((2, part, cols), F32),
            pltpu.VMEM((2, part, cols), F32),
            low,
            low,
            low,
            low,
            low,
            pltpu.VMEM((3, 2, 2, rows, cols), LOW),
            pltpu.VMEM((2, 3, 2, 2, rows, cols), LOW),
            pltpu.VMEM((4, rows, cols), LOW),
            pltpu.VMEM((4, 8, chunk), F32),
            pltpu.VMEM((2, 2, 8, chunk), F32),
            pltpu.VMEM((8, 8, chunk), F32),
            three,
            three,
            DMA((2, 3, 2, 2)),
            DMA((2, 3, 2, 2)),
            three,
            DMA((3, 4)),
            DMA((8,)),
            DMA((8,)),
            DMA((2, 2)),
            DMA((2, 2)),
            DMA((8,)),
            DMA((4,)),
            DMA((2,)),
            DMA((4,)),
            DMA((2, 2)),
            DMA((8,)),
            DMA((8,)),
        ],
        compiler_params=pltpu.CompilerParams(
            collective_id=1, has_side_effects=True, vmem_limit_bytes=63 << 20
        ),
    )(*args)


def fast_body(
    tokens,
    time_embed,
    segments,
    micro_order,
    head_mask,
    group_mask,
    keep_route,
    w_qkv,
    w_proj,
    w_fc1,
    w_fc2,
    w_ada,
    b_ada,
    cotangent,
):
    width = tokens.shape[2]
    length = segments.shape[1]
    qcols = w_qkv.shape[1]
    swap = micro_order[:, None] == 1

    lines = jnp.concatenate(
        [
            jnp.where(swap, head_mask[1:2], head_mask[0:1]),
            jnp.where(swap, group_mask[1:2], group_mask[0:1]),
            segments[:, :: length // 4],
            jnp.zeros((2, 116), jnp.int32),
        ],
        axis=1,
    )
    meta = jnp.concatenate(
        [keep_route.reshape(4, 128), lines, jnp.zeros((2, 128), jnp.int32)], axis=0
    ).astype(jnp.float32)
    te = time_embed.reshape(8, 8, width // 8).transpose(1, 0, 2).astype(jnp.float32)
    whead = jnp.concatenate([w_qkv, w_proj], axis=1)
    (
        full_fc2,
        full_fc1,
        head_w,
        dealt,
        dealt_grad,
        h_first,
        qkv,
        probs,
        att,
        first,
        branch,
        h_second,
        d_mlp,
        act,
        slope,
        grad_fc2,
        cond,
        mod,
        gains,
        _,
        kept,
        select,
    ) = run_front(whead, w_fc1, w_fc2, tokens, cotangent, meta, te, w_ada, b_ada[None, :])
    result, d_input, grads, _, g_ada, g_bias = run_back(
        act,
        slope,
        d_mlp,
        h_second,
        full_fc1,
        full_fc2.reshape(full_fc1.shape),
        grad_fc2,
        first,
        branch,
        dealt,
        dealt_grad,
        h_first,
        qkv,
        probs,
        att,
        head_w,
        mod,
        gains,
        kept,
        select,
        cond,
    )
    total = jnp.sum(grads.astype(jnp.float32), axis=1)
    return (
        result,
        d_input,
        total[0, :, :qcols],
        total[0, :, qcols:],
        total[1],
        total[2],
        g_ada,
        g_bias[0],
    )


def solution(mesh):
    placed = (
        P("dp", "tensor", None),
        P("dp", None, None),
        P("dp", None),
        P("dp"),
        P("dp", "tensor"),
        P("dp", "tensor"),
        P("dp", "tensor"),
        P("dp", "tensor"),
        P("dp", "tensor"),
        P("dp", "tensor"),
        P("dp", "tensor"),
        P("dp", "tensor"),
        P("tensor"),
        P("dp", "tensor", None),
    )
    return jax.shard_map(
        fast_body if mesh.shape["dp"] == 8 and mesh.shape["tensor"] == 4 else body,
        mesh=mesh,
        in_specs=placed,
        out_specs=(
            P("dp", "tensor", None),
            P("dp", "tensor", None),
            P("dp", "tensor"),
            P("dp", "tensor"),
            P("dp", "tensor"),
            P("dp", "tensor"),
            P("dp", "tensor"),
            P("tensor"),
        ),
        check_vma=False,
    )
```

```python
import jax
import jax.numpy as jnp
from jax import lax
from jax.experimental import pallas as pl
from jax.experimental.pallas import tpu as pltpu
from jax.sharding import PartitionSpec as P

HD = 72
FF = 4608
GROUPS = 16


EPSILON = 1e-06
HIGH = lax.Precision.HIGHEST


def layer_norm(values):
    middle = jnp.mean(values, axis=-1, keepdims=True)
    centred = values - middle
    spread = jnp.mean(centred * centred, axis=-1, keepdims=True)
    factor = lax.rsqrt(spread + EPSILON)
    return (centred * factor, factor)


def norm_back(grad, normed, factor):
    inner = (
        grad
        - jnp.mean(grad, axis=-1, keepdims=True)
        - normed * jnp.mean(grad * normed, axis=-1, keepdims=True)
    )
    return factor * inner


def contract_rows(left, right):
    return lax.dot_general(
        left, right, (((0,), (0,)), ((), ())), preferred_element_type=jnp.float32
    )


def contract_cols(left, right):
    return lax.dot_general(
        left, right, (((1,), (1,)), ((), ())), preferred_element_type=jnp.float32
    )


def score_block(query_block, keys, seg_block, seg_ids):
    scores = jnp.einsum(
        "qhe,khe->hqk", query_block, keys, preferred_element_type=jnp.float32
    ) * HD ** (-0.5)
    same = seg_block[:, None] == seg_ids[None, :]
    return jnp.where(same[None], scores, -1e30)


def attention_forward(query, keys, values, seg_ids):
    length = query.shape[0]
    block = min(512, length)
    outs = []
    totals = []
    for offset in range(0, length, block):
        scores = score_block(
            query[offset : offset + block], keys, seg_ids[offset : offset + block], seg_ids
        )
        peak = jnp.max(scores, axis=-1, keepdims=True)
        denom = jnp.sum(jnp.exp(scores - peak), axis=-1, keepdims=True)
        log_total = peak + jnp.log(denom)
        probs = jnp.exp(scores - log_total).astype(jnp.bfloat16)
        outs.append(jnp.einsum("hqk,khe->qhe", probs, values, preferred_element_type=jnp.float32))
        totals.append(log_total)
    return (jnp.concatenate(outs, axis=0), totals)


def attention_backward(query, keys, values, seg_ids, totals, d_attn):
    length = query.shape[0]
    block = min(512, length)
    scale = HD ** (-0.5)
    d_keys = jnp.zeros(keys.shape, jnp.float32)
    d_values = jnp.zeros(values.shape, jnp.float32)
    d_queries = []
    for number, offset in enumerate(range(0, length, block)):
        query_block = query[offset : offset + block]
        scores = score_block(query_block, keys, seg_ids[offset : offset + block], seg_ids)
        probs = jnp.exp(scores - totals[number])
        grad_block = d_attn[offset : offset + block]
        d_values = d_values + jnp.einsum(
            "hqk,qhe->khe",
            probs.astype(jnp.bfloat16),
            grad_block,
            preferred_element_type=jnp.float32,
        )
        d_probs = jnp.einsum("qhe,khe->hqk", grad_block, values, preferred_element_type=jnp.float32)
        d_scores = (probs * (d_probs - jnp.sum(probs * d_probs, axis=-1, keepdims=True))).astype(
            jnp.bfloat16
        )
        d_queries.append(
            jnp.einsum("hqk,khe->qhe", d_scores, keys, preferred_element_type=jnp.float32) * scale
        )
        d_keys = (
            d_keys
            + jnp.einsum("hqk,qhe->khe", d_scores, query_block, preferred_element_type=jnp.float32)
            * scale
        )
    stacked = jnp.stack([jnp.concatenate(d_queries, axis=0), d_keys, d_values], axis=2)
    return stacked.astype(jnp.bfloat16).reshape(length, -1)


def body(
    tokens,
    time_embed,
    segments,
    micro_order,
    head_mask,
    group_mask,
    keep_route,
    w_qkv,
    w_proj,
    w_fc1,
    w_fc2,
    w_ada,
    b_ada,
    cotangent,
):
    micro = tokens.shape[0]
    local_rows = tokens.shape[1]
    length = segments.shape[1]
    heads_here = head_mask.shape[1]
    segs = time_embed.shape[1]
    tensor_index = lax.axis_index("tensor")
    chooser = (micro_order[:, None] == jnp.arange(micro, dtype=jnp.int32)[None, :]).astype(
        jnp.float32
    )
    head_sel = jnp.dot(chooser, head_mask.astype(jnp.float32), precision=HIGH)
    group_sel = jnp.repeat(
        jnp.dot(chooser, group_mask.astype(jnp.float32), precision=HIGH), FF // GROUPS, axis=1
    )
    keep_float = keep_route.astype(jnp.float32)

    def reduce_grads(grad_qkv, grad_proj, grad_fc1, grad_fc2, grad_ada):
        return (
            lax.psum_scatter(
                grad_qkv.astype(jnp.bfloat16), "dp", scatter_dimension=0, tiled=True
            ).astype(jnp.float32),
            lax.psum_scatter(
                grad_proj.astype(jnp.bfloat16), "dp", scatter_dimension=0, tiled=True
            ).astype(jnp.float32),
            lax.psum_scatter(
                grad_fc1.astype(jnp.bfloat16), "dp", scatter_dimension=0, tiled=True
            ).astype(jnp.float32),
            lax.psum_scatter(
                grad_fc2.astype(jnp.bfloat16), "dp", scatter_dimension=0, tiled=True
            ).astype(jnp.float32),
            lax.psum_scatter(
                grad_ada.astype(jnp.bfloat16), "dp", scatter_dimension=0, tiled=True
            ).astype(jnp.float32),
        )

    shard_shapes = [w.shape for w in (w_qkv, w_proj, w_fc1, w_fc2, w_ada)]
    start_acc = tuple((jnp.zeros(shape, jnp.float32) for shape in shard_shapes))

    def slot_step(carry, items):
        acc, bias_acc = carry
        slot_tokens, slot_grad, seg_ids, embed, hmask, gcols, keepf = items
        full = (
            lax.all_gather(w_qkv, "dp", axis=0, tiled=True),
            lax.all_gather(w_proj, "dp", axis=0, tiled=True),
            lax.all_gather(w_fc1, "dp", axis=0, tiled=True),
            lax.all_gather(w_fc2, "dp", axis=0, tiled=True),
            lax.all_gather(w_ada, "dp", axis=0, tiled=True),
        )
        full_qkv, full_proj, full_fc1, full_fc2, full_ada = full
        seg_local = lax.dynamic_slice_in_dim(seg_ids, tensor_index * local_rows, local_rows)
        scond = jax.nn.silu(embed.astype(jnp.float32)).astype(jnp.bfloat16)
        part_mods = jnp.dot(scond, full_ada, preferred_element_type=jnp.float32) + b_ada[None, :]
        mods = lax.all_gather(part_mods, "tensor", axis=1, tiled=True)
        onehot = (seg_local[:, None] == jnp.arange(segs, dtype=jnp.int32)[None, :]).astype(
            jnp.float32
        )
        modtok = jnp.dot(onehot, mods, precision=HIGH)
        shift1, scale1, gate1, shift2, scale2, gate2 = jnp.split(modtok, 6, axis=1)
        token_vals = slot_tokens.astype(jnp.float32)
        normed1, factor1 = layer_norm(token_vals)
        h_first = lax.all_gather(
            (normed1 * (1.0 + scale1) + shift1).astype(jnp.bfloat16), "tensor", axis=0, tiled=True
        )
        packed = jnp.dot(h_first, full_qkv, preferred_element_type=jnp.float32).astype(jnp.bfloat16)
        packed = packed.reshape(length, heads_here, 3, HD)
        query = packed[:, :, 0]
        keys = packed[:, :, 1]
        values = packed[:, :, 2]
        outs, totals = attention_forward(query, keys, values, seg_ids)
        attn = (outs * hmask[None, :, None]).astype(jnp.bfloat16).reshape(length, heads_here * HD)
        branch = lax.psum_scatter(
            contract_cols(attn, full_proj).astype(jnp.bfloat16),
            "tensor",
            scatter_dimension=0,
            tiled=True,
        ).astype(jnp.float32)
        first = token_vals + gate1 * branch
        normed2, factor2 = layer_norm(first)
        h_second = lax.all_gather(
            (normed2 * (1.0 + scale2) + shift2).astype(jnp.bfloat16), "tensor", axis=0, tiled=True
        )
        upward = jnp.dot(h_second, full_fc1, preferred_element_type=jnp.float32)
        gelu_val, gelu_pull = jax.vjp(lambda inner: jax.nn.gelu(inner, approximate=True), upward)
        act = (gelu_val * gcols[None, :]).astype(jnp.bfloat16)
        mlp = lax.psum_scatter(
            contract_cols(act, full_fc2).astype(jnp.bfloat16),
            "tensor",
            scatter_dimension=0,
            tiled=True,
        ).astype(jnp.float32)
        keep_col = keepf[:, None]
        result = (first + gate2 * keep_col * mlp).astype(jnp.bfloat16)
        grad_out = slot_grad.astype(jnp.float32)
        d_mlp = lax.all_gather(
            (gate2 * keep_col * grad_out).astype(jnp.bfloat16), "tensor", axis=0, tiled=True
        )
        grad_fc2 = contract_rows(d_mlp, act)
        d_act = jnp.dot(d_mlp, full_fc2, preferred_element_type=jnp.float32)
        d_up = gelu_pull(d_act * gcols[None, :])[0].astype(jnp.bfloat16)
        grad_fc1 = contract_rows(h_second, d_up)
        d_second = lax.psum_scatter(
            contract_cols(d_up, full_fc1).astype(jnp.bfloat16),
            "tensor",
            scatter_dimension=0,
            tiled=True,
        ).astype(jnp.float32)
        d_first = grad_out + norm_back(d_second * (1.0 + scale2), normed2, factor2)
        d_branch = lax.all_gather(
            (gate1 * d_first).astype(jnp.bfloat16), "tensor", axis=0, tiled=True
        )
        grad_proj = contract_rows(d_branch, attn)
        d_attn = jnp.dot(d_branch, full_proj, preferred_element_type=jnp.float32).astype(
            jnp.bfloat16
        )
        d_attn = d_attn.reshape(length, heads_here, HD) * hmask[None, :, None].astype(jnp.bfloat16)
        d_packed = attention_backward(query, keys, values, seg_ids, totals, d_attn)
        grad_qkv = contract_rows(h_first, d_packed)
        d_h_first = lax.psum_scatter(
            contract_cols(d_packed, full_qkv).astype(jnp.bfloat16),
            "tensor",
            scatter_dimension=0,
            tiled=True,
        ).astype(jnp.float32)
        d_input = d_first + norm_back(d_h_first * (1.0 + scale1), normed1, factor1)
        d_modtok = jnp.concatenate(
            [
                d_h_first,
                d_h_first * normed1,
                d_first * branch,
                d_second,
                d_second * normed2,
                grad_out * keep_col * mlp,
            ],
            axis=1,
        )
        part_dmods = lax.dot_general(onehot, d_modtok, (((0,), (0,)), ((), ())), precision=HIGH)
        d_mods = lax.psum_scatter(
            part_dmods.astype(jnp.bfloat16), "tensor", scatter_dimension=1, tiled=True
        ).astype(jnp.float32)
        grad_ada = jnp.dot(scond.astype(jnp.float32).T, d_mods, precision=HIGH)
        bias_acc = bias_acc + jnp.sum(d_mods, axis=0)
        parts = reduce_grads(grad_qkv, grad_proj, grad_fc1, grad_fc2, grad_ada)
        acc = tuple((held + piece for held, piece in zip(acc, parts)))
        return ((acc, bias_acc), (result, d_input.astype(jnp.bfloat16)))

    start_bias = jnp.zeros(b_ada.shape, jnp.float32)
    (acc, bias_acc), (results, d_tokens) = lax.scan(
        slot_step,
        (start_acc, start_bias),
        (tokens, cotangent, segments, time_embed, head_sel, group_sel, keep_float),
    )
    g_bias = lax.psum(bias_acc, "dp")
    return (results, d_tokens, acc[0], acc[1], acc[2], acc[3], acc[4], g_bias)


MESH = pl.DeviceIdType.MESH
ANY = pl.BlockSpec(memory_space=pl.ANY)
DMA = pltpu.SemaphoreType.DMA


class Place:
    def __init__(self):
        self.dp = lax.axis_index("dp")
        self.line = lax.axis_index("tensor")
        self.core = self.dp % 2
        self.base = self.dp - self.core
        self.half = self.line // 2
        x, y = (self.dp // 2) % 2, self.dp // 4
        self.dp_x = self.dp + 2 * (1 - 2 * x)
        self.dp_y = self.dp + 4 * (1 - 2 * y)
        self.base_x = self.dp_x - self.core
        self.base_y = self.dp_y - self.core
        self.base_far = self.base_x + self.base_y - self.base

    def barrier(self):
        bar = pltpu.get_barrier_semaphore()
        spot = self.core * 4 + self.line
        for step in range(1, 8):
            other = (spot + step) % 8
            pl.semaphore_signal(
                bar,
                inc=1,
                device_id=(self.base + other // 4, other % 4),
                device_id_type=MESH,
            )
        for step in range(1, 8):
            other = (self.dp + step) % 8
            pl.semaphore_signal(bar, inc=1, device_id=(other, self.line), device_id_type=MESH)
        pl.semaphore_wait(bar, 14)


def remote(src, dst, send, recv, dp, line):
    return pltpu.make_async_remote_copy(
        src_ref=src,
        dst_ref=dst,
        send_sem=send,
        recv_sem=recv,
        device_id=(dp, line),
        device_id_type=MESH,
    )


def move(src, dst, send, recv, dp, line, here):
    @pl.when(here)
    def _():
        pltpu.make_async_copy(src, dst, recv).start()

    @pl.when(jnp.logical_not(here))
    def _():
        remote(src, dst, send, recv, dp, line).start()


LOG2E = 1.4426950408889634
LOW = jnp.bfloat16
F32 = jnp.float32
SHADE = -1e30


def dot_nn(left, right):
    return jnp.dot(left, right, preferred_element_type=F32)


def dot_nt(left, right):
    return lax.dot_general(left, right, (((1,), (1,)), ((), ())), preferred_element_type=F32)


def dot_tn(left, right):
    return lax.dot_general(left, right, (((0,), (0,)), ((), ())), preferred_element_type=F32)


def lanes(rows):
    return lax.broadcasted_iota(jnp.int32, (rows, 128), 1)


def window(value, start):
    tile, rest = start // 128, start % 128
    here = value[:, 128 * tile : 128 * tile + 128]
    if rest == 0:
        return here
    here = pltpu.roll(here, 128 - rest, 1)
    if rest + HD <= 128:
        return here
    after = pltpu.roll(value[:, 128 * tile + 128 : 128 * tile + 256], 128 - rest, 1)
    return jnp.where(lanes(value.shape[0]) < 128 - rest, here, after)


def pack(parts, start, tiles):
    rows = parts[0].shape[0]
    lane = lanes(rows)
    out = []
    for tile in range(tiles):
        total = jnp.zeros((rows, 128), F32)
        for number, part in enumerate(parts):
            low = start + HD * number - 128 * tile
            if low >= 128 or low + HD <= 0:
                continue
            moved = pltpu.roll(part, low % 128, 1) if low % 128 else part
            inside = jnp.logical_and(lane >= low, lane < low + HD)
            total = jnp.where(inside, moved, total)
        out.append(total)
    return out


def turned(value, tile):
    start = 128 * tile
    stop = min(start + 128, value.shape[1])
    part = value[:, start:stop]
    if stop - start < 128:
        part = jnp.concatenate([part, jnp.zeros((part.shape[0], 64), F32)], axis=1)
    return pltpu.roll(part, 64, 1)


def to_blocks(even, odd):
    low = lanes(even.shape[0]) < 64
    turn = [turned(odd, tile) for tile in range(14)]
    tail = jnp.concatenate([even[:, 1664:1728], jnp.zeros((even.shape[0], 64), F32)], axis=1)
    one = [even[:, 0:1152]]
    two = [even[:, 1152:1664], jnp.where(low, tail, turn[0])]
    two += [jnp.where(low, turn[t], turn[t + 1]) for t in range(4)]
    three = [jnp.where(low, turn[t], turn[t + 1]) for t in range(4, 13)]
    return [jnp.concatenate(parts, axis=1) for parts in (one, two, three)]


def to_chunks(one, two, three):
    low = lanes(one.shape[0]) < 64
    even = jnp.concatenate([one, two[:, 0:576]], axis=1)
    turn = [turned(two, tile) for tile in range(4, 9)] + [turned(three, t) for t in range(9)]
    odd = [jnp.where(low, turn[t], turn[t + 1]) for t in range(13)]
    return even, jnp.concatenate(odd + [turn[13][:, 0:64]], axis=1)


def front_kernel(
    wh,
    w1,
    w2,
    tok,
    cot,
    meta,
    te,
    wa,
    ba,
    weights,
    w1_out,
    head_out,
    x_out,
    g_out,
    h1_out,
    qkv_out,
    pt_out,
    att_out,
    x1_out,
    br_out,
    h2_out,
    dm_out,
    act_out,
    gp_out,
    gf_out,
    cond,
    mod,
    gains,
    groups,
    kept,
    select,
    xt,
    w0,
    h1,
    qkv,
    obuf,
    pt,
    gst,
    att,
    sb,
    rb,
    br,
    x1,
    h2,
    ct,
    dm,
    w1v,
    act,
    gp,
    gc,
    mt,
    te_all,
    pb,
    pr,
    mine,
    mr,
    feat,
    zs,
    zr,
    fs,
    ns,
    nr,
    ds,
    dr,
    ts,
    tr,
    es,
    er,
    ls,
    ps,
    gs,
    ms,
    mrs,
    tes,
    ter,
    pbs,
    pbr,
    mms,
    mmr,
):
    at = Place()
    dp, line, core, half = at.dp, at.line, at.core, at.half
    units = (wh, w1, w2)
    lane = line % 2
    rows_u = w1.shape[0]
    sib = at.base + 1 - core
    at.barrier()

    def spot(u, zi, row):
        if u < 2:
            return (w0, w1v)[u].at[zi, pl.ds(pl.multiple_of(row * rows_u, 16), rows_u)]
        return weights.at[zi, row]

    def deal(kind, start):
        src, dst = ((tok, xt), (cot, ct))[kind]
        for slot in range(2):
            there = 2 * core + slot
            here = jnp.logical_and(half == core, there == line)
            send, recv = ts.at[kind, slot], tr.at[kind, lane]
            if start:
                move(src.at[slot], dst.at[lane], send, recv, at.base + half, there, here)
            else:

                @pl.when(jnp.logical_not(here))
                def _():
                    remote(
                        src.at[slot], dst.at[lane], send, recv, at.base + half, there
                    ).wait_send()

    def deal_arrive(kind):
        src, dst = ((tok, xt), (cot, ct))[kind]
        for block in range(2):
            pltpu.make_async_copy(src.at[0], dst.at[block], tr.at[kind, block]).wait()

    def source(u, start):
        dst = spot(u, lane, dp)
        recv = zr.at[u, lane, core]
        home = at.base + half
        if start:
            move(units[u], dst, zs.at[u, 0], recv, home, line, half == core)
        else:

            @pl.when(half != core)
            def _():
                remote(units[u], dst, zs.at[u, 0], recv, home, line).wait_send()

        for which, step in ((1, 1), (2, -1)):
            inside = line < 3 if step == 1 else line > 0

            @pl.when(inside)
            def _():
                copy = remote(units[u], dst, zs.at[u, which], recv, home, line + step)
                copy.start() if start else copy.wait_send()

    first = jnp.where(core == 0, jnp.where(line == 0, 0, 1), jnp.where(line == 3, 1, 0))

    def z_stage(u, k, other, start):
        zi = first + k - 2 * first * k
        origin = 2 * core + zi
        ref = spot(u, zi, at.base + other)
        if start:
            pltpu.make_async_copy(w1, ref, zr.at[u, zi, other]).wait()
        up = jnp.logical_and(origin < line, line < 3)
        down = jnp.logical_and(origin > line, line > 0)
        for go, step in ((up, 1), (down, -1)):

            @pl.when(go)
            def _():
                copy = remote(
                    ref, ref, fs.at[u, zi, other], zr.at[u, zi, other], dp, line + step
                )
                copy.start() if start else copy.wait_send()

        for which, near in ((0, at.dp_x), (1, at.dp_y)):
            copy = remote(
                ref, ref, ns.at[which, u, zi, other], nr.at[which, u, zi, other], near, line
            )
            copy.start() if start else copy.wait_send()

    def far_stage(u, zi, other, start):
        base = at.base_x + other * (at.base_y - at.base_x)
        near = at.dp_y + other * (at.dp_x - at.dp_y)
        ref = spot(u, zi, base + other)
        if start:
            pltpu.make_async_copy(w1, ref, nr.at[other, u, zi, other]).wait()
        copy = remote(ref, ref, ds.at[u, zi, other], dr.at[u, zi, other], near, line)
        copy.start() if start else copy.wait_send()

    def last_stage(u, zi, other):
        base = at.base_y + other * (at.base_x - at.base_y)
        ref = spot(u, zi, base + other)
        pltpu.make_async_copy(w1, ref, nr.at[1 - other, u, zi, other]).wait()
        ref = spot(u, zi, at.base_far + other)
        pltpu.make_async_copy(w1, ref, dr.at[u, zi, other]).wait()

    def pump(number):
        k, other = (number % 4) // 2, number % 2
        for quarter in range(4):
            u, stage = ((1, z_stage), (2, z_stage), (1, far_stage), (2, far_stage))[quarter]

            @pl.when(number // 4 == quarter)
            def _():
                stage(u, k, other, True)

    def keep(src, dst, number):
        return pltpu.make_async_copy(src, dst, ls.at[number])

    def each_column(start):
        for step in range(1, 8):
            other = (core * 4 + line + step) % 8
            copy = remote(
                meta, mt.at[core * 4 + line], ms.at[step], mrs.at[core * 4 + line],
                at.base + other // 4, other % 4,
            )
            copy.start() if start else copy.wait_send()

    def each_row(src, dst, send, recv, start, pieces):
        for step in range(1, 8):
            other = (dp + step) % 8
            part = src.at[other] if pieces else src
            copy = remote(part, dst.at[dp], send.at[step], recv.at[dp], other, line)
            copy.start() if start else copy.wait_send()

    def row_arrive(dst, recv):
        for step in range(1, 8):
            other = (dp + step) % 8
            pltpu.make_async_copy(dst.at[other], dst.at[other], recv.at[other]).wait()

    each_row(te, te_all, tes, ter, True, True)
    each_column(True)
    te_all[dp] = te[dp]
    mt[core * 4 + line] = meta[...]

    source(0, True)
    row_arrive(te_all, ter)
    for number in range(8):
        spread = te_all[number]
        cond[8 * number : 8 * number + 8, :] = spread * (1.0 / (1.0 + jnp.exp(-spread)))
    value = dot_nn(cond[...].astype(LOW), wa[...])
    for number in range(8):
        pb[number] = value[8 * number : 8 * number + 8, :]
    each_row(pb, pr, pbs, pbr, True, True)
    deal(0, True)
    pr[dp] = pb[dp]
    for other in range(2):
        z_stage(0, 0, other, True)
    row_arrive(pr, pbr)
    total = ba[...] + pr[0]
    for number in range(1, 8):
        total = total + pr[number]
    mine[...] = total

    def each_slot(start):
        for slot in range(2):
            there = 2 * core + slot
            for to in range(2):
                here = jnp.logical_and(core == to, there == line)
                send, recv = mms.at[slot, to], mmr.at[line]
                if start:
                    move(mine, mr.at[line], send, recv, at.base + to, there, here)
                else:

                    @pl.when(jnp.logical_not(here))
                    def _():
                        remote(mine, mr.at[line], send, recv, at.base + to, there).wait_send()

    each_slot(True)
    for other in range(2):
        z_stage(0, 1, other, True)
    source(1, True)
    deal(1, True)

    for step in range(1, 8):
        other = (core * 4 + line + step) % 8
        pltpu.make_async_copy(meta, mt.at[other], mrs.at[other]).wait()
    one_row = lanes(1)
    spots = (one_row - HD).astype(F32)
    inside = jnp.logical_and(one_row >= HD, one_row < HD + 4)

    def lane_of(row, place):
        return jnp.sum(jnp.where(one_row == place, row, 0.0), axis=1, keepdims=True)

    for zi in range(2):
        info = mt[half * 4 + 2 * core + zi, pl.ds(4 + lane, 1), :]
        for number in range(4):
            head = zi * 4 + number
            gains[head : head + 1, :] = jnp.broadcast_to(lane_of(info, number), (1, 128))
            groups[head : head + 1, :] = jnp.broadcast_to(lane_of(info, 4 + number), (1, 128))
    unit = lax.broadcasted_iota(jnp.int32, (1, gc.shape[1]), 1) // (gc.shape[1] // 4)
    for zi in range(2):
        row = jnp.zeros((1, gc.shape[1]), F32)
        for number in range(4):
            head = zi * 4 + number
            row = jnp.where(unit == number, groups[head : head + 1, 0:1], row)
        gc[8 * zi : 8 * zi + 8, :] = jnp.broadcast_to(row, (8, gc.shape[1]))
    info = mt[half * 4 + line, pl.ds(4 + lane, 1), :]
    for tile in range(4):
        same = jnp.where(spots == lane_of(info, 8 + tile), 1.0, 0.0)
        feat[0, tile : tile + 1, :] = jnp.where(inside, SHADE * (1.0 - same), 0.0)
        feat[1, tile : tile + 1, :] = jnp.where(inside, same, 0.0)
    row_ids = lax.broadcasted_iota(jnp.int32, (8, 128), 0)
    diagonal = lax.broadcasted_iota(jnp.int32, (128, 128), 0) == lanes(128)
    for block in range(2):
        item = jnp.sum(
            jnp.where(one_row == 8 + 2 * core + block, info, 0.0), axis=1, keepdims=True
        )
        hit = row_ids.astype(F32) == item + (4 * lane).astype(F32)
        select[block] = jnp.where(hit, 1.0, 0.0)
        for number in range(2):
            row = mt[half * 4 + 2 * core + block, pl.ds(2 * lane + number, 1), :]
            column = jnp.sum(jnp.where(diagonal, row, 0.0), axis=1, keepdims=True)
            kept[block, 128 * number : 128 * number + 128, :] = jnp.broadcast_to(column, (128, 128))
    for source_line in range(4):
        pltpu.make_async_copy(mine, mr.at[source_line], mmr.at[source_line]).wait()
    for block in range(2):
        weight = select[block][:, 0:1]
        rows = [jnp.sum(weight * mr[n], axis=0, keepdims=True) for n in range(4)]
        pieces = to_blocks(rows[0], rows[1]) + to_blocks(rows[2], rows[3])
        for number, piece in enumerate(pieces):
            mod[block, number : number + 1, :] = piece
        mod[block, 6:8, :] = jnp.zeros((2, mod.shape[2]), F32)

    def exchange(src, dst, number):
        return remote(src, dst, es.at[number], er.at[number], sib, line)

    deal_arrive(0)
    keep(xt, x_out, 0).start()

    for block in range(2):
        shift, scale = mod[block, 0:1, :], 1.0 + mod[block, 1:2, :]

        def norm_first(step, _):
            at_row = pl.ds(pl.multiple_of(step * 128, 128), 128)
            normed, _f = layer_norm(xt[block, at_row, :].astype(F32))
            to_row = pl.ds(pl.multiple_of(block * 256 + step * 128, 128), 128)
            h1[core, to_row, :] = (normed * scale + shift).astype(LOW)
            return 0

        lax.fori_loop(0, 2, norm_first, 0)
        part = h1.at[core, pl.ds(block * 256, 256)]
        exchange(part, part, block).start()
    for zi in range(2):
        for other in range(2):
            far_stage(0, zi, other, True)
    source(2, True)
    for zi in range(2):
        for other in range(2):
            last_stage(0, zi, other)
    keep(w0, head_out, 1).start()

    def project(step, _):
        @pl.when(step >= 2)
        def _():
            part = h1.at[1 - core, pl.ds(pl.multiple_of((step - 2) * 256, 256), 256)]
            pltpu.make_async_copy(part, part, er.at[step - 2]).wait()

        pump(step)
        tile = (2 * core + step) % 4
        rows = h1[tile // 2, pl.ds(pl.multiple_of((tile % 2) * 256, 256), 256), :]
        to_row = pl.ds(pl.multiple_of(tile * 256, 256), 256)
        narrow = lanes(256) < HD
        fills = (feat[0, pl.ds(tile, 1), :], feat[1, pl.ds(tile, 1), :], jnp.zeros((1, 128), F32))
        for zi in range(2):
            value = dot_nn(rows, w0[zi, :, 0:896])
            for number in range(12):
                head, part = zi * 4 + number // 3, number % 3
                piece = jnp.where(narrow, window(value, HD * number), fills[part])
                qkv[head, part, to_row, :] = piece.astype(LOW)
        return 0

    lax.fori_loop(0, 4, project, 0)
    keep(h1, h1_out, 2).start()
    keep(qkv, qkv_out, 3).start()

    factor = HD ** (-0.5) * LOG2E

    def attend(head, _):
        pump(4 + head)
        gain = gains[pl.ds(head, 1), :]

        def tile_step(tile, _):
            rows = pl.ds(pl.multiple_of(tile * 256, 256), 256)
            number = 4 * head + tile
            slot = number % 2
            scores = dot_nt(qkv[head, 1], qkv[head, 0, rows, :])
            peak = jnp.max(scores, axis=0, keepdims=True)
            power = jnp.exp2((scores - peak) * factor)
            total = jnp.sum(power, axis=0, keepdims=True)
            probs = (power * (1.0 / total)).astype(LOW)
            obuf[head, rows, :] = (dot_tn(probs, qkv[head, 2]) * gain).astype(LOW)

            @pl.when(number >= 2)
            def _():
                pltpu.make_async_copy(pt.at[slot], pt_out.at[number - 2], ps.at[slot]).wait()

            pt[slot] = probs
            pltpu.make_async_copy(pt.at[slot], pt_out.at[number], ps.at[slot]).start()
            return 0

        lax.fori_loop(0, 4, tile_step, 0)
        return 0

    lax.fori_loop(0, 8, attend, 0)

    def lay(step, _):
        rows = pl.ds(pl.multiple_of(step * 128, 128), 128)
        for zi in range(2):
            parts = [obuf[zi * 4 + n, rows, :].astype(F32) for n in range(4)]
            for tile, value in enumerate(pack(parts, 96, 3)):
                att[zi, rows, 128 * tile : 128 * tile + 128] = value.astype(LOW)
        return 0

    lax.fori_loop(0, 8, lay, 0)
    keep(att, att_out, 5).start()

    for step in range(4):
        tile = (2 * (1 - core) + step) % 4
        rows = pl.ds(pl.multiple_of(tile * 256, 256), 256)
        value = dot_nt(att[0, rows, :], w0[0, :, 768:1152])
        value = value + dot_nt(att[1, rows, :], w0[1, :, 768:1152])
        if step < 2:
            sb[step] = value.astype(LOW)
            exchange(sb.at[step], rb.at[step], 2 + step).start()
        else:
            br[step - 2] = value
    for block in range(2):
        exchange(sb.at[block], rb.at[block], 2 + block).wait_recv()
        gate = mod[block, 2:3, :]
        shift, scale = mod[block, 3:4, :], 1.0 + mod[block, 4:5, :]

        def norm_second(step, _):
            at_row = pl.ds(pl.multiple_of(step * 128, 128), 128)
            branch = br[block, at_row, :] + rb[block, at_row, :].astype(F32)
            br[block, at_row, :] = branch
            value = xt[block, at_row, :].astype(F32) + gate * branch
            x1[block, at_row, :] = value
            normed, _f = layer_norm(value)
            to_row = pl.ds(pl.multiple_of(block * 256 + step * 128, 128), 128)
            h2[core, to_row, :] = (normed * scale + shift).astype(LOW)
            return 0

        lax.fori_loop(0, 2, norm_second, 0)
        part = h2.at[core, pl.ds(block * 256, 256)]
        exchange(part, part, 4 + block).start()
    keep(x1, x1_out, 6).start()
    keep(br, br_out, 7).start()

    deal_arrive(1)
    keep(ct, g_out, 9).start()
    for block in range(2):
        gate2 = mod[block, 5:6, :]

        def grad_rows(step, _):
            at_row = pl.ds(pl.multiple_of(step * 128, 128), 128)
            value = gate2 * kept[block, at_row, 0:1] * ct[block, at_row, :].astype(F32)
            to_row = pl.ds(pl.multiple_of(block * 256 + step * 128, 128), 128)
            dm[core, to_row, :] = value.astype(LOW)
            return 0

        lax.fori_loop(0, 2, grad_rows, 0)
        part = dm.at[core, pl.ds(block * 256, 256)]
        exchange(part, part, 6 + block).start()

    for block in range(2):
        part = h2.at[1 - core, pl.ds(block * 256, 256)]
        pltpu.make_async_copy(part, part, er.at[4 + block]).wait()
    keep(h2, h2_out, 8).start()
    for block in range(2):
        part = dm.at[1 - core, pl.ds(block * 256, 256)]
        pltpu.make_async_copy(part, part, er.at[6 + block]).wait()
    keep(dm, dm_out, 10).start()

    for zi in range(2):
        for other in range(2):
            last_stage(1, zi, other)
    keep(w1v, w1_out, 11).start()
    ratio = (2.0 / 3.141592653589793) ** 0.5

    def widen(step, _):
        tile, zi = (2 * core + step // 2) % 4, step % 2
        rows = h2[tile // 2, pl.ds(pl.multiple_of((tile % 2) * 256, 256), 256), :]
        value = dot_nn(rows, w1v[zi])
        mask = gc[pl.ds(pl.multiple_of(8 * zi, 8), 8), :][0:1, :]
        square = value * value
        bend = jnp.tanh(ratio * (value + 0.044715 * (value * square)))
        grown = 0.5 * (1.0 + bend)
        slope = grown + 0.5 * value * (1.0 - bend * bend) * (
            ratio * (1.0 + (3.0 * 0.044715) * square)
        )
        to_row = pl.ds(pl.multiple_of(tile * 256, 256), 256)
        act[zi, to_row, :] = (value * grown * mask).astype(LOW)
        gp[zi, to_row, :] = (slope * mask).astype(LOW)

        @pl.when(step % 2 == 1)
        def _():
            pump(12 + step // 2)

        return 0

    lax.fori_loop(0, 8, widen, 0)
    keep(act, act_out, 12).start()
    keep(gp, gp_out, 13).start()

    def grad_piece(number):
        rows = pl.ds(384 * (number % 3), 384)
        if not isinstance(number, int):
            rows = pl.ds(pl.multiple_of(384 * (number % 3), 128), 384)
        return gf_out.at[number // 3, rows]

    def fc2_grad(number, _):
        zi, slot = number // 3, number % 3
        some = pl.ds(pl.multiple_of(384 * slot, 128), 384)
        value = dot_tn(dm[0, :, some], act[zi, 0:512, :])
        value = value + dot_tn(dm[1, :, some], act[zi, 512:1024, :])

        @pl.when(number >= 3)
        def _():
            pltpu.make_async_copy(gst.at[slot], grad_piece(number - 3), gs.at[slot]).wait()

        gst[slot] = value.astype(LOW)
        pltpu.make_async_copy(gst.at[slot], grad_piece(number), gs.at[slot]).start()
        return 0

    lax.fori_loop(0, 6, fc2_grad, 0)

    for u in range(3):
        source(u, False)
        for k in range(2):
            for other in range(2):
                z_stage(u, k, other, False)
                far_stage(u, k, other, False)
                if u == 2:
                    last_stage(u, k, other)
    for kind in range(2):
        deal(kind, False)
    each_column(False)
    each_row(te, te_all, tes, ter, False, True)
    each_row(pb, pr, pbs, pbr, False, True)
    each_slot(False)
    for block in range(2):
        own1 = h1.at[core, pl.ds(block * 256, 256)]
        own2 = h2.at[core, pl.ds(block * 256, 256)]
        exchange(own1, own1, block).wait_send()
        exchange(sb.at[block], rb.at[block], 2 + block).wait_send()
        exchange(own2, own2, 4 + block).wait_send()
        own3 = dm.at[core, pl.ds(block * 256, 256)]
        exchange(own3, own3, 6 + block).wait_send()
    pairs = (
        (xt, x_out),
        (w0, head_out),
        (h1, h1_out),
        (qkv, qkv_out),
        (None, None),
        (att, att_out),
        (x1, x1_out),
        (br, br_out),
        (h2, h2_out),
        (ct, g_out),
        (dm, dm_out),
        (w1v, w1_out),
        (act, act_out),
        (gp, gp_out),
    )
    for number, (src, dst) in enumerate(pairs):
        if number != 4:
            keep(src, dst, number).wait()
    for slot in range(2):
        pltpu.make_async_copy(pt.at[slot], pt_out.at[30 + slot], ps.at[slot]).wait()
    for slot in range(3):
        pltpu.make_async_copy(gst.at[slot], grad_piece(3 + slot), gs.at[slot]).wait()


def run_front(wh, w1, w2, tok, cot, meta, te, wa, ba):
    rows, cols = w1.shape
    part = tok.shape[1]
    length = 4 * part
    shape = jax.ShapeDtypeStruct
    vmem = pl.BlockSpec(memory_space=pltpu.VMEM)
    shared = shape((2, 2 * part, cols), LOW)
    single = shape((2, part, cols), F32)
    outs = (
        shape((2, 8, rows, cols), LOW),
        shape((2, 8 * rows, cols), LOW),
        shape((2, 8 * rows, cols), LOW),
        shape(tok.shape, LOW),
        shape(tok.shape, LOW),
        shared,
        shape((8, 3, length, 128), LOW),
        shape((32, length, part), LOW),
        shape((2, length, 384), LOW),
        single,
        single,
        shared,
        shared,
        shape((2, length, cols), LOW),
        shape((2, length, cols), LOW),
        shape((2, 8 * rows, cols), LOW),
    )
    small = (
        shape((64, rows), F32),
        shape((2, 8, cols), F32),
        shape((8, 128), F32),
        shape((8, 128), F32),
        shape((2, part, 128), F32),
        shape((2, 8, 128), F32),
    )
    three = DMA((3, 2, 2))
    return pl.pallas_call(
        front_kernel,
        out_shape=outs + small,
        in_specs=[ANY] * 5 + [vmem] * 4,
        out_specs=(ANY,) * len(outs) + (vmem,) * len(small),
        scratch_shapes=[
            pltpu.VMEM(tok.shape, LOW),
            pltpu.VMEM((2, 8 * rows, cols), LOW),
            pltpu.VMEM((2, 2 * part, cols), LOW),
            pltpu.VMEM((8, 3, length, 128), LOW),
            pltpu.VMEM((8, length, 128), LOW),
            pltpu.VMEM((2, length, part), LOW),
            pltpu.VMEM((3, 384, cols), LOW),
            pltpu.VMEM((2, length, 384), LOW),
            pltpu.VMEM((2, part, cols), LOW),
            pltpu.VMEM((2, part, cols), LOW),
            pltpu.VMEM((2, part, cols), F32),
            pltpu.VMEM((2, part, cols), F32),
            pltpu.VMEM((2, 2 * part, cols), LOW),
            pltpu.VMEM(tok.shape, LOW),
            pltpu.VMEM((2, 2 * part, cols), LOW),
            pltpu.VMEM((2, 8 * rows, cols), LOW),
            pltpu.VMEM((2, length, cols), LOW),
            pltpu.VMEM((2, length, cols), LOW),
            pltpu.VMEM((16, cols), F32),
            pltpu.VMEM((8, 8, 128), F32),
            pltpu.VMEM((8, 8, rows), F32),
            pltpu.VMEM((8, 8, wa.shape[1]), F32),
            pltpu.VMEM((8, 8, wa.shape[1]), F32),
            pltpu.VMEM((8, wa.shape[1]), F32),
            pltpu.VMEM((4, 8, wa.shape[1]), F32),
            pltpu.VMEM((2, 8, 128), F32),
            DMA((3, 3)),
            three,
            three,
            DMA((2, 3, 2, 2)),
            DMA((2, 3, 2, 2)),
            three,
            three,
            DMA((2, 2)),
            DMA((2, 2)),
            DMA((8,)),
            DMA((8,)),
            DMA((14,)),
            DMA((2,)),
            DMA((3,)),
            DMA((8,)),
            DMA((8,)),
            DMA((8,)),
            DMA((8,)),
            DMA((8,)),
            DMA((8,)),
            DMA((2, 2)),
            DMA((4,)),
        ],
        compiler_params=pltpu.CompilerParams(
            collective_id=0, has_side_effects=True, vmem_limit_bytes=60 << 20
        ),
    )(wh, w1, w2, tok, cot, meta, te, wa, ba)


def back_kernel(
    act_in,
    gp_in,
    dm_in,
    h2_in,
    w1_in,
    w2_in,
    gf_in,
    x1_in,
    br_in,
    x_in,
    g_in,
    h1_in,
    qkv_in,
    pt_in,
    att_in,
    head_in,
    mod,
    gains,
    keep_col,
    select,
    cond,
    out_tok,
    out_dtok,
    rz,
    pq,
    gf1,
    g_ada,
    g_bias,
    sums,
    db,
    yb,
    zb,
    sb,
    sm,
    rb,
    rm,
    ob,
    r1,
    rn,
    stage,
    dc,
    nr,
    da,
    s1s,
    s1r,
    nss,
    nsr,
    zss,
    zsr,
    pqr,
    es,
    er,
    ts,
    tr,
    ls,
    gs,
    ps,
    dcs,
    dcr,
    das,
    dar,
):
    at = Place()
    dp, line, core, half = at.dp, at.line, at.core, at.half
    lane = line % 2
    rows_u = stage.shape[1]
    local = {}
    sib = at.base + 1 - core
    scale_q = HD ** (-0.5)
    factor = HD ** (-0.5) * LOG2E

    def load(src, dst, number):
        return pltpu.make_async_copy(src, dst, ls.at[number])

    def exchange(src, dst, number):
        return remote(src, dst, es.at[number], er.at[number], sib, line)

    def grad_ref(u, zi, row):
        here = pl.ds(pl.multiple_of(row * rows_u, 16), rows_u)
        return (local.get("g0"), gf1, gf_in)[u].at[zi, here]

    def base_of(which):
        return at.base_x + which * (at.base_y - at.base_x)

    def near_of(which):
        return at.dp_x + which * (at.dp_y - at.dp_x)

    def far_send(u, zi, o):
        return remote(
            grad_ref(u, zi, at.base_far + o),
            r1.at[u, zi, o],
            s1s.at[u, zi, o],
            s1r.at[u, zi, o],
            near_of(o),
            line,
        )

    def plain_send(u, zi, o):
        return remote(
            grad_ref(u, zi, base_of(o) + o),
            rn.at[o, u, zi, o],
            nss.at[o, u, zi, o],
            nsr.at[o, u, zi, o],
            near_of(o),
            line,
        )

    def relay_send(u, zi, o):
        return remote(
            r1.at[u, zi, o],
            rn.at[1 - o, u, zi, o],
            nss.at[1 - o, u, zi, o],
            nsr.at[1 - o, u, zi, o],
            near_of(1 - o),
            line,
        )

    def fetch(u, zi, o, which):
        row = (base_of(1 - o), at.base)[which] + o
        slot = 2 * which + o
        return pltpu.make_async_copy(grad_ref(u, zi, row), stage.at[slot], gs.at[slot])

    def own_term(u, zi, o, which):
        if u == 0:
            return grad_ref(u, zi, (base_of(1 - o), at.base)[which] + o)
        return stage.at[2 * which + o]

    def relay(u, zi, o):
        far_send(u, zi, o).wait_recv()
        if u:
            fetch(u, zi, o, 0).wait()
        ref = own_term(u, zi, o, 0)
        r1[u, zi, o] = (r1[u, zi, o].astype(F32) + ref[...].astype(F32)).astype(LOW)
        relay_send(u, zi, o).start()

    near_half = half == core
    edge = jnp.logical_or(line == 0, line == 3)
    outer = jnp.logical_and(jnp.logical_not(near_half), edge)
    inner = jnp.logical_and(jnp.logical_not(near_half), jnp.logical_not(edge))

    def column_send(u, zi, o, slot):
        return remote(
            rn.at[0, u, zi, o],
            rz.at[u, slot],
            zss.at[u, zi, o],
            zsr.at[u, slot],
            at.base + o,
            2 * core + zi,
        )

    def settle(u, zi, o):
        for which in range(2):
            there = rn.at[which, u, zi, o]
            pltpu.make_async_copy(there, there, nsr.at[which, u, zi, o]).wait()
        if u:
            fetch(u, zi, o, 1).wait()
        ref = own_term(u, zi, o, 1)
        total = rn[0, u, zi, o].astype(F32) + rn[1, u, zi, o].astype(F32)
        rn[0, u, zi, o] = (total + ref[...].astype(F32)).astype(LOW)
        here = jnp.logical_and(core == o, line == 2 * core + zi)

        @pl.when(here)
        def _():
            pltpu.make_async_copy(rn.at[0, u, zi, o], rz.at[u, lane], zsr.at[u, lane]).start()

        @pl.when(jnp.logical_and(near_half, jnp.logical_not(here)))
        def _():
            column_send(u, zi, o, lane).start()

        @pl.when(outer)
        def _():
            remote(
                rn.at[0, u, zi, o],
                pq.at[u, zi, o],
                zss.at[u, zi, o],
                pqr.at[u, zi, o],
                dp,
                line + 1 - 2 * half,
            ).start()

    def merge(u, zi, o):
        @pl.when(inner)
        def _():
            pltpu.make_async_copy(pq.at[u, zi, o], pq.at[u, zi, o], pqr.at[u, zi, o]).wait()
            copy = pltpu.make_async_copy(pq.at[u, zi, o], stage.at[o], gs.at[o])
            copy.start()
            copy.wait()
            total = rn[0, u, zi, o].astype(F32) + stage[o].astype(F32)
            rn[0, u, zi, o] = total.astype(LOW)
            column_send(u, zi, o, 2).start()

    def settled(u, zi, o):
        here = jnp.logical_and(core == o, line == 2 * core + zi)

        @pl.when(jnp.logical_not(here))
        def _():
            column_send(u, zi, o, 0).wait_send()

    def finish(u):
        for source in range(3):
            ref = rz.at[u, source]
            pltpu.make_async_copy(ref, ref, zsr.at[u, source]).wait()

    def fetch_pair(u, zi, which):
        for o in range(2):
            fetch(u, zi, o, which).start()

    def relay_pair(u, zi):
        for o in range(2):
            relay(u, zi, o)

    def settle_pair(u, zi):
        for o in range(2):
            settle(u, zi, o)

    def merge_pair(u, zi):
        for o in range(2):
            merge(u, zi, o)

    def give_back(block, kind, start):
        dst = (out_tok, out_dtok)[kind].at[lane]
        there = 2 * core + block
        here = jnp.logical_and(half == core, there == line)
        send, recv = ts.at[kind, block], tr.at[kind, lane]
        if start:
            move(ob.at[block], dst, send, recv, at.base + half, there, here)
        else:

            @pl.when(here)
            def _():
                pltpu.make_async_copy(ob.at[block], dst, recv).wait()

            @pl.when(jnp.logical_not(here))
            def _():
                remote(ob.at[block], dst, send, recv, at.base + half, there).wait_send()

    def mlp_phase(act, gp, w1v, w2v, dm, h2, gst):
        pairs = ((dm_in, dm), (w2_in, w2v), (gp_in, gp), (h2_in, h2), (w1_in, w1v), (act_in, act))
        copies = [load(src, dst, number) for number, (src, dst) in enumerate(pairs)]
        for copy in copies:
            copy.start()
        at.barrier()
        for zi in range(2):
            for o in range(2):
                far_send(2, zi, o).start()
            for o in range(2):
                plain_send(2, zi, o).start()
        length = act.shape[1]
        mid = length // 2

        def weight_grad(u, left, right):
            def column_half(zi, _):
                def piece(tile, _):
                    cols = pl.ds(pl.multiple_of(384 * tile, 128), 384)
                    value = dot_tn(left[0, :, cols], right[zi, 0:mid, :])
                    value = value + dot_tn(left[1, :, cols], right[zi, mid:length, :])
                    gst[tile] = value.astype(LOW)
                    rows = pl.ds(pl.multiple_of(384 * tile, 128), 384)
                    pltpu.make_async_copy(gst.at[tile], gf1.at[zi, rows], gs.at[tile]).start()
                    return 0

                lax.fori_loop(0, 3, piece, 0)
                for tile in range(3):
                    rows = pl.ds(384 * tile, 384)
                    pltpu.make_async_copy(gst.at[tile], gf1.at[zi, rows], gs.at[tile]).wait()
                for o in range(2):
                    far_send(u, zi, o).start()
                for o in range(2):
                    plain_send(u, zi, o).start()
                return 0

            lax.fori_loop(0, 2, column_half, 0)

        for copy in copies[0:3]:
            copy.wait()

        def down(step, _):
            tile, zi = step // 2, step % 2
            rows = dm[tile // 2, pl.ds(pl.multiple_of((tile % 2) * 256, 256), 256), :]
            to_row = pl.ds(pl.multiple_of(tile * 256, 256), 256)
            value = dot_nn(rows, w2v[zi]) * gp[zi, to_row, :].astype(F32)
            gp[zi, to_row, :] = value.astype(LOW)
            return 0

        lax.fori_loop(0, 8, down, 0)
        def partial(left, right, send, recv, own, number):
            def part(step, _):
                tile = (2 * (1 - core) + step) % 4
                rows = pl.ds(pl.multiple_of(tile * 256, 256), 256)
                value = dot_nt(left[0, rows, :], right[0])
                value = value + dot_nt(left[1, rows, :], right[1])

                @pl.when(step < 2)
                def _():
                    send[step] = value.astype(LOW)
                    exchange(send.at[step], recv.at[step], number + step).start()

                @pl.when(step >= 2)
                def _():
                    own[step - 2] = value

                return 0

            lax.fori_loop(0, 4, part, 0)

        for copy in copies[3:6]:
            copy.wait()
        partial(gp, w1v, sb, rb, yb, 0)
        weight_grad(1, h2, gp)
        fetch_pair(2, 0, 0)
        partial(act, w2v, sm, rm, zb, 2)
        relay_pair(2, 0)
        fetch_pair(2, 1, 0)

    cols = gf1.shape[2]
    length = act_in.shape[1]
    mid = length // 2
    pl.run_scoped(
        mlp_phase,
        pltpu.VMEM((2, length, cols), LOW),
        pltpu.VMEM((2, length, cols), LOW),
        pltpu.VMEM((2, 8 * rows_u, cols), LOW),
        pltpu.VMEM((2, 8 * rows_u, cols), LOW),
        pltpu.VMEM((2, mid, cols), LOW),
        pltpu.VMEM((2, mid, cols), LOW),
        pltpu.VMEM((3, 384, cols), LOW),
    )
    def attention_phase(w0, h1, qkv, pt, dpk, do, g0, xb, gb, acc):
        local["g0"] = g0
        pairs = (
            (head_in, w0),
            (qkv_in, qkv),
            (att_in, dpk.at[:, :, 0:384]),
            (h1_in, h1),
        )
        early = [load(src, dst, number) for number, (src, dst) in enumerate(pairs)]
        for copy in early:
            copy.start()

        def probs_in(number):
            slot = number % 2
            return pltpu.make_async_copy(pt_in.at[number], pt.at[slot], ps.at[slot])

        probs_in(0).start()
        fetch_pair(2, 0, 1)

        for block in range(2):
            copies = (
                load(x1_in.at[block], xb.at[0], 5),
                load(br_in.at[block], xb.at[1], 6),
                load(g_in.at[block], gb, 7),
            )
            for copy in copies:
                copy.start()
            for copy in copies:
                copy.wait()
            exchange(sb.at[block], rb.at[block], block).wait_recv()
            exchange(sm.at[block], rm.at[block], 2 + block).wait_recv()
            gate1, scale2 = mod[block, 2:3, :], 1.0 + mod[block, 4:5, :]
            gate2 = mod[block, 5:6, :]

            def norm_second(step, sums_now):
                at_row = pl.ds(pl.multiple_of(step * 128, 128), 128)
                grad = gb[at_row, :].astype(F32)
                first = xb[0, at_row, :]
                d_second = yb[block, at_row, :] + rb[block, at_row, :].astype(F32)
                kept = keep_col[block, at_row, 0:1] * (
                    zb[block, at_row, :] + rm[block, at_row, :].astype(F32)
                )
                ob[block, at_row, :] = (first + gate2 * kept).astype(LOW)
                normed, spread = layer_norm(first)
                d_first = grad + norm_back(d_second * scale2, normed, spread)
                yb[block, at_row, :] = d_first
                to_row = pl.ds(pl.multiple_of(block * 256 + step * 128, 128), 128)
                db[core, to_row, :] = (gate1 * d_first).astype(LOW)
                terms = (d_first * xb[1, at_row, :], d_second, d_second * normed, grad * kept)
                return tuple(
                    now + jnp.sum(term, axis=0, keepdims=True) for now, term in zip(sums_now, terms)
                )

            zero = jnp.zeros((1, gb.shape[1]), F32)
            totals = lax.fori_loop(0, 2, norm_second, (zero,) * 4)
            for place, value in zip((2, 3, 4, 5), totals):
                sums[block, place : place + 1, :] = value
            part = db.at[core, pl.ds(block * 256, 256)]
            exchange(part, part, 4 + block).start()
            give_back(block, 0, True)

        for copy in early[0:3]:
            copy.wait()

        relay_pair(2, 1)
        fetch_pair(1, 0, 0)

        def to_heads(step, _):
            @pl.when(step >= 2)
            def _():
                part = db.at[1 - core, pl.ds(pl.multiple_of((step - 2) * 256, 256), 256)]
                pltpu.make_async_copy(part, part, er.at[4 + step - 2]).wait()

            tile = (2 * core + step) % 4
            rows = db[tile // 2, pl.ds(pl.multiple_of((tile % 2) * 256, 256), 256), :]
            to_row = pl.ds(pl.multiple_of(tile * 256, 256), 256)
            narrow = lanes(256) < HD
            for zi in range(2):
                value = dot_nn(rows, w0[zi, :, 768:1152])
                for number in range(4):
                    piece = jnp.where(narrow, window(value, 96 + HD * number), 0.0)
                    head = zi * 4 + number
                    do[head, to_row, :] = (piece * gains[head : head + 1, :]).astype(LOW)
            return 0

        lax.fori_loop(0, 4, to_heads, 0)
        def proj_grad(number, _):
            zi, tile = number // 3, number % 3
            some = pl.ds(pl.multiple_of(384 * tile, 128), 384)
            value = dot_tn(db[0, :, some], dpk[zi, 0:mid, 0:384])
            value = value + dot_tn(db[1, :, some], dpk[zi, mid:length, 0:384])
            g0[zi, some, 768:1152] = value.astype(LOW)
            return 0

        lax.fori_loop(0, 6, proj_grad, 0)

        def attend(head, _):
            step_of = (
                lambda: (relay_pair(1, 0), fetch_pair(1, 1, 0)),
                lambda: (relay_pair(1, 1), settle_pair(2, 0), fetch_pair(2, 1, 1)),
                lambda: (settle_pair(2, 1), fetch_pair(1, 0, 1)),
                lambda: (settle_pair(1, 0), merge_pair(2, 0), fetch_pair(1, 1, 1)),
                lambda: (settle_pair(1, 1), merge_pair(2, 1)),
                lambda: (merge_pair(1, 0),),
                lambda: (merge_pair(1, 1),),
                lambda: (relay_pair(0, 0),),
            )
            for place, task in enumerate(step_of):

                @pl.when(head == place)
                def _():
                    task()

            acc[...] = jnp.zeros_like(acc)

            def tile_step(tile, _):
                number = 4 * head + tile
                rows = pl.ds(pl.multiple_of(tile * 256, 256), 256)

                @pl.when(number < 31)
                def _():
                    probs_in(number + 1).start()

                probs_in(number).wait()
                grad = do[head, rows, :]
                probs = pt[number % 2]
                acc[1] += dot_nn(probs, grad)
                d_probs = dot_nt(qkv[head, 2], grad)
                wide = probs.astype(F32)
                inner = jnp.sum(wide * d_probs, axis=0, keepdims=True)
                d_scores = (wide * (d_probs - inner)).astype(LOW)
                acc[0] += dot_nn(d_scores, qkv[head, 0, rows, :])
                qkv[head, 0, rows, :] = (dot_tn(d_scores, qkv[head, 1]) * scale_q).astype(LOW)
                return 0

            lax.fori_loop(0, 4, tile_step, 0)
            qkv[head, 1] = (acc[0] * scale_q).astype(LOW)
            qkv[head, 2] = acc[1].astype(LOW)
            return 0

        early[3].wait()

        def column_half(zi, _):
            def one_head(number, _):
                return attend(4 * zi + number, 0)

            lax.fori_loop(0, 4, one_head, 0)

            def lay(step, _):
                rows = pl.ds(pl.multiple_of(step * 128, 128), 128)
                narrow = lanes(128) < HD
                parts = [
                    jnp.where(narrow, qkv[zi * 4 + n // 3, n % 3, rows, :].astype(F32), 0.0)
                    for n in range(12)
                ]
                for tile, value in enumerate(pack(parts, 0, 7)):
                    dpk[zi, rows, 128 * tile : 128 * tile + 128] = value.astype(LOW)
                return 0

            lax.fori_loop(0, 8, lay, 0)

            def head_grad(tile, _):
                some = pl.ds(pl.multiple_of(384 * tile, 128), 384)
                value = dot_tn(h1[0, :, some], dpk[zi, 0:mid, :])
                value = value + dot_tn(h1[1, :, some], dpk[zi, mid:length, :])
                g0[zi, some, 0:768] = value[:, 0:768].astype(LOW)
                both = value[:, 768:896] + g0[zi, some, 768:896].astype(F32)
                g0[zi, some, 768:896] = both.astype(LOW)
                return 0

            lax.fori_loop(0, 3, head_grad, 0)
            for o in range(2):
                far_send(0, zi, o).start()
            for o in range(2):
                plain_send(0, zi, o).start()
            return 0

        lax.fori_loop(0, 2, column_half, 0)

        for block in range(2):
            load(x_in.at[block], rm.at[block], 5 + block).start()
        for block in range(2):
            exchange(sb.at[block], rb.at[block], block).wait_send()
        for step in range(4):
            tile = (2 * (1 - core) + step) % 4
            rows = pl.ds(pl.multiple_of(tile * 256, 256), 256)
            value = dot_nt(dpk[0, rows, :], w0[0, :, 0:896])
            value = value + dot_nt(dpk[1, rows, :], w0[1, :, 0:896])
            if step < 2:
                sb[step] = value.astype(LOW)
                exchange(sb.at[step], rb.at[step], 6 + step).start()
            else:
                zb[step - 2] = value
            if step == 1:
                settle_pair(0, 0)
        relay_pair(0, 1)
        merge_pair(0, 0)
        for block in range(2):
            give_back(block, 0, False)
            load(x_in.at[block], rm.at[block], 5 + block).wait()
            exchange(sb.at[block], rb.at[block], 6 + block).wait_recv()
            scale1 = 1.0 + mod[block, 1:2, :]

            def norm_first(step, sums_now):
                at_row = pl.ds(pl.multiple_of(step * 128, 128), 128)
                d_norm = zb[block, at_row, :] + rb[block, at_row, :].astype(F32)
                normed, spread = layer_norm(rm[block, at_row, :].astype(F32))
                d_input = yb[block, at_row, :] + norm_back(d_norm * scale1, normed, spread)
                ob[block, at_row, :] = d_input.astype(LOW)
                terms = (d_norm, d_norm * normed)
                return tuple(
                    now + jnp.sum(term, axis=0, keepdims=True) for now, term in zip(sums_now, terms)
                )

            zero = jnp.zeros((1, gb.shape[1]), F32)
            totals = lax.fori_loop(0, 2, norm_first, (zero,) * 2)
            for place, value in zip((0, 1), totals):
                sums[block, place : place + 1, :] = value
            give_back(block, 1, True)

        blocks = []
        for number in range(6):
            value = select[0][:, 0:1] * sums[0, number : number + 1, :]
            blocks.append(value + select[1][:, 0:1] * sums[1, number : number + 1, :])
        chunks = to_chunks(*blocks[0:3]) + to_chunks(*blocks[3:6])
        for number in range(4):
            dc[number] = chunks[number]

        def each_chunk(start):
            for number in range(4):
                here = jnp.logical_and(half == core, line == number)
                dst, send, recv = nr.at[lane, core], dcs.at[number], dcr.at[lane, core]
                if start:
                    move(dc.at[number], dst, send, recv, at.base + half, number, here)
                else:

                    @pl.when(jnp.logical_not(here))
                    def _():
                        remote(dc.at[number], dst, send, recv, at.base + half, number).wait_send()

        def each_row(start):
            for step in range(1, 8):
                other = (dp + step) % 8
                copy = remote(da.at[dp], da.at[dp], das.at[step], dar.at[dp], other, line)
                copy.start() if start else copy.wait_send()

        each_chunk(True)

        settle_pair(0, 1)
        for zi in range(2):
            for o in range(2):
                pltpu.make_async_copy(dc.at[0], nr.at[zi, o], dcr.at[zi, o]).wait()
        da[dp] = (nr[0, 0] + nr[0, 1]) + (nr[1, 0] + nr[1, 1])
        each_row(True)
        merge_pair(0, 1)
        for step in range(1, 8):
            other = (dp + step) % 8
            pltpu.make_async_copy(da.at[other], da.at[other], dar.at[other]).wait()
        value = jnp.concatenate([da[n] for n in range(8)], axis=0)
        g_bias[...] = jnp.sum(value, axis=0, keepdims=True)
        g_ada[...] = lax.dot_general(
            cond[...].astype(LOW).astype(F32), value, (((0,), (0,)), ((), ())), precision=HIGH, preferred_element_type=F32
        )
        for u in range(3):
            finish(u)

        each_chunk(False)
        each_row(False)
        for u in range(3):
            for zi in range(2):
                for o in range(2):
                    far_send(u, zi, o).wait_send()
                    plain_send(u, zi, o).wait_send()
                    relay_send(u, zi, o).wait_send()
                    settled(u, zi, o)
        for block in range(2):
            give_back(block, 1, False)
            exchange(sm.at[block], rm.at[block], 2 + block).wait_send()
            part = db.at[core, pl.ds(block * 256, 256)]
            exchange(part, part, 4 + block).wait_send()
            exchange(sb.at[block], rb.at[block], 6 + block).wait_send()
        for kind in range(2):
            dst = (out_tok, out_dtok)[kind]
            for slot in range(2):
                source = 2 * core + slot
                here = jnp.logical_and(source == line, half == core)

                @pl.when(jnp.logical_not(here))
                def _():
                    pltpu.make_async_copy(dst.at[slot], dst.at[slot], tr.at[kind, slot]).wait()

    pl.run_scoped(
        attention_phase,
        pltpu.VMEM((2, 8 * rows_u, cols), LOW),
        pltpu.VMEM((2, mid, cols), LOW),
        pltpu.VMEM((8, 3, length, 128), LOW),
        pltpu.VMEM((2, length, mid // 2), LOW),
        pltpu.VMEM((2, length, 896), LOW),
        pltpu.VMEM((8, length, 128), LOW),
        pltpu.VMEM((2, 8 * rows_u, cols), LOW),
        pltpu.VMEM((2, mid // 2, cols), F32),
        pltpu.VMEM((mid // 2, cols), LOW),
        pltpu.VMEM((2, length, 128), F32),
    )


def run_back(*args):
    rows, part = args[-1].shape[1], args[7].shape[1]
    length, cols = args[0].shape[1:]
    chunk = 6 * cols // 4
    shape = jax.ShapeDtypeStruct
    vmem = pl.BlockSpec(memory_space=pltpu.VMEM)
    outs = (
        shape((2, part, cols), LOW),
        shape((2, part, cols), LOW),
        shape((3, 3, rows, cols), LOW),
        shape((3, 2, 2, rows, cols), LOW),
        shape((2, 8 * rows, cols), LOW),
        shape((rows, chunk), F32),
        shape((1, chunk), F32),
    )
    three = DMA((3, 2, 2))
    low = pltpu.VMEM((2, part, cols), LOW)
    return pl.pallas_call(
        back_kernel,
        out_shape=outs,
        in_specs=[ANY] * 16 + [vmem] * 5,
        out_specs=(ANY,) * 5 + (vmem,) * 2,
        scratch_shapes=[
            pltpu.VMEM((2, 8, cols), F32),
            pltpu.VMEM((2, 2 * part, cols), LOW),
            pltpu.VMEM((2, part, cols), F32),
            pltpu.VMEM((2, part, cols), F32),
            low,
            low,
            low,
            low,
            low,
            pltpu.VMEM((3, 2, 2, rows, cols), LOW),
            pltpu.VMEM((2, 3, 2, 2, rows, cols), LOW),
            pltpu.VMEM((4, rows, cols), LOW),
            pltpu.VMEM((4, 8, chunk), F32),
            pltpu.VMEM((2, 2, 8, chunk), F32),
            pltpu.VMEM((8, 8, chunk), F32),
            three,
            three,
            DMA((2, 3, 2, 2)),
            DMA((2, 3, 2, 2)),
            three,
            DMA((3, 3)),
            three,
            DMA((8,)),
            DMA((8,)),
            DMA((2, 2)),
            DMA((2, 2)),
            DMA((8,)),
            DMA((4,)),
            DMA((2,)),
            DMA((4,)),
            DMA((2, 2)),
            DMA((8,)),
            DMA((8,)),
        ],
        compiler_params=pltpu.CompilerParams(
            collective_id=1, has_side_effects=True, vmem_limit_bytes=63 << 20
        ),
    )(*args)


def fast_body(
    tokens,
    time_embed,
    segments,
    micro_order,
    head_mask,
    group_mask,
    keep_route,
    w_qkv,
    w_proj,
    w_fc1,
    w_fc2,
    w_ada,
    b_ada,
    cotangent,
):
    width = tokens.shape[2]
    length = segments.shape[1]
    qcols = w_qkv.shape[1]
    swap = micro_order[:, None] == 1

    lines = jnp.concatenate(
        [
            jnp.where(swap, head_mask[1:2], head_mask[0:1]),
            jnp.where(swap, group_mask[1:2], group_mask[0:1]),
            segments[:, :: length // 4],
            jnp.zeros((2, 116), jnp.int32),
        ],
        axis=1,
    )
    meta = jnp.concatenate(
        [keep_route.reshape(4, 128), lines, jnp.zeros((2, 128), jnp.int32)], axis=0
    ).astype(jnp.float32)
    te = time_embed.reshape(8, 8, width // 8).transpose(1, 0, 2).astype(jnp.float32)
    whead = jnp.concatenate([w_qkv, w_proj], axis=1)
    (
        full_fc2,
        full_fc1,
        head_w,
        dealt,
        dealt_grad,
        h_first,
        qkv,
        probs,
        att,
        first,
        branch,
        h_second,
        d_mlp,
        act,
        slope,
        grad_fc2,
        cond,
        mod,
        gains,
        _,
        kept,
        select,
    ) = run_front(whead, w_fc1, w_fc2, tokens, cotangent, meta, te, w_ada, b_ada[None, :])
    result, d_input, grads, _, _, g_ada, g_bias = run_back(
        act,
        slope,
        d_mlp,
        h_second,
        full_fc1,
        full_fc2.reshape(full_fc1.shape),
        grad_fc2,
        first,
        branch,
        dealt,
        dealt_grad,
        h_first,
        qkv,
        probs,
        att,
        head_w,
        mod,
        gains,
        kept,
        select,
        cond,
    )
    total = jnp.sum(grads.astype(jnp.float32), axis=1)
    return (
        result,
        d_input,
        total[0, :, :qcols],
        total[0, :, qcols:],
        total[1],
        total[2],
        g_ada,
        g_bias[0],
    )


def solution(mesh):
    placed = (
        P("dp", "tensor", None),
        P("dp", None, None),
        P("dp", None),
        P("dp"),
        P("dp", "tensor"),
        P("dp", "tensor"),
        P("dp", "tensor"),
        P("dp", "tensor"),
        P("dp", "tensor"),
        P("dp", "tensor"),
        P("dp", "tensor"),
        P("dp", "tensor"),
        P("tensor"),
        P("dp", "tensor", None),
    )
    return jax.shard_map(
        fast_body if mesh.shape["dp"] == 8 and mesh.shape["tensor"] == 4 else body,
        mesh=mesh,
        in_specs=placed,
        out_specs=(
            P("dp", "tensor", None),
            P("dp", "tensor", None),
            P("dp", "tensor"),
            P("dp", "tensor"),
            P("dp", "tensor"),
            P("dp", "tensor"),
            P("dp", "tensor"),
            P("tensor"),
        ),
        check_vma=False,
    )
```

```python
import jax
import jax.numpy as jnp
from jax import lax
from jax.experimental import pallas as pl
from jax.experimental.pallas import tpu as pltpu
from jax.sharding import PartitionSpec as P

HD = 72
FF = 4608
GROUPS = 16


EPSILON = 1e-06
HIGH = lax.Precision.HIGHEST


def layer_norm(values):
    middle = jnp.mean(values, axis=-1, keepdims=True)
    centred = values - middle
    spread = jnp.mean(centred * centred, axis=-1, keepdims=True)
    factor = lax.rsqrt(spread + EPSILON)
    return (centred * factor, factor)


def norm_back(grad, normed, factor):
    inner = (
        grad
        - jnp.mean(grad, axis=-1, keepdims=True)
        - normed * jnp.mean(grad * normed, axis=-1, keepdims=True)
    )
    return factor * inner


def contract_rows(left, right):
    return lax.dot_general(
        left, right, (((0,), (0,)), ((), ())), preferred_element_type=jnp.float32
    )


def contract_cols(left, right):
    return lax.dot_general(
        left, right, (((1,), (1,)), ((), ())), preferred_element_type=jnp.float32
    )


def score_block(query_block, keys, seg_block, seg_ids):
    scores = jnp.einsum(
        "qhe,khe->hqk", query_block, keys, preferred_element_type=jnp.float32
    ) * HD ** (-0.5)
    same = seg_block[:, None] == seg_ids[None, :]
    return jnp.where(same[None], scores, -1e30)


def attention_forward(query, keys, values, seg_ids):
    length = query.shape[0]
    block = min(512, length)
    outs = []
    totals = []
    for offset in range(0, length, block):
        scores = score_block(
            query[offset : offset + block], keys, seg_ids[offset : offset + block], seg_ids
        )
        peak = jnp.max(scores, axis=-1, keepdims=True)
        denom = jnp.sum(jnp.exp(scores - peak), axis=-1, keepdims=True)
        log_total = peak + jnp.log(denom)
        probs = jnp.exp(scores - log_total).astype(jnp.bfloat16)
        outs.append(jnp.einsum("hqk,khe->qhe", probs, values, preferred_element_type=jnp.float32))
        totals.append(log_total)
    return (jnp.concatenate(outs, axis=0), totals)


def attention_backward(query, keys, values, seg_ids, totals, d_attn):
    length = query.shape[0]
    block = min(512, length)
    scale = HD ** (-0.5)
    d_keys = jnp.zeros(keys.shape, jnp.float32)
    d_values = jnp.zeros(values.shape, jnp.float32)
    d_queries = []
    for number, offset in enumerate(range(0, length, block)):
        query_block = query[offset : offset + block]
        scores = score_block(query_block, keys, seg_ids[offset : offset + block], seg_ids)
        probs = jnp.exp(scores - totals[number])
        grad_block = d_attn[offset : offset + block]
        d_values = d_values + jnp.einsum(
            "hqk,qhe->khe",
            probs.astype(jnp.bfloat16),
            grad_block,
            preferred_element_type=jnp.float32,
        )
        d_probs = jnp.einsum("qhe,khe->hqk", grad_block, values, preferred_element_type=jnp.float32)
        d_scores = (probs * (d_probs - jnp.sum(probs * d_probs, axis=-1, keepdims=True))).astype(
            jnp.bfloat16
        )
        d_queries.append(
            jnp.einsum("hqk,khe->qhe", d_scores, keys, preferred_element_type=jnp.float32) * scale
        )
        d_keys = (
            d_keys
            + jnp.einsum("hqk,qhe->khe", d_scores, query_block, preferred_element_type=jnp.float32)
            * scale
        )
    stacked = jnp.stack([jnp.concatenate(d_queries, axis=0), d_keys, d_values], axis=2)
    return stacked.astype(jnp.bfloat16).reshape(length, -1)


def body(
    tokens,
    time_embed,
    segments,
    micro_order,
    head_mask,
    group_mask,
    keep_route,
    w_qkv,
    w_proj,
    w_fc1,
    w_fc2,
    w_ada,
    b_ada,
    cotangent,
):
    micro = tokens.shape[0]
    local_rows = tokens.shape[1]
    length = segments.shape[1]
    heads_here = head_mask.shape[1]
    segs = time_embed.shape[1]
    tensor_index = lax.axis_index("tensor")
    chooser = (micro_order[:, None] == jnp.arange(micro, dtype=jnp.int32)[None, :]).astype(
        jnp.float32
    )
    head_sel = jnp.dot(chooser, head_mask.astype(jnp.float32), precision=HIGH)
    group_sel = jnp.repeat(
        jnp.dot(chooser, group_mask.astype(jnp.float32), precision=HIGH), FF // GROUPS, axis=1
    )
    keep_float = keep_route.astype(jnp.float32)

    def reduce_grads(grad_qkv, grad_proj, grad_fc1, grad_fc2, grad_ada):
        return (
            lax.psum_scatter(
                grad_qkv.astype(jnp.bfloat16), "dp", scatter_dimension=0, tiled=True
            ).astype(jnp.float32),
            lax.psum_scatter(
                grad_proj.astype(jnp.bfloat16), "dp", scatter_dimension=0, tiled=True
            ).astype(jnp.float32),
            lax.psum_scatter(
                grad_fc1.astype(jnp.bfloat16), "dp", scatter_dimension=0, tiled=True
            ).astype(jnp.float32),
            lax.psum_scatter(
                grad_fc2.astype(jnp.bfloat16), "dp", scatter_dimension=0, tiled=True
            ).astype(jnp.float32),
            lax.psum_scatter(
                grad_ada.astype(jnp.bfloat16), "dp", scatter_dimension=0, tiled=True
            ).astype(jnp.float32),
        )

    shard_shapes = [w.shape for w in (w_qkv, w_proj, w_fc1, w_fc2, w_ada)]
    start_acc = tuple((jnp.zeros(shape, jnp.float32) for shape in shard_shapes))

    def slot_step(carry, items):
        acc, bias_acc = carry
        slot_tokens, slot_grad, seg_ids, embed, hmask, gcols, keepf = items
        full = (
            lax.all_gather(w_qkv, "dp", axis=0, tiled=True),
            lax.all_gather(w_proj, "dp", axis=0, tiled=True),
            lax.all_gather(w_fc1, "dp", axis=0, tiled=True),
            lax.all_gather(w_fc2, "dp", axis=0, tiled=True),
            lax.all_gather(w_ada, "dp", axis=0, tiled=True),
        )
        full_qkv, full_proj, full_fc1, full_fc2, full_ada = full
        seg_local = lax.dynamic_slice_in_dim(seg_ids, tensor_index * local_rows, local_rows)
        scond = jax.nn.silu(embed.astype(jnp.float32)).astype(jnp.bfloat16)
        part_mods = jnp.dot(scond, full_ada, preferred_element_type=jnp.float32) + b_ada[None, :]
        mods = lax.all_gather(part_mods, "tensor", axis=1, tiled=True)
        onehot = (seg_local[:, None] == jnp.arange(segs, dtype=jnp.int32)[None, :]).astype(
            jnp.float32
        )
        modtok = jnp.dot(onehot, mods, precision=HIGH)
        shift1, scale1, gate1, shift2, scale2, gate2 = jnp.split(modtok, 6, axis=1)
        token_vals = slot_tokens.astype(jnp.float32)
        normed1, factor1 = layer_norm(token_vals)
        h_first = lax.all_gather(
            (normed1 * (1.0 + scale1) + shift1).astype(jnp.bfloat16), "tensor", axis=0, tiled=True
        )
        packed = jnp.dot(h_first, full_qkv, preferred_element_type=jnp.float32).astype(jnp.bfloat16)
        packed = packed.reshape(length, heads_here, 3, HD)
        query = packed[:, :, 0]
        keys = packed[:, :, 1]
        values = packed[:, :, 2]
        outs, totals = attention_forward(query, keys, values, seg_ids)
        attn = (outs * hmask[None, :, None]).astype(jnp.bfloat16).reshape(length, heads_here * HD)
        branch = lax.psum_scatter(
            contract_cols(attn, full_proj).astype(jnp.bfloat16),
            "tensor",
            scatter_dimension=0,
            tiled=True,
        ).astype(jnp.float32)
        first = token_vals + gate1 * branch
        normed2, factor2 = layer_norm(first)
        h_second = lax.all_gather(
            (normed2 * (1.0 + scale2) + shift2).astype(jnp.bfloat16), "tensor", axis=0, tiled=True
        )
        upward = jnp.dot(h_second, full_fc1, preferred_element_type=jnp.float32)
        gelu_val, gelu_pull = jax.vjp(lambda inner: jax.nn.gelu(inner, approximate=True), upward)
        act = (gelu_val * gcols[None, :]).astype(jnp.bfloat16)
        mlp = lax.psum_scatter(
            contract_cols(act, full_fc2).astype(jnp.bfloat16),
            "tensor",
            scatter_dimension=0,
            tiled=True,
        ).astype(jnp.float32)
        keep_col = keepf[:, None]
        result = (first + gate2 * keep_col * mlp).astype(jnp.bfloat16)
        grad_out = slot_grad.astype(jnp.float32)
        d_mlp = lax.all_gather(
            (gate2 * keep_col * grad_out).astype(jnp.bfloat16), "tensor", axis=0, tiled=True
        )
        grad_fc2 = contract_rows(d_mlp, act)
        d_act = jnp.dot(d_mlp, full_fc2, preferred_element_type=jnp.float32)
        d_up = gelu_pull(d_act * gcols[None, :])[0].astype(jnp.bfloat16)
        grad_fc1 = contract_rows(h_second, d_up)
        d_second = lax.psum_scatter(
            contract_cols(d_up, full_fc1).astype(jnp.bfloat16),
            "tensor",
            scatter_dimension=0,
            tiled=True,
        ).astype(jnp.float32)
        d_first = grad_out + norm_back(d_second * (1.0 + scale2), normed2, factor2)
        d_branch = lax.all_gather(
            (gate1 * d_first).astype(jnp.bfloat16), "tensor", axis=0, tiled=True
        )
        grad_proj = contract_rows(d_branch, attn)
        d_attn = jnp.dot(d_branch, full_proj, preferred_element_type=jnp.float32).astype(
            jnp.bfloat16
        )
        d_attn = d_attn.reshape(length, heads_here, HD) * hmask[None, :, None].astype(jnp.bfloat16)
        d_packed = attention_backward(query, keys, values, seg_ids, totals, d_attn)
        grad_qkv = contract_rows(h_first, d_packed)
        d_h_first = lax.psum_scatter(
            contract_cols(d_packed, full_qkv).astype(jnp.bfloat16),
            "tensor",
            scatter_dimension=0,
            tiled=True,
        ).astype(jnp.float32)
        d_input = d_first + norm_back(d_h_first * (1.0 + scale1), normed1, factor1)
        d_modtok = jnp.concatenate(
            [
                d_h_first,
                d_h_first * normed1,
                d_first * branch,
                d_second,
                d_second * normed2,
                grad_out * keep_col * mlp,
            ],
            axis=1,
        )
        part_dmods = lax.dot_general(onehot, d_modtok, (((0,), (0,)), ((), ())), precision=HIGH)
        d_mods = lax.psum_scatter(
            part_dmods.astype(jnp.bfloat16), "tensor", scatter_dimension=1, tiled=True
        ).astype(jnp.float32)
        grad_ada = jnp.dot(scond.astype(jnp.float32).T, d_mods, precision=HIGH)
        bias_acc = bias_acc + jnp.sum(d_mods, axis=0)
        parts = reduce_grads(grad_qkv, grad_proj, grad_fc1, grad_fc2, grad_ada)
        acc = tuple((held + piece for held, piece in zip(acc, parts)))
        return ((acc, bias_acc), (result, d_input.astype(jnp.bfloat16)))

    start_bias = jnp.zeros(b_ada.shape, jnp.float32)
    (acc, bias_acc), (results, d_tokens) = lax.scan(
        slot_step,
        (start_acc, start_bias),
        (tokens, cotangent, segments, time_embed, head_sel, group_sel, keep_float),
    )
    g_bias = lax.psum(bias_acc, "dp")
    return (results, d_tokens, acc[0], acc[1], acc[2], acc[3], acc[4], g_bias)


MESH = pl.DeviceIdType.MESH
ANY = pl.BlockSpec(memory_space=pl.ANY)
DMA = pltpu.SemaphoreType.DMA


class Place:
    def __init__(self):
        self.dp = lax.axis_index("dp")
        self.line = lax.axis_index("tensor")
        self.core = self.dp % 2
        self.base = self.dp - self.core
        self.half = self.line // 2
        x, y = (self.dp // 2) % 2, self.dp // 4
        self.dp_x = self.dp + 2 * (1 - 2 * x)
        self.dp_y = self.dp + 4 * (1 - 2 * y)
        self.base_x = self.dp_x - self.core
        self.base_y = self.dp_y - self.core
        self.base_far = self.base_x + self.base_y - self.base

    def barrier(self):
        bar = pltpu.get_barrier_semaphore()
        spot = self.core * 4 + self.line
        for step in range(1, 8):
            other = (spot + step) % 8
            pl.semaphore_signal(
                bar,
                inc=1,
                device_id=(self.base + other // 4, other % 4),
                device_id_type=MESH,
            )
        for step in range(1, 8):
            other = (self.dp + step) % 8
            pl.semaphore_signal(bar, inc=1, device_id=(other, self.line), device_id_type=MESH)
        pl.semaphore_wait(bar, 14)


def remote(src, dst, send, recv, dp, line):
    return pltpu.make_async_remote_copy(
        src_ref=src,
        dst_ref=dst,
        send_sem=send,
        recv_sem=recv,
        device_id=(dp, line),
        device_id_type=MESH,
    )


def move(src, dst, send, recv, dp, line, here):
    @pl.when(here)
    def _():
        pltpu.make_async_copy(src, dst, recv).start()

    @pl.when(jnp.logical_not(here))
    def _():
        remote(src, dst, send, recv, dp, line).start()


LOG2E = 1.4426950408889634
LOW = jnp.bfloat16
F32 = jnp.float32
SHADE = -1e30


def dot_nn(left, right):
    return jnp.dot(left, right, preferred_element_type=F32)


def dot_nt(left, right):
    return lax.dot_general(left, right, (((1,), (1,)), ((), ())), preferred_element_type=F32)


def dot_tn(left, right):
    return lax.dot_general(left, right, (((0,), (0,)), ((), ())), preferred_element_type=F32)


def lanes(rows):
    return lax.broadcasted_iota(jnp.int32, (rows, 128), 1)


def window(value, start):
    tile, rest = start // 128, start % 128
    here = value[:, 128 * tile : 128 * tile + 128]
    if rest == 0:
        return here
    here = pltpu.roll(here, 128 - rest, 1)
    if rest + HD <= 128:
        return here
    after = pltpu.roll(value[:, 128 * tile + 128 : 128 * tile + 256], 128 - rest, 1)
    return jnp.where(lanes(value.shape[0]) < 128 - rest, here, after)


def pack(parts, start, tiles):
    rows = parts[0].shape[0]
    lane = lanes(rows)
    out = []
    for tile in range(tiles):
        total = jnp.zeros((rows, 128), F32)
        for number, part in enumerate(parts):
            low = start + HD * number - 128 * tile
            if low >= 128 or low + HD <= 0:
                continue
            moved = pltpu.roll(part, low % 128, 1) if low % 128 else part
            inside = jnp.logical_and(lane >= low, lane < low + HD)
            total = jnp.where(inside, moved, total)
        out.append(total)
    return out


def turned(value, tile):
    start = 128 * tile
    stop = min(start + 128, value.shape[1])
    part = value[:, start:stop]
    if stop - start < 128:
        part = jnp.concatenate([part, jnp.zeros((part.shape[0], 64), F32)], axis=1)
    return pltpu.roll(part, 64, 1)


def to_blocks(even, odd):
    low = lanes(even.shape[0]) < 64
    turn = [turned(odd, tile) for tile in range(14)]
    tail = jnp.concatenate([even[:, 1664:1728], jnp.zeros((even.shape[0], 64), F32)], axis=1)
    one = [even[:, 0:1152]]
    two = [even[:, 1152:1664], jnp.where(low, tail, turn[0])]
    two += [jnp.where(low, turn[t], turn[t + 1]) for t in range(4)]
    three = [jnp.where(low, turn[t], turn[t + 1]) for t in range(4, 13)]
    return [jnp.concatenate(parts, axis=1) for parts in (one, two, three)]


def to_chunks(one, two, three):
    low = lanes(one.shape[0]) < 64
    even = jnp.concatenate([one, two[:, 0:576]], axis=1)
    turn = [turned(two, tile) for tile in range(4, 9)] + [turned(three, t) for t in range(9)]
    odd = [jnp.where(low, turn[t], turn[t + 1]) for t in range(13)]
    return even, jnp.concatenate(odd + [turn[13][:, 0:64]], axis=1)


def front_kernel(
    wh,
    w1,
    w2,
    tok,
    cot,
    meta,
    te,
    wa,
    ba,
    weights,
    w1_out,
    head_out,
    x_out,
    g_out,
    h1_out,
    qkv_out,
    pt_out,
    att_out,
    x1_out,
    br_out,
    h2_out,
    dm_out,
    act_out,
    gp_out,
    gf_out,
    cond,
    mod,
    gains,
    groups,
    kept,
    select,
    xt,
    w0,
    h1,
    qkv,
    obuf,
    pt,
    gst,
    att,
    sb,
    rb,
    br,
    x1,
    h2,
    ct,
    dm,
    w1v,
    act,
    gp,
    gc,
    mt,
    te_all,
    pb,
    pr,
    mine,
    mr,
    feat,
    zs,
    zr,
    fs,
    ns,
    nr,
    ds,
    dr,
    ts,
    tr,
    es,
    er,
    ls,
    ps,
    gs,
    ms,
    mrs,
    tes,
    ter,
    pbs,
    pbr,
    mms,
    mmr,
):
    at = Place()
    dp, line, core, half = at.dp, at.line, at.core, at.half
    units = (wh, w1, w2)
    lane = line % 2
    rows_u = w1.shape[0]
    sib = at.base + 1 - core
    at.barrier()

    def spot(u, zi, row):
        if u < 2:
            return (w0, w1v)[u].at[zi, pl.ds(pl.multiple_of(row * rows_u, 16), rows_u)]
        return weights.at[zi, row]

    def deal(kind, start):
        src, dst = ((tok, xt), (cot, ct))[kind]
        for slot in range(2):
            there = 2 * core + slot
            here = jnp.logical_and(half == core, there == line)
            send, recv = ts.at[kind, slot], tr.at[kind, lane]
            if start:
                move(src.at[slot], dst.at[lane], send, recv, at.base + half, there, here)
            else:

                @pl.when(jnp.logical_not(here))
                def _():
                    remote(
                        src.at[slot], dst.at[lane], send, recv, at.base + half, there
                    ).wait_send()

    def deal_arrive(kind):
        src, dst = ((tok, xt), (cot, ct))[kind]
        for block in range(2):
            pltpu.make_async_copy(src.at[0], dst.at[block], tr.at[kind, block]).wait()

    def source(u, start):
        dst = spot(u, lane, dp)
        recv = zr.at[u, lane, core]
        home = at.base + half
        if start:
            move(units[u], dst, zs.at[u, 0], recv, home, line, half == core)
        else:

            @pl.when(half != core)
            def _():
                remote(units[u], dst, zs.at[u, 0], recv, home, line).wait_send()

        for which, step in ((1, 1), (2, -1)):
            inside = line < 3 if step == 1 else line > 0

            @pl.when(inside)
            def _():
                copy = remote(units[u], dst, zs.at[u, which], recv, home, line + step)
                copy.start() if start else copy.wait_send()

    first = jnp.where(core == 0, jnp.where(line == 0, 0, 1), jnp.where(line == 3, 1, 0))

    def z_stage(u, k, other, start):
        zi = first + k - 2 * first * k
        origin = 2 * core + zi
        ref = spot(u, zi, at.base + other)
        if start:
            pltpu.make_async_copy(w1, ref, zr.at[u, zi, other]).wait()
        up = jnp.logical_and(origin < line, line < 3)
        down = jnp.logical_and(origin > line, line > 0)
        for go, step in ((up, 1), (down, -1)):

            @pl.when(go)
            def _():
                copy = remote(
                    ref, ref, fs.at[u, zi, other], zr.at[u, zi, other], dp, line + step
                )
                copy.start() if start else copy.wait_send()

        for which, near in ((0, at.dp_x), (1, at.dp_y)):
            copy = remote(
                ref, ref, ns.at[which, u, zi, other], nr.at[which, u, zi, other], near, line
            )
            copy.start() if start else copy.wait_send()

    def far_stage(u, zi, other, start):
        base = at.base_x + other * (at.base_y - at.base_x)
        near = at.dp_y + other * (at.dp_x - at.dp_y)
        ref = spot(u, zi, base + other)
        if start:
            pltpu.make_async_copy(w1, ref, nr.at[other, u, zi, other]).wait()
        copy = remote(ref, ref, ds.at[u, zi, other], dr.at[u, zi, other], near, line)
        copy.start() if start else copy.wait_send()

    def last_stage(u, zi, other):
        base = at.base_y + other * (at.base_x - at.base_y)
        ref = spot(u, zi, base + other)
        pltpu.make_async_copy(w1, ref, nr.at[1 - other, u, zi, other]).wait()
        ref = spot(u, zi, at.base_far + other)
        pltpu.make_async_copy(w1, ref, dr.at[u, zi, other]).wait()

    def pump(number):
        k, other = (number % 4) // 2, number % 2
        for quarter in range(4):
            u, stage = ((1, z_stage), (2, z_stage), (1, far_stage), (2, far_stage))[quarter]

            @pl.when(number // 4 == quarter)
            def _():
                stage(u, k, other, True)

    def keep(src, dst, number):
        return pltpu.make_async_copy(src, dst, ls.at[number])

    def each_column(start):
        for step in range(1, 8):
            other = (core * 4 + line + step) % 8
            copy = remote(
                meta, mt.at[core * 4 + line], ms.at[step], mrs.at[core * 4 + line],
                at.base + other // 4, other % 4,
            )
            copy.start() if start else copy.wait_send()

    def each_row(src, dst, send, recv, start, pieces):
        for step in range(1, 8):
            other = (dp + step) % 8
            part = src.at[other] if pieces else src
            copy = remote(part, dst.at[dp], send.at[step], recv.at[dp], other, line)
            copy.start() if start else copy.wait_send()

    def row_arrive(dst, recv):
        for step in range(1, 8):
            other = (dp + step) % 8
            pltpu.make_async_copy(dst.at[other], dst.at[other], recv.at[other]).wait()

    each_row(te, te_all, tes, ter, True, True)
    each_column(True)
    te_all[dp] = te[dp]
    mt[core * 4 + line] = meta[...]

    source(0, True)
    row_arrive(te_all, ter)
    for number in range(8):
        spread = te_all[number]
        cond[8 * number : 8 * number + 8, :] = spread * (1.0 / (1.0 + jnp.exp(-spread)))
    value = dot_nn(cond[...].astype(LOW), wa[...])
    for number in range(8):
        pb[number] = value[8 * number : 8 * number + 8, :]
    each_row(pb, pr, pbs, pbr, True, True)
    deal(0, True)
    pr[dp] = pb[dp]
    for other in range(2):
        z_stage(0, 0, other, True)
    row_arrive(pr, pbr)
    total = ba[...] + pr[0]
    for number in range(1, 8):
        total = total + pr[number]
    mine[...] = total

    def each_slot(start):
        for slot in range(2):
            there = 2 * core + slot
            for to in range(2):
                here = jnp.logical_and(core == to, there == line)
                send, recv = mms.at[slot, to], mmr.at[line]
                if start:
                    move(mine, mr.at[line], send, recv, at.base + to, there, here)
                else:

                    @pl.when(jnp.logical_not(here))
                    def _():
                        remote(mine, mr.at[line], send, recv, at.base + to, there).wait_send()

    each_slot(True)
    for other in range(2):
        z_stage(0, 1, other, True)
    source(1, True)
    deal(1, True)

    for step in range(1, 8):
        other = (core * 4 + line + step) % 8
        pltpu.make_async_copy(meta, mt.at[other], mrs.at[other]).wait()
    one_row = lanes(1)
    spots = (one_row - HD).astype(F32)
    inside = jnp.logical_and(one_row >= HD, one_row < HD + 4)

    def lane_of(row, place):
        return jnp.sum(jnp.where(one_row == place, row, 0.0), axis=1, keepdims=True)

    for zi in range(2):
        info = mt[half * 4 + 2 * core + zi, pl.ds(4 + lane, 1), :]
        for number in range(4):
            head = zi * 4 + number
            gains[head : head + 1, :] = jnp.broadcast_to(lane_of(info, number), (1, 128))
            groups[head : head + 1, :] = jnp.broadcast_to(lane_of(info, 4 + number), (1, 128))
    unit = lax.broadcasted_iota(jnp.int32, (1, gc.shape[1]), 1) // (gc.shape[1] // 4)
    for zi in range(2):
        row = jnp.zeros((1, gc.shape[1]), F32)
        for number in range(4):
            head = zi * 4 + number
            row = jnp.where(unit == number, groups[head : head + 1, 0:1], row)
        gc[8 * zi : 8 * zi + 8, :] = jnp.broadcast_to(row, (8, gc.shape[1]))
    info = mt[half * 4 + line, pl.ds(4 + lane, 1), :]
    for tile in range(4):
        same = jnp.where(spots == lane_of(info, 8 + tile), 1.0, 0.0)
        feat[0, tile : tile + 1, :] = jnp.where(inside, SHADE * (1.0 - same), 0.0)
        feat[1, tile : tile + 1, :] = jnp.where(inside, same, 0.0)
    row_ids = lax.broadcasted_iota(jnp.int32, (8, 128), 0)
    diagonal = lax.broadcasted_iota(jnp.int32, (128, 128), 0) == lanes(128)
    for block in range(2):
        item = jnp.sum(
            jnp.where(one_row == 8 + 2 * core + block, info, 0.0), axis=1, keepdims=True
        )
        hit = row_ids.astype(F32) == item + (4 * lane).astype(F32)
        select[block] = jnp.where(hit, 1.0, 0.0)
        for number in range(2):
            row = mt[half * 4 + 2 * core + block, pl.ds(2 * lane + number, 1), :]
            column = jnp.sum(jnp.where(diagonal, row, 0.0), axis=1, keepdims=True)
            kept[block, 128 * number : 128 * number + 128, :] = jnp.broadcast_to(column, (128, 128))
    for source_line in range(4):
        pltpu.make_async_copy(mine, mr.at[source_line], mmr.at[source_line]).wait()
    for block in range(2):
        weight = select[block][:, 0:1]
        rows = [jnp.sum(weight * mr[n], axis=0, keepdims=True) for n in range(4)]
        pieces = to_blocks(rows[0], rows[1]) + to_blocks(rows[2], rows[3])
        for number, piece in enumerate(pieces):
            mod[block, number : number + 1, :] = piece
        mod[block, 6:8, :] = jnp.zeros((2, mod.shape[2]), F32)

    def exchange(src, dst, number):
        return remote(src, dst, es.at[number], er.at[number], sib, line)

    deal_arrive(0)
    keep(xt, x_out, 0).start()

    for block in range(2):
        shift, scale = mod[block, 0:1, :], 1.0 + mod[block, 1:2, :]

        def norm_first(step, _):
            at_row = pl.ds(pl.multiple_of(step * 128, 128), 128)
            normed, _f = layer_norm(xt[block, at_row, :].astype(F32))
            to_row = pl.ds(pl.multiple_of(block * 256 + step * 128, 128), 128)
            h1[core, to_row, :] = (normed * scale + shift).astype(LOW)
            return 0

        lax.fori_loop(0, 2, norm_first, 0)
        part = h1.at[core, pl.ds(block * 256, 256)]
        exchange(part, part, block).start()
    for zi in range(2):
        for other in range(2):
            far_stage(0, zi, other, True)
    source(2, True)
    for zi in range(2):
        for other in range(2):
            last_stage(0, zi, other)
    keep(w0, head_out, 1).start()

    def project(step, _):
        @pl.when(step >= 2)
        def _():
            part = h1.at[1 - core, pl.ds(pl.multiple_of((step - 2) * 256, 256), 256)]
            pltpu.make_async_copy(part, part, er.at[step - 2]).wait()

        pump(step)
        tile = (2 * core + step) % 4
        rows = h1[tile // 2, pl.ds(pl.multiple_of((tile % 2) * 256, 256), 256), :]
        to_row = pl.ds(pl.multiple_of(tile * 256, 256), 256)
        narrow = lanes(256) < HD
        fills = (feat[0, pl.ds(tile, 1), :], feat[1, pl.ds(tile, 1), :], jnp.zeros((1, 128), F32))
        for zi in range(2):
            value = dot_nn(rows, w0[zi, :, 0:896])
            for number in range(12):
                head, part = zi * 4 + number // 3, number % 3
                piece = jnp.where(narrow, window(value, HD * number), fills[part])
                qkv[head, part, to_row, :] = piece.astype(LOW)
        return 0

    lax.fori_loop(0, 4, project, 0)
    keep(h1, h1_out, 2).start()
    keep(qkv, qkv_out, 3).start()

    factor = HD ** (-0.5) * LOG2E

    def attend(head, _):
        pump(4 + head)
        gain = gains[pl.ds(head, 1), :]

        def tile_step(tile, _):
            rows = pl.ds(pl.multiple_of(tile * 256, 256), 256)
            number = 4 * head + tile
            slot = number % 2
            scores = dot_nt(qkv[head, 1], qkv[head, 0, rows, :])
            peak = jnp.max(scores, axis=0, keepdims=True)
            power = jnp.exp2((scores - peak) * factor)
            total = jnp.sum(power, axis=0, keepdims=True)
            probs = (power * (1.0 / total)).astype(LOW)
            obuf[head, rows, :] = (dot_tn(probs, qkv[head, 2]) * gain).astype(LOW)

            @pl.when(number >= 2)
            def _():
                pltpu.make_async_copy(pt.at[slot], pt_out.at[number - 2], ps.at[slot]).wait()

            pt[slot] = probs
            pltpu.make_async_copy(pt.at[slot], pt_out.at[number], ps.at[slot]).start()
            return 0

        lax.fori_loop(0, 4, tile_step, 0)
        return 0

    lax.fori_loop(0, 8, attend, 0)

    def lay(step, _):
        rows = pl.ds(pl.multiple_of(step * 128, 128), 128)
        for zi in range(2):
            parts = [obuf[zi * 4 + n, rows, :].astype(F32) for n in range(4)]
            for tile, value in enumerate(pack(parts, 96, 3)):
                att[zi, rows, 128 * tile : 128 * tile + 128] = value.astype(LOW)
        return 0

    lax.fori_loop(0, 8, lay, 0)
    keep(att, att_out, 5).start()

    for step in range(4):
        tile = (2 * (1 - core) + step) % 4
        rows = pl.ds(pl.multiple_of(tile * 256, 256), 256)
        value = dot_nt(att[0, rows, :], w0[0, :, 768:1152])
        value = value + dot_nt(att[1, rows, :], w0[1, :, 768:1152])
        if step < 2:
            sb[step] = value.astype(LOW)
            exchange(sb.at[step], rb.at[step], 2 + step).start()
        else:
            br[step - 2] = value
    for block in range(2):
        exchange(sb.at[block], rb.at[block], 2 + block).wait_recv()
        gate = mod[block, 2:3, :]
        shift, scale = mod[block, 3:4, :], 1.0 + mod[block, 4:5, :]

        def norm_second(step, _):
            at_row = pl.ds(pl.multiple_of(step * 128, 128), 128)
            branch = br[block, at_row, :] + rb[block, at_row, :].astype(F32)
            br[block, at_row, :] = branch
            value = xt[block, at_row, :].astype(F32) + gate * branch
            x1[block, at_row, :] = value
            normed, _f = layer_norm(value)
            to_row = pl.ds(pl.multiple_of(block * 256 + step * 128, 128), 128)
            h2[core, to_row, :] = (normed * scale + shift).astype(LOW)
            return 0

        lax.fori_loop(0, 2, norm_second, 0)
        part = h2.at[core, pl.ds(block * 256, 256)]
        exchange(part, part, 4 + block).start()
    keep(x1, x1_out, 6).start()
    keep(br, br_out, 7).start()

    deal_arrive(1)
    keep(ct, g_out, 9).start()
    for block in range(2):
        gate2 = mod[block, 5:6, :]

        def grad_rows(step, _):
            at_row = pl.ds(pl.multiple_of(step * 128, 128), 128)
            value = gate2 * kept[block, at_row, 0:1] * ct[block, at_row, :].astype(F32)
            to_row = pl.ds(pl.multiple_of(block * 256 + step * 128, 128), 128)
            dm[core, to_row, :] = value.astype(LOW)
            return 0

        lax.fori_loop(0, 2, grad_rows, 0)
        part = dm.at[core, pl.ds(block * 256, 256)]
        exchange(part, part, 6 + block).start()

    for block in range(2):
        part = h2.at[1 - core, pl.ds(block * 256, 256)]
        pltpu.make_async_copy(part, part, er.at[4 + block]).wait()
    keep(h2, h2_out, 8).start()
    for block in range(2):
        part = dm.at[1 - core, pl.ds(block * 256, 256)]
        pltpu.make_async_copy(part, part, er.at[6 + block]).wait()
    keep(dm, dm_out, 10).start()

    for zi in range(2):
        for other in range(2):
            last_stage(1, zi, other)
    keep(w1v, w1_out, 11).start()
    ratio = (2.0 / 3.141592653589793) ** 0.5

    def widen(step, _):
        tile, zi = (2 * core + step // 2) % 4, step % 2
        rows = h2[tile // 2, pl.ds(pl.multiple_of((tile % 2) * 256, 256), 256), :]
        value = dot_nn(rows, w1v[zi])
        mask = gc[pl.ds(pl.multiple_of(8 * zi, 8), 8), :][0:1, :]
        square = value * value
        bend = jnp.tanh(ratio * (value + 0.044715 * (value * square)))
        grown = 0.5 * (1.0 + bend)
        slope = grown + 0.5 * value * (1.0 - bend * bend) * (
            ratio * (1.0 + (3.0 * 0.044715) * square)
        )
        to_row = pl.ds(pl.multiple_of(tile * 256, 256), 256)
        act[zi, to_row, :] = (value * grown * mask).astype(LOW)
        gp[zi, to_row, :] = (slope * mask).astype(LOW)

        @pl.when(step < 4)
        def _():
            pump(12 + step)

        return 0

    lax.fori_loop(0, 8, widen, 0)
    keep(act, act_out, 12).start()
    keep(gp, gp_out, 13).start()

    def grad_piece(number):
        rows = pl.ds(384 * (number % 3), 384)
        if not isinstance(number, int):
            rows = pl.ds(pl.multiple_of(384 * (number % 3), 128), 384)
        return gf_out.at[number // 3, rows]

    def fc2_grad(number, _):
        zi, slot = number // 3, number % 3
        some = pl.ds(pl.multiple_of(384 * slot, 128), 384)
        value = dot_tn(dm[0, :, some], act[zi, 0:512, :])
        value = value + dot_tn(dm[1, :, some], act[zi, 512:1024, :])

        @pl.when(number >= 3)
        def _():
            pltpu.make_async_copy(gst.at[slot], grad_piece(number - 3), gs.at[slot]).wait()

        gst[slot] = value.astype(LOW)
        pltpu.make_async_copy(gst.at[slot], grad_piece(number), gs.at[slot]).start()
        return 0

    lax.fori_loop(0, 6, fc2_grad, 0)

    for u in range(3):
        source(u, False)
        for k in range(2):
            for other in range(2):
                z_stage(u, k, other, False)
                far_stage(u, k, other, False)
                if u == 2:
                    last_stage(u, k, other)
    for kind in range(2):
        deal(kind, False)
    each_column(False)
    each_row(te, te_all, tes, ter, False, True)
    each_row(pb, pr, pbs, pbr, False, True)
    each_slot(False)
    for block in range(2):
        own1 = h1.at[core, pl.ds(block * 256, 256)]
        own2 = h2.at[core, pl.ds(block * 256, 256)]
        exchange(own1, own1, block).wait_send()
        exchange(sb.at[block], rb.at[block], 2 + block).wait_send()
        exchange(own2, own2, 4 + block).wait_send()
        own3 = dm.at[core, pl.ds(block * 256, 256)]
        exchange(own3, own3, 6 + block).wait_send()
    pairs = (
        (xt, x_out),
        (w0, head_out),
        (h1, h1_out),
        (qkv, qkv_out),
        (None, None),
        (att, att_out),
        (x1, x1_out),
        (br, br_out),
        (h2, h2_out),
        (ct, g_out),
        (dm, dm_out),
        (w1v, w1_out),
        (act, act_out),
        (gp, gp_out),
    )
    for number, (src, dst) in enumerate(pairs):
        if number != 4:
            keep(src, dst, number).wait()
    for slot in range(2):
        pltpu.make_async_copy(pt.at[slot], pt_out.at[30 + slot], ps.at[slot]).wait()
    for slot in range(3):
        pltpu.make_async_copy(gst.at[slot], grad_piece(3 + slot), gs.at[slot]).wait()


def run_front(wh, w1, w2, tok, cot, meta, te, wa, ba):
    rows, cols = w1.shape
    part = tok.shape[1]
    length = 4 * part
    shape = jax.ShapeDtypeStruct
    vmem = pl.BlockSpec(memory_space=pltpu.VMEM)
    shared = shape((2, 2 * part, cols), LOW)
    single = shape((2, part, cols), F32)
    outs = (
        shape((2, 8, rows, cols), LOW),
        shape((2, 8 * rows, cols), LOW),
        shape((2, 8 * rows, cols), LOW),
        shape(tok.shape, LOW),
        shape(tok.shape, LOW),
        shared,
        shape((8, 3, length, 128), LOW),
        shape((32, length, part), LOW),
        shape((2, length, 384), LOW),
        single,
        single,
        shared,
        shared,
        shape((2, length, cols), LOW),
        shape((2, length, cols), LOW),
        shape((2, 8 * rows, cols), LOW),
    )
    small = (
        shape((64, rows), F32),
        shape((2, 8, cols), F32),
        shape((8, 128), F32),
        shape((8, 128), F32),
        shape((2, part, 128), F32),
        shape((2, 8, 128), F32),
    )
    three = DMA((3, 2, 2))
    return pl.pallas_call(
        front_kernel,
        out_shape=outs + small,
        in_specs=[ANY] * 5 + [vmem] * 4,
        out_specs=(ANY,) * len(outs) + (vmem,) * len(small),
        scratch_shapes=[
            pltpu.VMEM(tok.shape, LOW),
            pltpu.VMEM((2, 8 * rows, cols), LOW),
            pltpu.VMEM((2, 2 * part, cols), LOW),
            pltpu.VMEM((8, 3, length, 128), LOW),
            pltpu.VMEM((8, length, 128), LOW),
            pltpu.VMEM((2, length, part), LOW),
            pltpu.VMEM((3, 384, cols), LOW),
            pltpu.VMEM((2, length, 384), LOW),
            pltpu.VMEM((2, part, cols), LOW),
            pltpu.VMEM((2, part, cols), LOW),
            pltpu.VMEM((2, part, cols), F32),
            pltpu.VMEM((2, part, cols), F32),
            pltpu.VMEM((2, 2 * part, cols), LOW),
            pltpu.VMEM(tok.shape, LOW),
            pltpu.VMEM((2, 2 * part, cols), LOW),
            pltpu.VMEM((2, 8 * rows, cols), LOW),
            pltpu.VMEM((2, length, cols), LOW),
            pltpu.VMEM((2, length, cols), LOW),
            pltpu.VMEM((16, cols), F32),
            pltpu.VMEM((8, 8, 128), F32),
            pltpu.VMEM((8, 8, rows), F32),
            pltpu.VMEM((8, 8, wa.shape[1]), F32),
            pltpu.VMEM((8, 8, wa.shape[1]), F32),
            pltpu.VMEM((8, wa.shape[1]), F32),
            pltpu.VMEM((4, 8, wa.shape[1]), F32),
            pltpu.VMEM((2, 8, 128), F32),
            DMA((3, 3)),
            three,
            three,
            DMA((2, 3, 2, 2)),
            DMA((2, 3, 2, 2)),
            three,
            three,
            DMA((2, 2)),
            DMA((2, 2)),
            DMA((8,)),
            DMA((8,)),
            DMA((14,)),
            DMA((2,)),
            DMA((3,)),
            DMA((8,)),
            DMA((8,)),
            DMA((8,)),
            DMA((8,)),
            DMA((8,)),
            DMA((8,)),
            DMA((2, 2)),
            DMA((4,)),
        ],
        compiler_params=pltpu.CompilerParams(
            collective_id=0, has_side_effects=True, vmem_limit_bytes=60 << 20
        ),
    )(wh, w1, w2, tok, cot, meta, te, wa, ba)


def back_kernel(
    act_in,
    gp_in,
    dm_in,
    h2_in,
    w1_in,
    w2_in,
    gf_in,
    x1_in,
    br_in,
    x_in,
    g_in,
    h1_in,
    qkv_in,
    pt_in,
    att_in,
    head_in,
    mod,
    gains,
    keep_col,
    select,
    cond,
    out_tok,
    out_dtok,
    rz,
    pq,
    gf1,
    g_ada,
    g_bias,
    sums,
    db,
    yb,
    zb,
    sb,
    sm,
    rb,
    rm,
    ob,
    r1,
    rn,
    stage,
    dc,
    nr,
    da,
    s1s,
    s1r,
    nss,
    nsr,
    zss,
    zsr,
    pqr,
    es,
    er,
    ts,
    tr,
    ls,
    gs,
    ps,
    dcs,
    dcr,
    das,
    dar,
):
    at = Place()
    dp, line, core, half = at.dp, at.line, at.core, at.half
    lane = line % 2
    rows_u = stage.shape[1]
    local = {}
    sib = at.base + 1 - core
    scale_q = HD ** (-0.5)
    factor = HD ** (-0.5) * LOG2E

    def load(src, dst, number):
        return pltpu.make_async_copy(src, dst, ls.at[number])

    def exchange(src, dst, number):
        return remote(src, dst, es.at[number], er.at[number], sib, line)

    def grad_ref(u, zi, row):
        here = pl.ds(pl.multiple_of(row * rows_u, 16), rows_u)
        return (local.get("g0"), gf1, gf_in)[u].at[zi, here]

    def base_of(which):
        return at.base_x + which * (at.base_y - at.base_x)

    def near_of(which):
        return at.dp_x + which * (at.dp_y - at.dp_x)

    def far_send(u, zi, o):
        return remote(
            grad_ref(u, zi, at.base_far + o),
            r1.at[u, zi, o],
            s1s.at[u, zi, o],
            s1r.at[u, zi, o],
            near_of(o),
            line,
        )

    def plain_send(u, zi, o):
        return remote(
            grad_ref(u, zi, base_of(o) + o),
            rn.at[o, u, zi, o],
            nss.at[o, u, zi, o],
            nsr.at[o, u, zi, o],
            near_of(o),
            line,
        )

    def relay_send(u, zi, o):
        return remote(
            r1.at[u, zi, o],
            rn.at[1 - o, u, zi, o],
            nss.at[1 - o, u, zi, o],
            nsr.at[1 - o, u, zi, o],
            near_of(1 - o),
            line,
        )

    def fetch(u, zi, o, which):
        row = (base_of(1 - o), at.base)[which] + o
        slot = 2 * which + o
        return pltpu.make_async_copy(grad_ref(u, zi, row), stage.at[slot], gs.at[slot])

    def own_term(u, zi, o, which):
        if u == 0:
            return grad_ref(u, zi, (base_of(1 - o), at.base)[which] + o)
        return stage.at[2 * which + o]

    def relay(u, zi, o):
        far_send(u, zi, o).wait_recv()
        if u:
            fetch(u, zi, o, 0).wait()
        ref = own_term(u, zi, o, 0)
        r1[u, zi, o] = (r1[u, zi, o].astype(F32) + ref[...].astype(F32)).astype(LOW)
        relay_send(u, zi, o).start()

    near_half = half == core
    edge = jnp.logical_or(line == 0, line == 3)
    outer = jnp.logical_and(jnp.logical_not(near_half), edge)
    inner = jnp.logical_and(jnp.logical_not(near_half), jnp.logical_not(edge))

    def column_send(u, zi, o, slot):
        return remote(
            rn.at[0, u, zi, o],
            rz.at[u, slot],
            zss.at[u, zi, o],
            zsr.at[u, slot],
            at.base + o,
            2 * core + zi,
        )

    def settle(u, zi, o):
        for which in range(2):
            there = rn.at[which, u, zi, o]
            pltpu.make_async_copy(there, there, nsr.at[which, u, zi, o]).wait()
        if u:
            fetch(u, zi, o, 1).wait()
        ref = own_term(u, zi, o, 1)
        total = rn[0, u, zi, o].astype(F32) + rn[1, u, zi, o].astype(F32)
        rn[0, u, zi, o] = (total + ref[...].astype(F32)).astype(LOW)
        here = jnp.logical_and(core == o, line == 2 * core + zi)

        @pl.when(here)
        def _():
            pltpu.make_async_copy(rn.at[0, u, zi, o], rz.at[u, lane], zsr.at[u, lane]).start()

        @pl.when(jnp.logical_and(near_half, jnp.logical_not(here)))
        def _():
            column_send(u, zi, o, lane).start()

        @pl.when(outer)
        def _():
            remote(
                rn.at[0, u, zi, o],
                pq.at[u, zi, o],
                zss.at[u, zi, o],
                pqr.at[u, zi, o],
                dp,
                line + 1 - 2 * half,
            ).start()

    def merge(u, zi, o):
        @pl.when(inner)
        def _():
            pltpu.make_async_copy(pq.at[u, zi, o], pq.at[u, zi, o], pqr.at[u, zi, o]).wait()
            copy = pltpu.make_async_copy(pq.at[u, zi, o], stage.at[o], gs.at[o])
            copy.start()
            copy.wait()
            total = rn[0, u, zi, o].astype(F32) + stage[o].astype(F32)
            rn[0, u, zi, o] = total.astype(LOW)
            column_send(u, zi, o, 2).start()

    def settled(u, zi, o):
        here = jnp.logical_and(core == o, line == 2 * core + zi)

        @pl.when(jnp.logical_not(here))
        def _():
            column_send(u, zi, o, 0).wait_send()

    def finish(u):
        for source in range(3):
            ref = rz.at[u, source]
            pltpu.make_async_copy(ref, ref, zsr.at[u, source]).wait()

    def fetch_pair(u, zi, which):
        for o in range(2):
            fetch(u, zi, o, which).start()

    def relay_pair(u, zi):
        for o in range(2):
            relay(u, zi, o)

    def settle_pair(u, zi):
        for o in range(2):
            settle(u, zi, o)

    def merge_pair(u, zi):
        for o in range(2):
            merge(u, zi, o)

    def give_back(block, kind, start):
        dst = (out_tok, out_dtok)[kind].at[lane]
        there = 2 * core + block
        here = jnp.logical_and(half == core, there == line)
        send, recv = ts.at[kind, block], tr.at[kind, lane]
        if start:
            move(ob.at[block], dst, send, recv, at.base + half, there, here)
        else:

            @pl.when(here)
            def _():
                pltpu.make_async_copy(ob.at[block], dst, recv).wait()

            @pl.when(jnp.logical_not(here))
            def _():
                remote(ob.at[block], dst, send, recv, at.base + half, there).wait_send()

    def mlp_phase(act, gp, w1v, w2v, dm, h2, gst):
        pairs = ((dm_in, dm), (w2_in, w2v), (gp_in, gp), (h2_in, h2), (w1_in, w1v), (act_in, act))
        copies = [load(src, dst, number) for number, (src, dst) in enumerate(pairs)]
        for copy in copies[0:3]:
            copy.start()
        at.barrier()
        for zi in range(2):
            for o in range(2):
                far_send(2, zi, o).start()
            for o in range(2):
                plain_send(2, zi, o).start()
        length = act.shape[1]
        mid = length // 2

        def weight_grad(u, left, right):
            def column_half(zi, _):
                def piece(tile, _):
                    cols = pl.ds(pl.multiple_of(384 * tile, 128), 384)
                    value = dot_tn(left[0, :, cols], right[zi, 0:mid, :])
                    value = value + dot_tn(left[1, :, cols], right[zi, mid:length, :])
                    gst[tile] = value.astype(LOW)
                    rows = pl.ds(pl.multiple_of(384 * tile, 128), 384)
                    pltpu.make_async_copy(gst.at[tile], gf1.at[zi, rows], gs.at[tile]).start()
                    return 0

                lax.fori_loop(0, 3, piece, 0)
                for tile in range(3):
                    rows = pl.ds(384 * tile, 384)
                    pltpu.make_async_copy(gst.at[tile], gf1.at[zi, rows], gs.at[tile]).wait()
                for o in range(2):
                    far_send(u, zi, o).start()
                for o in range(2):
                    plain_send(u, zi, o).start()
                return 0

            lax.fori_loop(0, 2, column_half, 0)

        for copy in copies[0:3]:
            copy.wait()
        for copy in copies[3:6]:
            copy.start()

        def down(step, _):
            tile, zi = step // 2, step % 2
            rows = dm[tile // 2, pl.ds(pl.multiple_of((tile % 2) * 256, 256), 256), :]
            to_row = pl.ds(pl.multiple_of(tile * 256, 256), 256)
            value = dot_nn(rows, w2v[zi]) * gp[zi, to_row, :].astype(F32)
            gp[zi, to_row, :] = value.astype(LOW)
            return 0

        lax.fori_loop(0, 8, down, 0)
        def partial(left, right, send, recv, own, number):
            def part(step, _):
                tile = (2 * (1 - core) + step) % 4
                rows = pl.ds(pl.multiple_of(tile * 256, 256), 256)
                value = dot_nt(left[0, rows, :], right[0])
                value = value + dot_nt(left[1, rows, :], right[1])

                @pl.when(step < 2)
                def _():
                    send[step] = value.astype(LOW)
                    exchange(send.at[step], recv.at[step], number + step).start()

                @pl.when(step >= 2)
                def _():
                    own[step - 2] = value

                return 0

            lax.fori_loop(0, 4, part, 0)

        for copy in copies[3:6]:
            copy.wait()
        partial(gp, w1v, sb, rb, yb, 0)
        weight_grad(1, h2, gp)
        fetch_pair(2, 0, 0)
        partial(act, w2v, sm, rm, zb, 2)
        relay_pair(2, 0)
        fetch_pair(2, 1, 0)

    cols = gf1.shape[2]
    length = act_in.shape[1]
    mid = length // 2
    pl.run_scoped(
        mlp_phase,
        pltpu.VMEM((2, length, cols), LOW),
        pltpu.VMEM((2, length, cols), LOW),
        pltpu.VMEM((2, 8 * rows_u, cols), LOW),
        pltpu.VMEM((2, 8 * rows_u, cols), LOW),
        pltpu.VMEM((2, mid, cols), LOW),
        pltpu.VMEM((2, mid, cols), LOW),
        pltpu.VMEM((3, 384, cols), LOW),
    )
    def attention_phase(w0, h1, qkv, pt, dpk, do, g0, xb, gb, acc):
        local["g0"] = g0
        pairs = (
            (head_in, w0),
            (qkv_in, qkv),
            (att_in, dpk.at[:, :, 0:384]),
            (h1_in, h1),
        )
        early = [load(src, dst, number) for number, (src, dst) in enumerate(pairs)]

        def rows_in(block):
            return (
                load(x1_in.at[block], xb.at[0], 5),
                load(br_in.at[block], xb.at[1], 6),
                load(g_in.at[block], gb, 7),
            )

        for copy in rows_in(0):
            copy.start()
        for copy in early:
            copy.start()

        def probs_in(number):
            slot = number % 2
            return pltpu.make_async_copy(pt_in.at[number], pt.at[slot], ps.at[slot])

        probs_in(0).start()
        fetch_pair(2, 0, 1)

        for block in range(2):
            for copy in rows_in(block):
                if block:
                    copy.start()
            for copy in rows_in(block):
                copy.wait()
            exchange(sb.at[block], rb.at[block], block).wait_recv()
            exchange(sm.at[block], rm.at[block], 2 + block).wait_recv()
            gate1, scale2 = mod[block, 2:3, :], 1.0 + mod[block, 4:5, :]
            gate2 = mod[block, 5:6, :]

            def norm_second(step, sums_now):
                at_row = pl.ds(pl.multiple_of(step * 128, 128), 128)
                grad = gb[at_row, :].astype(F32)
                first = xb[0, at_row, :]
                d_second = yb[block, at_row, :] + rb[block, at_row, :].astype(F32)
                kept = keep_col[block, at_row, 0:1] * (
                    zb[block, at_row, :] + rm[block, at_row, :].astype(F32)
                )
                ob[block, at_row, :] = (first + gate2 * kept).astype(LOW)
                normed, spread = layer_norm(first)
                d_first = grad + norm_back(d_second * scale2, normed, spread)
                yb[block, at_row, :] = d_first
                to_row = pl.ds(pl.multiple_of(block * 256 + step * 128, 128), 128)
                db[core, to_row, :] = (gate1 * d_first).astype(LOW)
                terms = (d_first * xb[1, at_row, :], d_second, d_second * normed, grad * kept)
                return tuple(
                    now + jnp.sum(term, axis=0, keepdims=True) for now, term in zip(sums_now, terms)
                )

            zero = jnp.zeros((1, gb.shape[1]), F32)
            totals = lax.fori_loop(0, 2, norm_second, (zero,) * 4)
            for place, value in zip((2, 3, 4, 5), totals):
                sums[block, place : place + 1, :] = value
            part = db.at[core, pl.ds(block * 256, 256)]
            exchange(part, part, 4 + block).start()
            give_back(block, 0, True)

        for copy in early[0:3]:
            copy.wait()

        relay_pair(2, 1)
        fetch_pair(1, 0, 0)

        def to_heads(step, _):
            @pl.when(step >= 2)
            def _():
                part = db.at[1 - core, pl.ds(pl.multiple_of((step - 2) * 256, 256), 256)]
                pltpu.make_async_copy(part, part, er.at[4 + step - 2]).wait()

            tile = (2 * core + step) % 4
            rows = db[tile // 2, pl.ds(pl.multiple_of((tile % 2) * 256, 256), 256), :]
            to_row = pl.ds(pl.multiple_of(tile * 256, 256), 256)
            narrow = lanes(256) < HD
            for zi in range(2):
                value = dot_nn(rows, w0[zi, :, 768:1152])
                for number in range(4):
                    piece = jnp.where(narrow, window(value, 96 + HD * number), 0.0)
                    head = zi * 4 + number
                    do[head, to_row, :] = (piece * gains[head : head + 1, :]).astype(LOW)
            return 0

        lax.fori_loop(0, 4, to_heads, 0)
        def proj_grad(number, _):
            zi, tile = number // 3, number % 3
            some = pl.ds(pl.multiple_of(384 * tile, 128), 384)
            value = dot_tn(db[0, :, some], dpk[zi, 0:mid, 0:384])
            value = value + dot_tn(db[1, :, some], dpk[zi, mid:length, 0:384])
            g0[zi, some, 768:1152] = value.astype(LOW)
            return 0

        lax.fori_loop(0, 6, proj_grad, 0)

        def attend(head, _):
            step_of = (
                lambda: (relay_pair(1, 0), fetch_pair(1, 1, 0)),
                lambda: (relay_pair(1, 1), settle_pair(2, 0), fetch_pair(2, 1, 1)),
                lambda: (settle_pair(2, 1), fetch_pair(1, 0, 1)),
                lambda: (settle_pair(1, 0), merge_pair(2, 0), fetch_pair(1, 1, 1)),
                lambda: (settle_pair(1, 1), merge_pair(2, 1)),
                lambda: (merge_pair(1, 0),),
                lambda: (merge_pair(1, 1),),
                lambda: (relay_pair(0, 0),),
            )
            for place, task in enumerate(step_of):

                @pl.when(head == place)
                def _():
                    task()

            acc[...] = jnp.zeros_like(acc)

            def tile_step(tile, _):
                number = 4 * head + tile
                rows = pl.ds(pl.multiple_of(tile * 256, 256), 256)

                @pl.when(number < 31)
                def _():
                    probs_in(number + 1).start()

                probs_in(number).wait()
                grad = do[head, rows, :]
                probs = pt[number % 2]
                acc[1] += dot_nn(probs, grad)
                d_probs = dot_nt(qkv[head, 2], grad)
                wide = probs.astype(F32)
                inner = jnp.sum(wide * d_probs, axis=0, keepdims=True)
                d_scores = (wide * (d_probs - inner)).astype(LOW)
                acc[0] += dot_nn(d_scores, qkv[head, 0, rows, :])
                qkv[head, 0, rows, :] = (dot_tn(d_scores, qkv[head, 1]) * scale_q).astype(LOW)
                return 0

            lax.fori_loop(0, 4, tile_step, 0)
            qkv[head, 1] = (acc[0] * scale_q).astype(LOW)
            qkv[head, 2] = acc[1].astype(LOW)
            return 0

        early[3].wait()

        def send_head(zi):
            def head_grad(tile, _):
                some = pl.ds(pl.multiple_of(384 * tile, 128), 384)
                value = dot_tn(h1[0, :, some], dpk[zi, 0:mid, :])
                value = value + dot_tn(h1[1, :, some], dpk[zi, mid:length, :])
                g0[zi, some, 0:768] = value[:, 0:768].astype(LOW)
                both = value[:, 768:896] + g0[zi, some, 768:896].astype(F32)
                g0[zi, some, 768:896] = both.astype(LOW)
                return 0

            lax.fori_loop(0, 3, head_grad, 0)
            for o in range(2):
                far_send(0, zi, o).start()
            for o in range(2):
                plain_send(0, zi, o).start()

        def column_half(zi, _):
            def one_head(number, _):
                return attend(4 * zi + number, 0)

            lax.fori_loop(0, 4, one_head, 0)

            def lay(step, _):
                rows = pl.ds(pl.multiple_of(step * 128, 128), 128)
                narrow = lanes(128) < HD
                parts = [
                    jnp.where(narrow, qkv[zi * 4 + n // 3, n % 3, rows, :].astype(F32), 0.0)
                    for n in range(12)
                ]
                for tile, value in enumerate(pack(parts, 0, 7)):
                    dpk[zi, rows, 128 * tile : 128 * tile + 128] = value.astype(LOW)
                return 0

            lax.fori_loop(0, 8, lay, 0)

            @pl.when(zi == 0)
            def _():
                send_head(0)

            return 0

        lax.fori_loop(0, 2, column_half, 0)

        for block in range(2):
            load(x_in.at[block], rm.at[block], 5 + block).start()
        for block in range(2):
            exchange(sb.at[block], rb.at[block], block).wait_send()
        for step in range(4):
            tile = (2 * (1 - core) + step) % 4
            rows = pl.ds(pl.multiple_of(tile * 256, 256), 256)
            value = dot_nt(dpk[0, rows, :], w0[0, :, 0:896])
            value = value + dot_nt(dpk[1, rows, :], w0[1, :, 0:896])
            if step < 2:
                sb[step] = value.astype(LOW)
                exchange(sb.at[step], rb.at[step], 6 + step).start()
            else:
                zb[step - 2] = value
        send_head(1)
        for block in range(2):
            give_back(block, 0, False)
            load(x_in.at[block], rm.at[block], 5 + block).wait()
            exchange(sb.at[block], rb.at[block], 6 + block).wait_recv()
            scale1 = 1.0 + mod[block, 1:2, :]

            def norm_first(step, sums_now):
                at_row = pl.ds(pl.multiple_of(step * 128, 128), 128)
                d_norm = zb[block, at_row, :] + rb[block, at_row, :].astype(F32)
                normed, spread = layer_norm(rm[block, at_row, :].astype(F32))
                d_input = yb[block, at_row, :] + norm_back(d_norm * scale1, normed, spread)
                ob[block, at_row, :] = d_input.astype(LOW)
                terms = (d_norm, d_norm * normed)
                return tuple(
                    now + jnp.sum(term, axis=0, keepdims=True) for now, term in zip(sums_now, terms)
                )

            zero = jnp.zeros((1, gb.shape[1]), F32)
            totals = lax.fori_loop(0, 2, norm_first, (zero,) * 2)
            for place, value in zip((0, 1), totals):
                sums[block, place : place + 1, :] = value

        blocks = []
        for number in range(6):
            value = select[0][:, 0:1] * sums[0, number : number + 1, :]
            blocks.append(value + select[1][:, 0:1] * sums[1, number : number + 1, :])
        chunks = to_chunks(*blocks[0:3]) + to_chunks(*blocks[3:6])
        for number in range(4):
            dc[number] = chunks[number]

        def each_chunk(start):
            for number in range(4):
                here = jnp.logical_and(half == core, line == number)
                dst, send, recv = nr.at[lane, core], dcs.at[number], dcr.at[lane, core]
                if start:
                    move(dc.at[number], dst, send, recv, at.base + half, number, here)
                else:

                    @pl.when(jnp.logical_not(here))
                    def _():
                        remote(dc.at[number], dst, send, recv, at.base + half, number).wait_send()

        def each_row(start):
            for step in range(1, 8):
                other = (dp + step) % 8
                copy = remote(da.at[dp], da.at[dp], das.at[step], dar.at[dp], other, line)
                copy.start() if start else copy.wait_send()

        each_chunk(True)
        for block in range(2):
            give_back(block, 1, True)
        settle_pair(0, 0)
        relay_pair(0, 1)
        merge_pair(0, 0)

        settle_pair(0, 1)
        for zi in range(2):
            for o in range(2):
                pltpu.make_async_copy(dc.at[0], nr.at[zi, o], dcr.at[zi, o]).wait()
        da[dp] = (nr[0, 0] + nr[0, 1]) + (nr[1, 0] + nr[1, 1])
        each_row(True)
        merge_pair(0, 1)
        for step in range(1, 8):
            other = (dp + step) % 8
            pltpu.make_async_copy(da.at[other], da.at[other], dar.at[other]).wait()
        value = jnp.concatenate([da[n] for n in range(8)], axis=0)
        g_bias[...] = jnp.sum(value, axis=0, keepdims=True)
        g_ada[...] = lax.dot_general(
            cond[...].astype(LOW).astype(F32), value, (((0,), (0,)), ((), ())), precision=HIGH, preferred_element_type=F32
        )
        for u in range(3):
            finish(u)

        each_chunk(False)
        each_row(False)
        for u in range(3):
            for zi in range(2):
                for o in range(2):
                    far_send(u, zi, o).wait_send()
                    plain_send(u, zi, o).wait_send()
                    relay_send(u, zi, o).wait_send()
                    settled(u, zi, o)
        for block in range(2):
            give_back(block, 1, False)
            exchange(sm.at[block], rm.at[block], 2 + block).wait_send()
            part = db.at[core, pl.ds(block * 256, 256)]
            exchange(part, part, 4 + block).wait_send()
            exchange(sb.at[block], rb.at[block], 6 + block).wait_send()
        for kind in range(2):
            dst = (out_tok, out_dtok)[kind]
            for slot in range(2):
                source = 2 * core + slot
                here = jnp.logical_and(source == line, half == core)

                @pl.when(jnp.logical_not(here))
                def _():
                    pltpu.make_async_copy(dst.at[slot], dst.at[slot], tr.at[kind, slot]).wait()

    pl.run_scoped(
        attention_phase,
        pltpu.VMEM((2, 8 * rows_u, cols), LOW),
        pltpu.VMEM((2, mid, cols), LOW),
        pltpu.VMEM((8, 3, length, 128), LOW),
        pltpu.VMEM((2, length, mid // 2), LOW),
        pltpu.VMEM((2, length, 896), LOW),
        pltpu.VMEM((8, length, 128), LOW),
        pltpu.VMEM((2, 8 * rows_u, cols), LOW),
        pltpu.VMEM((2, mid // 2, cols), F32),
        pltpu.VMEM((mid // 2, cols), LOW),
        pltpu.VMEM((2, length, 128), F32),
    )


def run_back(*args):
    rows, part = args[-1].shape[1], args[7].shape[1]
    length, cols = args[0].shape[1:]
    chunk = 6 * cols // 4
    shape = jax.ShapeDtypeStruct
    vmem = pl.BlockSpec(memory_space=pltpu.VMEM)
    outs = (
        shape((2, part, cols), LOW),
        shape((2, part, cols), LOW),
        shape((3, 3, rows, cols), LOW),
        shape((3, 2, 2, rows, cols), LOW),
        shape((2, 8 * rows, cols), LOW),
        shape((rows, chunk), F32),
        shape((1, chunk), F32),
    )
    three = DMA((3, 2, 2))
    low = pltpu.VMEM((2, part, cols), LOW)
    return pl.pallas_call(
        back_kernel,
        out_shape=outs,
        in_specs=[ANY] * 16 + [vmem] * 5,
        out_specs=(ANY,) * 5 + (vmem,) * 2,
        scratch_shapes=[
            pltpu.VMEM((2, 8, cols), F32),
            pltpu.VMEM((2, 2 * part, cols), LOW),
            pltpu.VMEM((2, part, cols), F32),
            pltpu.VMEM((2, part, cols), F32),
            low,
            low,
            low,
            low,
            low,
            pltpu.VMEM((3, 2, 2, rows, cols), LOW),
            pltpu.VMEM((2, 3, 2, 2, rows, cols), LOW),
            pltpu.VMEM((4, rows, cols), LOW),
            pltpu.VMEM((4, 8, chunk), F32),
            pltpu.VMEM((2, 2, 8, chunk), F32),
            pltpu.VMEM((8, 8, chunk), F32),
            three,
            three,
            DMA((2, 3, 2, 2)),
            DMA((2, 3, 2, 2)),
            three,
            DMA((3, 3)),
            three,
            DMA((8,)),
            DMA((8,)),
            DMA((2, 2)),
            DMA((2, 2)),
            DMA((8,)),
            DMA((4,)),
            DMA((2,)),
            DMA((4,)),
            DMA((2, 2)),
            DMA((8,)),
            DMA((8,)),
        ],
        compiler_params=pltpu.CompilerParams(
            collective_id=1, has_side_effects=True, vmem_limit_bytes=63 << 20
        ),
    )(*args)


def fast_body(
    tokens,
    time_embed,
    segments,
    micro_order,
    head_mask,
    group_mask,
    keep_route,
    w_qkv,
    w_proj,
    w_fc1,
    w_fc2,
    w_ada,
    b_ada,
    cotangent,
):
    width = tokens.shape[2]
    length = segments.shape[1]
    qcols = w_qkv.shape[1]
    swap = micro_order[:, None] == 1

    lines = jnp.concatenate(
        [
            jnp.where(swap, head_mask[1:2], head_mask[0:1]),
            jnp.where(swap, group_mask[1:2], group_mask[0:1]),
            segments[:, :: length // 4],
            jnp.zeros((2, 116), jnp.int32),
        ],
        axis=1,
    )
    meta = jnp.concatenate(
        [keep_route.reshape(4, 128), lines, jnp.zeros((2, 128), jnp.int32)], axis=0
    ).astype(jnp.float32)
    te = time_embed.reshape(8, 8, width // 8).transpose(1, 0, 2).astype(jnp.float32)
    whead = jnp.concatenate([w_qkv, w_proj], axis=1)
    (
        full_fc2,
        full_fc1,
        head_w,
        dealt,
        dealt_grad,
        h_first,
        qkv,
        probs,
        att,
        first,
        branch,
        h_second,
        d_mlp,
        act,
        slope,
        grad_fc2,
        cond,
        mod,
        gains,
        _,
        kept,
        select,
    ) = run_front(whead, w_fc1, w_fc2, tokens, cotangent, meta, te, w_ada, b_ada[None, :])
    result, d_input, grads, _, _, g_ada, g_bias = run_back(
        act,
        slope,
        d_mlp,
        h_second,
        full_fc1,
        full_fc2.reshape(full_fc1.shape),
        grad_fc2,
        first,
        branch,
        dealt,
        dealt_grad,
        h_first,
        qkv,
        probs,
        att,
        head_w,
        mod,
        gains,
        kept,
        select,
        cond,
    )
    total = jnp.sum(grads.astype(jnp.float32), axis=1)
    return (
        result,
        d_input,
        total[0, :, :qcols],
        total[0, :, qcols:],
        total[1],
        total[2],
        g_ada,
        g_bias[0],
    )


def solution(mesh):
    placed = (
        P("dp", "tensor", None),
        P("dp", None, None),
        P("dp", None),
        P("dp"),
        P("dp", "tensor"),
        P("dp", "tensor"),
        P("dp", "tensor"),
        P("dp", "tensor"),
        P("dp", "tensor"),
        P("dp", "tensor"),
        P("dp", "tensor"),
        P("dp", "tensor"),
        P("tensor"),
        P("dp", "tensor", None),
    )
    return jax.shard_map(
        fast_body if mesh.shape["dp"] == 8 and mesh.shape["tensor"] == 4 else body,
        mesh=mesh,
        in_specs=placed,
        out_specs=(
            P("dp", "tensor", None),
            P("dp", "tensor", None),
            P("dp", "tensor"),
            P("dp", "tensor"),
            P("dp", "tensor"),
            P("dp", "tensor"),
            P("dp", "tensor"),
            P("tensor"),
        ),
        check_vma=False,
    )
```

```python
import jax
import jax.numpy as jnp
from jax import lax
from jax.experimental import pallas as pl
from jax.experimental.pallas import tpu as pltpu
from jax.sharding import PartitionSpec as P

HD = 72
FF = 4608
GROUPS = 16


EPSILON = 1e-06
HIGH = lax.Precision.HIGHEST


def layer_norm(values):
    middle = jnp.mean(values, axis=-1, keepdims=True)
    centred = values - middle
    spread = jnp.mean(centred * centred, axis=-1, keepdims=True)
    factor = lax.rsqrt(spread + EPSILON)
    return (centred * factor, factor)


def norm_back(grad, normed, factor):
    inner = (
        grad
        - jnp.mean(grad, axis=-1, keepdims=True)
        - normed * jnp.mean(grad * normed, axis=-1, keepdims=True)
    )
    return factor * inner


def contract_rows(left, right):
    return lax.dot_general(
        left, right, (((0,), (0,)), ((), ())), preferred_element_type=jnp.float32
    )


def contract_cols(left, right):
    return lax.dot_general(
        left, right, (((1,), (1,)), ((), ())), preferred_element_type=jnp.float32
    )


def score_block(query_block, keys, seg_block, seg_ids):
    scores = jnp.einsum(
        "qhe,khe->hqk", query_block, keys, preferred_element_type=jnp.float32
    ) * HD ** (-0.5)
    same = seg_block[:, None] == seg_ids[None, :]
    return jnp.where(same[None], scores, -1e30)


def attention_forward(query, keys, values, seg_ids):
    length = query.shape[0]
    block = min(512, length)
    outs = []
    totals = []
    for offset in range(0, length, block):
        scores = score_block(
            query[offset : offset + block], keys, seg_ids[offset : offset + block], seg_ids
        )
        peak = jnp.max(scores, axis=-1, keepdims=True)
        denom = jnp.sum(jnp.exp(scores - peak), axis=-1, keepdims=True)
        log_total = peak + jnp.log(denom)
        probs = jnp.exp(scores - log_total).astype(jnp.bfloat16)
        outs.append(jnp.einsum("hqk,khe->qhe", probs, values, preferred_element_type=jnp.float32))
        totals.append(log_total)
    return (jnp.concatenate(outs, axis=0), totals)


def attention_backward(query, keys, values, seg_ids, totals, d_attn):
    length = query.shape[0]
    block = min(512, length)
    scale = HD ** (-0.5)
    d_keys = jnp.zeros(keys.shape, jnp.float32)
    d_values = jnp.zeros(values.shape, jnp.float32)
    d_queries = []
    for number, offset in enumerate(range(0, length, block)):
        query_block = query[offset : offset + block]
        scores = score_block(query_block, keys, seg_ids[offset : offset + block], seg_ids)
        probs = jnp.exp(scores - totals[number])
        grad_block = d_attn[offset : offset + block]
        d_values = d_values + jnp.einsum(
            "hqk,qhe->khe",
            probs.astype(jnp.bfloat16),
            grad_block,
            preferred_element_type=jnp.float32,
        )
        d_probs = jnp.einsum("qhe,khe->hqk", grad_block, values, preferred_element_type=jnp.float32)
        d_scores = (probs * (d_probs - jnp.sum(probs * d_probs, axis=-1, keepdims=True))).astype(
            jnp.bfloat16
        )
        d_queries.append(
            jnp.einsum("hqk,khe->qhe", d_scores, keys, preferred_element_type=jnp.float32) * scale
        )
        d_keys = (
            d_keys
            + jnp.einsum("hqk,qhe->khe", d_scores, query_block, preferred_element_type=jnp.float32)
            * scale
        )
    stacked = jnp.stack([jnp.concatenate(d_queries, axis=0), d_keys, d_values], axis=2)
    return stacked.astype(jnp.bfloat16).reshape(length, -1)


def body(
    tokens,
    time_embed,
    segments,
    micro_order,
    head_mask,
    group_mask,
    keep_route,
    w_qkv,
    w_proj,
    w_fc1,
    w_fc2,
    w_ada,
    b_ada,
    cotangent,
):
    micro = tokens.shape[0]
    local_rows = tokens.shape[1]
    length = segments.shape[1]
    heads_here = head_mask.shape[1]
    segs = time_embed.shape[1]
    tensor_index = lax.axis_index("tensor")
    chooser = (micro_order[:, None] == jnp.arange(micro, dtype=jnp.int32)[None, :]).astype(
        jnp.float32
    )
    head_sel = jnp.dot(chooser, head_mask.astype(jnp.float32), precision=HIGH)
    group_sel = jnp.repeat(
        jnp.dot(chooser, group_mask.astype(jnp.float32), precision=HIGH), FF // GROUPS, axis=1
    )
    keep_float = keep_route.astype(jnp.float32)

    def reduce_grads(grad_qkv, grad_proj, grad_fc1, grad_fc2, grad_ada):
        return (
            lax.psum_scatter(
                grad_qkv.astype(jnp.bfloat16), "dp", scatter_dimension=0, tiled=True
            ).astype(jnp.float32),
            lax.psum_scatter(
                grad_proj.astype(jnp.bfloat16), "dp", scatter_dimension=0, tiled=True
            ).astype(jnp.float32),
            lax.psum_scatter(
                grad_fc1.astype(jnp.bfloat16), "dp", scatter_dimension=0, tiled=True
            ).astype(jnp.float32),
            lax.psum_scatter(
                grad_fc2.astype(jnp.bfloat16), "dp", scatter_dimension=0, tiled=True
            ).astype(jnp.float32),
            lax.psum_scatter(
                grad_ada.astype(jnp.bfloat16), "dp", scatter_dimension=0, tiled=True
            ).astype(jnp.float32),
        )

    shard_shapes = [w.shape for w in (w_qkv, w_proj, w_fc1, w_fc2, w_ada)]
    start_acc = tuple((jnp.zeros(shape, jnp.float32) for shape in shard_shapes))

    def slot_step(carry, items):
        acc, bias_acc = carry
        slot_tokens, slot_grad, seg_ids, embed, hmask, gcols, keepf = items
        full = (
            lax.all_gather(w_qkv, "dp", axis=0, tiled=True),
            lax.all_gather(w_proj, "dp", axis=0, tiled=True),
            lax.all_gather(w_fc1, "dp", axis=0, tiled=True),
            lax.all_gather(w_fc2, "dp", axis=0, tiled=True),
            lax.all_gather(w_ada, "dp", axis=0, tiled=True),
        )
        full_qkv, full_proj, full_fc1, full_fc2, full_ada = full
        seg_local = lax.dynamic_slice_in_dim(seg_ids, tensor_index * local_rows, local_rows)
        scond = jax.nn.silu(embed.astype(jnp.float32)).astype(jnp.bfloat16)
        part_mods = jnp.dot(scond, full_ada, preferred_element_type=jnp.float32) + b_ada[None, :]
        mods = lax.all_gather(part_mods, "tensor", axis=1, tiled=True)
        onehot = (seg_local[:, None] == jnp.arange(segs, dtype=jnp.int32)[None, :]).astype(
            jnp.float32
        )
        modtok = jnp.dot(onehot, mods, precision=HIGH)
        shift1, scale1, gate1, shift2, scale2, gate2 = jnp.split(modtok, 6, axis=1)
        token_vals = slot_tokens.astype(jnp.float32)
        normed1, factor1 = layer_norm(token_vals)
        h_first = lax.all_gather(
            (normed1 * (1.0 + scale1) + shift1).astype(jnp.bfloat16), "tensor", axis=0, tiled=True
        )
        packed = jnp.dot(h_first, full_qkv, preferred_element_type=jnp.float32).astype(jnp.bfloat16)
        packed = packed.reshape(length, heads_here, 3, HD)
        query = packed[:, :, 0]
        keys = packed[:, :, 1]
        values = packed[:, :, 2]
        outs, totals = attention_forward(query, keys, values, seg_ids)
        attn = (outs * hmask[None, :, None]).astype(jnp.bfloat16).reshape(length, heads_here * HD)
        branch = lax.psum_scatter(
            contract_cols(attn, full_proj).astype(jnp.bfloat16),
            "tensor",
            scatter_dimension=0,
            tiled=True,
        ).astype(jnp.float32)
        first = token_vals + gate1 * branch
        normed2, factor2 = layer_norm(first)
        h_second = lax.all_gather(
            (normed2 * (1.0 + scale2) + shift2).astype(jnp.bfloat16), "tensor", axis=0, tiled=True
        )
        upward = jnp.dot(h_second, full_fc1, preferred_element_type=jnp.float32)
        gelu_val, gelu_pull = jax.vjp(lambda inner: jax.nn.gelu(inner, approximate=True), upward)
        act = (gelu_val * gcols[None, :]).astype(jnp.bfloat16)
        mlp = lax.psum_scatter(
            contract_cols(act, full_fc2).astype(jnp.bfloat16),
            "tensor",
            scatter_dimension=0,
            tiled=True,
        ).astype(jnp.float32)
        keep_col = keepf[:, None]
        result = (first + gate2 * keep_col * mlp).astype(jnp.bfloat16)
        grad_out = slot_grad.astype(jnp.float32)
        d_mlp = lax.all_gather(
            (gate2 * keep_col * grad_out).astype(jnp.bfloat16), "tensor", axis=0, tiled=True
        )
        grad_fc2 = contract_rows(d_mlp, act)
        d_act = jnp.dot(d_mlp, full_fc2, preferred_element_type=jnp.float32)
        d_up = gelu_pull(d_act * gcols[None, :])[0].astype(jnp.bfloat16)
        grad_fc1 = contract_rows(h_second, d_up)
        d_second = lax.psum_scatter(
            contract_cols(d_up, full_fc1).astype(jnp.bfloat16),
            "tensor",
            scatter_dimension=0,
            tiled=True,
        ).astype(jnp.float32)
        d_first = grad_out + norm_back(d_second * (1.0 + scale2), normed2, factor2)
        d_branch = lax.all_gather(
            (gate1 * d_first).astype(jnp.bfloat16), "tensor", axis=0, tiled=True
        )
        grad_proj = contract_rows(d_branch, attn)
        d_attn = jnp.dot(d_branch, full_proj, preferred_element_type=jnp.float32).astype(
            jnp.bfloat16
        )
        d_attn = d_attn.reshape(length, heads_here, HD) * hmask[None, :, None].astype(jnp.bfloat16)
        d_packed = attention_backward(query, keys, values, seg_ids, totals, d_attn)
        grad_qkv = contract_rows(h_first, d_packed)
        d_h_first = lax.psum_scatter(
            contract_cols(d_packed, full_qkv).astype(jnp.bfloat16),
            "tensor",
            scatter_dimension=0,
            tiled=True,
        ).astype(jnp.float32)
        d_input = d_first + norm_back(d_h_first * (1.0 + scale1), normed1, factor1)
        d_modtok = jnp.concatenate(
            [
                d_h_first,
                d_h_first * normed1,
                d_first * branch,
                d_second,
                d_second * normed2,
                grad_out * keep_col * mlp,
            ],
            axis=1,
        )
        part_dmods = lax.dot_general(onehot, d_modtok, (((0,), (0,)), ((), ())), precision=HIGH)
        d_mods = lax.psum_scatter(
            part_dmods.astype(jnp.bfloat16), "tensor", scatter_dimension=1, tiled=True
        ).astype(jnp.float32)
        grad_ada = jnp.dot(scond.astype(jnp.float32).T, d_mods, precision=HIGH)
        bias_acc = bias_acc + jnp.sum(d_mods, axis=0)
        parts = reduce_grads(grad_qkv, grad_proj, grad_fc1, grad_fc2, grad_ada)
        acc = tuple((held + piece for held, piece in zip(acc, parts)))
        return ((acc, bias_acc), (result, d_input.astype(jnp.bfloat16)))

    start_bias = jnp.zeros(b_ada.shape, jnp.float32)
    (acc, bias_acc), (results, d_tokens) = lax.scan(
        slot_step,
        (start_acc, start_bias),
        (tokens, cotangent, segments, time_embed, head_sel, group_sel, keep_float),
    )
    g_bias = lax.psum(bias_acc, "dp")
    return (results, d_tokens, acc[0], acc[1], acc[2], acc[3], acc[4], g_bias)


MESH = pl.DeviceIdType.MESH
ANY = pl.BlockSpec(memory_space=pl.ANY)
DMA = pltpu.SemaphoreType.DMA


class Place:
    def __init__(self):
        self.dp = lax.axis_index("dp")
        self.line = lax.axis_index("tensor")
        self.core = self.dp % 2
        self.base = self.dp - self.core
        self.half = self.line // 2
        x, y = (self.dp // 2) % 2, self.dp // 4
        self.dp_x = self.dp + 2 * (1 - 2 * x)
        self.dp_y = self.dp + 4 * (1 - 2 * y)
        self.base_x = self.dp_x - self.core
        self.base_y = self.dp_y - self.core
        self.base_far = self.base_x + self.base_y - self.base

    def barrier(self):
        bar = pltpu.get_barrier_semaphore()
        spot = self.core * 4 + self.line
        for step in range(1, 8):
            other = (spot + step) % 8
            pl.semaphore_signal(
                bar,
                inc=1,
                device_id=(self.base + other // 4, other % 4),
                device_id_type=MESH,
            )
        for step in range(1, 8):
            other = (self.dp + step) % 8
            pl.semaphore_signal(bar, inc=1, device_id=(other, self.line), device_id_type=MESH)
        pl.semaphore_wait(bar, 14)


def remote(src, dst, send, recv, dp, line):
    return pltpu.make_async_remote_copy(
        src_ref=src,
        dst_ref=dst,
        send_sem=send,
        recv_sem=recv,
        device_id=(dp, line),
        device_id_type=MESH,
    )


def move(src, dst, send, recv, dp, line, here):
    @pl.when(here)
    def _():
        pltpu.make_async_copy(src, dst, recv).start()

    @pl.when(jnp.logical_not(here))
    def _():
        remote(src, dst, send, recv, dp, line).start()


LOG2E = 1.4426950408889634
LOW = jnp.bfloat16
F32 = jnp.float32
SHADE = -1e30


def dot_nn(left, right):
    return jnp.dot(left, right, preferred_element_type=F32)


def dot_nt(left, right):
    return lax.dot_general(left, right, (((1,), (1,)), ((), ())), preferred_element_type=F32)


def dot_tn(left, right):
    return lax.dot_general(left, right, (((0,), (0,)), ((), ())), preferred_element_type=F32)


def lanes(rows):
    return lax.broadcasted_iota(jnp.int32, (rows, 128), 1)


def window(value, start):
    tile, rest = start // 128, start % 128
    here = value[:, 128 * tile : 128 * tile + 128]
    if rest == 0:
        return here
    here = pltpu.roll(here, 128 - rest, 1)
    if rest + HD <= 128:
        return here
    after = pltpu.roll(value[:, 128 * tile + 128 : 128 * tile + 256], 128 - rest, 1)
    return jnp.where(lanes(value.shape[0]) < 128 - rest, here, after)


def pack(parts, start, tiles):
    rows = parts[0].shape[0]
    lane = lanes(rows)
    out = []
    for tile in range(tiles):
        total = jnp.zeros((rows, 128), F32)
        for number, part in enumerate(parts):
            low = start + HD * number - 128 * tile
            if low >= 128 or low + HD <= 0:
                continue
            moved = pltpu.roll(part, low % 128, 1) if low % 128 else part
            inside = jnp.logical_and(lane >= low, lane < low + HD)
            total = jnp.where(inside, moved, total)
        out.append(total)
    return out


def turned(value, tile):
    start = 128 * tile
    stop = min(start + 128, value.shape[1])
    part = value[:, start:stop]
    if stop - start < 128:
        part = jnp.concatenate([part, jnp.zeros((part.shape[0], 64), F32)], axis=1)
    return pltpu.roll(part, 64, 1)


def to_blocks(even, odd):
    low = lanes(even.shape[0]) < 64
    turn = [turned(odd, tile) for tile in range(14)]
    tail = jnp.concatenate([even[:, 1664:1728], jnp.zeros((even.shape[0], 64), F32)], axis=1)
    one = [even[:, 0:1152]]
    two = [even[:, 1152:1664], jnp.where(low, tail, turn[0])]
    two += [jnp.where(low, turn[t], turn[t + 1]) for t in range(4)]
    three = [jnp.where(low, turn[t], turn[t + 1]) for t in range(4, 13)]
    return [jnp.concatenate(parts, axis=1) for parts in (one, two, three)]


def to_chunks(one, two, three):
    low = lanes(one.shape[0]) < 64
    even = jnp.concatenate([one, two[:, 0:576]], axis=1)
    turn = [turned(two, tile) for tile in range(4, 9)] + [turned(three, t) for t in range(9)]
    odd = [jnp.where(low, turn[t], turn[t + 1]) for t in range(13)]
    return even, jnp.concatenate(odd + [turn[13][:, 0:64]], axis=1)


def front_kernel(
    wh,
    w1,
    w2,
    tok,
    cot,
    meta,
    te,
    wa,
    ba,
    weights,
    w1_out,
    head_out,
    x_out,
    g_out,
    h1_out,
    qkv_out,
    pt_out,
    att_out,
    x1_out,
    br_out,
    h2_out,
    dm_out,
    act_out,
    gp_out,
    gf_out,
    cond,
    mod,
    gains,
    groups,
    kept,
    select,
    xt,
    w0,
    h1,
    qkv,
    obuf,
    pt,
    gst,
    att,
    sb,
    rb,
    br,
    x1,
    h2,
    ct,
    dm,
    w1v,
    act,
    gp,
    gc,
    mt,
    te_all,
    pb,
    pr,
    mine,
    mr,
    feat,
    zs,
    zr,
    fs,
    ns,
    nr,
    ds,
    dr,
    ts,
    tr,
    es,
    er,
    ls,
    ps,
    gs,
    ms,
    mrs,
    tes,
    ter,
    pbs,
    pbr,
    mms,
    mmr,
):
    at = Place()
    dp, line, core, half = at.dp, at.line, at.core, at.half
    units = (wh, w1, w2)
    lane = line % 2
    rows_u = w1.shape[0]
    sib = at.base + 1 - core
    at.barrier()

    def spot(u, zi, row):
        if u < 2:
            return (w0, w1v)[u].at[zi, pl.ds(pl.multiple_of(row * rows_u, 16), rows_u)]
        return weights.at[zi, row]

    def deal(kind, start):
        src, dst = ((tok, xt), (cot, ct))[kind]
        for slot in range(2):
            there = 2 * core + slot
            here = jnp.logical_and(half == core, there == line)
            send, recv = ts.at[kind, slot], tr.at[kind, lane]
            if start:
                move(src.at[slot], dst.at[lane], send, recv, at.base + half, there, here)
            else:

                @pl.when(jnp.logical_not(here))
                def _():
                    remote(
                        src.at[slot], dst.at[lane], send, recv, at.base + half, there
                    ).wait_send()

    def deal_arrive(kind):
        src, dst = ((tok, xt), (cot, ct))[kind]
        for block in range(2):
            pltpu.make_async_copy(src.at[0], dst.at[block], tr.at[kind, block]).wait()

    def source(u, start):
        dst = spot(u, lane, dp)
        recv = zr.at[u, lane, core]
        home = at.base + half
        if start:
            move(units[u], dst, zs.at[u, 0], recv, home, line, half == core)
        else:

            @pl.when(half != core)
            def _():
                remote(units[u], dst, zs.at[u, 0], recv, home, line).wait_send()

        for which, step in ((1, 1), (2, -1)):
            inside = line < 3 if step == 1 else line > 0

            @pl.when(inside)
            def _():
                copy = remote(units[u], dst, zs.at[u, which], recv, home, line + step)
                copy.start() if start else copy.wait_send()

    first = jnp.where(core == 0, jnp.where(line == 0, 0, 1), jnp.where(line == 3, 1, 0))

    def z_stage(u, k, other, start):
        zi = first + k - 2 * first * k
        origin = 2 * core + zi
        ref = spot(u, zi, at.base + other)
        if start:
            pltpu.make_async_copy(w1, ref, zr.at[u, zi, other]).wait()
        up = jnp.logical_and(origin < line, line < 3)
        down = jnp.logical_and(origin > line, line > 0)
        for go, step in ((up, 1), (down, -1)):

            @pl.when(go)
            def _():
                copy = remote(
                    ref, ref, fs.at[u, zi, other], zr.at[u, zi, other], dp, line + step
                )
                copy.start() if start else copy.wait_send()

        for which, near in ((0, at.dp_x), (1, at.dp_y)):
            copy = remote(
                ref, ref, ns.at[which, u, zi, other], nr.at[which, u, zi, other], near, line
            )
            copy.start() if start else copy.wait_send()

    def far_stage(u, zi, other, start):
        base = at.base_x + other * (at.base_y - at.base_x)
        near = at.dp_y + other * (at.dp_x - at.dp_y)
        ref = spot(u, zi, base + other)
        if start:
            pltpu.make_async_copy(w1, ref, nr.at[other, u, zi, other]).wait()
        copy = remote(ref, ref, ds.at[u, zi, other], dr.at[u, zi, other], near, line)
        copy.start() if start else copy.wait_send()

    def last_stage(u, zi, other):
        base = at.base_y + other * (at.base_x - at.base_y)
        ref = spot(u, zi, base + other)
        pltpu.make_async_copy(w1, ref, nr.at[1 - other, u, zi, other]).wait()
        ref = spot(u, zi, at.base_far + other)
        pltpu.make_async_copy(w1, ref, dr.at[u, zi, other]).wait()

    def pump(number):
        k, other = (number % 4) // 2, number % 2
        for quarter in range(4):
            u, stage = ((1, z_stage), (2, z_stage), (1, far_stage), (2, far_stage))[quarter]

            @pl.when(number // 4 == quarter)
            def _():
                stage(u, k, other, True)

    def keep(src, dst, number):
        return pltpu.make_async_copy(src, dst, ls.at[number])

    def each_column(start):
        for step in range(1, 8):
            other = (core * 4 + line + step) % 8
            copy = remote(
                meta, mt.at[core * 4 + line], ms.at[step], mrs.at[core * 4 + line],
                at.base + other // 4, other % 4,
            )
            copy.start() if start else copy.wait_send()

    def each_row(src, dst, send, recv, start, pieces):
        for step in range(1, 8):
            other = (dp + step) % 8
            part = src.at[other] if pieces else src
            copy = remote(part, dst.at[dp], send.at[step], recv.at[dp], other, line)
            copy.start() if start else copy.wait_send()

    def row_arrive(dst, recv):
        for step in range(1, 8):
            other = (dp + step) % 8
            pltpu.make_async_copy(dst.at[other], dst.at[other], recv.at[other]).wait()

    each_row(te, te_all, tes, ter, True, True)
    each_column(True)
    te_all[dp] = te[dp]
    mt[core * 4 + line] = meta[...]

    source(0, True)
    row_arrive(te_all, ter)
    for number in range(8):
        spread = te_all[number]
        cond[8 * number : 8 * number + 8, :] = spread * (1.0 / (1.0 + jnp.exp(-spread)))
    value = dot_nn(cond[...].astype(LOW), wa[...])
    for number in range(8):
        pb[number] = value[8 * number : 8 * number + 8, :]
    each_row(pb, pr, pbs, pbr, True, True)
    deal(0, True)
    pr[dp] = pb[dp]
    for other in range(2):
        z_stage(0, 0, other, True)
    row_arrive(pr, pbr)
    total = ba[...] + pr[0]
    for number in range(1, 8):
        total = total + pr[number]
    mine[...] = total

    def each_slot(start):
        for slot in range(2):
            there = 2 * core + slot
            for to in range(2):
                here = jnp.logical_and(core == to, there == line)
                send, recv = mms.at[slot, to], mmr.at[line]
                if start:
                    move(mine, mr.at[line], send, recv, at.base + to, there, here)
                else:

                    @pl.when(jnp.logical_not(here))
                    def _():
                        remote(mine, mr.at[line], send, recv, at.base + to, there).wait_send()

    each_slot(True)
    for other in range(2):
        z_stage(0, 1, other, True)
    source(1, True)
    deal(1, True)

    for step in range(1, 8):
        other = (core * 4 + line + step) % 8
        pltpu.make_async_copy(meta, mt.at[other], mrs.at[other]).wait()
    one_row = lanes(1)
    spots = (one_row - HD).astype(F32)
    inside = jnp.logical_and(one_row >= HD, one_row < HD + 4)

    def lane_of(row, place):
        return jnp.sum(jnp.where(one_row == place, row, 0.0), axis=1, keepdims=True)

    for zi in range(2):
        info = mt[half * 4 + 2 * core + zi, pl.ds(4 + lane, 1), :]
        for number in range(4):
            head = zi * 4 + number
            gains[head : head + 1, :] = jnp.broadcast_to(lane_of(info, number), (1, 128))
            groups[head : head + 1, :] = jnp.broadcast_to(lane_of(info, 4 + number), (1, 128))
    unit = lax.broadcasted_iota(jnp.int32, (1, gc.shape[1]), 1) // (gc.shape[1] // 4)
    for zi in range(2):
        row = jnp.zeros((1, gc.shape[1]), F32)
        for number in range(4):
            head = zi * 4 + number
            row = jnp.where(unit == number, groups[head : head + 1, 0:1], row)
        gc[8 * zi : 8 * zi + 8, :] = jnp.broadcast_to(row, (8, gc.shape[1]))
    info = mt[half * 4 + line, pl.ds(4 + lane, 1), :]
    for tile in range(4):
        same = jnp.where(spots == lane_of(info, 8 + tile), 1.0, 0.0)
        feat[0, tile : tile + 1, :] = jnp.where(inside, SHADE * (1.0 - same), 0.0)
        feat[1, tile : tile + 1, :] = jnp.where(inside, same, 0.0)
    row_ids = lax.broadcasted_iota(jnp.int32, (8, 128), 0)
    diagonal = lax.broadcasted_iota(jnp.int32, (128, 128), 0) == lanes(128)
    for block in range(2):
        item = jnp.sum(
            jnp.where(one_row == 8 + 2 * core + block, info, 0.0), axis=1, keepdims=True
        )
        hit = row_ids.astype(F32) == item + (4 * lane).astype(F32)
        select[block] = jnp.where(hit, 1.0, 0.0)
        for number in range(2):
            row = mt[half * 4 + 2 * core + block, pl.ds(2 * lane + number, 1), :]
            column = jnp.sum(jnp.where(diagonal, row, 0.0), axis=1, keepdims=True)
            kept[block, 128 * number : 128 * number + 128, :] = jnp.broadcast_to(column, (128, 128))
    for source_line in range(4):
        pltpu.make_async_copy(mine, mr.at[source_line], mmr.at[source_line]).wait()
    for block in range(2):
        weight = select[block][:, 0:1]
        rows = [jnp.sum(weight * mr[n], axis=0, keepdims=True) for n in range(4)]
        pieces = to_blocks(rows[0], rows[1]) + to_blocks(rows[2], rows[3])
        for number, piece in enumerate(pieces):
            mod[block, number : number + 1, :] = piece
        mod[block, 6:8, :] = jnp.zeros((2, mod.shape[2]), F32)

    def exchange(src, dst, number):
        return remote(src, dst, es.at[number], er.at[number], sib, line)

    deal_arrive(0)
    keep(xt, x_out, 0).start()

    for block in range(2):
        shift, scale = mod[block, 0:1, :], 1.0 + mod[block, 1:2, :]

        def norm_first(step, _):
            at_row = pl.ds(pl.multiple_of(step * 128, 128), 128)
            normed, _f = layer_norm(xt[block, at_row, :].astype(F32))
            to_row = pl.ds(pl.multiple_of(block * 256 + step * 128, 128), 128)
            h1[core, to_row, :] = (normed * scale + shift).astype(LOW)
            return 0

        lax.fori_loop(0, 2, norm_first, 0)
        part = h1.at[core, pl.ds(block * 256, 256)]
        exchange(part, part, block).start()
    for zi in range(2):
        for other in range(2):
            far_stage(0, zi, other, True)
    source(2, True)
    for zi in range(2):
        for other in range(2):
            last_stage(0, zi, other)
    keep(w0, head_out, 1).start()

    def project(step, _):
        @pl.when(step >= 2)
        def _():
            part = h1.at[1 - core, pl.ds(pl.multiple_of((step - 2) * 256, 256), 256)]
            pltpu.make_async_copy(part, part, er.at[step - 2]).wait()

        pump(step)
        tile = (2 * core + step) % 4
        rows = h1[tile // 2, pl.ds(pl.multiple_of((tile % 2) * 256, 256), 256), :]
        to_row = pl.ds(pl.multiple_of(tile * 256, 256), 256)
        narrow = lanes(256) < HD
        fills = (feat[0, pl.ds(tile, 1), :], feat[1, pl.ds(tile, 1), :], jnp.zeros((1, 128), F32))
        for zi in range(2):
            value = dot_nn(rows, w0[zi, :, 0:896])
            for number in range(12):
                head, part = zi * 4 + number // 3, number % 3
                piece = jnp.where(narrow, window(value, HD * number), fills[part])
                qkv[head, part, to_row, :] = piece.astype(LOW)
        return 0

    lax.fori_loop(0, 4, project, 0)
    keep(h1, h1_out, 2).start()
    keep(qkv, qkv_out, 3).start()

    factor = HD ** (-0.5) * LOG2E

    def attend(head, _):
        pump(4 + head)
        gain = gains[pl.ds(head, 1), :]

        def tile_step(tile, _):
            rows = pl.ds(pl.multiple_of(tile * 256, 256), 256)
            number = 4 * head + tile
            slot = number % 2
            scores = dot_nt(qkv[head, 1], qkv[head, 0, rows, :])
            peak = jnp.max(scores, axis=0, keepdims=True)
            power = jnp.exp2((scores - peak) * factor)
            total = jnp.sum(power, axis=0, keepdims=True)
            probs = (power * (1.0 / total)).astype(LOW)
            obuf[head, rows, :] = (dot_tn(probs, qkv[head, 2]) * gain).astype(LOW)

            @pl.when(number >= 2)
            def _():
                pltpu.make_async_copy(pt.at[slot], pt_out.at[number - 2], ps.at[slot]).wait()

            pt[slot] = probs
            pltpu.make_async_copy(pt.at[slot], pt_out.at[number], ps.at[slot]).start()
            return 0

        lax.fori_loop(0, 4, tile_step, 0)
        return 0

    lax.fori_loop(0, 8, attend, 0)

    def lay(step, _):
        rows = pl.ds(pl.multiple_of(step * 128, 128), 128)
        for zi in range(2):
            parts = [obuf[zi * 4 + n, rows, :].astype(F32) for n in range(4)]
            for tile, value in enumerate(pack(parts, 96, 3)):
                att[zi, rows, 128 * tile : 128 * tile + 128] = value.astype(LOW)
        return 0

    lax.fori_loop(0, 8, lay, 0)
    keep(att, att_out, 5).start()

    for step in range(4):
        tile = (2 * (1 - core) + step) % 4
        rows = pl.ds(pl.multiple_of(tile * 256, 256), 256)
        value = dot_nt(att[0, rows, :], w0[0, :, 768:1152])
        value = value + dot_nt(att[1, rows, :], w0[1, :, 768:1152])
        if step < 2:
            sb[step] = value.astype(LOW)
            exchange(sb.at[step], rb.at[step], 2 + step).start()
        else:
            br[step - 2] = value
    for block in range(2):
        exchange(sb.at[block], rb.at[block], 2 + block).wait_recv()
        gate = mod[block, 2:3, :]
        shift, scale = mod[block, 3:4, :], 1.0 + mod[block, 4:5, :]

        def norm_second(step, _):
            at_row = pl.ds(pl.multiple_of(step * 128, 128), 128)
            branch = br[block, at_row, :] + rb[block, at_row, :].astype(F32)
            br[block, at_row, :] = branch
            value = xt[block, at_row, :].astype(F32) + gate * branch
            x1[block, at_row, :] = value
            normed, _f = layer_norm(value)
            to_row = pl.ds(pl.multiple_of(block * 256 + step * 128, 128), 128)
            h2[core, to_row, :] = (normed * scale + shift).astype(LOW)
            return 0

        lax.fori_loop(0, 2, norm_second, 0)
        part = h2.at[core, pl.ds(block * 256, 256)]
        exchange(part, part, 4 + block).start()
    keep(x1, x1_out, 6).start()
    keep(br, br_out, 7).start()

    deal_arrive(1)
    keep(ct, g_out, 9).start()
    for block in range(2):
        gate2 = mod[block, 5:6, :]

        def grad_rows(step, _):
            at_row = pl.ds(pl.multiple_of(step * 128, 128), 128)
            value = gate2 * kept[block, at_row, 0:1] * ct[block, at_row, :].astype(F32)
            to_row = pl.ds(pl.multiple_of(block * 256 + step * 128, 128), 128)
            dm[core, to_row, :] = value.astype(LOW)
            return 0

        lax.fori_loop(0, 2, grad_rows, 0)
        part = dm.at[core, pl.ds(block * 256, 256)]
        exchange(part, part, 6 + block).start()

    for block in range(2):
        part = h2.at[1 - core, pl.ds(block * 256, 256)]
        pltpu.make_async_copy(part, part, er.at[4 + block]).wait()
    keep(h2, h2_out, 8).start()
    for block in range(2):
        part = dm.at[1 - core, pl.ds(block * 256, 256)]
        pltpu.make_async_copy(part, part, er.at[6 + block]).wait()
    keep(dm, dm_out, 10).start()

    for zi in range(2):
        for other in range(2):
            last_stage(1, zi, other)
    keep(w1v, w1_out, 11).start()
    ratio = (2.0 / 3.141592653589793) ** 0.5

    def widen(step, _):
        tile, zi = (2 * core + step // 2) % 4, step % 2
        rows = h2[tile // 2, pl.ds(pl.multiple_of((tile % 2) * 256, 256), 256), :]
        value = dot_nn(rows, w1v[zi])
        mask = gc[pl.ds(pl.multiple_of(8 * zi, 8), 8), :][0:1, :]
        square = value * value
        bend = jnp.tanh(ratio * (value + 0.044715 * (value * square)))
        grown = 0.5 * (1.0 + bend)
        slope = grown + 0.5 * value * (1.0 - bend * bend) * (
            ratio * (1.0 + (3.0 * 0.044715) * square)
        )
        to_row = pl.ds(pl.multiple_of(tile * 256, 256), 256)
        act[zi, to_row, :] = (value * grown * mask).astype(LOW)
        gp[zi, to_row, :] = (slope * mask).astype(LOW)

        @pl.when(step < 4)
        def _():
            pump(12 + step)

        return 0

    lax.fori_loop(0, 8, widen, 0)
    keep(act, act_out, 12).start()
    keep(gp, gp_out, 13).start()

    def grad_piece(number):
        rows = pl.ds(384 * (number % 3), 384)
        if not isinstance(number, int):
            rows = pl.ds(pl.multiple_of(384 * (number % 3), 128), 384)
        return gf_out.at[number // 3, rows]

    def fc2_grad(number, _):
        zi, slot = number // 3, number % 3
        some = pl.ds(pl.multiple_of(384 * slot, 128), 384)
        value = dot_tn(dm[0, :, some], act[zi, 0:512, :])
        value = value + dot_tn(dm[1, :, some], act[zi, 512:1024, :])

        @pl.when(number >= 3)
        def _():
            pltpu.make_async_copy(gst.at[slot], grad_piece(number - 3), gs.at[slot]).wait()

        gst[slot] = value.astype(LOW)
        pltpu.make_async_copy(gst.at[slot], grad_piece(number), gs.at[slot]).start()
        return 0

    lax.fori_loop(0, 6, fc2_grad, 0)

    for u in range(3):
        source(u, False)
        for k in range(2):
            for other in range(2):
                z_stage(u, k, other, False)
                far_stage(u, k, other, False)
                if u == 2:
                    last_stage(u, k, other)
    for kind in range(2):
        deal(kind, False)
    each_column(False)
    each_row(te, te_all, tes, ter, False, True)
    each_row(pb, pr, pbs, pbr, False, True)
    each_slot(False)
    for block in range(2):
        own1 = h1.at[core, pl.ds(block * 256, 256)]
        own2 = h2.at[core, pl.ds(block * 256, 256)]
        exchange(own1, own1, block).wait_send()
        exchange(sb.at[block], rb.at[block], 2 + block).wait_send()
        exchange(own2, own2, 4 + block).wait_send()
        own3 = dm.at[core, pl.ds(block * 256, 256)]
        exchange(own3, own3, 6 + block).wait_send()
    pairs = (
        (xt, x_out),
        (w0, head_out),
        (h1, h1_out),
        (qkv, qkv_out),
        (None, None),
        (att, att_out),
        (x1, x1_out),
        (br, br_out),
        (h2, h2_out),
        (ct, g_out),
        (dm, dm_out),
        (w1v, w1_out),
        (act, act_out),
        (gp, gp_out),
    )
    for number, (src, dst) in enumerate(pairs):
        if number != 4:
            keep(src, dst, number).wait()
    for slot in range(2):
        pltpu.make_async_copy(pt.at[slot], pt_out.at[30 + slot], ps.at[slot]).wait()
    for slot in range(3):
        pltpu.make_async_copy(gst.at[slot], grad_piece(3 + slot), gs.at[slot]).wait()


def run_front(wh, w1, w2, tok, cot, meta, te, wa, ba):
    rows, cols = w1.shape
    part = tok.shape[1]
    length = 4 * part
    shape = jax.ShapeDtypeStruct
    vmem = pl.BlockSpec(memory_space=pltpu.VMEM)
    shared = shape((2, 2 * part, cols), LOW)
    single = shape((2, part, cols), F32)
    outs = (
        shape((2, 8, rows, cols), LOW),
        shape((2, 8 * rows, cols), LOW),
        shape((2, 8 * rows, cols), LOW),
        shape(tok.shape, LOW),
        shape(tok.shape, LOW),
        shared,
        shape((8, 3, length, 128), LOW),
        shape((32, length, part), LOW),
        shape((2, length, 384), LOW),
        single,
        single,
        shared,
        shared,
        shape((2, length, cols), LOW),
        shape((2, length, cols), LOW),
        shape((2, 8 * rows, cols), LOW),
    )
    small = (
        shape((64, rows), F32),
        shape((2, 8, cols), F32),
        shape((8, 128), F32),
        shape((8, 128), F32),
        shape((2, part, 128), F32),
        shape((2, 8, 128), F32),
    )
    three = DMA((3, 2, 2))
    return pl.pallas_call(
        front_kernel,
        out_shape=outs + small,
        in_specs=[ANY] * 5 + [vmem] * 4,
        out_specs=(ANY,) * len(outs) + (vmem,) * len(small),
        scratch_shapes=[
            pltpu.VMEM(tok.shape, LOW),
            pltpu.VMEM((2, 8 * rows, cols), LOW),
            pltpu.VMEM((2, 2 * part, cols), LOW),
            pltpu.VMEM((8, 3, length, 128), LOW),
            pltpu.VMEM((8, length, 128), LOW),
            pltpu.VMEM((2, length, part), LOW),
            pltpu.VMEM((3, 384, cols), LOW),
            pltpu.VMEM((2, length, 384), LOW),
            pltpu.VMEM((2, part, cols), LOW),
            pltpu.VMEM((2, part, cols), LOW),
            pltpu.VMEM((2, part, cols), F32),
            pltpu.VMEM((2, part, cols), F32),
            pltpu.VMEM((2, 2 * part, cols), LOW),
            pltpu.VMEM(tok.shape, LOW),
            pltpu.VMEM((2, 2 * part, cols), LOW),
            pltpu.VMEM((2, 8 * rows, cols), LOW),
            pltpu.VMEM((2, length, cols), LOW),
            pltpu.VMEM((2, length, cols), LOW),
            pltpu.VMEM((16, cols), F32),
            pltpu.VMEM((8, 8, 128), F32),
            pltpu.VMEM((8, 8, rows), F32),
            pltpu.VMEM((8, 8, wa.shape[1]), F32),
            pltpu.VMEM((8, 8, wa.shape[1]), F32),
            pltpu.VMEM((8, wa.shape[1]), F32),
            pltpu.VMEM((4, 8, wa.shape[1]), F32),
            pltpu.VMEM((2, 8, 128), F32),
            DMA((3, 3)),
            three,
            three,
            DMA((2, 3, 2, 2)),
            DMA((2, 3, 2, 2)),
            three,
            three,
            DMA((2, 2)),
            DMA((2, 2)),
            DMA((8,)),
            DMA((8,)),
            DMA((14,)),
            DMA((2,)),
            DMA((3,)),
            DMA((8,)),
            DMA((8,)),
            DMA((8,)),
            DMA((8,)),
            DMA((8,)),
            DMA((8,)),
            DMA((2, 2)),
            DMA((4,)),
        ],
        compiler_params=pltpu.CompilerParams(
            collective_id=0, has_side_effects=True, vmem_limit_bytes=60 << 20
        ),
    )(wh, w1, w2, tok, cot, meta, te, wa, ba)


def back_kernel(
    act_in,
    gp_in,
    dm_in,
    h2_in,
    w1_in,
    w2_in,
    gf_in,
    x1_in,
    br_in,
    x_in,
    g_in,
    h1_in,
    qkv_in,
    pt_in,
    att_in,
    head_in,
    mod,
    gains,
    keep_col,
    select,
    cond,
    out_tok,
    out_dtok,
    rz,
    pq,
    gf1,
    g_ada,
    g_bias,
    sums,
    db,
    yb,
    zb,
    sb,
    sm,
    rb,
    rm,
    ob,
    r1,
    rn,
    stage,
    dc,
    nr,
    da,
    s1s,
    s1r,
    nss,
    nsr,
    zss,
    zsr,
    pqr,
    es,
    er,
    ts,
    tr,
    ls,
    gs,
    ps,
    dcs,
    dcr,
    das,
    dar,
):
    at = Place()
    dp, line, core, half = at.dp, at.line, at.core, at.half
    lane = line % 2
    rows_u = stage.shape[1]
    local = {}
    sib = at.base + 1 - core
    scale_q = HD ** (-0.5)
    factor = HD ** (-0.5) * LOG2E

    def load(src, dst, number):
        return pltpu.make_async_copy(src, dst, ls.at[number])

    def exchange(src, dst, number):
        return remote(src, dst, es.at[number], er.at[number], sib, line)

    def grad_ref(u, zi, row):
        here = pl.ds(pl.multiple_of(row * rows_u, 16), rows_u)
        return (local.get("g0"), gf1, gf_in)[u].at[zi, here]

    def base_of(which):
        return at.base_x + which * (at.base_y - at.base_x)

    def near_of(which):
        return at.dp_x + which * (at.dp_y - at.dp_x)

    def far_send(u, zi, o):
        return remote(
            grad_ref(u, zi, at.base_far + o),
            r1.at[u, zi, o],
            s1s.at[u, zi, o],
            s1r.at[u, zi, o],
            near_of(o),
            line,
        )

    def plain_send(u, zi, o):
        return remote(
            grad_ref(u, zi, base_of(o) + o),
            rn.at[o, u, zi, o],
            nss.at[o, u, zi, o],
            nsr.at[o, u, zi, o],
            near_of(o),
            line,
        )

    def relay_send(u, zi, o):
        return remote(
            r1.at[u, zi, o],
            rn.at[1 - o, u, zi, o],
            nss.at[1 - o, u, zi, o],
            nsr.at[1 - o, u, zi, o],
            near_of(1 - o),
            line,
        )

    def fetch(u, zi, o, which):
        row = (base_of(1 - o), at.base)[which] + o
        slot = 2 * which + o
        return pltpu.make_async_copy(grad_ref(u, zi, row), stage.at[slot], gs.at[slot])

    def own_term(u, zi, o, which):
        if u == 0:
            return grad_ref(u, zi, (base_of(1 - o), at.base)[which] + o)
        return stage.at[2 * which + o]

    def relay(u, zi, o):
        far_send(u, zi, o).wait_recv()
        if u:
            fetch(u, zi, o, 0).wait()
        ref = own_term(u, zi, o, 0)
        r1[u, zi, o] = (r1[u, zi, o].astype(F32) + ref[...].astype(F32)).astype(LOW)
        relay_send(u, zi, o).start()

    near_half = half == core
    edge = jnp.logical_or(line == 0, line == 3)
    outer = jnp.logical_and(jnp.logical_not(near_half), edge)
    inner = jnp.logical_and(jnp.logical_not(near_half), jnp.logical_not(edge))

    def column_send(u, zi, o, slot):
        return remote(
            rn.at[0, u, zi, o],
            rz.at[u, slot],
            zss.at[u, zi, o],
            zsr.at[u, slot],
            at.base + o,
            2 * core + zi,
        )

    def settle(u, zi, o):
        for which in range(2):
            there = rn.at[which, u, zi, o]
            pltpu.make_async_copy(there, there, nsr.at[which, u, zi, o]).wait()
        if u:
            fetch(u, zi, o, 1).wait()
        ref = own_term(u, zi, o, 1)
        total = rn[0, u, zi, o].astype(F32) + rn[1, u, zi, o].astype(F32)
        rn[0, u, zi, o] = (total + ref[...].astype(F32)).astype(LOW)
        here = jnp.logical_and(core == o, line == 2 * core + zi)

        @pl.when(here)
        def _():
            pltpu.make_async_copy(rn.at[0, u, zi, o], rz.at[u, lane], zsr.at[u, lane]).start()

        @pl.when(jnp.logical_and(near_half, jnp.logical_not(here)))
        def _():
            column_send(u, zi, o, lane).start()

        @pl.when(outer)
        def _():
            remote(
                rn.at[0, u, zi, o],
                pq.at[u, zi, o],
                zss.at[u, zi, o],
                pqr.at[u, zi, o],
                dp,
                line + 1 - 2 * half,
            ).start()

    def merge(u, zi, o):
        @pl.when(inner)
        def _():
            pltpu.make_async_copy(pq.at[u, zi, o], pq.at[u, zi, o], pqr.at[u, zi, o]).wait()
            copy = pltpu.make_async_copy(pq.at[u, zi, o], stage.at[o], gs.at[o])
            copy.start()
            copy.wait()
            total = rn[0, u, zi, o].astype(F32) + stage[o].astype(F32)
            rn[0, u, zi, o] = total.astype(LOW)
            column_send(u, zi, o, 2).start()

    def settled(u, zi, o):
        here = jnp.logical_and(core == o, line == 2 * core + zi)

        @pl.when(jnp.logical_not(here))
        def _():
            column_send(u, zi, o, 0).wait_send()

    def finish(u):
        for source in range(3):
            ref = rz.at[u, source]
            pltpu.make_async_copy(ref, ref, zsr.at[u, source]).wait()

    def fetch_pair(u, zi, which):
        for o in range(2):
            fetch(u, zi, o, which).start()

    def relay_pair(u, zi):
        for o in range(2):
            relay(u, zi, o)

    def settle_pair(u, zi):
        for o in range(2):
            settle(u, zi, o)

    def merge_pair(u, zi):
        for o in range(2):
            merge(u, zi, o)

    def give_back(block, kind, start):
        dst = (out_tok, out_dtok)[kind].at[lane]
        there = 2 * core + block
        here = jnp.logical_and(half == core, there == line)
        send, recv = ts.at[kind, block], tr.at[kind, lane]
        if start:
            move(ob.at[block], dst, send, recv, at.base + half, there, here)
        else:

            @pl.when(here)
            def _():
                pltpu.make_async_copy(ob.at[block], dst, recv).wait()

            @pl.when(jnp.logical_not(here))
            def _():
                remote(ob.at[block], dst, send, recv, at.base + half, there).wait_send()

    def mlp_phase(act, gp, w1v, w2v, dm, h2, gst):
        pairs = ((dm_in, dm), (w2_in, w2v), (gp_in, gp), (h2_in, h2), (w1_in, w1v), (act_in, act))
        copies = [load(src, dst, number) for number, (src, dst) in enumerate(pairs)]
        for copy in copies[0:3]:
            copy.start()
        at.barrier()
        for zi in range(2):
            for o in range(2):
                far_send(2, zi, o).start()
            for o in range(2):
                plain_send(2, zi, o).start()
        length = act.shape[1]
        mid = length // 2

        def weight_grad(u, left, right):
            def column_half(zi, _):
                def piece(tile, _):
                    cols = pl.ds(pl.multiple_of(384 * tile, 128), 384)
                    value = dot_tn(left[0, :, cols], right[zi, 0:mid, :])
                    value = value + dot_tn(left[1, :, cols], right[zi, mid:length, :])
                    gst[tile] = value.astype(LOW)
                    rows = pl.ds(pl.multiple_of(384 * tile, 128), 384)
                    pltpu.make_async_copy(gst.at[tile], gf1.at[zi, rows], gs.at[tile]).start()
                    return 0

                lax.fori_loop(0, 3, piece, 0)
                for tile in range(3):
                    rows = pl.ds(384 * tile, 384)
                    pltpu.make_async_copy(gst.at[tile], gf1.at[zi, rows], gs.at[tile]).wait()
                for o in range(2):
                    far_send(u, zi, o).start()
                for o in range(2):
                    plain_send(u, zi, o).start()
                return 0

            lax.fori_loop(0, 2, column_half, 0)

        for copy in copies[0:3]:
            copy.wait()
        for copy in copies[3:6]:
            copy.start()

        def down(step, _):
            tile, zi = step // 2, step % 2
            rows = dm[tile // 2, pl.ds(pl.multiple_of((tile % 2) * 256, 256), 256), :]
            to_row = pl.ds(pl.multiple_of(tile * 256, 256), 256)
            value = dot_nn(rows, w2v[zi]) * gp[zi, to_row, :].astype(F32)
            gp[zi, to_row, :] = value.astype(LOW)
            return 0

        lax.fori_loop(0, 8, down, 0)
        def partial(left, right, send, recv, own, number):
            def part(step, _):
                tile = (2 * (1 - core) + step) % 4
                rows = pl.ds(pl.multiple_of(tile * 256, 256), 256)
                value = dot_nt(left[0, rows, :], right[0])
                value = value + dot_nt(left[1, rows, :], right[1])

                @pl.when(step < 2)
                def _():
                    send[step] = value.astype(LOW)
                    exchange(send.at[step], recv.at[step], number + step).start()

                @pl.when(step >= 2)
                def _():
                    own[step - 2] = value

                return 0

            lax.fori_loop(0, 4, part, 0)

        for copy in copies[3:6]:
            copy.wait()
        partial(gp, w1v, sb, rb, yb, 0)
        weight_grad(1, h2, gp)
        fetch_pair(2, 0, 0)
        partial(act, w2v, sm, rm, zb, 2)
        relay_pair(2, 0)
        fetch_pair(2, 1, 0)

    cols = gf1.shape[2]
    length = act_in.shape[1]
    mid = length // 2
    pl.run_scoped(
        mlp_phase,
        pltpu.VMEM((2, length, cols), LOW),
        pltpu.VMEM((2, length, cols), LOW),
        pltpu.VMEM((2, 8 * rows_u, cols), LOW),
        pltpu.VMEM((2, 8 * rows_u, cols), LOW),
        pltpu.VMEM((2, mid, cols), LOW),
        pltpu.VMEM((2, mid, cols), LOW),
        pltpu.VMEM((3, 384, cols), LOW),
    )
    def attention_phase(w0, h1, qkv, pt, dpk, do, g0, xb, gb, acc):
        local["g0"] = g0
        pairs = (
            (head_in, w0),
            (qkv_in, qkv),
            (att_in, dpk.at[:, :, 0:384]),
            (h1_in, h1),
        )
        early = [load(src, dst, number) for number, (src, dst) in enumerate(pairs)]

        def rows_in(block):
            return (
                load(x1_in.at[block], xb.at[0], 5),
                load(br_in.at[block], xb.at[1], 6),
                load(g_in.at[block], gb, 7),
            )

        for copy in rows_in(0):
            copy.start()
        for copy in early:
            copy.start()

        def probs_in(number):
            slot = number % 2
            return pltpu.make_async_copy(pt_in.at[number], pt.at[slot], ps.at[slot])

        probs_in(0).start()
        fetch_pair(2, 0, 1)

        for block in range(2):
            for copy in rows_in(block):
                if block:
                    copy.start()
            for copy in rows_in(block):
                copy.wait()
            exchange(sb.at[block], rb.at[block], block).wait_recv()
            exchange(sm.at[block], rm.at[block], 2 + block).wait_recv()
            gate1, scale2 = mod[block, 2:3, :], 1.0 + mod[block, 4:5, :]
            gate2 = mod[block, 5:6, :]

            def norm_second(step, sums_now):
                at_row = pl.ds(pl.multiple_of(step * 128, 128), 128)
                grad = gb[at_row, :].astype(F32)
                first = xb[0, at_row, :]
                d_second = yb[block, at_row, :] + rb[block, at_row, :].astype(F32)
                kept = keep_col[block, at_row, 0:1] * (
                    zb[block, at_row, :] + rm[block, at_row, :].astype(F32)
                )
                ob[block, at_row, :] = (first + gate2 * kept).astype(LOW)
                normed, spread = layer_norm(first)
                d_first = grad + norm_back(d_second * scale2, normed, spread)
                yb[block, at_row, :] = d_first
                to_row = pl.ds(pl.multiple_of(block * 256 + step * 128, 128), 128)
                db[core, to_row, :] = (gate1 * d_first).astype(LOW)
                terms = (d_first * xb[1, at_row, :], d_second, d_second * normed, grad * kept)
                return tuple(
                    now + jnp.sum(term, axis=0, keepdims=True) for now, term in zip(sums_now, terms)
                )

            zero = jnp.zeros((1, gb.shape[1]), F32)
            totals = lax.fori_loop(0, 2, norm_second, (zero,) * 4)
            for place, value in zip((2, 3, 4, 5), totals):
                sums[block, place : place + 1, :] = value
            part = db.at[core, pl.ds(block * 256, 256)]
            exchange(part, part, 4 + block).start()
            give_back(block, 0, True)

        for copy in early[0:3]:
            copy.wait()

        relay_pair(2, 1)
        fetch_pair(1, 0, 0)

        def to_heads(step, _):
            @pl.when(step >= 2)
            def _():
                part = db.at[1 - core, pl.ds(pl.multiple_of((step - 2) * 256, 256), 256)]
                pltpu.make_async_copy(part, part, er.at[4 + step - 2]).wait()

            tile = (2 * core + step) % 4
            rows = db[tile // 2, pl.ds(pl.multiple_of((tile % 2) * 256, 256), 256), :]
            to_row = pl.ds(pl.multiple_of(tile * 256, 256), 256)
            narrow = lanes(256) < HD
            for zi in range(2):
                value = dot_nn(rows, w0[zi, :, 768:1152])
                for number in range(4):
                    piece = jnp.where(narrow, window(value, 96 + HD * number), 0.0)
                    head = zi * 4 + number
                    do[head, to_row, :] = (piece * gains[head : head + 1, :]).astype(LOW)
            return 0

        lax.fori_loop(0, 4, to_heads, 0)
        def proj_grad(number, _):
            zi, tile = number // 3, number % 3
            some = pl.ds(pl.multiple_of(384 * tile, 128), 384)
            value = dot_tn(db[0, :, some], dpk[zi, 0:mid, 0:384])
            value = value + dot_tn(db[1, :, some], dpk[zi, mid:length, 0:384])
            g0[zi, some, 768:1152] = value.astype(LOW)
            return 0

        lax.fori_loop(0, 6, proj_grad, 0)

        def attend(head, _):
            step_of = (
                lambda: (relay_pair(1, 0), fetch_pair(1, 1, 0)),
                lambda: (relay_pair(1, 1), settle_pair(2, 0), fetch_pair(2, 1, 1)),
                lambda: (settle_pair(2, 1), fetch_pair(1, 0, 1)),
                lambda: (settle_pair(1, 0), merge_pair(2, 0), fetch_pair(1, 1, 1)),
                lambda: (settle_pair(1, 1), merge_pair(2, 1)),
                lambda: (merge_pair(1, 0),),
                lambda: (merge_pair(1, 1),),
                lambda: (relay_pair(0, 0),),
            )
            for place, task in enumerate(step_of):

                @pl.when(head == place)
                def _():
                    task()

            acc[...] = jnp.zeros_like(acc)

            def tile_step(tile, _):
                number = 4 * head + tile
                rows = pl.ds(pl.multiple_of(tile * 256, 256), 256)

                @pl.when(number < 31)
                def _():
                    probs_in(number + 1).start()

                probs_in(number).wait()
                grad = do[head, rows, :]
                probs = pt[number % 2]
                acc[1] += dot_nn(probs, grad)
                d_probs = dot_nt(qkv[head, 2], grad)
                wide = probs.astype(F32)
                inner = jnp.sum(wide * d_probs, axis=0, keepdims=True)
                d_scores = (wide * (d_probs - inner)).astype(LOW)
                acc[0] += dot_nn(d_scores, qkv[head, 0, rows, :])
                qkv[head, 0, rows, :] = (dot_tn(d_scores, qkv[head, 1]) * scale_q).astype(LOW)
                return 0

            lax.fori_loop(0, 4, tile_step, 0)
            qkv[head, 1] = (acc[0] * scale_q).astype(LOW)
            qkv[head, 2] = acc[1].astype(LOW)
            return 0

        early[3].wait()

        def send_head(zi):
            def head_grad(tile, _):
                some = pl.ds(pl.multiple_of(384 * tile, 128), 384)
                value = dot_tn(h1[0, :, some], dpk[zi, 0:mid, :])
                value = value + dot_tn(h1[1, :, some], dpk[zi, mid:length, :])
                g0[zi, some, 0:768] = value[:, 0:768].astype(LOW)
                both = value[:, 768:896] + g0[zi, some, 768:896].astype(F32)
                g0[zi, some, 768:896] = both.astype(LOW)
                return 0

            lax.fori_loop(0, 3, head_grad, 0)
            for o in range(2):
                far_send(0, zi, o).start()
            for o in range(2):
                plain_send(0, zi, o).start()

        def column_half(zi, _):
            def one_head(number, _):
                return attend(4 * zi + number, 0)

            lax.fori_loop(0, 4, one_head, 0)

            def lay(step, _):
                rows = pl.ds(pl.multiple_of(step * 128, 128), 128)
                narrow = lanes(128) < HD
                parts = [
                    jnp.where(narrow, qkv[zi * 4 + n // 3, n % 3, rows, :].astype(F32), 0.0)
                    for n in range(12)
                ]
                for tile, value in enumerate(pack(parts, 0, 7)):
                    dpk[zi, rows, 128 * tile : 128 * tile + 128] = value.astype(LOW)
                return 0

            lax.fori_loop(0, 8, lay, 0)

            @pl.when(zi == 0)
            def _():
                send_head(0)

            return 0

        lax.fori_loop(0, 2, column_half, 0)

        for block in range(2):
            load(x_in.at[block], rm.at[block], 5 + block).start()
        for block in range(2):
            exchange(sb.at[block], rb.at[block], block).wait_send()
        for step in range(4):
            tile = (2 * (1 - core) + step) % 4
            rows = pl.ds(pl.multiple_of(tile * 256, 256), 256)
            value = dot_nt(dpk[0, rows, :], w0[0, :, 0:896])
            value = value + dot_nt(dpk[1, rows, :], w0[1, :, 0:896])
            if step < 2:
                sb[step] = value.astype(LOW)
                exchange(sb.at[step], rb.at[step], 6 + step).start()
            else:
                zb[step - 2] = value
        for block in range(2):
            give_back(block, 0, False)
            load(x_in.at[block], rm.at[block], 5 + block).wait()
            exchange(sb.at[block], rb.at[block], 6 + block).wait_recv()
            scale1 = 1.0 + mod[block, 1:2, :]

            def norm_first(step, sums_now):
                at_row = pl.ds(pl.multiple_of(step * 128, 128), 128)
                d_norm = zb[block, at_row, :] + rb[block, at_row, :].astype(F32)
                normed, spread = layer_norm(rm[block, at_row, :].astype(F32))
                d_input = yb[block, at_row, :] + norm_back(d_norm * scale1, normed, spread)
                ob[block, at_row, :] = d_input.astype(LOW)
                terms = (d_norm, d_norm * normed)
                return tuple(
                    now + jnp.sum(term, axis=0, keepdims=True) for now, term in zip(sums_now, terms)
                )

            zero = jnp.zeros((1, gb.shape[1]), F32)
            totals = lax.fori_loop(0, 2, norm_first, (zero,) * 2)
            for place, value in zip((0, 1), totals):
                sums[block, place : place + 1, :] = value

        blocks = []
        for number in range(6):
            value = select[0][:, 0:1] * sums[0, number : number + 1, :]
            blocks.append(value + select[1][:, 0:1] * sums[1, number : number + 1, :])
        chunks = to_chunks(*blocks[0:3]) + to_chunks(*blocks[3:6])
        for number in range(4):
            dc[number] = chunks[number]

        def each_chunk(start):
            for number in range(4):
                here = jnp.logical_and(half == core, line == number)
                dst, send, recv = nr.at[lane, core], dcs.at[number], dcr.at[lane, core]
                if start:
                    move(dc.at[number], dst, send, recv, at.base + half, number, here)
                else:

                    @pl.when(jnp.logical_not(here))
                    def _():
                        remote(dc.at[number], dst, send, recv, at.base + half, number).wait_send()

        def each_row(start):
            for step in range(1, 8):
                other = (dp + step) % 8
                copy = remote(da.at[dp], da.at[dp], das.at[step], dar.at[dp], other, line)
                copy.start() if start else copy.wait_send()

        each_chunk(True)
        for block in range(2):
            give_back(block, 1, True)
        send_head(1)
        settle_pair(0, 0)
        relay_pair(0, 1)
        merge_pair(0, 0)

        settle_pair(0, 1)
        for zi in range(2):
            for o in range(2):
                pltpu.make_async_copy(dc.at[0], nr.at[zi, o], dcr.at[zi, o]).wait()
        da[dp] = (nr[0, 0] + nr[0, 1]) + (nr[1, 0] + nr[1, 1])
        each_row(True)
        merge_pair(0, 1)
        for step in range(1, 8):
            other = (dp + step) % 8
            pltpu.make_async_copy(da.at[other], da.at[other], dar.at[other]).wait()
        value = jnp.concatenate([da[n] for n in range(8)], axis=0)
        g_bias[...] = jnp.sum(value, axis=0, keepdims=True)
        g_ada[...] = lax.dot_general(
            cond[...].astype(LOW).astype(F32), value, (((0,), (0,)), ((), ())), precision=HIGH, preferred_element_type=F32
        )
        for u in range(3):
            finish(u)

        each_chunk(False)
        each_row(False)
        for u in range(3):
            for zi in range(2):
                for o in range(2):
                    far_send(u, zi, o).wait_send()
                    plain_send(u, zi, o).wait_send()
                    relay_send(u, zi, o).wait_send()
                    settled(u, zi, o)
        for block in range(2):
            give_back(block, 1, False)
            exchange(sm.at[block], rm.at[block], 2 + block).wait_send()
            part = db.at[core, pl.ds(block * 256, 256)]
            exchange(part, part, 4 + block).wait_send()
            exchange(sb.at[block], rb.at[block], 6 + block).wait_send()
        for kind in range(2):
            dst = (out_tok, out_dtok)[kind]
            for slot in range(2):
                source = 2 * core + slot
                here = jnp.logical_and(source == line, half == core)

                @pl.when(jnp.logical_not(here))
                def _():
                    pltpu.make_async_copy(dst.at[slot], dst.at[slot], tr.at[kind, slot]).wait()

    pl.run_scoped(
        attention_phase,
        pltpu.VMEM((2, 8 * rows_u, cols), LOW),
        pltpu.VMEM((2, mid, cols), LOW),
        pltpu.VMEM((8, 3, length, 128), LOW),
        pltpu.VMEM((2, length, mid // 2), LOW),
        pltpu.VMEM((2, length, 896), LOW),
        pltpu.VMEM((8, length, 128), LOW),
        pltpu.VMEM((2, 8 * rows_u, cols), LOW),
        pltpu.VMEM((2, mid // 2, cols), F32),
        pltpu.VMEM((mid // 2, cols), LOW),
        pltpu.VMEM((2, length, 128), F32),
    )


def run_back(*args):
    rows, part = args[-1].shape[1], args[7].shape[1]
    length, cols = args[0].shape[1:]
    chunk = 6 * cols // 4
    shape = jax.ShapeDtypeStruct
    vmem = pl.BlockSpec(memory_space=pltpu.VMEM)
    outs = (
        shape((2, part, cols), LOW),
        shape((2, part, cols), LOW),
        shape((3, 3, rows, cols), LOW),
        shape((3, 2, 2, rows, cols), LOW),
        shape((2, 8 * rows, cols), LOW),
        shape((rows, chunk), F32),
        shape((1, chunk), F32),
    )
    three = DMA((3, 2, 2))
    low = pltpu.VMEM((2, part, cols), LOW)
    return pl.pallas_call(
        back_kernel,
        out_shape=outs,
        in_specs=[ANY] * 16 + [vmem] * 5,
        out_specs=(ANY,) * 5 + (vmem,) * 2,
        scratch_shapes=[
            pltpu.VMEM((2, 8, cols), F32),
            pltpu.VMEM((2, 2 * part, cols), LOW),
            pltpu.VMEM((2, part, cols), F32),
            pltpu.VMEM((2, part, cols), F32),
            low,
            low,
            low,
            low,
            low,
            pltpu.VMEM((3, 2, 2, rows, cols), LOW),
            pltpu.VMEM((2, 3, 2, 2, rows, cols), LOW),
            pltpu.VMEM((4, rows, cols), LOW),
            pltpu.VMEM((4, 8, chunk), F32),
            pltpu.VMEM((2, 2, 8, chunk), F32),
            pltpu.VMEM((8, 8, chunk), F32),
            three,
            three,
            DMA((2, 3, 2, 2)),
            DMA((2, 3, 2, 2)),
            three,
            DMA((3, 3)),
            three,
            DMA((8,)),
            DMA((8,)),
            DMA((2, 2)),
            DMA((2, 2)),
            DMA((8,)),
            DMA((4,)),
            DMA((2,)),
            DMA((4,)),
            DMA((2, 2)),
            DMA((8,)),
            DMA((8,)),
        ],
        compiler_params=pltpu.CompilerParams(
            collective_id=1, has_side_effects=True, vmem_limit_bytes=63 << 20
        ),
    )(*args)


def fast_body(
    tokens,
    time_embed,
    segments,
    micro_order,
    head_mask,
    group_mask,
    keep_route,
    w_qkv,
    w_proj,
    w_fc1,
    w_fc2,
    w_ada,
    b_ada,
    cotangent,
):
    width = tokens.shape[2]
    length = segments.shape[1]
    qcols = w_qkv.shape[1]
    swap = micro_order[:, None] == 1

    lines = jnp.concatenate(
        [
            jnp.where(swap, head_mask[1:2], head_mask[0:1]),
            jnp.where(swap, group_mask[1:2], group_mask[0:1]),
            segments[:, :: length // 4],
            jnp.zeros((2, 116), jnp.int32),
        ],
        axis=1,
    )
    meta = jnp.concatenate(
        [keep_route.reshape(4, 128), lines, jnp.zeros((2, 128), jnp.int32)], axis=0
    ).astype(jnp.float32)
    te = time_embed.reshape(8, 8, width // 8).transpose(1, 0, 2).astype(jnp.float32)
    whead = jnp.concatenate([w_qkv, w_proj], axis=1)
    (
        full_fc2,
        full_fc1,
        head_w,
        dealt,
        dealt_grad,
        h_first,
        qkv,
        probs,
        att,
        first,
        branch,
        h_second,
        d_mlp,
        act,
        slope,
        grad_fc2,
        cond,
        mod,
        gains,
        _,
        kept,
        select,
    ) = run_front(whead, w_fc1, w_fc2, tokens, cotangent, meta, te, w_ada, b_ada[None, :])
    result, d_input, grads, _, _, g_ada, g_bias = run_back(
        act,
        slope,
        d_mlp,
        h_second,
        full_fc1,
        full_fc2.reshape(full_fc1.shape),
        grad_fc2,
        first,
        branch,
        dealt,
        dealt_grad,
        h_first,
        qkv,
        probs,
        att,
        head_w,
        mod,
        gains,
        kept,
        select,
        cond,
    )
    total = jnp.sum(grads.astype(jnp.float32), axis=1)
    return (
        result,
        d_input,
        total[0, :, :qcols],
        total[0, :, qcols:],
        total[1],
        total[2],
        g_ada,
        g_bias[0],
    )


def solution(mesh):
    placed = (
        P("dp", "tensor", None),
        P("dp", None, None),
        P("dp", None),
        P("dp"),
        P("dp", "tensor"),
        P("dp", "tensor"),
        P("dp", "tensor"),
        P("dp", "tensor"),
        P("dp", "tensor"),
        P("dp", "tensor"),
        P("dp", "tensor"),
        P("dp", "tensor"),
        P("tensor"),
        P("dp", "tensor", None),
    )
    return jax.shard_map(
        fast_body if mesh.shape["dp"] == 8 and mesh.shape["tensor"] == 4 else body,
        mesh=mesh,
        in_specs=placed,
        out_specs=(
            P("dp", "tensor", None),
            P("dp", "tensor", None),
            P("dp", "tensor"),
            P("dp", "tensor"),
            P("dp", "tensor"),
            P("dp", "tensor"),
            P("dp", "tensor"),
            P("tensor"),
        ),
        check_vma=False,
    )
```
